32 devices in a mesh: col: 4 (over y, x), seq: 8 (over z, core).
Axes of the slice: x: 2, y: 2, z: 4, core: 2. Of those that a mesh axis runs over, the one named last changes fastest.
Arguments:
- tokens: bfloat16 [8, 512, 768], P('seq', 'col'), may hold values from -6 to 6
- offsets: int32 [2], replicated, may hold values from 0 to 1023
- band: int32 [512, 65], P('col'), may hold values 0 or 1
- col_counts: int32 [4], P('col'), may hold values from 32 to 128, as said below
- norm1_gain: bfloat16 [768], P('seq'), may hold values from 0.5 to 1.5
- norm1_shift: bfloat16 [768], P('seq'), may hold values from -4 to 4
- norm2_gain: bfloat16 [768], P('seq'), may hold values from 0.5 to 1.5
- norm2_shift: bfloat16 [768], P('seq'), may hold values from -4 to 4
- norm3_gain: bfloat16 [768], P('seq'), may hold values from 0.5 to 1.5
- norm3_shift: bfloat16 [768], P('seq'), may hold values from -4 to 4
- row_query: bfloat16 [768, 768], P('seq'), may hold values from -0.21875 to 0.21875
- row_key: bfloat16 [768, 768], P('seq'), may hold values from -0.21875 to 0.21875
- row_value: bfloat16 [768, 768], P('seq'), may hold values from -0.21875 to 0.21875
- row_output: bfloat16 [768, 768], P('seq'), may hold values from -0.875 to 0.875
- col_query: bfloat16 [768, 768], P('seq'), may hold values from -0.21875 to 0.21875
- col_key: bfloat16 [768, 768], P('seq'), may hold values from -0.21875 to 0.21875
- col_value: bfloat16 [768, 768], P('seq'), may hold values from -0.21875 to 0.21875
- col_output: bfloat16 [768, 768], P('seq'), may hold values from -0.3125 to 0.3125
- feed_in: bfloat16 [768, 3072], P('seq'), may hold values from -0.21875 to 0.21875
- feed_out: bfloat16 [3072, 768], P('seq'), may hold values from -0.109375 to 0.109375
- cotangent: bfloat16 [8, 512, 768], P('seq', 'col'), may hold values from -6 to 6
Outputs:
- output: bfloat16 [8, 512, 768], P('seq', 'col')
- entropy: float32 [], replicated
- input_grad: bfloat16 [8, 512, 768], P('seq', 'col')
- grad_norm1_gain: float32 [768], P('seq')
- grad_norm1_shift: float32 [768], P('seq')
- grad_norm2_gain: float32 [768], P('seq')
- grad_norm2_shift: float32 [768], P('seq')
- grad_norm3_gain: float32 [768], P('seq')
- grad_norm3_shift: float32 [768], P('seq')
- grad_row_query: float32 [768, 768], P('seq')
- grad_row_key: float32 [768, 768], P('seq')
- grad_row_value: float32 [768, 768], P('seq')
- grad_row_output: float32 [768, 768], P('seq')
- grad_col_query: float32 [768, 768], P('seq')
- grad_col_key: float32 [768, 768], P('seq')
- grad_col_value: float32 [768, 768], P('seq')
- grad_col_output: float32 [768, 768], P('seq')
- grad_feed_in: float32 [768, 3072], P('seq')
- grad_feed_out: float32 [3072, 768], P('seq')
The draws below stay inside these ranges and needn't reach their ends.
Inputs may be any that keep to these rules, and one draw needn't show every extreme that they name: `col_counts`: block 0 has 32 true columns and the last block all 128.
All inputs are finite; a program needn't handle non-finite values. No bound on the sum of `band` on one device may be relied on, other than what follows from the above.
Results may differ from the reference program's by a relative error of at most 0.035.
Values may be sent and summed in bfloat16 or wider, within the bound.
No kernel may reach another device: no remote copies, remote signals or barrier semaphores. Data moves between devices by JAX's collectives and lax.ppermute only.
A program may use at most 192 MiB of HBM per device.

```python
import math
import jax
import jax.numpy as jnp
from jax import lax

D = 768
HEADS = 12
HEAD_DIM = 64
FF = 3072
WINDOW = 32
COLS = 512
C_DEV = 128
R = 8
N_COL = 4


def draw_col_counts(key, part):
    quarter = C_DEV // 4
    steps_up = jnp.arange(N_COL, dtype=jnp.int32)
    base_count = quarter + steps_up * (C_DEV // 2) // max(N_COL - 1, 1)
    extra_count = jax.random.randint(key, (N_COL,), 0, quarter + 1, dtype=jnp.int32)
    counts_out = jnp.minimum(base_count + extra_count, C_DEV)
    counts_out = counts_out.at[0].set(quarter)
    counts_out = counts_out.at[N_COL - 1].set(C_DEV)
    return counts_out.astype(jnp.int32)


def touch_ends(array, stream_key, least, high):
    shape = array.shape
    place = [jax.random.randint(jax.random.fold_in(stream_key, axis), (), 0, shape[axis]) for axis in range(len(shape))]
    array = array.at[tuple(place)].set(least)
    longest = shape.index(max(shape))
    place[longest] = (place[longest] + 1) % shape[longest]
    return array.at[tuple(place)].set(high)


def block_levels(key, shape, split, least, high):
    factor_of, own = 1.0, jax.random.fold_in(key, 6)
    for position, shards_of in split:
        steps = jnp.exp(jax.random.uniform(jax.random.fold_in(own, position), (shards_of,), jnp.float32, least / len(split), high / len(split)))
        factor_of = factor_of * jnp.repeat(steps, shape[position] // shards_of).reshape([-1 if axis == position else 1 for axis in range(len(shape))])
    return factor_of


def gaussian(key, extent, spread, bound, cuts=(), kind=jnp.bfloat16):
    loudness = block_levels(key, extent, cuts, -0.22, 0.18) if cuts else 1.0
    values = jax.random.normal(key, extent, jnp.float32) * spread * loudness
    return jnp.minimum(jnp.maximum(values, -bound), bound).astype(kind)


def setup_inputs(seed: int = 0) -> dict:
    key_of = jax.random.split(jax.random.key(seed), 22)
    tokens = gaussian(key_of[0], (R, COLS, D), 1.0, 6.0, ((0, 8), (1, 4)))
    offsets = jax.random.randint(key_of[1], (2,), 0, 1024).astype(jnp.int32)
    band = touch_ends((jax.random.randint(key_of[2], (COLS, 2 * WINDOW + 1), 0, 4) < 3).astype(jnp.int32), jax.random.fold_in(key_of[2], 1), 0, 1)
    col_counts = draw_col_counts(jax.random.fold_in(key_of[21], 71), 0)
    norm1_gain = jnp.clip(1.0 + 0.1 * jax.random.normal(key_of[4], (D,), jnp.float32), 0.5, 1.5).astype(jnp.bfloat16)
    norm1_shift = gaussian(key_of[5], (D,), 0.3, 4.0, ((0, 8),))
    norm2_gain = jnp.clip(1.0 + 0.1 * jax.random.normal(key_of[6], (D,), jnp.float32), 0.5, 1.5).astype(jnp.bfloat16)
    norm2_shift = gaussian(key_of[7], (D,), 0.3, 4.0, ((0, 8),))
    norm3_gain = jnp.clip(1.0 + 0.1 * jax.random.normal(key_of[8], (D,), jnp.float32), 0.5, 1.5).astype(jnp.bfloat16)
    norm3_shift = gaussian(key_of[9], (D,), 0.3, 4.0, ((0, 8),))
    row_query = gaussian(key_of[10], (D, D), D ** -0.5, 0.21875, ((0, 8),))
    row_key = gaussian(key_of[11], (D, D), D ** -0.5, 0.21875, ((0, 8),))
    row_value = gaussian(key_of[12], (D, D), D ** -0.5, 0.21875, ((0, 8),))
    row_output = gaussian(key_of[13], (D, D), (D // 16) ** -0.5, 0.875, ((0, 8),))
    col_query = gaussian(key_of[14], (D, D), D ** -0.5, 0.21875, ((0, 8),))
    col_key = gaussian(key_of[15], (D, D), D ** -0.5, 0.21875, ((0, 8),))
    col_value = gaussian(key_of[16], (D, D), D ** -0.5, 0.21875, ((0, 8),))
    col_output = gaussian(key_of[17], (D, D), (4 * D // R) ** -0.5, 0.3125, ((0, 8),))
    feed_in = gaussian(key_of[18], (D, FF), D ** -0.5, 0.21875, ((0, 8),))
    feed_out = gaussian(key_of[19], (FF, D), FF ** -0.5, 0.109375, ((0, 8),))
    cotangent = gaussian(key_of[20], (R, COLS, D), 1.0, 6.0, ((0, 8), (1, 4)))
    return {"tokens": tokens, "offsets": offsets, "band": band, "col_counts": col_counts, "norm1_gain": norm1_gain, "norm1_shift": norm1_shift, "norm2_gain": norm2_gain, "norm2_shift": norm2_shift, "norm3_gain": norm3_gain, "norm3_shift": norm3_shift, "row_query": row_query, "row_key": row_key, "row_value": row_value, "row_output": row_output, "col_query": col_query, "col_key": col_key, "col_value": col_value, "col_output": col_output, "feed_in": feed_in, "feed_out": feed_out, "cotangent": cotangent}


@jax.custom_vjp
def low(v):
    return lax.optimization_barrier(v.astype(jnp.bfloat16)).astype(jnp.float32)

@jax.custom_vjp
def low_back(v):
    return v

def low_keep(v):
    return (low(v), None)

def low_pass(kept, grad):
    return (grad,)

def back_keep(v):
    return (v, None)

def back_low(kept, grad):
    return (low(grad),)
low.defvjp(low_keep, low_pass)
low_back.defvjp(back_keep, back_low)
entropy_weight = 8192.0
norm_eps = 1e-05

def layer_norm(inputs, norm_gain, norm_shift):
    average = lax.optimization_barrier(jnp.mean(inputs, axis=-1, keepdims=True))
    centred = inputs - average
    variance = lax.optimization_barrier(jnp.mean(centred * centred, axis=-1, keepdims=True))
    return centred * lax.rsqrt(variance + norm_eps) * norm_gain + norm_shift

def position_table(offsets, row_first, col_first, row_count, col_count, model_width):
    half_width = model_width // 2
    frequency = jnp.exp(-math.log(1000.0) * jnp.arange(half_width, dtype=jnp.float32) / half_width)
    col_place = (jnp.arange(col_count, dtype=jnp.int32) + col_first + offsets[1]).astype(jnp.float32)
    row_place = (jnp.arange(row_count, dtype=jnp.int32) + row_first + offsets[0]).astype(jnp.float32)
    col_wave = jnp.sin(col_place[:, None] * frequency[None, :])
    row_wave = jnp.sin(row_place[:, None] * frequency[None, :])
    col_full = jnp.broadcast_to(col_wave[None, :, :], (row_count, col_count, half_width))
    row_full = jnp.broadcast_to(row_wave[:, None, :], (row_count, col_count, half_width))
    return 0.5 * jnp.concatenate([col_full, row_full], axis=-1)

def softmax_entropy(scores, allowed, valid):
    masked = jnp.where(allowed[None], scores, -1000000000.0)
    largest = lax.optimization_barrier(jnp.max(masked, axis=-1, keepdims=True))
    powers = jnp.exp(masked - largest)
    row_total = lax.optimization_barrier(jnp.sum(powers, axis=-1, keepdims=True))
    probs_out = powers / row_total
    log_total = largest[..., 0] + jnp.log(row_total[..., 0])
    entropies = log_total - lax.optimization_barrier(jnp.sum(probs_out * jnp.where(allowed[None], scores, 0.0), axis=-1))
    return (probs_out, jnp.sum(entropies * valid[None, :]))

def plain_softmax(scores):
    largest = lax.optimization_barrier(jnp.max(scores, axis=-1, keepdims=True))
    powers = jnp.exp(scores - largest)
    return powers / lax.optimization_barrier(jnp.sum(powers, axis=-1, keepdims=True))

def project(activations, weight):
    return jnp.einsum('rci,ij->rcj', activations, weight, precision=lax.Precision.HIGHEST)

def column_block(blocks):
    queries_blk, keys_blk, values_blk = blocks
    raw_scores = jnp.einsum('rchd,schd->chrs', queries_blk, keys_blk, precision=lax.Precision.HIGHEST)
    col_scores = low_back(raw_scores * (1.0 / math.sqrt(HEAD_DIM)))
    col_probs = plain_softmax(col_scores)
    return jnp.einsum('chrs,schd->rchd', low(col_probs), values_blk, precision=lax.Precision.HIGHEST)

def split_blocks(values_in, block_cols):
    return values_in.reshape(R, COLS // block_cols, block_cols, HEADS, HEAD_DIM).transpose(1, 0, 2, 3, 4)

def forward(stream_in, offsets, allowed, valid, count_total, gain_one, shift_one, gain_two, shift_two, gain_three, shift_three, query_row, key_row, value_row, output_row, query_col, key_col, value_col, output_col, feed_up, feed_down):
    stream_zero = stream_in + position_table(offsets, 0, 0, R, COLS, D)
    normed_one = low(layer_norm(stream_zero, gain_one, shift_one))
    row_queries = low_back(low(project(normed_one, query_row))).reshape(R, COLS, HEADS, HEAD_DIM)
    row_keys = low_back(low(project(normed_one, key_row))).reshape(R, COLS, HEADS, HEAD_DIM)
    row_values = low_back(low(project(normed_one, value_row))).reshape(R, COLS, HEADS, HEAD_DIM)
    logits = jnp.einsum('rchd,rehd->hce', row_queries, row_keys, precision=lax.Precision.HIGHEST)
    row_scores = low_back(logits * (1.0 / math.sqrt(HEAD_DIM * R)))
    row_probs, ent_sum = softmax_entropy(row_scores, allowed, valid)
    row_mix = jnp.einsum('hce,rehd->rchd', low(row_probs), row_values, precision=lax.Precision.HIGHEST)
    row_mix = low_back(low(row_mix)).reshape(R, COLS, D)
    stream_one = stream_zero + low_back(project(row_mix, output_row))
    normed_two = low(layer_norm(stream_one, gain_two, shift_two))
    col_queries = low_back(low(project(normed_two, query_col)))
    col_keys = low_back(low(project(normed_two, key_col)))
    col_values = low_back(low(project(normed_two, value_col)))
    block_cols = 64
    mixed = lax.map(jax.checkpoint(column_block), (split_blocks(col_queries, block_cols), split_blocks(col_keys, block_cols), split_blocks(col_values, block_cols)))
    col_mix = mixed.transpose(1, 0, 2, 3, 4).reshape(R, COLS, D)
    col_mix = low_back(low(col_mix))
    stream_two = stream_one + low_back(project(col_mix, output_col))
    normed_three = low(layer_norm(stream_two, gain_three, shift_three))
    hidden_pre = low_back(project(normed_three, feed_up))
    hidden_act = low(jax.nn.gelu(hidden_pre, approximate=False))
    result = stream_two + low_back(project(hidden_act, feed_down))
    return (result, ent_sum / (HEADS * count_total))

def reference(tokens, offsets, band, col_counts, norm1_gain, norm1_shift, norm2_gain, norm2_shift, norm3_gain, norm3_shift, row_query, row_key, row_value, row_output, col_query, col_key, col_value, col_output, feed_in, feed_out, cotangent):
    columns = jnp.arange(COLS, dtype=jnp.int32)
    distance = columns[None, :] - columns[:, None]
    index_band = jnp.clip(distance + WINDOW, 0, 2 * WINDOW).astype(jnp.int32)
    picked = jnp.take_along_axis(band, index_band, axis=1)
    allowed = (jnp.abs(distance) <= WINDOW) & ((picked == 1) | (distance == 0))
    block_of = (columns // C_DEV).astype(jnp.int32)
    valid = (columns % C_DEV < col_counts[block_of]).astype(jnp.float32)
    count_total = jnp.sum(col_counts).astype(jnp.float32)
    params = tuple((item.astype(jnp.float32) for item in (norm1_gain, norm1_shift, norm2_gain, norm2_shift, norm3_gain, norm3_shift, row_query, row_key, row_value, row_output, col_query, col_key, col_value, col_output, feed_in, feed_out)))

    def loss_parts(stream_in, *weights):
        return forward(stream_in, offsets, allowed, valid, count_total, *weights)
    (result, entropy), pull_back = jax.vjp(loss_parts, tokens.astype(jnp.float32), *params)
    grads = pull_back((cotangent.astype(jnp.float32), jnp.asarray(entropy_weight, dtype=jnp.float32)))
    return (result.astype(jnp.bfloat16), entropy, grads[0].astype(jnp.bfloat16), grads[1], grads[2], grads[3], grads[4], grads[5], grads[6], grads[7], grads[8], grads[9], grads[10], grads[11], grads[12], grads[13], grads[14], grads[15], grads[16])
```

```python
from functools import partial
import math

import jax
import jax.numpy as jnp
from jax import lax
from jax.experimental import pallas as pl
from jax.experimental.pallas import tpu as pltpu
from jax.sharding import PartitionSpec as P

HEADS = 12
HEAD_DIM = 64
WINDOW = 32


entropy_weight = 8192.0
norm_eps = 1e-05


def with_halo(cells, sides, width):
    for axis, dim in sides:
        count = lax.axis_size(axis)
        ends = count - 1
        head = lax.slice_in_dim(cells, 0, width, axis=dim)
        tail = lax.slice_in_dim(cells, cells.shape[dim] - width, cells.shape[dim], axis=dim)
        cells = jnp.concatenate(
            [
                lax.ppermute(tail, axis, [(i, (i + 1) % count) for i in range(ends)]),
                cells,
                lax.ppermute(head, axis, [((i + 1) % count, i) for i in range(ends)]),
            ],
            axis=dim,
        )
    return cells


def layer_norm(inputs, norm_gain, norm_shift):
    average = jnp.mean(inputs, axis=-1, keepdims=True)
    centred = inputs - average
    variance = jnp.mean(centred * centred, axis=-1, keepdims=True)
    return centred * lax.rsqrt(variance + norm_eps) * norm_gain + norm_shift


def position_table(offsets, row_first, col_first, row_count, col_count, model_width):
    half_width = model_width // 2
    frequency = jnp.exp(-math.log(1000.0) * jnp.arange(half_width, dtype=jnp.float32) / half_width)
    col_place = (jnp.arange(col_count, dtype=jnp.int32) + col_first + offsets[1]).astype(
        jnp.float32
    )
    row_place = (jnp.arange(row_count, dtype=jnp.int32) + row_first + offsets[0]).astype(
        jnp.float32
    )
    col_wave = jnp.sin(col_place[:, None] * frequency[None, :])
    row_wave = jnp.sin(row_place[:, None] * frequency[None, :])
    col_full = jnp.broadcast_to(col_wave[None, :, :], (row_count, col_count, half_width))
    row_full = jnp.broadcast_to(row_wave[:, None, :], (row_count, col_count, half_width))
    return 0.5 * jnp.concatenate([col_full, row_full], axis=-1)


def softmax_entropy(scores, allowed, valid):
    masked = jnp.where(allowed[None], scores, -1000000000.0)
    largest = jnp.max(masked, axis=-1, keepdims=True)
    powers = jnp.exp(masked - largest)
    row_total = jnp.sum(powers, axis=-1, keepdims=True)
    probs_out = powers / row_total
    log_total = largest[..., 0] + jnp.log(row_total[..., 0])
    entropies = log_total - jnp.sum(probs_out * jnp.where(allowed[None], scores, 0.0), axis=-1)
    return (probs_out, jnp.sum(entropies * valid[None, :]))


def plain_softmax(scores):
    largest = jnp.max(scores, axis=-1, keepdims=True)
    powers = jnp.exp(scores - largest)
    return powers / jnp.sum(powers, axis=-1, keepdims=True)


def project(activations, weight):
    return jnp.einsum("rci,ij->rcj", activations, weight, preferred_element_type=jnp.float32)


def project_back(gradient, weight):
    return jnp.einsum("rcj,ij->rci", gradient, weight, preferred_element_type=jnp.float32)


def weight_grad(activations, gradient):
    return jnp.einsum("rci,rcj->ij", activations, gradient, preferred_element_type=jnp.float32)


def general_plan(
    tokens,
    offsets,
    band,
    col_counts,
    norm1_gain,
    norm1_shift,
    norm2_gain,
    norm2_shift,
    norm3_gain,
    norm3_shift,
    row_query,
    row_key,
    row_value,
    row_output,
    col_query,
    col_key,
    col_value,
    col_output,
    feed_in,
    feed_out,
    cotangent,
):
    rows_dev, cols_dev, model_width = tokens.shape
    total_rows = rows_dev * lax.axis_size("seq")
    total_cols = cols_dev * lax.axis_size("col")
    row_first = lax.axis_index("seq") * rows_dev
    col_first = lax.axis_index("col") * cols_dev
    count_here = col_counts[0].astype(jnp.float32)
    count_early = lax.psum(count_here, "col")
    params = (
        lax.all_gather(norm1_gain, "seq", axis=0, tiled=True),
        lax.all_gather(norm1_shift, "seq", axis=0, tiled=True),
        lax.all_gather(norm2_gain, "seq", axis=0, tiled=True),
        lax.all_gather(norm2_shift, "seq", axis=0, tiled=True),
        lax.all_gather(norm3_gain, "seq", axis=0, tiled=True),
        lax.all_gather(norm3_shift, "seq", axis=0, tiled=True),
        lax.all_gather(row_query, "seq", axis=0, tiled=True),
        lax.all_gather(row_key, "seq", axis=0, tiled=True),
        lax.all_gather(row_value, "seq", axis=0, tiled=True),
        lax.all_gather(row_output, "seq", axis=0, tiled=True),
        lax.all_gather(col_query, "seq", axis=0, tiled=True),
        lax.all_gather(col_key, "seq", axis=0, tiled=True),
        lax.all_gather(col_value, "seq", axis=0, tiled=True),
        lax.all_gather(col_output, "seq", axis=0, tiled=True),
        lax.all_gather(feed_in, "seq", axis=0, tiled=True),
        lax.all_gather(feed_out, "seq", axis=0, tiled=True),
    )
    gain_one = params[0].astype(jnp.float32)
    shift_one = params[1].astype(jnp.float32)
    gain_two = params[2].astype(jnp.float32)
    shift_two = params[3].astype(jnp.float32)
    gain_three = params[4].astype(jnp.float32)
    shift_three = params[5].astype(jnp.float32)
    query_row, key_row, value_row, output_row = (params[6], params[7], params[8], params[9])
    query_col, key_col, value_col, output_col = (params[10], params[11], params[12], params[13])
    feed_up, feed_down = (params[14], params[15])
    stream_zero = tokens.astype(jnp.float32) + position_table(
        offsets, row_first, col_first, rows_dev, cols_dev, model_width
    )
    normed_one, norm_back_one = jax.vjp(layer_norm, stream_zero, gain_one, shift_one)
    normed_one = normed_one.astype(jnp.bfloat16)
    row_queries = project(normed_one, query_row).astype(jnp.bfloat16)
    row_keys = project(normed_one, key_row).astype(jnp.bfloat16)
    row_values = project(normed_one, value_row).astype(jnp.bfloat16)
    extended = with_halo(jnp.stack([row_keys, row_values]), (("col", 2),), WINDOW)
    ext_cols = cols_dev + 2 * WINDOW
    queries_heads = row_queries.reshape(rows_dev, cols_dev, HEADS, HEAD_DIM)
    keys_ext = extended[0].reshape(rows_dev, ext_cols, HEADS, HEAD_DIM)
    values_ext = extended[1].reshape(rows_dev, ext_cols, HEADS, HEAD_DIM)
    partial_logits = jnp.einsum(
        "rchd,rehd->hce", queries_heads, keys_ext, preferred_element_type=jnp.float32
    )
    row_scale = 1.0 / math.sqrt(HEAD_DIM * total_rows)
    row_scores = lax.psum(partial_logits, "seq") * row_scale
    query_index = jnp.arange(cols_dev, dtype=jnp.int32)[:, None]
    key_index = jnp.arange(ext_cols, dtype=jnp.int32)[None, :]
    distance = key_index - query_index
    choose = jnp.arange(2 * WINDOW + 1, dtype=jnp.int32)
    matches = (distance[:, None, :] == choose[None, :, None]) & (band[:, :, None] == 1)
    key_global = col_first - WINDOW + key_index
    inside = (key_global >= 0) & (key_global < total_cols)
    allowed = (jnp.any(matches, axis=1) | (distance == WINDOW)) & inside
    valid = (jnp.arange(cols_dev, dtype=jnp.int32) < col_counts[0]).astype(jnp.float32)
    (row_probs, ent_part), ent_back = jax.vjp(
        lambda given: softmax_entropy(given, allowed, valid), row_scores
    )
    payload = ent_part[None]
    sums = lax.psum(payload, "col")
    entropy = sums[0] / (HEADS * count_early)
    row_probs_low = row_probs.astype(jnp.bfloat16)
    row_mix = jnp.einsum(
        "hce,rehd->rchd", row_probs_low, values_ext, preferred_element_type=jnp.float32
    )
    row_mix = row_mix.reshape(rows_dev, cols_dev, model_width).astype(jnp.bfloat16)
    stream_one = stream_zero + project(row_mix, output_row)
    normed_two, norm_back_two = jax.vjp(layer_norm, stream_one, gain_two, shift_two)
    normed_two = normed_two.astype(jnp.bfloat16)
    col_queries = project(normed_two, query_col).astype(jnp.bfloat16)
    col_keys = project(normed_two, key_col).astype(jnp.bfloat16)
    col_values = project(normed_two, value_col).astype(jnp.bfloat16)
    col_scale = 1.0 / math.sqrt(HEAD_DIM)
    keys_all, values_all = (
        lax.all_gather(col_keys, "seq", axis=0, tiled=True),
        lax.all_gather(col_values, "seq", axis=0, tiled=True),
    )
    col_heads_q = col_queries.reshape(rows_dev, cols_dev, HEADS, HEAD_DIM)
    keys_heads = keys_all.reshape(total_rows, cols_dev, HEADS, HEAD_DIM)
    values_heads = values_all.reshape(total_rows, cols_dev, HEADS, HEAD_DIM)
    col_raw = jnp.einsum(
        "rchd,schd->chrs", col_heads_q, keys_heads, preferred_element_type=jnp.float32
    )
    col_probs = plain_softmax(col_raw * col_scale)
    col_probs_low = col_probs.astype(jnp.bfloat16)
    col_mix = jnp.einsum(
        "chrs,schd->rchd", col_probs_low, values_heads, preferred_element_type=jnp.float32
    )
    col_mix = col_mix.reshape(rows_dev, cols_dev, model_width).astype(jnp.bfloat16)
    stream_two = stream_one + project(col_mix, output_col)
    normed_three, norm_back_three = jax.vjp(layer_norm, stream_two, gain_three, shift_three)
    normed_three = normed_three.astype(jnp.bfloat16)
    hidden_pre = project(normed_three, feed_up)
    hidden_act, gelu_back = jax.vjp(partial(jax.nn.gelu, approximate=False), hidden_pre)
    hidden_low = hidden_act.astype(jnp.bfloat16)
    output = (stream_two + project(hidden_low, feed_down)).astype(jnp.bfloat16)
    grad_feed_down = weight_grad(hidden_low, cotangent)
    grad_hidden = gelu_back(project_back(cotangent, feed_down))[0].astype(jnp.bfloat16)
    grad_feed_up = weight_grad(normed_three, grad_hidden)
    back_stream, grad_gain_three, grad_shift_three = norm_back_three(
        project_back(grad_hidden, feed_up)
    )
    grad_two = cotangent.astype(jnp.float32) + back_stream
    grad_two_low = grad_two.astype(jnp.bfloat16)
    grad_output_col = weight_grad(col_mix, grad_two_low)
    grad_mix_flat = project_back(grad_two_low, output_col).astype(jnp.bfloat16)
    grad_col_mix = grad_mix_flat.reshape(rows_dev, cols_dev, HEADS, HEAD_DIM)
    col_dprobs = jnp.einsum(
        "rchd,schd->chrs", grad_col_mix, values_heads, preferred_element_type=jnp.float32
    )
    col_dscores = col_probs * (col_dprobs - jnp.sum(col_probs * col_dprobs, axis=-1, keepdims=True))
    col_dscores = col_dscores.astype(jnp.bfloat16)
    grad_col_q = (
        jnp.einsum("chrs,schd->rchd", col_dscores, keys_heads, preferred_element_type=jnp.float32)
        * col_scale
    )
    grad_col_q = grad_col_q.reshape(rows_dev, cols_dev, model_width).astype(jnp.bfloat16)
    row_count = lax.axis_size("seq") * rows_dev
    key_part = (
        jnp.einsum("chrs,rchd->schd", col_dscores, col_heads_q, preferred_element_type=jnp.float32)
        * col_scale
    )
    value_part = jnp.einsum(
        "chrs,rchd->schd", col_probs_low, grad_col_mix, preferred_element_type=jnp.float32
    )
    key_value_grads = lax.psum_scatter(
        jnp.concatenate(
            [
                key_part.reshape(row_count, cols_dev, model_width),
                value_part.reshape(row_count, cols_dev, model_width),
            ],
            axis=-1,
        ),
        "seq",
        scatter_dimension=0,
        tiled=True,
    )
    grad_col_k = key_value_grads[..., :model_width].astype(jnp.bfloat16)
    grad_col_v = key_value_grads[..., model_width:].astype(jnp.bfloat16)
    grad_query_col = weight_grad(normed_two, grad_col_q)
    grad_key_col = weight_grad(normed_two, grad_col_k)
    grad_value_col = weight_grad(normed_two, grad_col_v)
    back_input = (
        project_back(grad_col_q, query_col)
        + project_back(grad_col_k, key_col)
        + project_back(grad_col_v, value_col)
    )
    back_stream, grad_gain_two, grad_shift_two = norm_back_two(back_input)
    grad_one = grad_two + back_stream
    grad_one_low = grad_one.astype(jnp.bfloat16)
    grad_output_row = weight_grad(row_mix, grad_one_low)
    grad_row_mix = project_back(grad_one_low, output_row).astype(jnp.bfloat16)
    grad_row_mix = grad_row_mix.reshape(rows_dev, cols_dev, HEADS, HEAD_DIM)
    dprobs_part = jnp.einsum(
        "rchd,rehd->hce", grad_row_mix, values_ext, preferred_element_type=jnp.float32
    )
    row_dprobs = lax.psum(dprobs_part.astype(jnp.bfloat16), "seq").astype(jnp.float32)
    ent_cot = jnp.asarray(entropy_weight, dtype=jnp.float32) / (HEADS * count_early)
    row_dscores = ent_back((row_dprobs, ent_cot))[0].astype(jnp.bfloat16)
    grad_row_q = (
        jnp.einsum("hce,rehd->rchd", row_dscores, keys_ext, preferred_element_type=jnp.float32)
        * row_scale
    )
    grad_row_q = grad_row_q.reshape(rows_dev, cols_dev, model_width).astype(jnp.bfloat16)
    grad_keys_ext = (
        jnp.einsum("hce,rchd->rehd", row_dscores, queries_heads, preferred_element_type=jnp.float32)
        * row_scale
    )
    grad_values_ext = jnp.einsum(
        "hce,rchd->rehd", row_probs_low, grad_row_mix, preferred_element_type=jnp.float32
    )
    grad_ext = jnp.stack([grad_keys_ext, grad_values_ext]).reshape(
        2, rows_dev, ext_cols, model_width
    )
    rims = jnp.concatenate([grad_ext[:, :, :WINDOW], grad_ext[:, :, WINDOW + cols_dev :]], axis=2)
    returned = with_halo(rims.astype(jnp.bfloat16), (("col", 2),), WINDOW).astype(rims.dtype)
    interior = grad_ext[:, :, WINDOW : WINDOW + cols_dev]
    interior = interior.at[:, :, :WINDOW].add(returned[:, :, :WINDOW])
    interior = interior.at[:, :, cols_dev - WINDOW :].add(returned[:, :, 3 * WINDOW :])
    grad_row_k = interior[0].astype(jnp.bfloat16)
    grad_row_v = interior[1].astype(jnp.bfloat16)
    grad_query_row = weight_grad(normed_one, grad_row_q)
    grad_key_row = weight_grad(normed_one, grad_row_k)
    grad_value_row = weight_grad(normed_one, grad_row_v)
    back_input = (
        project_back(grad_row_q, query_row)
        + project_back(grad_row_k, key_row)
        + project_back(grad_row_v, value_row)
    )
    back_stream, grad_gain_one, grad_shift_one = norm_back_one(back_input)
    input_grad = (grad_one + back_stream).astype(jnp.bfloat16)
    shares = (
        lax.psum_scatter(
            grad_gain_one.astype(jnp.bfloat16), "seq", scatter_dimension=0, tiled=True
        ).astype(jnp.float32),
        lax.psum_scatter(
            grad_shift_one.astype(jnp.bfloat16), "seq", scatter_dimension=0, tiled=True
        ).astype(jnp.float32),
        lax.psum_scatter(
            grad_gain_two.astype(jnp.bfloat16), "seq", scatter_dimension=0, tiled=True
        ).astype(jnp.float32),
        lax.psum_scatter(
            grad_shift_two.astype(jnp.bfloat16), "seq", scatter_dimension=0, tiled=True
        ).astype(jnp.float32),
        lax.psum_scatter(
            grad_gain_three.astype(jnp.bfloat16), "seq", scatter_dimension=0, tiled=True
        ).astype(jnp.float32),
        lax.psum_scatter(
            grad_shift_three.astype(jnp.bfloat16), "seq", scatter_dimension=0, tiled=True
        ).astype(jnp.float32),
        lax.psum_scatter(
            grad_query_row.astype(jnp.bfloat16), "seq", scatter_dimension=0, tiled=True
        ).astype(jnp.float32),
        lax.psum_scatter(
            grad_key_row.astype(jnp.bfloat16), "seq", scatter_dimension=0, tiled=True
        ).astype(jnp.float32),
        lax.psum_scatter(
            grad_value_row.astype(jnp.bfloat16), "seq", scatter_dimension=0, tiled=True
        ).astype(jnp.float32),
        lax.psum_scatter(
            grad_output_row.astype(jnp.bfloat16), "seq", scatter_dimension=0, tiled=True
        ).astype(jnp.float32),
        lax.psum_scatter(
            grad_query_col.astype(jnp.bfloat16), "seq", scatter_dimension=0, tiled=True
        ).astype(jnp.float32),
        lax.psum_scatter(
            grad_key_col.astype(jnp.bfloat16), "seq", scatter_dimension=0, tiled=True
        ).astype(jnp.float32),
        lax.psum_scatter(
            grad_value_col.astype(jnp.bfloat16), "seq", scatter_dimension=0, tiled=True
        ).astype(jnp.float32),
        lax.psum_scatter(
            grad_output_col.astype(jnp.bfloat16), "seq", scatter_dimension=0, tiled=True
        ).astype(jnp.float32),
        lax.psum_scatter(
            grad_feed_up.astype(jnp.bfloat16), "seq", scatter_dimension=0, tiled=True
        ).astype(jnp.float32),
        lax.psum_scatter(
            grad_feed_down.astype(jnp.bfloat16), "seq", scatter_dimension=0, tiled=True
        ).astype(jnp.float32),
    )
    totals = (
        lax.psum(shares[0].astype(jnp.bfloat16), "col").astype(jnp.float32),
        lax.psum(shares[1].astype(jnp.bfloat16), "col").astype(jnp.float32),
        lax.psum(shares[2].astype(jnp.bfloat16), "col").astype(jnp.float32),
        lax.psum(shares[3].astype(jnp.bfloat16), "col").astype(jnp.float32),
        lax.psum(shares[4].astype(jnp.bfloat16), "col").astype(jnp.float32),
        lax.psum(shares[5].astype(jnp.bfloat16), "col").astype(jnp.float32),
        lax.psum(shares[6].astype(jnp.bfloat16), "col").astype(jnp.float32),
        lax.psum(shares[7].astype(jnp.bfloat16), "col").astype(jnp.float32),
        lax.psum(shares[8].astype(jnp.bfloat16), "col").astype(jnp.float32),
        lax.psum(shares[9].astype(jnp.bfloat16), "col").astype(jnp.float32),
        lax.psum(shares[10].astype(jnp.bfloat16), "col").astype(jnp.float32),
        lax.psum(shares[11].astype(jnp.bfloat16), "col").astype(jnp.float32),
        lax.psum(shares[12].astype(jnp.bfloat16), "col").astype(jnp.float32),
        lax.psum(shares[13].astype(jnp.bfloat16), "col").astype(jnp.float32),
        lax.psum(shares[14].astype(jnp.bfloat16), "col").astype(jnp.float32),
        lax.psum(shares[15].astype(jnp.bfloat16), "col").astype(jnp.float32),
    )
    return (
        output,
        entropy,
        input_grad,
        totals[0],
        totals[1],
        totals[2],
        totals[3],
        totals[4],
        totals[5],
        totals[6],
        totals[7],
        totals[8],
        totals[9],
        totals[10],
        totals[11],
        totals[12],
        totals[13],
        totals[14],
        totals[15],
    )


def kernel_call(body, outs, args, smem=(), anywhere=(), scratch=(), flops=0):
    out_shapes = [jax.ShapeDtypeStruct(shape, kind) for shape, kind in outs]
    moved = sum(item.size * item.dtype.itemsize for item in args) + sum(
        item.size * item.dtype.itemsize for item in out_shapes
    )
    in_specs = []
    for place in range(len(args)):
        if place in smem:
            in_specs.append(pl.BlockSpec(memory_space=pltpu.SMEM))
        elif place in anywhere:
            in_specs.append(pl.BlockSpec(memory_space=pl.ANY))
        else:
            in_specs.append(pl.BlockSpec(memory_space=pltpu.VMEM))
    return pl.pallas_call(
        body,
        out_shape=out_shapes,
        in_specs=in_specs,
        out_specs=[pl.BlockSpec(memory_space=pltpu.VMEM)] * len(outs),
        scratch_shapes=list(scratch),
        compiler_params=pltpu.CompilerParams(vmem_limit_bytes=48 << 20),
        cost_estimate=pl.CostEstimate(
            flops=int(flops), bytes_accessed=int(moved), transcendentals=0
        ),
    )(*args)


def dot(left, right):
    return jnp.dot(left, right, preferred_element_type=jnp.float32)


def dot_back(left, right):
    return lax.dot_general(
        left, right, (((1,), (1,)), ((), ())), preferred_element_type=jnp.float32
    )


def dot_tokens(left, right):
    return lax.dot_general(
        left, right, (((0,), (0,)), ((), ())), preferred_element_type=jnp.float32
    )


def unit_norm(inputs):
    centred = inputs - jnp.mean(inputs, axis=-1, keepdims=True)
    scale = lax.rsqrt(jnp.mean(centred * centred, axis=-1, keepdims=True) + norm_eps)
    return centred * scale, scale


def unit_norm_back(given, unit, scale, gain):
    scaled = given * gain
    first = jnp.mean(scaled, axis=-1, keepdims=True)
    second = jnp.mean(scaled * unit, axis=-1, keepdims=True)
    return scale * (scaled - first - unit * second)


def norm_sums(given, unit):
    return jnp.concatenate(
        [
            jnp.sum(given * unit, axis=0, keepdims=True),
            jnp.sum(given, axis=0, keepdims=True),
        ],
        axis=0,
    )


def head_mask(width, model_width):
    rows = lax.broadcasted_iota(jnp.int32, (HEADS * width, model_width), 0) // width
    lanes = lax.broadcasted_iota(jnp.int32, (HEADS * width, model_width), 1) // HEAD_DIM
    return rows == lanes


def spread_heads(block, mask):
    tiled = jnp.concatenate([block] * HEADS, axis=0)
    return jnp.where(mask, tiled, jnp.zeros_like(tiled))


def fold_heads(product, mask, width):
    kept = jnp.where(mask, product, 0.0)
    total = kept[:width]
    for head in range(1, HEADS):
        total = total + kept[head * width : (head + 1) * width]
    return total


def head_of_lane(model_width):
    rows = lax.broadcasted_iota(jnp.int32, (model_width, 128), 0) // HEAD_DIM
    lanes = lax.broadcasted_iota(jnp.int32, (model_width, 128), 1)
    return (rows == lanes).astype(jnp.bfloat16)


def per_head_sum(product, lane_heads):
    high = product.astype(jnp.bfloat16)
    rest = (product - high.astype(jnp.float32)).astype(jnp.bfloat16)
    return dot(high, lane_heads) + dot(rest, lane_heads)


def slot_span(spot_ref, side, slot, width):
    return pl.ds(pl.multiple_of((slot ^ spot_ref[side]) * width, width), width)


def window_rows(spot_ref, near_ref, left_ref, right_ref, which, slot, width):
    return jnp.concatenate(
        [
            left_ref[which, slot_span(spot_ref, 5, slot, width)],
            near_ref[which, slot * width : (slot + 1) * width],
            right_ref[which, slot_span(spot_ref, 6, slot, width)],
        ],
        axis=0,
    )


def half_of(values, core, width):
    return jnp.where(core == 0, values[:, :width], values[:, width:])


def fast_plan(
    tokens,
    offsets,
    band,
    col_counts,
    norms,
    row_weights,
    col_weights,
    feed_in,
    feed_out,
    cotangent,
):
    f32, bf16 = jnp.float32, jnp.bfloat16
    cols_dev, model = tokens.shape[1:]
    cols_axis, seqs = lax.axis_size("col"), lax.axis_size("seq")
    chips = seqs // 2
    width = cols_dev // chips
    toks = chips * width
    shard = model // seqs
    half = model // 2
    hidden = feed_out.shape[0] * seqs // cols_axis
    fold = HEADS * width
    span = 3 * width
    col_at = lax.axis_index("col")
    seq_at = lax.axis_index("seq")
    chip, core = seq_at // 2, seq_at % 2
    flip = col_at % 2

    def chunk_of(chip_index):
        return jnp.where(flip == 0, chip_index, chips - 1 - chip_index)

    chunk = chunk_of(chip)
    piece = col_at * chips + chunk

    def along_chips(values, step):
        return lax.ppermute(values, "seq", [(i, i ^ (2 * step)) for i in range(seqs)])

    def along_core(values):
        return lax.ppermute(values, "seq", [(i, i ^ 1) for i in range(seqs)])

    def along_cols(values, step):
        return lax.ppermute(values, "col", [(i, i ^ step) for i in range(cols_axis)])

    def place_of(piece_index, core_index):
        block, part = divmod(piece_index, chips)
        chip_index = part if block % 2 == 0 else chips - 1 - part
        return block * seqs + chip_index * 2 + core_index

    rightward = [
        (place_of(i, k), place_of(i + 1, k)) for i in range(cols_axis * chips - 1) for k in (0, 1)
    ]
    leftward = [(target, source) for source, target in rightward]

    def to_right(values):
        return lax.ppermute(values, ("col", "seq"), rightward)

    def to_left(values):
        return lax.ppermute(values, ("col", "seq"), leftward)

    steps = range(1, chips)
    col_steps = range(1, cols_axis)

    def turn_to(other):
        block, rest = other // chips, other % chips
        return chip ^ jnp.where(block % 2 == 0, rest, chips - 1 - rest)

    to_left_turn = turn_to(jnp.maximum(piece - 1, 0))
    to_right_turn = turn_to(jnp.minimum(piece + 1, cols_axis * chips - 1))
    spot = jnp.stack(
        [col_at, chip, core, chunk, col_counts[0], to_left_turn, to_right_turn]
    ).astype(jnp.int32)

    both = jnp.concatenate([tokens, cotangent], axis=0)

    def chunk_rows(values, index):
        return lax.dynamic_slice_in_dim(values, chunk_of(index) * width, width, axis=1)

    got = [chunk_rows(both, chip)] + [
        along_chips(chunk_rows(both, chip ^ step), step) for step in steps
    ]
    stream_in = jnp.concatenate([item[0] for item in got], axis=0)
    given_out = jnp.concatenate([item[1] for item in got], axis=0)

    norm_line = jnp.concatenate(
        list(norms)
        + [
            col_counts.astype(bf16),
            jnp.zeros((model - 6 * shard - 1,), bf16),
        ]
    )
    norm_tile = jnp.broadcast_to(norm_line[None, None], (cols_axis, 8, model))

    def gather_layer(weights, extra):
        own = jnp.stack(weights)
        if extra is not None:
            own = jnp.concatenate([own, extra], axis=1)
        mine = lax.dynamic_index_in_dim(own, col_at, axis=0, keepdims=False)
        rows = jnp.stack([along_chips(mine, step) for step in steps])
        near = [rows] + [along_cols(rows, step) for step in col_steps]
        own_pair = (own, along_core(own))
        near_pair = (near, [along_core(item) for item in near])
        return own_pair, near_pair

    def assemble_layer(own_pair, near_pair):
        def body(spot_ref, *refs):
            count = 2 * (1 + cols_axis)
            pieces, out_ref, sems = refs[:count], refs[count], refs[count + 1]
            at_col, at_chip, at_core = spot_ref[0], spot_ref[1], spot_ref[2]
            copies = []

            def move(source, matrix, from_chip, from_core):
                row = pl.multiple_of((from_chip * 2 + from_core) * shard, shard)
                copies.append(
                    pltpu.make_async_copy(
                        source, out_ref.at[matrix, pl.ds(row, shard)], sems.at[len(copies)]
                    )
                )
                copies[-1].start()

            for other in (0, 1):
                base = other * (1 + cols_axis)
                from_core = at_core ^ other
                for matrix in range(cols_axis):
                    move(pieces[base].at[matrix, pl.ds(0, shard)], matrix, at_chip, from_core)
                for step in range(cols_axis):
                    for hop in steps:
                        move(
                            pieces[base + 1 + step].at[hop - 1, pl.ds(0, shard)],
                            at_col ^ step,
                            at_chip ^ hop,
                            from_core,
                        )
            for copy in copies:
                copy.wait()

        args = [spot, own_pair[0], *near_pair[0], own_pair[1], *near_pair[1]]
        total = 2 * cols_axis * chips
        return kernel_call(
            body,
            [((cols_axis, model, model), bf16)],
            args,
            smem=(0,),
            anywhere=tuple(range(1, len(args))),
            scratch=[pltpu.SemaphoreType.DMA((total,))],
        )[0]

    row_own, row_near = gather_layer(row_weights, norm_tile)
    weights_row = assemble_layer(row_own, row_near)
    lines = jnp.stack(
        [
            line
            for side in (0, 1)
            for line in [row_own[side][0, shard]]
            + [row_near[side][0][step - 1, shard] for step in steps]
        ]
    )
    line_shard = jnp.stack(
        [(chip ^ step) * 2 + (core ^ side) for side in (0, 1) for step in range(chips)]
    )
    order = (jnp.arange(seqs)[:, None] == line_shard[None, :]).astype(bf16)
    ordered = jnp.dot(order, lines, preferred_element_type=f32)
    norm_rows = ordered[:, : 6 * shard].reshape(seqs, 6, shard).transpose(1, 0, 2)
    norm_rows = jnp.pad(norm_rows.reshape(6, model), ((0, 2), (0, 0)))
    count_total = col_counts[0].astype(f32)
    for step in col_steps:
        count_total = count_total + row_near[0][step][0, shard, 6 * shard].astype(f32)
    entropy_scale = jnp.reshape(entropy_weight / (HEADS * count_total), (1,))

    col_own, col_near = gather_layer(col_weights, None)
    weights_col = assemble_layer(col_own, col_near)

    part = feed_out.shape[0] // cols_axis
    feed_cols = lax.dynamic_slice_in_dim(
        feed_in.reshape(shard, seqs, feed_out.shape[0]), col_at * part, part, axis=2
    ).reshape(shard, hidden)
    feed_rows = lax.dynamic_slice_in_dim(feed_out, col_at * part, part, axis=0)
    feed_own = jnp.stack([feed_cols, feed_rows])
    feed_all = jnp.stack([feed_own] + [along_chips(feed_own, step) for step in steps])
    feed_other = along_core(feed_all)

    def assemble_feed():
        def body(spot_ref, near_ref, far_ref, out_ref, sems):
            at_chip, at_core = spot_ref[1], spot_ref[2]
            copies = []
            for other, ref in enumerate((near_ref, far_ref)):
                for hop in range(chips):
                    row = ((at_chip ^ hop) * 2 + (at_core ^ other)) * shard
                    for matrix in (0, 1):
                        copies.append(
                            pltpu.make_async_copy(
                                ref.at[hop, matrix],
                                out_ref.at[matrix, pl.ds(pl.multiple_of(row, shard), shard)],
                                sems.at[len(copies)],
                            )
                        )
                        copies[-1].start()
            for copy in copies:
                copy.wait()

        return kernel_call(
            body,
            [((2, model, hidden), bf16)],
            [spot, feed_all, feed_other],
            smem=(0,),
            anywhere=(1, 2),
            scratch=[pltpu.SemaphoreType.DMA((4 * chips,))],
        )[0]

    weights_feed = assemble_feed()
    given_near = [given_out] + [along_cols(given_out, step) for step in col_steps]

    half_width = model // 2
    frequency = jnp.exp(-math.log(1000.0) * jnp.arange(half_width, dtype=f32) / half_width)
    col_place = (jnp.arange(width, dtype=jnp.int32) + piece * width + offsets[1]).astype(f32)
    seq_slots = jnp.stack([(chip ^ step) * 2 + core for step in range(chips)])
    row_place = (seq_slots + offsets[0]).astype(f32)
    waves = 0.5 * jnp.sin(
        jnp.concatenate([col_place, row_place])[:, None] * frequency[None, :]
    )
    band_here = lax.dynamic_slice_in_dim(band, chunk * width, width, axis=0)
    query_index = jnp.arange(width, dtype=jnp.int32)[:, None]
    key_index = jnp.arange(span, dtype=jnp.int32)[None, :]
    distance = key_index - query_index
    choose = jnp.arange(2 * WINDOW + 1, dtype=jnp.int32)
    matches = (distance[:, None, :] == choose[None, :, None]) & (band_here[:, :, None] == 1)
    key_global = (piece - 1) * width + key_index
    inside = (key_global >= 0) & (key_global < cols_axis * cols_dev)
    allowed = ((jnp.any(matches, axis=1) | (distance == WINDOW)) & inside).astype(f32)

    def project_row(stream_ref, waves_ref, norm_ref, weight_ref, zero_ref, low_ref, q_ref, kv_ref):
        for slot in range(chips):
            rows = slice(slot * width, (slot + 1) * width)
            zero_ref[rows, :half] = stream_ref[rows, :half].astype(f32) + waves_ref[:width]
            zero_ref[rows, half:] = (
                stream_ref[rows, half:].astype(f32) + waves_ref[width + slot : width + slot + 1]
            )
        unit, _ = unit_norm(zero_ref[...])
        low = (unit * norm_ref[0:1] + norm_ref[1:2]).astype(bf16)
        low_ref[...] = low
        q_ref[...] = dot(low, weight_ref[0]).astype(bf16)
        kv_ref[0] = dot(low, weight_ref[1]).astype(bf16)
        kv_ref[1] = dot(low, weight_ref[2]).astype(bf16)

    big = 2.0 * toks * model * model
    stream_zero, normed_one, row_q, row_kv = kernel_call(
        project_row,
        [
            ((toks, model), f32),
            ((toks, model), bf16),
            ((toks, model), bf16),
            ((2, toks, model), bf16),
        ],
        [stream_in, waves, norm_rows, weights_row],
        flops=3 * big,
    )
    kv_left = to_right(row_kv)
    kv_right = to_left(row_kv)

    def tied_logits(spot_ref, q_ref, near_ref, left_ref, right_ref, out_ref):
        mask = head_mask(width, model)
        total = None
        for slot in range(chips):
            keys = window_rows(spot_ref, near_ref, left_ref, right_ref, 0, slot, width)
            spread = spread_heads(q_ref[slot * width : (slot + 1) * width], mask)
            term = dot_back(spread, keys)
            total = term if total is None else total + term
        out_ref[...] = total

    logits = kernel_call(
        tied_logits,
        [((fold, span), f32)],
        [spot, row_q, row_kv, kv_left, kv_right],
        smem=(0,),
        flops=chips * 2.0 * fold * model * span,
    )[0]
    logits_other = along_core(logits)
    row_scale = 1.0 / math.sqrt(HEAD_DIM * seqs)
    col_scale = 1.0 / math.sqrt(HEAD_DIM)

    def attend_row(
        spot_ref,
        logits_ref,
        other_ref,
        allowed_ref,
        near_ref,
        left_ref,
        right_ref,
        zero_ref,
        norm_ref,
        weight_ref,
        scores_ref,
        probs_ref,
        mix_ref,
        stream_ref,
        low_ref,
        entropy_ref,
    ):
        mask = head_mask(width, model)
        scores = (logits_ref[...] + other_ref[...]) * row_scale
        open_here = jnp.concatenate([allowed_ref[...]] * HEADS, axis=0) > 0.5
        masked = jnp.where(open_here, scores, -1000000000.0)
        largest = jnp.max(masked, axis=-1, keepdims=True)
        powers = jnp.exp(masked - largest)
        total = jnp.sum(powers, axis=-1, keepdims=True)
        probs = powers / total
        kept = jnp.where(open_here, scores, 0.0)
        entropies = largest + jnp.log(total) - jnp.sum(probs * kept, axis=-1, keepdims=True)
        rows = lax.broadcasted_iota(jnp.int32, (fold, 1), 0) % width
        entropies = jnp.where(rows + spot_ref[3] * width < spot_ref[4], entropies, 0.0)
        lanes = lax.broadcasted_iota(jnp.int32, (1, model), 1)
        found = jnp.sum(entropies, axis=0, keepdims=True)
        entropy_ref[...] = jnp.where((lanes == 0) & (spot_ref[2] == 0), found, 0.0)
        scores_ref[...] = kept
        probs_ref[...] = probs
        low_probs = probs.astype(bf16)
        for slot in range(chips):
            values = window_rows(spot_ref, near_ref, left_ref, right_ref, 1, slot, width)
            mix_ref[slot * width : (slot + 1) * width] = fold_heads(
                dot(low_probs, values), mask, width
            ).astype(bf16)
        stream = zero_ref[...] + dot(mix_ref[...], weight_ref[3])
        stream_ref[...] = stream
        unit, _ = unit_norm(stream)
        low_ref[...] = (unit * norm_ref[2:3] + norm_ref[3:4]).astype(bf16)

    scores, probs, row_mix, stream_one, normed_two, entropy_row = kernel_call(
        attend_row,
        [
            ((fold, span), f32),
            ((fold, span), f32),
            ((toks, model), bf16),
            ((toks, model), f32),
            ((toks, model), bf16),
            ((1, model), f32),
        ],
        [
            spot,
            logits,
            logits_other,
            allowed,
            row_kv,
            kv_left,
            kv_right,
            stream_zero,
            norm_rows,
            weights_row,
        ],
        smem=(0,),
        flops=chips * 2.0 * fold * model * span + big,
    )

    def project_col(low_ref, weight_ref, q_ref, kv_ref):
        low = low_ref[...]
        q_ref[...] = dot(low, weight_ref[0]).astype(bf16)
        kv_ref[0] = dot(low, weight_ref[1]).astype(bf16)
        kv_ref[1] = dot(low, weight_ref[2]).astype(bf16)

    col_q, col_kv = kernel_call(
        project_col,
        [((toks, model), bf16), ((2, toks, model), bf16)],
        [normed_two, weights_col],
        flops=3 * big,
    )
    kv_other = along_core(col_kv)

    def slot_rows(slot):
        return slice(slot * width, (slot + 1) * width)

    def attend_col(
        q_ref,
        near_ref,
        far_ref,
        one_ref,
        norm_ref,
        weight_ref,
        probs_ref,
        mix_ref,
        stream_ref,
        low_ref,
    ):
        lane_heads = head_of_lane(model)
        sides = (near_ref, far_ref)
        for slot in range(chips):
            query = q_ref[slot_rows(slot)].astype(f32)
            products = jnp.concatenate(
                [
                    query * sides[s // chips][0, slot_rows(s % chips)].astype(f32)
                    for s in range(seqs)
                ],
                axis=0,
            )
            found = per_head_sum(products, lane_heads) * col_scale
            parts = [found[s * width : (s + 1) * width] for s in range(seqs)]
            largest = parts[0]
            for item in parts[1:]:
                largest = jnp.maximum(largest, item)
            powers = [jnp.exp(item - largest) for item in parts]
            total = powers[0]
            for item in powers[1:]:
                total = total + item
            weights = jnp.concatenate([item / total for item in powers], axis=0)
            probs_ref[slot] = weights
            wide = dot_back(weights.astype(bf16), lane_heads)
            mixed = None
            for s in range(seqs):
                term = wide[s * width : (s + 1) * width] * sides[s // chips][
                    1, slot_rows(s % chips)
                ].astype(f32)
                mixed = term if mixed is None else mixed + term
            mix_ref[slot_rows(slot)] = mixed.astype(bf16)
        stream = one_ref[...] + dot(mix_ref[...], weight_ref[3])
        stream_ref[...] = stream
        unit, _ = unit_norm(stream)
        low_ref[...] = (unit * norm_ref[4:5] + norm_ref[5:6]).astype(bf16)

    col_probs, col_mix, stream_two, normed_three = kernel_call(
        attend_col,
        [
            ((chips, seqs * width, 128), f32),
            ((toks, model), bf16),
            ((toks, model), f32),
            ((toks, model), bf16),
        ],
        [col_q, col_kv, kv_other, stream_one, norm_rows, weights_col],
        flops=big + 6.0 * chips * seqs * width * model * 128,
    )
    low_near = [normed_three] + [along_cols(normed_three, step) for step in col_steps]

    def feed_main(a0, a1, a2, a3, d0, d1, d2, d3, weight_ref, act_ref, grad_ref, *back_refs):
        up, down = weight_ref[0], weight_ref[1]
        for step, (low_ref, given_ref) in enumerate(((a0, d0), (a1, d1), (a2, d2), (a3, d3))):
            pre = dot(low_ref[...], up)
            bell = 0.5 * (1.0 + lax.erf(pre * (0.5**0.5)))
            slope = bell + pre * jnp.exp(-0.5 * pre * pre) * ((0.5 / math.pi) ** 0.5)
            act_ref[step] = (pre * bell).astype(bf16)
            grad = (slope * dot_back(given_ref[...], down)).astype(bf16)
            grad_ref[step] = grad
            back_refs[step][...] = dot_back(grad, up).astype(bf16)

    feed_big = 2.0 * toks * cols_axis * model * hidden
    feed_results = kernel_call(
        feed_main,
        [((cols_axis, toks, hidden), bf16)] * 2 + [((toks, model), bf16)] * cols_axis,
        [*low_near, *given_near, weights_feed],
        flops=3 * feed_big,
    )
    act, grad_hidden, back_parts = feed_results[0], feed_results[1], feed_results[2:]
    back_near = [back_parts[0]] + [along_cols(back_parts[step], step) for step in col_steps]

    def feed_weights(
        spot_ref, a0, a1, a2, a3, d0, d1, d2, d3, act_ref, grad_ref, weight_ref, mine_ref, give_ref, *outs
    ):
        at_core = spot_ref[2]
        low = jnp.concatenate([a0[...], a1[...], a2[...], a3[...]], axis=0)
        given = jnp.concatenate([d0[...], d1[...], d2[...], d3[...]], axis=0)
        rows = cols_axis * toks
        acts = act_ref[...].reshape(rows, hidden)
        grads = grad_ref[...].reshape(rows, hidden)
        for step in range(cols_axis):
            outs[step][...] = dot(act_ref[step], weight_ref[1]).astype(bf16)
        for ref, at in ((mine_ref, at_core), (give_ref, 1 - at_core)):
            ref[0] = dot_tokens(low, half_of(grads, at, half)).astype(bf16)
            ref[1] = dot_tokens(acts, half_of(given, at, half)).astype(bf16)

    feed_grads = kernel_call(
        feed_weights,
        [((2, model, half), bf16)] * 2 + [((toks, model), bf16)] * cols_axis,
        [spot, *low_near, *given_near, act, grad_hidden, weights_feed],
        smem=(0,),
        flops=3 * feed_big,
    )
    feed_mine, feed_give, out_parts = feed_grads[0], feed_grads[1], feed_grads[2:]
    out_near = [out_parts[0]] + [along_cols(out_parts[step], step) for step in col_steps]
    feed_got = along_core(feed_give)

    def attend_col_back(
        spot_ref,
        b0,
        b1,
        b2,
        b3,
        given_ref,
        two_ref,
        norm_ref,
        weight_ref,
        q_ref,
        near_ref,
        far_ref,
        probs_ref,
        dtwo_ref,
        low_ref,
        dq_ref,
        dkv_ref,
        send_ref,
        sums_ref,
        wide_ref,
    ):
        lane_heads = head_of_lane(model)
        back = b0[...].astype(f32) + b1[...].astype(f32) + b2[...].astype(f32) + b3[...].astype(f32)
        unit, scale = unit_norm(two_ref[...])
        sums_ref[...] = norm_sums(back, unit)
        dtwo = given_ref[...].astype(f32) + unit_norm_back(back, unit, scale, norm_ref[4:5])
        dtwo_ref[...] = dtwo
        low = dtwo.astype(bf16)
        low_ref[...] = low
        dmix = dot_back(low, weight_ref[3]).astype(bf16).astype(f32)
        wide_ref[...] = jnp.zeros_like(wide_ref)
        sides = (near_ref, far_ref)
        for slot in range(chips):
            dout = dmix[slot_rows(slot)]
            query = q_ref[slot_rows(slot)].astype(f32)
            products = jnp.concatenate(
                [
                    dout * sides[s // chips][1, slot_rows(s % chips)].astype(f32)
                    for s in range(seqs)
                ],
                axis=0,
            )
            found = per_head_sum(products, lane_heads)
            weights = probs_ref[slot]
            mean = None
            for s in range(seqs):
                rows = slice(s * width, (s + 1) * width)
                term = weights[rows] * found[rows]
                mean = term if mean is None else mean + term
            dscores = (weights * (found - jnp.concatenate([mean] * seqs, axis=0))).astype(bf16)
            wide_d = dot_back(dscores, lane_heads)
            wide_p = dot_back(weights.astype(bf16), lane_heads)
            dquery = None
            for s in range(seqs):
                rows = slice(s * width, (s + 1) * width)
                term = wide_d[rows] * sides[s // chips][0, slot_rows(s % chips)].astype(f32)
                dquery = term if dquery is None else dquery + term
                wide_ref[0, rows] += wide_d[rows] * query
                wide_ref[1, rows] += wide_p[rows] * dout
            dq_ref[slot_rows(slot)] = (dquery * col_scale).astype(bf16)
        dkv_ref[0] = wide_ref[0, :toks] * col_scale
        dkv_ref[1] = wide_ref[1, :toks]
        send_ref[0] = (wide_ref[0, toks:] * col_scale).astype(bf16)
        send_ref[1] = wide_ref[1, toks:].astype(bf16)

    grad_two, grad_two_low, col_dq, col_dkv, col_send, sums_three = kernel_call(
        attend_col_back,
        [
            ((toks, model), f32),
            ((toks, model), bf16),
            ((toks, model), bf16),
            ((2, toks, model), f32),
            ((2, toks, model), bf16),
            ((2, model), f32),
        ],
        [
            spot,
            *back_near,
            given_out,
            stream_two,
            norm_rows,
            weights_col,
            col_q,
            col_kv,
            kv_other,
            col_probs,
        ],
        smem=(0,),
        scratch=[pltpu.VMEM((2, 2 * toks, model), f32)],
        flops=big + 10.0 * chips * seqs * width * model * 128,
    )
    col_got = along_core(col_send)

    def row_entry_back(
        spot_ref,
        dq_ref,
        dkv_ref,
        got_ref,
        low_two_ref,
        dtwo_ref,
        one_ref,
        norm_ref,
        col_ref,
        row_ref,
        near_ref,
        left_ref,
        right_ref,
        mine_ref,
        give_ref,
        done_ref,
        low_ref,
        dmix_ref,
        dprobs_ref,
        sums_ref,
    ):
        at_core = spot_ref[2]
        dq = dq_ref[...]
        dk = (dkv_ref[0] + got_ref[0].astype(f32)).astype(bf16)
        dv = (dkv_ref[1] + got_ref[1].astype(f32)).astype(bf16)
        for index, item in enumerate((dq, dk, dv, low_two_ref[...])):
            mine_ref[index] = half_of(item, at_core, half)
            give_ref[index] = half_of(item, 1 - at_core, half)
        back = dot_back(dq, col_ref[0]) + dot_back(dk, col_ref[1]) + dot_back(dv, col_ref[2])
        unit, scale = unit_norm(one_ref[...])
        sums_ref[...] = norm_sums(back, unit)
        done = dtwo_ref[...] + unit_norm_back(back, unit, scale, norm_ref[2:3])
        done_ref[...] = done
        low = done.astype(bf16)
        low_ref[...] = low
        dmix = dot_back(low, row_ref[3]).astype(bf16)
        dmix_ref[...] = dmix
        mask = head_mask(width, model)
        total = None
        for slot in range(chips):
            values = window_rows(spot_ref, near_ref, left_ref, right_ref, 1, slot, width)
            term = dot_back(spread_heads(dmix[slot_rows(slot)], mask), values)
            total = term if total is None else total + term
        dprobs_ref[...] = total

    (
        col_mine,
        col_give,
        grad_one,
        grad_one_low,
        row_dmix,
        dprobs,
        sums_two,
    ) = kernel_call(
        row_entry_back,
        [
            ((4, toks, half), bf16),
            ((4, toks, half), bf16),
            ((toks, model), f32),
            ((toks, model), bf16),
            ((toks, model), bf16),
            ((fold, span), f32),
            ((2, model), f32),
        ],
        [
            spot,
            col_dq,
            col_dkv,
            col_got,
            grad_two_low,
            grad_two,
            stream_one,
            norm_rows,
            weights_col,
            weights_row,
            row_kv,
            kv_left,
            kv_right,
        ],
        smem=(0,),
        flops=4 * big + chips * 2.0 * fold * model * span,
    )
    dprobs_other = along_core(dprobs)

    def attend_row_back(
        spot_ref,
        weight_ref,
        dprobs_ref,
        other_ref,
        scores_ref,
        probs_ref,
        q_ref,
        near_ref,
        left_ref,
        right_ref,
        dmix_ref,
        dq_ref,
        dkv_ref,
        to_left_ref,
        to_right_ref,
    ):
        mask = head_mask(width, model)
        dprob = dprobs_ref[...] + other_ref[...]
        probs_here, scores_here = probs_ref[...], scores_ref[...]
        rows = lax.broadcasted_iota(jnp.int32, (fold, 1), 0) % width
        weight = jnp.where(rows + spot_ref[3] * width < spot_ref[4], weight_ref[0], 0.0)
        first = dprob - jnp.sum(probs_here * dprob, axis=-1, keepdims=True)
        second = scores_here - jnp.sum(probs_here * scores_here, axis=-1, keepdims=True)
        dscores = (probs_here * (first - weight * second)).astype(bf16)
        low_probs = probs_here.astype(bf16)
        for slot in range(chips):
            at = slot_rows(slot)
            keys = window_rows(spot_ref, near_ref, left_ref, right_ref, 0, slot, width)
            dq_ref[at] = (
                fold_heads(dot(dscores, keys), mask, width) * row_scale
            ).astype(bf16)
            dkeys = dot_tokens(dscores, spread_heads(q_ref[at], mask)) * row_scale
            dvalues = dot_tokens(low_probs, spread_heads(dmix_ref[at], mask))
            for index, item in enumerate((dkeys, dvalues)):
                to_left_ref[index, at] = item[:width].astype(bf16)
                dkv_ref[index, at] = item[width : 2 * width]
                to_right_ref[index, at] = item[2 * width :].astype(bf16)

    row_dq, row_dkv, edge_left, edge_right = kernel_call(
        attend_row_back,
        [
            ((toks, model), bf16),
            ((2, toks, model), f32),
            ((2, toks, model), bf16),
            ((2, toks, model), bf16),
        ],
        [
            spot,
            entropy_scale,
            dprobs,
            dprobs_other,
            scores,
            probs,
            row_q,
            row_kv,
            kv_left,
            kv_right,
            row_dmix,
        ],
        smem=(0, 1),
        flops=3 * chips * 2.0 * fold * model * span,
    )
    edge_from_right = to_left(edge_left)
    edge_from_left = to_right(edge_right)

    def input_back(
        spot_ref,
        dq_ref,
        dkv_ref,
        from_right_ref,
        from_left_ref,
        low_one_ref,
        done_ref,
        zero_ref,
        norm_ref,
        row_ref,
        mine_ref,
        give_ref,
        out_ref,
        sums_ref,
    ):
        at_core = spot_ref[2]
        dq = dq_ref[...]
        dk, dv = (
            jnp.concatenate(
                [
                    (
                        dkv_ref[index, slot_rows(slot)]
                        + from_left_ref[index, slot_span(spot_ref, 5, slot, width)].astype(f32)
                        + from_right_ref[index, slot_span(spot_ref, 6, slot, width)].astype(f32)
                    ).astype(bf16)
                    for slot in range(chips)
                ],
                axis=0,
            )
            for index in (0, 1)
        )
        for index, item in enumerate((dq, dk, dv, low_one_ref[...])):
            mine_ref[index] = half_of(item, at_core, half)
            give_ref[index] = half_of(item, 1 - at_core, half)
        back = dot_back(dq, row_ref[0]) + dot_back(dk, row_ref[1]) + dot_back(dv, row_ref[2])
        unit, scale = unit_norm(zero_ref[...])
        sums_ref[...] = norm_sums(back, unit)
        out_ref[...] = (done_ref[...] + unit_norm_back(back, unit, scale, norm_ref[0:1])).astype(
            bf16
        )

    row_mine, row_give, grad_in, sums_one = kernel_call(
        input_back,
        [
            ((4, toks, half), bf16),
            ((4, toks, half), bf16),
            ((toks, model), bf16),
            ((2, model), f32),
        ],
        [
            spot,
            row_dq,
            row_dkv,
            edge_from_right,
            edge_from_left,
            grad_one_low,
            grad_one,
            stream_zero,
            norm_rows,
            weights_row,
        ],
        smem=(0,),
        flops=3 * big,
    )

    def layer_grads(low, mix, low_other, mix_other, mine, given):
        def body(
            spot_ref, low_ref, mix_ref, low2_ref, mix2_ref, mine_ref, given_ref, *outs_and_scratch
        ):
            outs, (left_ref, right_ref) = outs_and_scratch[:cols_axis], outs_and_scratch[cols_axis:]
            at_col = spot_ref[0]
            left_ref[0, :toks] = low_ref[...]
            left_ref[0, toks:] = low2_ref[...]
            left_ref[1, :toks] = mix_ref[...]
            left_ref[1, toks:] = mix2_ref[...]
            right_ref[:, :toks] = mine_ref[...]
            right_ref[:, toks:] = given_ref[...]
            for step in range(cols_axis):
                matrix = at_col ^ step
                left = left_ref[matrix // 3]
                outs[step][...] = dot_tokens(left, right_ref[matrix]).astype(bf16)

        return kernel_call(
            body,
            [((model, half), bf16)] * cols_axis,
            [spot, low, mix, low_other, mix_other, mine, given],
            smem=(0,),
            scratch=[
                pltpu.VMEM((2, 2 * toks, model), bf16),
                pltpu.VMEM((4, 2 * toks, half), bf16),
            ],
            flops=4 * big,
        )

    def add_parts(items):
        total = items[0].astype(f32)
        for item in items[1:]:
            total = total + item.astype(f32)
        return total.astype(bf16)

    def settle(items):
        def rows_for(index):
            return add_parts(
                [
                    lax.dynamic_slice_in_dim(item, index * 2 * shard, 2 * shard, axis=1)
                    for item in items
                ]
            )

        total = add_parts(
            [rows_for(chip)] + [along_chips(rows_for(chip ^ step), step) for step in steps]
        )
        keep = lax.dynamic_slice_in_dim(total, core * shard, shard, axis=1)
        other = along_core(lax.dynamic_slice_in_dim(total, (1 - core) * shard, shard, axis=1))
        sides = jnp.where(
            core == 0,
            jnp.concatenate([keep, other], axis=2),
            jnp.concatenate([other, keep], axis=2),
        )
        near = [sides] + [along_cols(sides, step) for step in col_steps]
        stacked = jnp.stack(near)
        return [
            lax.dynamic_index_in_dim(stacked, col_at ^ block, axis=0, keepdims=False)
            for block in range(cols_axis)
        ]

    def layer_settle(low, mix, mine, give):
        low_other, mix_other = along_core(low), along_core(mix)
        partial_sums = layer_grads(low, mix, low_other, mix_other, mine, along_core(give))
        near = [partial_sums[0]] + [
            along_cols(partial_sums[step], step) for step in col_steps
        ]
        return [item[0].astype(f32) for item in settle([item[None] for item in near])]

    feed_parts = settle([feed_mine, feed_got])
    grad_feed_in = jnp.stack([item[0].reshape(shard, seqs, part) for item in feed_parts], axis=2)
    grad_feed_in = grad_feed_in.reshape(shard, feed_in.shape[1]).astype(f32)
    grad_feed_out = jnp.concatenate([item[1] for item in feed_parts], axis=0).astype(f32)
    col_grads = layer_settle(normed_two, col_mix, col_mine, col_give)
    row_grads = layer_settle(normed_one, row_mix, row_mine, row_give)

    small = jnp.concatenate(
        [sums_one, sums_two, sums_three, entropy_row, jnp.zeros((1, model), f32)], axis=0
    )
    small = small + along_core(small)
    step = 1
    while step < chips:
        small = small + along_chips(small, step)
        step *= 2
    step = 1
    while step < cols_axis:
        small = small + along_cols(small, step)
        step *= 2
    entropy = small[6, 0] / (HEADS * count_total)
    norm_here = lax.dynamic_slice_in_dim(small, seq_at * shard, shard, axis=1)

    result = stream_two
    for item in out_near:
        result = result + item.astype(f32)
    result = result.astype(bf16)

    def to_sequence(values):
        slots = [values[slot_rows(slot)] for slot in range(chips)]
        arrived = [slots[0]] + [along_chips(slots[step], step) for step in steps]
        whole = jnp.stack(arrived)
        return jnp.concatenate(
            [
                lax.dynamic_index_in_dim(whole, chunk_of(index) ^ chip, axis=0, keepdims=False)
                for index in range(chips)
            ],
            axis=0,
        )[None]

    return (
        to_sequence(result),
        entropy,
        to_sequence(grad_in),
        *[norm_here[index] for index in range(6)],
        *row_grads,
        *col_grads,
        grad_feed_in,
        grad_feed_out,
    )


def fits_fast(tokens, feed_out):
    chips = lax.axis_size("seq") // 2
    return (
        lax.axis_size("col") == 4
        and lax.axis_size("seq") == 8
        and tokens.shape[0] == 1
        and tokens.shape[1] == chips * WINDOW
        and tokens.shape[2] == HEADS * HEAD_DIM
        and feed_out.shape[0] * 2 == tokens.shape[2]
    )


def on_device(tokens, offsets, band, col_counts, *rest):
    if not fits_fast(tokens, rest[15]):
        return general_plan(tokens, offsets, band, col_counts, *rest)
    return fast_plan(
        tokens,
        offsets,
        band,
        col_counts,
        rest[0:6],
        rest[6:10],
        rest[10:14],
        rest[14],
        rest[15],
        rest[16],
    )


def solution(mesh):
    return jax.shard_map(
        on_device,
        mesh=mesh,
        in_specs=(
            P("seq", "col", None),
            P(),
            P("col", None),
            P("col"),
            P("seq"),
            P("seq"),
            P("seq"),
            P("seq"),
            P("seq"),
            P("seq"),
            P("seq", None),
            P("seq", None),
            P("seq", None),
            P("seq", None),
            P("seq", None),
            P("seq", None),
            P("seq", None),
            P("seq", None),
            P("seq", None),
            P("seq", None),
            P("seq", "col", None),
        ),
        out_specs=(
            P("seq", "col", None),
            P(),
            P("seq", "col", None),
            P("seq"),
            P("seq"),
            P("seq"),
            P("seq"),
            P("seq"),
            P("seq"),
            P("seq", None),
            P("seq", None),
            P("seq", None),
            P("seq", None),
            P("seq", None),
            P("seq", None),
            P("seq", None),
            P("seq", None),
            P("seq", None),
            P("seq", None),
        ),
        check_vma=False,
    )
```

```python
from functools import partial
import math

import jax
import jax.numpy as jnp
from jax import lax
from jax.experimental import pallas as pl
from jax.experimental.pallas import tpu as pltpu
from jax.sharding import PartitionSpec as P

HEADS = 12
HEAD_DIM = 64
WINDOW = 32


entropy_weight = 8192.0
norm_eps = 1e-05


def with_halo(cells, sides, width):
    for axis, dim in sides:
        count = lax.axis_size(axis)
        ends = count - 1
        head = lax.slice_in_dim(cells, 0, width, axis=dim)
        tail = lax.slice_in_dim(cells, cells.shape[dim] - width, cells.shape[dim], axis=dim)
        cells = jnp.concatenate(
            [
                lax.ppermute(tail, axis, [(i, (i + 1) % count) for i in range(ends)]),
                cells,
                lax.ppermute(head, axis, [((i + 1) % count, i) for i in range(ends)]),
            ],
            axis=dim,
        )
    return cells


def layer_norm(inputs, norm_gain, norm_shift):
    average = jnp.mean(inputs, axis=-1, keepdims=True)
    centred = inputs - average
    variance = jnp.mean(centred * centred, axis=-1, keepdims=True)
    return centred * lax.rsqrt(variance + norm_eps) * norm_gain + norm_shift


def position_table(offsets, row_first, col_first, row_count, col_count, model_width):
    half_width = model_width // 2
    frequency = jnp.exp(-math.log(1000.0) * jnp.arange(half_width, dtype=jnp.float32) / half_width)
    col_place = (jnp.arange(col_count, dtype=jnp.int32) + col_first + offsets[1]).astype(
        jnp.float32
    )
    row_place = (jnp.arange(row_count, dtype=jnp.int32) + row_first + offsets[0]).astype(
        jnp.float32
    )
    col_wave = jnp.sin(col_place[:, None] * frequency[None, :])
    row_wave = jnp.sin(row_place[:, None] * frequency[None, :])
    col_full = jnp.broadcast_to(col_wave[None, :, :], (row_count, col_count, half_width))
    row_full = jnp.broadcast_to(row_wave[:, None, :], (row_count, col_count, half_width))
    return 0.5 * jnp.concatenate([col_full, row_full], axis=-1)


def softmax_entropy(scores, allowed, valid):
    masked = jnp.where(allowed[None], scores, -1000000000.0)
    largest = jnp.max(masked, axis=-1, keepdims=True)
    powers = jnp.exp(masked - largest)
    row_total = jnp.sum(powers, axis=-1, keepdims=True)
    probs_out = powers / row_total
    log_total = largest[..., 0] + jnp.log(row_total[..., 0])
    entropies = log_total - jnp.sum(probs_out * jnp.where(allowed[None], scores, 0.0), axis=-1)
    return (probs_out, jnp.sum(entropies * valid[None, :]))


def plain_softmax(scores):
    largest = jnp.max(scores, axis=-1, keepdims=True)
    powers = jnp.exp(scores - largest)
    return powers / jnp.sum(powers, axis=-1, keepdims=True)


def project(activations, weight):
    return jnp.einsum("rci,ij->rcj", activations, weight, preferred_element_type=jnp.float32)


def project_back(gradient, weight):
    return jnp.einsum("rcj,ij->rci", gradient, weight, preferred_element_type=jnp.float32)


def weight_grad(activations, gradient):
    return jnp.einsum("rci,rcj->ij", activations, gradient, preferred_element_type=jnp.float32)


def general_plan(
    tokens,
    offsets,
    band,
    col_counts,
    norm1_gain,
    norm1_shift,
    norm2_gain,
    norm2_shift,
    norm3_gain,
    norm3_shift,
    row_query,
    row_key,
    row_value,
    row_output,
    col_query,
    col_key,
    col_value,
    col_output,
    feed_in,
    feed_out,
    cotangent,
):
    rows_dev, cols_dev, model_width = tokens.shape
    total_rows = rows_dev * lax.axis_size("seq")
    total_cols = cols_dev * lax.axis_size("col")
    row_first = lax.axis_index("seq") * rows_dev
    col_first = lax.axis_index("col") * cols_dev
    count_here = col_counts[0].astype(jnp.float32)
    count_early = lax.psum(count_here, "col")
    params = (
        lax.all_gather(norm1_gain, "seq", axis=0, tiled=True),
        lax.all_gather(norm1_shift, "seq", axis=0, tiled=True),
        lax.all_gather(norm2_gain, "seq", axis=0, tiled=True),
        lax.all_gather(norm2_shift, "seq", axis=0, tiled=True),
        lax.all_gather(norm3_gain, "seq", axis=0, tiled=True),
        lax.all_gather(norm3_shift, "seq", axis=0, tiled=True),
        lax.all_gather(row_query, "seq", axis=0, tiled=True),
        lax.all_gather(row_key, "seq", axis=0, tiled=True),
        lax.all_gather(row_value, "seq", axis=0, tiled=True),
        lax.all_gather(row_output, "seq", axis=0, tiled=True),
        lax.all_gather(col_query, "seq", axis=0, tiled=True),
        lax.all_gather(col_key, "seq", axis=0, tiled=True),
        lax.all_gather(col_value, "seq", axis=0, tiled=True),
        lax.all_gather(col_output, "seq", axis=0, tiled=True),
        lax.all_gather(feed_in, "seq", axis=0, tiled=True),
        lax.all_gather(feed_out, "seq", axis=0, tiled=True),
    )
    gain_one = params[0].astype(jnp.float32)
    shift_one = params[1].astype(jnp.float32)
    gain_two = params[2].astype(jnp.float32)
    shift_two = params[3].astype(jnp.float32)
    gain_three = params[4].astype(jnp.float32)
    shift_three = params[5].astype(jnp.float32)
    query_row, key_row, value_row, output_row = (params[6], params[7], params[8], params[9])
    query_col, key_col, value_col, output_col = (params[10], params[11], params[12], params[13])
    feed_up, feed_down = (params[14], params[15])
    stream_zero = tokens.astype(jnp.float32) + position_table(
        offsets, row_first, col_first, rows_dev, cols_dev, model_width
    )
    normed_one, norm_back_one = jax.vjp(layer_norm, stream_zero, gain_one, shift_one)
    normed_one = normed_one.astype(jnp.bfloat16)
    row_queries = project(normed_one, query_row).astype(jnp.bfloat16)
    row_keys = project(normed_one, key_row).astype(jnp.bfloat16)
    row_values = project(normed_one, value_row).astype(jnp.bfloat16)
    extended = with_halo(jnp.stack([row_keys, row_values]), (("col", 2),), WINDOW)
    ext_cols = cols_dev + 2 * WINDOW
    queries_heads = row_queries.reshape(rows_dev, cols_dev, HEADS, HEAD_DIM)
    keys_ext = extended[0].reshape(rows_dev, ext_cols, HEADS, HEAD_DIM)
    values_ext = extended[1].reshape(rows_dev, ext_cols, HEADS, HEAD_DIM)
    partial_logits = jnp.einsum(
        "rchd,rehd->hce", queries_heads, keys_ext, preferred_element_type=jnp.float32
    )
    row_scale = 1.0 / math.sqrt(HEAD_DIM * total_rows)
    row_scores = lax.psum(partial_logits, "seq") * row_scale
    query_index = jnp.arange(cols_dev, dtype=jnp.int32)[:, None]
    key_index = jnp.arange(ext_cols, dtype=jnp.int32)[None, :]
    distance = key_index - query_index
    choose = jnp.arange(2 * WINDOW + 1, dtype=jnp.int32)
    matches = (distance[:, None, :] == choose[None, :, None]) & (band[:, :, None] == 1)
    key_global = col_first - WINDOW + key_index
    inside = (key_global >= 0) & (key_global < total_cols)
    allowed = (jnp.any(matches, axis=1) | (distance == WINDOW)) & inside
    valid = (jnp.arange(cols_dev, dtype=jnp.int32) < col_counts[0]).astype(jnp.float32)
    (row_probs, ent_part), ent_back = jax.vjp(
        lambda given: softmax_entropy(given, allowed, valid), row_scores
    )
    payload = ent_part[None]
    sums = lax.psum(payload, "col")
    entropy = sums[0] / (HEADS * count_early)
    row_probs_low = row_probs.astype(jnp.bfloat16)
    row_mix = jnp.einsum(
        "hce,rehd->rchd", row_probs_low, values_ext, preferred_element_type=jnp.float32
    )
    row_mix = row_mix.reshape(rows_dev, cols_dev, model_width).astype(jnp.bfloat16)
    stream_one = stream_zero + project(row_mix, output_row)
    normed_two, norm_back_two = jax.vjp(layer_norm, stream_one, gain_two, shift_two)
    normed_two = normed_two.astype(jnp.bfloat16)
    col_queries = project(normed_two, query_col).astype(jnp.bfloat16)
    col_keys = project(normed_two, key_col).astype(jnp.bfloat16)
    col_values = project(normed_two, value_col).astype(jnp.bfloat16)
    col_scale = 1.0 / math.sqrt(HEAD_DIM)
    keys_all, values_all = (
        lax.all_gather(col_keys, "seq", axis=0, tiled=True),
        lax.all_gather(col_values, "seq", axis=0, tiled=True),
    )
    col_heads_q = col_queries.reshape(rows_dev, cols_dev, HEADS, HEAD_DIM)
    keys_heads = keys_all.reshape(total_rows, cols_dev, HEADS, HEAD_DIM)
    values_heads = values_all.reshape(total_rows, cols_dev, HEADS, HEAD_DIM)
    col_raw = jnp.einsum(
        "rchd,schd->chrs", col_heads_q, keys_heads, preferred_element_type=jnp.float32
    )
    col_probs = plain_softmax(col_raw * col_scale)
    col_probs_low = col_probs.astype(jnp.bfloat16)
    col_mix = jnp.einsum(
        "chrs,schd->rchd", col_probs_low, values_heads, preferred_element_type=jnp.float32
    )
    col_mix = col_mix.reshape(rows_dev, cols_dev, model_width).astype(jnp.bfloat16)
    stream_two = stream_one + project(col_mix, output_col)
    normed_three, norm_back_three = jax.vjp(layer_norm, stream_two, gain_three, shift_three)
    normed_three = normed_three.astype(jnp.bfloat16)
    hidden_pre = project(normed_three, feed_up)
    hidden_act, gelu_back = jax.vjp(partial(jax.nn.gelu, approximate=False), hidden_pre)
    hidden_low = hidden_act.astype(jnp.bfloat16)
    output = (stream_two + project(hidden_low, feed_down)).astype(jnp.bfloat16)
    grad_feed_down = weight_grad(hidden_low, cotangent)
    grad_hidden = gelu_back(project_back(cotangent, feed_down))[0].astype(jnp.bfloat16)
    grad_feed_up = weight_grad(normed_three, grad_hidden)
    back_stream, grad_gain_three, grad_shift_three = norm_back_three(
        project_back(grad_hidden, feed_up)
    )
    grad_two = cotangent.astype(jnp.float32) + back_stream
    grad_two_low = grad_two.astype(jnp.bfloat16)
    grad_output_col = weight_grad(col_mix, grad_two_low)
    grad_mix_flat = project_back(grad_two_low, output_col).astype(jnp.bfloat16)
    grad_col_mix = grad_mix_flat.reshape(rows_dev, cols_dev, HEADS, HEAD_DIM)
    col_dprobs = jnp.einsum(
        "rchd,schd->chrs", grad_col_mix, values_heads, preferred_element_type=jnp.float32
    )
    col_dscores = col_probs * (col_dprobs - jnp.sum(col_probs * col_dprobs, axis=-1, keepdims=True))
    col_dscores = col_dscores.astype(jnp.bfloat16)
    grad_col_q = (
        jnp.einsum("chrs,schd->rchd", col_dscores, keys_heads, preferred_element_type=jnp.float32)
        * col_scale
    )
    grad_col_q = grad_col_q.reshape(rows_dev, cols_dev, model_width).astype(jnp.bfloat16)
    row_count = lax.axis_size("seq") * rows_dev
    key_part = (
        jnp.einsum("chrs,rchd->schd", col_dscores, col_heads_q, preferred_element_type=jnp.float32)
        * col_scale
    )
    value_part = jnp.einsum(
        "chrs,rchd->schd", col_probs_low, grad_col_mix, preferred_element_type=jnp.float32
    )
    key_value_grads = lax.psum_scatter(
        jnp.concatenate(
            [
                key_part.reshape(row_count, cols_dev, model_width),
                value_part.reshape(row_count, cols_dev, model_width),
            ],
            axis=-1,
        ),
        "seq",
        scatter_dimension=0,
        tiled=True,
    )
    grad_col_k = key_value_grads[..., :model_width].astype(jnp.bfloat16)
    grad_col_v = key_value_grads[..., model_width:].astype(jnp.bfloat16)
    grad_query_col = weight_grad(normed_two, grad_col_q)
    grad_key_col = weight_grad(normed_two, grad_col_k)
    grad_value_col = weight_grad(normed_two, grad_col_v)
    back_input = (
        project_back(grad_col_q, query_col)
        + project_back(grad_col_k, key_col)
        + project_back(grad_col_v, value_col)
    )
    back_stream, grad_gain_two, grad_shift_two = norm_back_two(back_input)
    grad_one = grad_two + back_stream
    grad_one_low = grad_one.astype(jnp.bfloat16)
    grad_output_row = weight_grad(row_mix, grad_one_low)
    grad_row_mix = project_back(grad_one_low, output_row).astype(jnp.bfloat16)
    grad_row_mix = grad_row_mix.reshape(rows_dev, cols_dev, HEADS, HEAD_DIM)
    dprobs_part = jnp.einsum(
        "rchd,rehd->hce", grad_row_mix, values_ext, preferred_element_type=jnp.float32
    )
    row_dprobs = lax.psum(dprobs_part.astype(jnp.bfloat16), "seq").astype(jnp.float32)
    ent_cot = jnp.asarray(entropy_weight, dtype=jnp.float32) / (HEADS * count_early)
    row_dscores = ent_back((row_dprobs, ent_cot))[0].astype(jnp.bfloat16)
    grad_row_q = (
        jnp.einsum("hce,rehd->rchd", row_dscores, keys_ext, preferred_element_type=jnp.float32)
        * row_scale
    )
    grad_row_q = grad_row_q.reshape(rows_dev, cols_dev, model_width).astype(jnp.bfloat16)
    grad_keys_ext = (
        jnp.einsum("hce,rchd->rehd", row_dscores, queries_heads, preferred_element_type=jnp.float32)
        * row_scale
    )
    grad_values_ext = jnp.einsum(
        "hce,rchd->rehd", row_probs_low, grad_row_mix, preferred_element_type=jnp.float32
    )
    grad_ext = jnp.stack([grad_keys_ext, grad_values_ext]).reshape(
        2, rows_dev, ext_cols, model_width
    )
    rims = jnp.concatenate([grad_ext[:, :, :WINDOW], grad_ext[:, :, WINDOW + cols_dev :]], axis=2)
    returned = with_halo(rims.astype(jnp.bfloat16), (("col", 2),), WINDOW).astype(rims.dtype)
    interior = grad_ext[:, :, WINDOW : WINDOW + cols_dev]
    interior = interior.at[:, :, :WINDOW].add(returned[:, :, :WINDOW])
    interior = interior.at[:, :, cols_dev - WINDOW :].add(returned[:, :, 3 * WINDOW :])
    grad_row_k = interior[0].astype(jnp.bfloat16)
    grad_row_v = interior[1].astype(jnp.bfloat16)
    grad_query_row = weight_grad(normed_one, grad_row_q)
    grad_key_row = weight_grad(normed_one, grad_row_k)
    grad_value_row = weight_grad(normed_one, grad_row_v)
    back_input = (
        project_back(grad_row_q, query_row)
        + project_back(grad_row_k, key_row)
        + project_back(grad_row_v, value_row)
    )
    back_stream, grad_gain_one, grad_shift_one = norm_back_one(back_input)
    input_grad = (grad_one + back_stream).astype(jnp.bfloat16)
    shares = (
        lax.psum_scatter(
            grad_gain_one.astype(jnp.bfloat16), "seq", scatter_dimension=0, tiled=True
        ).astype(jnp.float32),
        lax.psum_scatter(
            grad_shift_one.astype(jnp.bfloat16), "seq", scatter_dimension=0, tiled=True
        ).astype(jnp.float32),
        lax.psum_scatter(
            grad_gain_two.astype(jnp.bfloat16), "seq", scatter_dimension=0, tiled=True
        ).astype(jnp.float32),
        lax.psum_scatter(
            grad_shift_two.astype(jnp.bfloat16), "seq", scatter_dimension=0, tiled=True
        ).astype(jnp.float32),
        lax.psum_scatter(
            grad_gain_three.astype(jnp.bfloat16), "seq", scatter_dimension=0, tiled=True
        ).astype(jnp.float32),
        lax.psum_scatter(
            grad_shift_three.astype(jnp.bfloat16), "seq", scatter_dimension=0, tiled=True
        ).astype(jnp.float32),
        lax.psum_scatter(
            grad_query_row.astype(jnp.bfloat16), "seq", scatter_dimension=0, tiled=True
        ).astype(jnp.float32),
        lax.psum_scatter(
            grad_key_row.astype(jnp.bfloat16), "seq", scatter_dimension=0, tiled=True
        ).astype(jnp.float32),
        lax.psum_scatter(
            grad_value_row.astype(jnp.bfloat16), "seq", scatter_dimension=0, tiled=True
        ).astype(jnp.float32),
        lax.psum_scatter(
            grad_output_row.astype(jnp.bfloat16), "seq", scatter_dimension=0, tiled=True
        ).astype(jnp.float32),
        lax.psum_scatter(
            grad_query_col.astype(jnp.bfloat16), "seq", scatter_dimension=0, tiled=True
        ).astype(jnp.float32),
        lax.psum_scatter(
            grad_key_col.astype(jnp.bfloat16), "seq", scatter_dimension=0, tiled=True
        ).astype(jnp.float32),
        lax.psum_scatter(
            grad_value_col.astype(jnp.bfloat16), "seq", scatter_dimension=0, tiled=True
        ).astype(jnp.float32),
        lax.psum_scatter(
            grad_output_col.astype(jnp.bfloat16), "seq", scatter_dimension=0, tiled=True
        ).astype(jnp.float32),
        lax.psum_scatter(
            grad_feed_up.astype(jnp.bfloat16), "seq", scatter_dimension=0, tiled=True
        ).astype(jnp.float32),
        lax.psum_scatter(
            grad_feed_down.astype(jnp.bfloat16), "seq", scatter_dimension=0, tiled=True
        ).astype(jnp.float32),
    )
    totals = (
        lax.psum(shares[0].astype(jnp.bfloat16), "col").astype(jnp.float32),
        lax.psum(shares[1].astype(jnp.bfloat16), "col").astype(jnp.float32),
        lax.psum(shares[2].astype(jnp.bfloat16), "col").astype(jnp.float32),
        lax.psum(shares[3].astype(jnp.bfloat16), "col").astype(jnp.float32),
        lax.psum(shares[4].astype(jnp.bfloat16), "col").astype(jnp.float32),
        lax.psum(shares[5].astype(jnp.bfloat16), "col").astype(jnp.float32),
        lax.psum(shares[6].astype(jnp.bfloat16), "col").astype(jnp.float32),
        lax.psum(shares[7].astype(jnp.bfloat16), "col").astype(jnp.float32),
        lax.psum(shares[8].astype(jnp.bfloat16), "col").astype(jnp.float32),
        lax.psum(shares[9].astype(jnp.bfloat16), "col").astype(jnp.float32),
        lax.psum(shares[10].astype(jnp.bfloat16), "col").astype(jnp.float32),
        lax.psum(shares[11].astype(jnp.bfloat16), "col").astype(jnp.float32),
        lax.psum(shares[12].astype(jnp.bfloat16), "col").astype(jnp.float32),
        lax.psum(shares[13].astype(jnp.bfloat16), "col").astype(jnp.float32),
        lax.psum(shares[14].astype(jnp.bfloat16), "col").astype(jnp.float32),
        lax.psum(shares[15].astype(jnp.bfloat16), "col").astype(jnp.float32),
    )
    return (
        output,
        entropy,
        input_grad,
        totals[0],
        totals[1],
        totals[2],
        totals[3],
        totals[4],
        totals[5],
        totals[6],
        totals[7],
        totals[8],
        totals[9],
        totals[10],
        totals[11],
        totals[12],
        totals[13],
        totals[14],
        totals[15],
    )


def after(values, *needed):
    return lax.optimization_barrier((values, needed))[0]


def kernel_call(
    body, outs, args, smem=(), scratch=(), flops=1, moved=1, stream=False, room=16
):
    out_shapes = [jax.ShapeDtypeStruct(shape, kind) for shape, kind in outs]

    def whole(item):
        if not stream:
            return pl.BlockSpec(memory_space=pltpu.VMEM)
        rank = len(item.shape)
        return pl.BlockSpec(item.shape, lambda step: (0,) * rank, pipeline_mode=pl.Buffered(1))

    return pl.pallas_call(
        body,
        grid=(1,) if stream else (),
        out_shape=out_shapes,
        in_specs=[
            pl.BlockSpec(memory_space=pltpu.SMEM) if place in smem else whole(item)
            for place, item in enumerate(args)
        ],
        out_specs=[whole(item) for item in out_shapes],
        scratch_shapes=list(scratch),
        compiler_params=pltpu.CompilerParams(vmem_limit_bytes=(56 if stream else room) << 20),
        cost_estimate=pl.CostEstimate(
            flops=int(flops), bytes_accessed=int(moved), transcendentals=0
        ),
        name=body.__name__,
    )(*args)


def dot(left, right):
    return jnp.dot(left, right, preferred_element_type=jnp.float32)


def dot_back(left, right):
    return lax.dot_general(
        left, right, (((1,), (1,)), ((), ())), preferred_element_type=jnp.float32
    )


def dot_tokens(left, right):
    return lax.dot_general(
        left, right, (((0,), (0,)), ((), ())), preferred_element_type=jnp.float32
    )


def unit_norm(inputs):
    centred = inputs - jnp.mean(inputs, axis=-1, keepdims=True)
    scale = lax.rsqrt(jnp.mean(centred * centred, axis=-1, keepdims=True) + norm_eps)
    return centred * scale, scale


def unit_norm_back(given, unit, scale, gain):
    scaled = given * gain
    first = jnp.mean(scaled, axis=-1, keepdims=True)
    second = jnp.mean(scaled * unit, axis=-1, keepdims=True)
    return scale * (scaled - first - unit * second)


def norm_sums(given, unit):
    return jnp.concatenate(
        [
            jnp.sum(given * unit, axis=0, keepdims=True),
            jnp.sum(given, axis=0, keepdims=True),
        ],
        axis=0,
    )


def head_mask(width, model_width):
    rows = lax.broadcasted_iota(jnp.int32, (HEADS * width, model_width), 0) // width
    lanes = lax.broadcasted_iota(jnp.int32, (HEADS * width, model_width), 1) // HEAD_DIM
    return rows == lanes


def spread_heads(block, mask):
    tiled = jnp.concatenate([block] * HEADS, axis=0)
    return jnp.where(mask, tiled, jnp.zeros_like(tiled))


def fold_heads(product, mask, width):
    kept = jnp.where(mask, product, 0.0)
    total = kept[:width]
    for head in range(1, HEADS):
        total = total + kept[head * width : (head + 1) * width]
    return total


def head_of_lane(model_width):
    rows = lax.broadcasted_iota(jnp.int32, (model_width, 128), 0) // HEAD_DIM
    lanes = lax.broadcasted_iota(jnp.int32, (model_width, 128), 1)
    return (rows == lanes).astype(jnp.bfloat16)


def per_head_sum(product, lane_heads):
    high = product.astype(jnp.bfloat16)
    rest = (product - high.astype(jnp.float32)).astype(jnp.bfloat16)
    return dot(high, lane_heads) + dot(rest, lane_heads)


def slot_span(spot_ref, side, slot, width):
    return pl.ds(pl.multiple_of((slot ^ spot_ref[side]) * width, width), width)


def window_rows(spot_ref, near_ref, left_ref, right_ref, which, slot, width):
    return jnp.concatenate(
        [
            left_ref[which, slot_span(spot_ref, 5, slot, width)],
            near_ref[which, slot * width : (slot + 1) * width],
            right_ref[which, slot_span(spot_ref, 6, slot, width)],
        ],
        axis=0,
    )


def half_of(values, core, width):
    return jnp.where(core == 0, values[:, :width], values[:, width:])


def fast_plan(
    tokens,
    offsets,
    band,
    col_counts,
    norms,
    row_weights,
    col_weights,
    feed_in,
    feed_out,
    cotangent,
):
    f32, bf16 = jnp.float32, jnp.bfloat16
    cols_dev, model = tokens.shape[1:]
    cols_axis, seqs = lax.axis_size("col"), lax.axis_size("seq")
    chips = seqs // 2
    width = cols_dev // chips
    toks = chips * width
    shard = model // seqs
    half = model // 2
    hidden = feed_out.shape[0] * seqs // cols_axis
    fold = HEADS * width
    span = 3 * width
    col_at = lax.axis_index("col")
    seq_at = lax.axis_index("seq")
    chip, core = seq_at // 2, seq_at % 2
    flip = col_at % 2

    def chunk_of(chip_index):
        return jnp.where(flip == 0, chip_index, chips - 1 - chip_index)

    chunk = chunk_of(chip)
    piece = col_at * chips + chunk

    def along_chips(values, step):
        return lax.ppermute(values, "seq", [(i, i ^ (2 * step)) for i in range(seqs)])

    def along_core(values):
        return lax.ppermute(values, "seq", [(i, i ^ 1) for i in range(seqs)])

    def along_cols(values, step):
        return lax.ppermute(values, "col", [(i, i ^ step) for i in range(cols_axis)])

    def pair_cols(values):
        pairs = [
            (c * seqs + i, (c ^ (1 + i % 2)) * seqs + i)
            for c in range(cols_axis)
            for i in range(seqs)
        ]
        return lax.ppermute(values, ("col", "seq"), pairs)

    def pair_chips(values):
        pairs = [(i, (i // 2 ^ (1 + i % 2)) * 2 + i % 2) for i in range(seqs)]
        return lax.ppermute(values, "seq", pairs)

    def place_of(piece_index, core_index):
        block, part = divmod(piece_index, chips)
        chip_index = part if block % 2 == 0 else chips - 1 - part
        return block * seqs + chip_index * 2 + core_index

    rightward = [
        (place_of(i, k), place_of(i + 1, k)) for i in range(cols_axis * chips - 1) for k in (0, 1)
    ]
    leftward = [(target, source) for source, target in rightward]

    def to_right(values):
        return lax.ppermute(values, ("col", "seq"), rightward)

    def to_left(values):
        return lax.ppermute(values, ("col", "seq"), leftward)

    steps = range(1, chips)
    col_steps = range(1, cols_axis)

    def turn_to(other):
        block, rest = other // chips, other % chips
        return chip ^ jnp.where(block % 2 == 0, rest, chips - 1 - rest)

    to_left_turn = turn_to(jnp.maximum(piece - 1, 0))
    to_right_turn = turn_to(jnp.minimum(piece + 1, cols_axis * chips - 1))
    spot = jnp.stack(
        [col_at, chip, core, chunk, col_counts[0], to_left_turn, to_right_turn]
    ).astype(jnp.int32)

    half_width = model // 2
    frequency = jnp.exp(-math.log(1000.0) * jnp.arange(half_width, dtype=f32) / half_width)
    col_place = (jnp.arange(width, dtype=jnp.int32) + piece * width + offsets[1]).astype(f32)
    seq_slots = jnp.stack([(chip ^ step) * 2 + core for step in range(chips)])
    row_place = (seq_slots + offsets[0]).astype(f32)
    waves = 0.5 * jnp.sin(
        jnp.concatenate([col_place, row_place])[:, None] * frequency[None, :]
    )
    band_here = lax.dynamic_slice_in_dim(band, chunk * width, width, axis=0)
    query_index = jnp.arange(width, dtype=jnp.int32)[:, None]
    key_index = jnp.arange(span, dtype=jnp.int32)[None, :]
    distance = key_index - query_index
    choose = jnp.arange(2 * WINDOW + 1, dtype=jnp.int32)
    matches = (distance[:, None, :] == choose[None, :, None]) & (band_here[:, :, None] == 1)
    key_global = (piece - 1) * width + key_index
    inside = (key_global >= 0) & (key_global < cols_axis * cols_dev)
    allowed = ((jnp.any(matches, axis=1) | (distance == WINDOW)) & inside).astype(f32)

    quarter = shard // cols_axis
    lines = 8
    hops = chips - 1
    col_rows = cols_axis * quarter
    row_rows = col_rows + lines

    def chunk_at(spot_ref, chip_index):
        at = jnp.where(spot_ref[0] % 2 == 0, chip_index, chips - 1 - chip_index)
        return pl.ds(pl.multiple_of(at * width, width), width)

    def pack(spot_ref, weights, token_ref, own_ref, chunk_ref, send_refs, block):
        at = pl.multiple_of(spot_ref[0] * quarter, quarter)
        size = len(weights) * quarter
        for index, ref in enumerate(weights):
            own_ref[index * shard : (index + 1) * shard] = ref[...]
            for send_ref in send_refs:
                send_ref[index * quarter : (index + 1) * quarter] = ref[pl.ds(at, quarter)]
        if block is not None:
            for ref, row in [(own_ref, len(weights) * shard)] + [
                (ref, size) for ref in send_refs
            ]:
                ref[row : row + lines] = jnp.zeros((lines, model), bf16)
                ref[row : row + lines, :128] = block
            size = size + lines
        chunk_ref[...] = token_ref[0, chunk_at(spot_ref, spot_ref[1])]
        for hop, ref in enumerate(send_refs):
            ref[size:] = token_ref[0, chunk_at(spot_ref, spot_ref[1] ^ (hop + 1))]

    def pack_row(spot_ref, *refs):
        norm_refs, token_ref, own_ref, chunk_ref = refs[4:10], refs[10], refs[11], refs[12]
        block = jnp.zeros((lines, 128), f32)
        rows = lax.broadcasted_iota(jnp.int32, (lines, 128), 0)
        for index, ref in enumerate(norm_refs):
            line = jnp.pad(ref[...].astype(f32), ((0, 0), (0, 128 - shard)))
            block = jnp.where(rows == index, line, block)
        block = jnp.where(rows == 6, spot_ref[4].astype(f32), block).astype(bf16)
        pack(spot_ref, refs[:4], token_ref, own_ref, chunk_ref, refs[13:], block)

    part = feed_out.shape[0] // cols_axis
    block_cols = feed_out.shape[0]

    def pack_rest(spot_ref, *refs):
        in_ref, out_ref, own_ref = refs[5], refs[6], refs[7]
        pack(spot_ref, refs[:4], refs[4], refs[8], refs[9], refs[10:], None)
        first = lax.broadcasted_iota(jnp.int32, (block_cols, 128), 0)
        lanes = lax.broadcasted_iota(jnp.int32, (block_cols, 128), 1)
        chosen = ((first == lanes + spot_ref[0] * part) & (lanes < part)).astype(bf16)
        for index in range(seqs):
            block = in_ref[:, index * block_cols : (index + 1) * block_cols]
            own_ref[0, :, index * part : (index + 1) * part] = dot(block, chosen)[
                :, :part
            ].astype(bf16)
        own_ref[1] = out_ref[pl.ds(pl.multiple_of(spot_ref[0] * part, part), part)]

    def split_got(own_ref, *refs):
        rows = refs[0].shape[0] - width
        ins, (hops_ref, stream_ref) = refs[:-2], refs[-2:]
        stream_ref[:width] = own_ref[...]
        for hop, ref in enumerate(ins):
            hops_ref[hop * rows : (hop + 1) * rows] = ref[:rows]
            stream_ref[(hop + 1) * width : (hop + 2) * width] = ref[rows:]

    def spread_plane(near, far):
        def join_cores(near_ref, far_ref, out_ref):
            rows = near_ref.shape[0]
            out_ref[:rows] = near_ref[...]
            out_ref[rows:] = far_ref[...]

        both_cores = kernel_call(join_cores, [((2 * near.shape[0], model), bf16)], [near, far])[0]
        return both_cores, pair_cols(both_cores), along_cols(near, cols_axis - 1)

    def place_rows(spot_ref, refs, outs, rows, unit):
        at_col, at_chip, at_core = spot_ref[0], spot_ref[1], spot_ref[2]
        other = 1 - at_core

        def row_of(from_chip, from_core, offset, size):
            return pl.ds(
                pl.multiple_of((from_chip * 2 + from_core) * shard + offset, quarter), size
            )

        pieces = (
            (refs[2], at_col, at_core, 2),
            (refs[3], at_col ^ (1 + at_core), at_core, 2),
            (refs[4], at_col ^ 3, at_core, 1),
            (refs[5], at_col ^ (1 + other), other, 2),
            (refs[6], at_col ^ 3, other, 1),
        )
        for index, (out_ref, lead) in enumerate(outs):
            for ref, core_at in ((refs[0], at_core), (refs[1], other)):
                out_ref[lead + (row_of(at_chip, core_at, 0, shard),)] = ref[
                    index * shard : (index + 1) * shard
                ]
            for ref, col, core_at, sides in pieces:
                for side in range(sides):
                    for hop in steps:
                        at = row_of(at_chip ^ hop, core_at ^ side, col * quarter, quarter)
                        start = side * unit + (hop - 1) * rows + index * quarter
                        out_ref[lead + (at,)] = ref[start : start + quarter]

    row_own, stream_own, *row_sends = kernel_call(
        pack_row,
        [((cols_axis * shard + lines, model), bf16), ((width, model), bf16)]
        + [((row_rows + width, model), bf16)] * hops,
        [spot, *row_weights, *[item[None] for item in norms], tokens],
        smem=(0,),
        stream=True,
    )
    row_got = [along_chips(row_sends[step - 1], step) for step in steps]
    feed_own, col_own, given_own, *col_sends = kernel_call(
        pack_rest,
        [
            ((2, shard, hidden), bf16),
            ((cols_axis * shard, model), bf16),
            ((width, model), bf16),
        ]
        + [((col_rows + width, model), bf16)] * hops,
        [spot, *col_weights, cotangent, feed_in, feed_out],
        smem=(0,),
        stream=True,
    )
    row_got = after(row_got, waves, allowed, col_sends)
    row_hops, stream_in = kernel_call(
        split_got,
        [((hops * row_rows, model), bf16), ((toks, model), bf16)],
        [stream_own, *row_got],
    )
    row_far_own = along_core(row_own)
    row_plane, row_pair, row_diagonal = spread_plane(row_hops, along_core(row_hops))
    col_sends = after(col_sends, row_plane)
    col_got = [along_chips(col_sends[step - 1], step) for step in steps]
    row_last = after((row_pair, row_diagonal), row_pair, row_diagonal, col_got)
    row_pieces = [row_own, row_far_own, row_plane, row_pair, row_diagonal] + [
        along_core(item) for item in row_last
    ]

    def stack_got(own_ref, *refs):
        rows = refs[0].shape[0] - width
        ins, out_ref = refs[:-1], refs[-1]
        at = hops * rows
        out_ref[at : at + width] = own_ref[...]
        for hop, ref in enumerate(ins):
            out_ref[hop * rows : (hop + 1) * rows] = ref[:rows]
            out_ref[at + (hop + 1) * width : at + (hop + 2) * width] = ref[rows:]

    col_unit = hops * col_rows + toks
    col_hops = kernel_call(stack_got, [((col_unit, model), bf16)], [given_own, *col_got])[0]
    col_far_own = along_core(col_own)
    col_plane, col_pair, col_diagonal = spread_plane(col_hops, along_core(col_hops))

    def project_row(spot_ref, stream_ref, waves_ref, *refs):
        pieces, outs = refs[:7], refs[7:]
        zero_ref, low_ref, q_ref, kv_ref, weight_ref, last_ref, norm_ref = outs
        place_rows(
            spot_ref,
            pieces,
            [(weight_ref, (index,)) for index in range(3)] + [(last_ref, ())],
            row_rows,
            hops * row_rows,
        )
        first = lax.broadcasted_iota(jnp.int32, (128, model), 0)
        lanes = lax.broadcasted_iota(jnp.int32, (128, model), 1)
        total = jnp.zeros((lines, model), f32)
        for side in (0, 1):
            for hop in range(chips):
                if hop == 0:
                    block = pieces[side][cols_axis * shard : cols_axis * shard + lines, :128]
                else:
                    at = (side * hops + hop) * row_rows - lines
                    block = pieces[2][at : at + lines, :128]
                start = ((spot_ref[1] ^ hop) * 2 + (spot_ref[2] ^ side)) * shard
                chosen = ((lanes == first + start) & (first < shard)).astype(bf16)
                total = total + dot(block, chosen)
        count = spot_ref[4].astype(f32)
        for ref in pieces[3:6]:
            count = count + ref[row_rows - lines : row_rows, :128][6:7, 0:1].astype(f32)
        rows = lax.broadcasted_iota(jnp.int32, (lines, model), 0)
        norm_ref[...] = jnp.where(rows == 6, count, total)
        for slot in range(chips):
            rows = slice(slot * width, (slot + 1) * width)
            zero_ref[rows, :half] = stream_ref[rows, :half].astype(f32) + waves_ref[:width]
            zero_ref[rows, half:] = (
                stream_ref[rows, half:].astype(f32) + waves_ref[width + slot : width + slot + 1]
            )
        unit, _ = unit_norm(zero_ref[...])
        low = (unit * norm_ref[0:1] + norm_ref[1:2]).astype(bf16)
        low_ref[...] = low
        q_ref[...] = dot(low, weight_ref[0]).astype(bf16)
        kv_ref[0] = dot(low, weight_ref[1]).astype(bf16)
        kv_ref[1] = dot(low, weight_ref[2]).astype(bf16)

    big = 2.0 * toks * model * model
    stream_zero, normed_one, row_q, row_kv, weights_row, weights_out, norm_rows = kernel_call(
        project_row,
        [
            ((toks, model), f32),
            ((toks, model), bf16),
            ((toks, model), bf16),
            ((2, toks, model), bf16),
            ((3, model, model), bf16),
            ((model, model), bf16),
            ((lines, model), f32),
        ],
        [spot, stream_in, waves, *row_pieces],
        smem=(0,),
    )
    kv_left = to_right(row_kv)
    kv_right = to_left(row_kv)

    feed_own = after(feed_own, kv_left, kv_right)
    feed_other = along_core(feed_own)

    def pair_feed(own_ref, other_ref, out_ref):
        out_ref[0] = own_ref[...]
        out_ref[1] = other_ref[...]

    feed_both = kernel_call(
        pair_feed, [((2, 2, shard, hidden), bf16)], [feed_own, feed_other]
    )[0]
    feed_pair, feed_diagonal = pair_chips(feed_both), along_chips(feed_own, chips - 1)

    def tied_logits(spot_ref, q_ref, near_ref, left_ref, right_ref, out_ref):
        mask = head_mask(width, model)
        total = None
        for slot in range(chips):
            keys = window_rows(spot_ref, near_ref, left_ref, right_ref, 0, slot, width)
            spread = spread_heads(q_ref[slot * width : (slot + 1) * width], mask)
            term = dot_back(spread, keys)
            total = term if total is None else total + term
        out_ref[...] = total

    logits = kernel_call(
        tied_logits,
        [((fold, span), f32)],
        [spot, row_q, row_kv, kv_left, kv_right],
        smem=(0,),
    )[0]
    logits_other = after(along_core(logits), col_pair, col_diagonal)
    row_scale = 1.0 / math.sqrt(HEAD_DIM * seqs)
    col_scale = 1.0 / math.sqrt(HEAD_DIM)

    def attend_row(
        spot_ref,
        logits_ref,
        other_ref,
        allowed_ref,
        near_ref,
        left_ref,
        right_ref,
        zero_ref,
        norm_ref,
        weight_ref,
        scores_ref,
        probs_ref,
        mix_ref,
        stream_ref,
        low_ref,
        entropy_ref,
    ):
        mask = head_mask(width, model)
        scores = (logits_ref[...] + other_ref[...]) * row_scale
        open_here = jnp.concatenate([allowed_ref[...]] * HEADS, axis=0) > 0.5
        masked = jnp.where(open_here, scores, -1000000000.0)
        largest = jnp.max(masked, axis=-1, keepdims=True)
        powers = jnp.exp(masked - largest)
        total = jnp.sum(powers, axis=-1, keepdims=True)
        probs = powers / total
        kept = jnp.where(open_here, scores, 0.0)
        entropies = largest + jnp.log(total) - jnp.sum(probs * kept, axis=-1, keepdims=True)
        rows = lax.broadcasted_iota(jnp.int32, (fold, 1), 0) % width
        entropies = jnp.where(rows + spot_ref[3] * width < spot_ref[4], entropies, 0.0)
        lanes = lax.broadcasted_iota(jnp.int32, (1, model), 1)
        found = jnp.sum(entropies, axis=0, keepdims=True)
        entropy_ref[...] = jnp.where((lanes == 0) & (spot_ref[2] == 0), found, 0.0)
        scores_ref[...] = kept
        probs_ref[...] = probs
        low_probs = probs.astype(bf16)
        for slot in range(chips):
            values = window_rows(spot_ref, near_ref, left_ref, right_ref, 1, slot, width)
            mix_ref[slot * width : (slot + 1) * width] = fold_heads(
                dot(low_probs, values), mask, width
            ).astype(bf16)
        stream = zero_ref[...] + dot(mix_ref[...], weight_ref[...])
        stream_ref[...] = stream
        unit, _ = unit_norm(stream)
        low_ref[...] = (unit * norm_ref[2:3] + norm_ref[3:4]).astype(bf16)

    scores, probs, row_mix, stream_one, normed_two, entropy_row = kernel_call(
        attend_row,
        [
            ((fold, span), f32),
            ((fold, span), f32),
            ((toks, model), bf16),
            ((toks, model), f32),
            ((toks, model), bf16),
            ((1, model), f32),
        ],
        [
            spot,
            logits,
            logits_other,
            allowed,
            row_kv,
            kv_left,
            kv_right,
            stream_zero,
            norm_rows,
            weights_out,
        ],
        smem=(0,),
    )

    col_last = after((col_pair, col_diagonal), normed_two)
    col_pieces = [col_own, col_far_own, col_plane, col_pair, col_diagonal] + [
        along_core(item) for item in col_last
    ]

    def assemble_col(spot_ref, *refs):
        three_ref, last_ref, given_ref = refs[7:]
        outs = [(three_ref, (index,)) for index in range(3)] + [(last_ref, ())]
        place_rows(spot_ref, refs[:7], outs, col_rows, col_unit)
        at_core = spot_ref[2]
        start = hops * col_rows
        given_ref[0] = refs[2][start:col_unit]
        given_ref[1 + at_core] = refs[3][start:col_unit]
        given_ref[2 - at_core] = refs[5][col_unit + start :]
        given_ref[3] = refs[4][start:]

    weights_three, weights_last, given_all = kernel_call(
        assemble_col,
        [
            ((3, model, model), bf16),
            ((model, model), bf16),
            ((cols_axis, toks, model), bf16),
        ],
        [spot, *col_pieces],
        smem=(0,),
    )

    def project_col(low_ref, weight_ref, q_ref, kv_ref):
        low = low_ref[...]
        q_ref[...] = dot(low, weight_ref[0]).astype(bf16)
        kv_ref[0] = dot(low, weight_ref[1]).astype(bf16)
        kv_ref[1] = dot(low, weight_ref[2]).astype(bf16)

    col_q, col_kv = kernel_call(
        project_col,
        [((toks, model), bf16), ((2, toks, model), bf16)],
        [normed_two, weights_three],
    )
    kv_other = along_core(col_kv)

    def slot_rows(slot):
        return slice(slot * width, (slot + 1) * width)

    def attend_col(
        q_ref,
        near_ref,
        far_ref,
        one_ref,
        norm_ref,
        weight_ref,
        probs_ref,
        mix_ref,
        stream_ref,
        low_ref,
    ):
        lane_heads = head_of_lane(model)
        sides = (near_ref, far_ref)
        for slot in range(chips):
            query = q_ref[slot_rows(slot)].astype(f32)
            products = jnp.concatenate(
                [
                    query * sides[s // chips][0, slot_rows(s % chips)].astype(f32)
                    for s in range(seqs)
                ],
                axis=0,
            )
            found = per_head_sum(products, lane_heads) * col_scale
            parts = [found[s * width : (s + 1) * width] for s in range(seqs)]
            largest = parts[0]
            for item in parts[1:]:
                largest = jnp.maximum(largest, item)
            powers = [jnp.exp(item - largest) for item in parts]
            total = powers[0]
            for item in powers[1:]:
                total = total + item
            weights = jnp.concatenate([item / total for item in powers], axis=0)
            probs_ref[slot] = weights
            wide = dot_back(weights.astype(bf16), lane_heads)
            mixed = None
            for s in range(seqs):
                term = wide[s * width : (s + 1) * width] * sides[s // chips][
                    1, slot_rows(s % chips)
                ].astype(f32)
                mixed = term if mixed is None else mixed + term
            mix_ref[slot_rows(slot)] = mixed.astype(bf16)
        stream = one_ref[...] + dot(mix_ref[...], weight_ref[...])
        stream_ref[...] = stream
        unit, _ = unit_norm(stream)
        low_ref[...] = (unit * norm_ref[4:5] + norm_ref[5:6]).astype(bf16)

    col_probs, col_mix, stream_two, normed_three = kernel_call(
        attend_col,
        [
            ((chips, seqs * width, 128), f32),
            ((toks, model), bf16),
            ((toks, model), f32),
            ((toks, model), bf16),
        ],
        [col_q, col_kv, kv_other, stream_one, norm_rows, weights_last],
    )
    low_near = [normed_three] + [along_cols(normed_three, step) for step in col_steps]

    feed_last = after((feed_pair, feed_diagonal), low_near)
    feed_far = [along_core(item) for item in feed_last]

    def assemble_feed(spot_ref, both_ref, pair_ref, last_ref, pair2_ref, last2_ref, out_ref):
        at_chip, at_core = spot_ref[1], spot_ref[2]
        other = 1 - at_core

        def move(rows, from_chip, from_core):
            at = pl.multiple_of((from_chip * 2 + from_core) * shard, shard)
            out_ref[:, pl.ds(at, shard)] = rows

        for side in (0, 1):
            move(both_ref[side], at_chip, at_core ^ side)
            move(pair_ref[side], at_chip ^ (1 + at_core), at_core ^ side)
            move(pair2_ref[side], at_chip ^ (1 + other), other ^ side)
        move(last_ref[...], at_chip ^ 3, at_core)
        move(last2_ref[...], at_chip ^ 3, other)

    weights_feed = kernel_call(
        assemble_feed,
        [((2, model, hidden), bf16)],
        [spot, feed_both, feed_pair, feed_diagonal, *feed_far],
        smem=(0,),
    )[0]

    def feed_main(a0, a1, a2, a3, given_ref, weight_ref, act_ref, grad_ref, *back_refs):
        up, down = weight_ref[0], weight_ref[1]
        for step, low_ref in enumerate((a0, a1, a2, a3)):
            pre = dot(low_ref[...], up)
            bell = 0.5 * (1.0 + lax.erf(pre * (0.5**0.5)))
            slope = bell + pre * jnp.exp(-0.5 * pre * pre) * ((0.5 / math.pi) ** 0.5)
            act_ref[step] = (pre * bell).astype(bf16)
            grad = (slope * dot_back(given_ref[step], down)).astype(bf16)
            grad_ref[step] = grad
            back_refs[step][...] = dot_back(grad, up).astype(bf16)

    feed_big = 2.0 * toks * cols_axis * model * hidden
    feed_results = kernel_call(
        feed_main,
        [((cols_axis, toks, hidden), bf16)] * 2 + [((toks, model), bf16)] * cols_axis,
        [*low_near, given_all, weights_feed],
    )
    act, grad_hidden, back_parts = feed_results[0], feed_results[1], feed_results[2:]
    back_near = [back_parts[0]] + [along_cols(back_parts[step], step) for step in col_steps]

    def feed_weights(
        spot_ref, a0, a1, a2, a3, given_ref, act_ref, grad_ref, weight_ref, mine_ref, give_ref, *outs
    ):
        at_core = spot_ref[2]
        low = jnp.concatenate([a0[...], a1[...], a2[...], a3[...]], axis=0)
        given = given_ref[...].reshape(cols_axis * toks, model)
        rows = cols_axis * toks
        acts = act_ref[...].reshape(rows, hidden)
        grads = grad_ref[...].reshape(rows, hidden)
        for step in range(cols_axis):
            outs[step][...] = dot(act_ref[step], weight_ref[1]).astype(bf16)
        for ref, at in ((mine_ref, at_core), (give_ref, 1 - at_core)):
            ref[:model] = dot_tokens(low, half_of(grads, at, half)).astype(bf16)
            ref[model:] = dot_tokens(acts, half_of(given, at, half)).astype(bf16)

    feed_grads = kernel_call(
        feed_weights,
        [((2 * model, half), bf16)] * 2 + [((toks, model), bf16)] * cols_axis,
        [spot, *low_near, given_all, act, grad_hidden, weights_feed],
        smem=(0,),
        flops=6.0 * toks * cols_axis * model * hidden,
        moved=16 << 20,
        room=24,
    )
    feed_mine, feed_give, out_parts = feed_grads[0], feed_grads[1], feed_grads[2:]
    feed_back_in = along_core(feed_give)

    block = 2 * shard
    extra = 2 * lines

    def renew(total, at):
        line = total[at : at + 1]
        whole = line[:, 0:1] + line[:, 1:2]
        high = whole.astype(bf16).astype(f32)
        lanes = lax.broadcasted_iota(jnp.int32, total.shape, 1)
        rows = lax.broadcasted_iota(jnp.int32, total.shape, 0)
        total = jnp.where((rows == at) & (lanes == 0), high, total)
        return jnp.where((rows == at) & (lanes == 1), whole - high, total)

    def layer_grads(low, mix, low_far, mix_far, mine, got, more):
        rows = model + (extra if len(more) == 1 else 2 * toks)

        def weight_sums(spot_ref, low_ref, mix_ref, low2_ref, mix2_ref, mine_ref, got_ref, *refs):
            more_refs, outs = refs[: len(more)], refs[len(more) : -2]
            left_ref, right_ref = refs[-2:]
            left_ref[0, :toks] = low_ref[...]
            left_ref[0, toks:] = low2_ref[...]
            left_ref[1, :toks] = mix_ref[...]
            left_ref[1, toks:] = mix2_ref[...]
            right_ref[:, :toks] = mine_ref[...]
            right_ref[:, toks:] = got_ref[...]
            for step in range(cols_axis):
                matrix = spot_ref[0] ^ step
                left = left_ref[matrix // 3]
                outs[step][:model] = dot_tokens(left, right_ref[matrix]).astype(bf16)
                if len(more) == 1:
                    sums_ref = more_refs[0]
                    tail = jnp.concatenate([sums_ref[:, :half], sums_ref[:, half:]], axis=0)
                    outs[step][model:] = renew(tail, 6).astype(bf16)
                else:
                    outs[step][model : model + toks] = more_refs[step][:, :half]
                    outs[step][model + toks :] = more_refs[step][:, half:]

        return kernel_call(
            weight_sums,
            [((rows, half), bf16)] * cols_axis,
            [spot, low, mix, low_far, mix_far, mine, got, *more],
            smem=(0,),
            scratch=[
                pltpu.VMEM((2, 2 * toks, model), bf16),
                pltpu.VMEM((4, 2 * toks, half), bf16),
            ],
        )

    def split_chips(items, count, tail, stream=None, slots=()):
        slot_rows_out = 2 * width if stream is not None or slots else 0

        def chip_parts(spot_ref, *refs):
            ins, outs, total_ref = refs[: len(items)], refs[-chips - 1 : -1], refs[-1]
            more = refs[len(items) : -chips - 1]
            total = ins[0][...].astype(f32)
            for ref in ins[1:]:
                total = total + ref[...].astype(f32)
            total_ref[...] = total.astype(bf16)
            if stream is not None:
                result = more[0][...] + jnp.concatenate(
                    [total[model : model + toks], total[model + toks :]], axis=1
                )
            for hop in range(chips):
                at = pl.multiple_of((spot_ref[1] ^ hop) * block, block)
                for index in range(count):
                    outs[hop][index * block : (index + 1) * block] = total_ref[
                        pl.ds(index * model + at, block)
                    ]
                row = count * block
                if tail:
                    outs[hop][row : row + tail] = renew(total[count * model :], 6).astype(bf16)
                    row = row + tail
                if slot_rows_out:
                    if stream is not None:
                        slot = result[slot_rows(hop)].astype(bf16)
                    else:
                        slot = more[hop][...]
                    outs[hop][row : row + width] = slot[:, :half]
                    outs[hop][row + width :] = slot[:, half:]

        size = count * block + tail + slot_rows_out
        return kernel_call(
            chip_parts,
            [((size, half), bf16)] * chips,
            [spot, *items] + ([] if stream is None else [stream]) + list(slots),
            smem=(0,),
            scratch=[pltpu.VMEM(items[0].shape, bf16)],
        )

    def split_cores(items, count, tail):
        rows_in = count * block + tail

        def core_parts(spot_ref, *refs):
            ins, (keep_ref, give_ref, total_ref) = refs[: len(items)], refs[len(items) :]
            total = ins[0][:rows_in].astype(f32)
            for ref in ins[1:]:
                total = total + ref[:rows_in].astype(f32)
            total_ref[...] = total.astype(bf16)
            for ref, at in ((keep_ref, spot_ref[2]), (give_ref, 1 - spot_ref[2])):
                for index in range(count):
                    row = pl.multiple_of(index * block + at * shard, shard)
                    ref[index * shard : (index + 1) * shard] = total_ref[pl.ds(row, shard)]
                if tail:
                    ref[count * shard :] = renew(total[count * block :], 6).astype(bf16)

        size = count * shard + tail
        return kernel_call(
            core_parts,
            [((size, half), bf16)] * 2,
            [spot, *items],
            smem=(0,),
            scratch=[pltpu.VMEM((rows_in, half), bf16)],
        )

    def over_chips(parts):
        return [parts[0]] + [along_chips(parts[step], step) for step in steps]

    feed_slices = split_chips([feed_mine, feed_back_in], 2, 0)
    back_near = after(back_near, feed_slices)

    def attend_col_back(
        spot_ref,
        b0,
        b1,
        b2,
        b3,
        given_ref,
        two_ref,
        norm_ref,
        weight_ref,
        q_ref,
        near_ref,
        far_ref,
        probs_ref,
        dtwo_ref,
        low_ref,
        dq_ref,
        dkv_ref,
        send_ref,
        sums_ref,
        wide_ref,
    ):
        lane_heads = head_of_lane(model)
        back = b0[...].astype(f32) + b1[...].astype(f32) + b2[...].astype(f32) + b3[...].astype(f32)
        unit, scale = unit_norm(two_ref[...])
        sums_ref[...] = norm_sums(back, unit)
        dtwo = given_ref[0].astype(f32) + unit_norm_back(back, unit, scale, norm_ref[4:5])
        dtwo_ref[...] = dtwo
        low = dtwo.astype(bf16)
        low_ref[...] = low
        dmix = dot_back(low, weight_ref[...]).astype(bf16).astype(f32)
        wide_ref[...] = jnp.zeros_like(wide_ref)
        sides = (near_ref, far_ref)
        for slot in range(chips):
            dout = dmix[slot_rows(slot)]
            query = q_ref[slot_rows(slot)].astype(f32)
            products = jnp.concatenate(
                [
                    dout * sides[s // chips][1, slot_rows(s % chips)].astype(f32)
                    for s in range(seqs)
                ],
                axis=0,
            )
            found = per_head_sum(products, lane_heads)
            weights = probs_ref[slot]
            mean = None
            for s in range(seqs):
                rows = slice(s * width, (s + 1) * width)
                term = weights[rows] * found[rows]
                mean = term if mean is None else mean + term
            dscores = (weights * (found - jnp.concatenate([mean] * seqs, axis=0))).astype(bf16)
            wide_d = dot_back(dscores, lane_heads)
            wide_p = dot_back(weights.astype(bf16), lane_heads)
            dquery = None
            for s in range(seqs):
                rows = slice(s * width, (s + 1) * width)
                term = wide_d[rows] * sides[s // chips][0, slot_rows(s % chips)].astype(f32)
                dquery = term if dquery is None else dquery + term
                wide_ref[0, rows] += wide_d[rows] * query
                wide_ref[1, rows] += wide_p[rows] * dout
            dq_ref[slot_rows(slot)] = (dquery * col_scale).astype(bf16)
        dkv_ref[0] = wide_ref[0, :toks] * col_scale
        dkv_ref[1] = wide_ref[1, :toks]
        send_ref[0] = (wide_ref[0, toks:] * col_scale).astype(bf16)
        send_ref[1] = wide_ref[1, toks:].astype(bf16)

    grad_two, grad_two_low, col_dq, col_dkv, col_send, sums_three = kernel_call(
        attend_col_back,
        [
            ((toks, model), f32),
            ((toks, model), bf16),
            ((toks, model), bf16),
            ((2, toks, model), f32),
            ((2, toks, model), bf16),
            ((2, model), f32),
        ],
        [
            spot,
            *back_near,
            given_all,
            stream_two,
            norm_rows,
            weights_last,
            col_q,
            col_kv,
            kv_other,
            col_probs,
        ],
        smem=(0,),
        scratch=[pltpu.VMEM((2, 2 * toks, model), f32)],
    )
    dkv_got = along_core(col_send)

    def row_entry_back(
        spot_ref,
        dq_ref,
        dkv_ref,
        got_ref,
        low_two_ref,
        dtwo_ref,
        one_ref,
        norm_ref,
        col_ref,
        row_ref,
        near_ref,
        left_ref,
        right_ref,
        mine_ref,
        give_ref,
        done_ref,
        low_ref,
        dmix_ref,
        dprobs_ref,
        sums_ref,
    ):
        at_core = spot_ref[2]
        dq = dq_ref[...]
        dk = (dkv_ref[0] + got_ref[0].astype(f32)).astype(bf16)
        dv = (dkv_ref[1] + got_ref[1].astype(f32)).astype(bf16)
        for index, item in enumerate((dq, dk, dv, low_two_ref[...])):
            mine_ref[index] = half_of(item, at_core, half)
            give_ref[index] = half_of(item, 1 - at_core, half)
        back = dot_back(dq, col_ref[0]) + dot_back(dk, col_ref[1]) + dot_back(dv, col_ref[2])
        unit, scale = unit_norm(one_ref[...])
        sums_ref[...] = norm_sums(back, unit)
        done = dtwo_ref[...] + unit_norm_back(back, unit, scale, norm_ref[2:3])
        done_ref[...] = done
        low = done.astype(bf16)
        low_ref[...] = low
        dmix = dot_back(low, row_ref[...]).astype(bf16)
        dmix_ref[...] = dmix
        mask = head_mask(width, model)
        total = None
        for slot in range(chips):
            values = window_rows(spot_ref, near_ref, left_ref, right_ref, 1, slot, width)
            term = dot_back(spread_heads(dmix[slot_rows(slot)], mask), values)
            total = term if total is None else total + term
        dprobs_ref[...] = total

    (
        col_mine,
        col_give,
        grad_one,
        grad_one_low,
        row_dmix,
        dprobs,
        sums_two,
    ) = kernel_call(
        row_entry_back,
        [
            ((4, toks, half), bf16),
            ((4, toks, half), bf16),
            ((toks, model), f32),
            ((toks, model), bf16),
            ((toks, model), bf16),
            ((fold, span), f32),
            ((2, model), f32),
        ],
        [
            spot,
            col_dq,
            col_dkv,
            dkv_got,
            grad_two_low,
            grad_two,
            stream_one,
            norm_rows,
            weights_three,
            weights_out,
            row_kv,
            kv_left,
            kv_right,
        ],
        smem=(0,),
    )
    dprobs_other = along_core(dprobs)
    col_sums = layer_grads(
        normed_two,
        col_mix,
        along_core(normed_two),
        along_core(col_mix),
        col_mine,
        along_core(col_give),
        out_parts,
    )
    dprobs_other = after(dprobs_other, col_sums)

    def attend_row_back(
        spot_ref,
        weight_ref,
        dprobs_ref,
        other_ref,
        scores_ref,
        probs_ref,
        q_ref,
        near_ref,
        left_ref,
        right_ref,
        dmix_ref,
        dq_ref,
        dkv_ref,
        to_left_ref,
        to_right_ref,
    ):
        mask = head_mask(width, model)
        dprob = dprobs_ref[...] + other_ref[...]
        probs_here, scores_here = probs_ref[...], scores_ref[...]
        rows = lax.broadcasted_iota(jnp.int32, (fold, 1), 0) % width
        weight = jnp.where(rows + spot_ref[3] * width < spot_ref[4], entropy_weight / (HEADS * weight_ref[6:7, 0:1]), 0.0)
        first = dprob - jnp.sum(probs_here * dprob, axis=-1, keepdims=True)
        second = scores_here - jnp.sum(probs_here * scores_here, axis=-1, keepdims=True)
        dscores = (probs_here * (first - weight * second)).astype(bf16)
        low_probs = probs_here.astype(bf16)
        for slot in range(chips):
            at = slot_rows(slot)
            keys = window_rows(spot_ref, near_ref, left_ref, right_ref, 0, slot, width)
            dq_ref[at] = (
                fold_heads(dot(dscores, keys), mask, width) * row_scale
            ).astype(bf16)
            dkeys = dot_tokens(dscores, spread_heads(q_ref[at], mask)) * row_scale
            dvalues = dot_tokens(low_probs, spread_heads(dmix_ref[at], mask))
            for index, item in enumerate((dkeys, dvalues)):
                to_left_ref[index, at] = item[:width].astype(bf16)
                dkv_ref[index, at] = item[width : 2 * width]
                to_right_ref[index, at] = item[2 * width :].astype(bf16)

    row_dq, row_dkv, edge_left, edge_right = kernel_call(
        attend_row_back,
        [
            ((toks, model), bf16),
            ((2, toks, model), f32),
            ((2, toks, model), bf16),
            ((2, toks, model), bf16),
        ],
        [
            spot,
            norm_rows,
            dprobs,
            dprobs_other,
            scores,
            probs,
            row_q,
            row_kv,
            kv_left,
            kv_right,
            row_dmix,
        ],
        smem=(0,),
    )
    edge_from_right = to_left(edge_left)
    edge_from_left = to_right(edge_right)
    feed_keep, feed_swap = split_cores(over_chips(feed_slices), 2, 0)
    edge_from_left = after(edge_from_left, feed_keep)

    def input_back(
        spot_ref,
        dq_ref,
        dkv_ref,
        from_right_ref,
        from_left_ref,
        low_one_ref,
        done_ref,
        zero_ref,
        norm_ref,
        row_ref,
        two_ref,
        three_ref,
        entropy_ref,
        mine_ref,
        give_ref,
        sums_ref,
        *slot_refs,
    ):
        at_core = spot_ref[2]
        dq = dq_ref[...]
        dk, dv = (
            jnp.concatenate(
                [
                    (
                        dkv_ref[index, slot_rows(slot)]
                        + from_left_ref[index, slot_span(spot_ref, 5, slot, width)].astype(f32)
                        + from_right_ref[index, slot_span(spot_ref, 6, slot, width)].astype(f32)
                    ).astype(bf16)
                    for slot in range(chips)
                ],
                axis=0,
            )
            for index in (0, 1)
        )
        for index, item in enumerate((dq, dk, dv, low_one_ref[...])):
            mine_ref[index] = half_of(item, at_core, half)
            give_ref[index] = half_of(item, 1 - at_core, half)
        back = dot_back(dq, row_ref[0]) + dot_back(dk, row_ref[1]) + dot_back(dv, row_ref[2])
        unit, scale = unit_norm(zero_ref[...])
        sums_ref[0:2] = norm_sums(back, unit)
        sums_ref[2:4] = two_ref[...]
        sums_ref[4:6] = three_ref[...]
        sums_ref[6:7] = entropy_ref[...]
        sums_ref[7:8] = jnp.zeros((1, model), f32)
        result = (done_ref[...] + unit_norm_back(back, unit, scale, norm_ref[0:1])).astype(bf16)
        for slot in range(chips):
            slot_refs[slot][...] = result[slot_rows(slot)]

    row_mine, row_give, sums, *grad_slots = kernel_call(
        input_back,
        [
            ((4, toks, half), bf16),
            ((4, toks, half), bf16),
            ((lines, model), f32),
        ]
        + [((width, model), bf16)] * chips,
        [
            spot,
            row_dq,
            row_dkv,
            edge_from_right,
            edge_from_left,
            grad_one_low,
            grad_one,
            stream_zero,
            norm_rows,
            weights_row,
            sums_two,
            sums_three,
            entropy_row,
        ],
        smem=(0,),
    )

    def join_halves(spot_ref, keep_rows, got_rows):
        first = spot_ref[2] == 0
        return jnp.concatenate(
            [jnp.where(first, keep_rows, got_rows), jnp.where(first, got_rows, keep_rows)], axis=1
        )

    def over_cols(whole):
        return [whole] + [along_cols(whole, step) for step in col_steps]

    def order_rows(slices, at):
        def order_slots(spot_ref, *refs):
            for hop, ref in enumerate(refs[:-1]):
                refs[-1][0, chunk_at(spot_ref, spot_ref[1] ^ hop)] = jnp.concatenate(
                    [ref[at : at + width], ref[at + width : at + 2 * width]], axis=1
                )

        return kernel_call(order_slots, [(tokens.shape, bf16)], [spot, *slices], smem=(0,))[0]

    feed_back = along_core(feed_swap)
    col_parts = [col_sums[0]] + [along_cols(col_sums[step], step) for step in col_steps]
    col_slices = split_chips(col_parts, 1, 0, stream=stream_two)
    col_slices = after(col_slices, sums)
    col_reached = over_chips(col_slices)
    col_keep, col_swap = split_cores(col_reached, 1, 0)

    def join_two(spot_ref, keep_ref, got_ref, keep2_ref, got2_ref, out_ref):
        rows = 2 * shard
        out_ref[:rows] = join_halves(spot_ref, keep_ref[...], got_ref[...])
        out_ref[rows:] = join_halves(spot_ref, keep2_ref[...], got2_ref[...])

    (pair,) = kernel_call(
        join_two,
        [((3 * shard, model), bf16)],
        [spot, feed_keep, feed_back, col_keep, along_core(col_swap)],
        smem=(0,),
    )
    pair_ends = over_cols(pair)
    result = order_rows(col_reached, block)

    def spread_pair(spot_ref, u0, u1, u2, u3, in_ref, out_ref, g0, g1, g2, g3, all_ref):
        for step, ref in enumerate((u0, u1, u2, u3)):
            all_ref[spot_ref[0] ^ step] = ref[...]
        for source, grad_ref in enumerate((g0, g1, g2, g3)):
            wide = all_ref[source, :shard].astype(f32)
            for index in range(seqs):
                at = index * block_cols + source * part
                in_ref[:, at : at + part] = wide[:, index * part : (index + 1) * part]
            out_ref[source * part : (source + 1) * part] = all_ref[
                source, shard : 2 * shard
            ].astype(f32)
            grad_ref[...] = all_ref[source, 2 * shard :].astype(f32)

    row_parts = layer_grads(
        normed_one,
        row_mix,
        along_core(normed_one),
        along_core(row_mix),
        row_mine,
        along_core(row_give),
        [sums],
    )
    row_parts = [row_parts[0]] + [along_cols(row_parts[step], step) for step in col_steps]
    row_slices = split_chips(row_parts, 1, extra, slots=grad_slots)
    row_reached = over_chips(row_slices)
    row_keep, row_swap = split_cores(row_reached, 1, extra)

    def join_row(spot_ref, keep_ref, got_ref, out_ref, norm_ref, entropy_ref):
        out_ref[...] = join_halves(spot_ref, keep_ref[:shard], got_ref[:shard])
        total = keep_ref[shard:].astype(f32) + got_ref[shard:].astype(f32)
        line = total[6:7]
        entropy_ref[...] = line[:, 0:1] + line[:, 1:2]
        wide = jnp.concatenate([total[:lines], total[lines:]], axis=1)
        at = spot_ref[1] * 2 + spot_ref[2]
        found = wide[:, :shard]
        for index in range(1, seqs):
            here = wide[:, index * shard : (index + 1) * shard]
            found = jnp.where(at == index, here, found)
        norm_ref[...] = found

    row_join, norm_here, entropy_sum = kernel_call(
        join_row,
        [((shard, model), bf16), ((lines, shard), f32), ((1, 1), f32)],
        [spot, row_keep, along_core(row_swap)],
        smem=(0,),
    )
    row_ends = over_cols(row_join)
    grad_in = order_rows(row_reached, block + extra)
    grad_feed_in, grad_feed_out, *col_grads = kernel_call(
        spread_pair,
        [(feed_in.shape, f32), (feed_out.shape, f32)] + [((shard, model), f32)] * cols_axis,
        [spot, *pair_ends],
        smem=(0,),
        scratch=[pltpu.VMEM((cols_axis, 3 * shard, model), bf16)],
        room=24,
    )

    def spread_row(spot_ref, *refs):
        ins, outs, all_ref = refs[:cols_axis], refs[cols_axis:-1], refs[-1]
        for step, ref in enumerate(ins):
            all_ref[spot_ref[0] ^ step] = ref[...]
        for matrix in range(cols_axis):
            outs[matrix][...] = all_ref[matrix].astype(f32)

    row_grads = kernel_call(
        spread_row,
        [((shard, model), f32)] * cols_axis,
        [spot, *row_ends],
        smem=(0,),
        scratch=[pltpu.VMEM((cols_axis, shard, model), bf16)],
    )
    entropy = entropy_sum[0, 0] / (HEADS * norm_rows[6, 0])

    return (
        result,
        entropy,
        grad_in,
        *[norm_here[index] for index in range(6)],
        *row_grads,
        *col_grads,
        grad_feed_in,
        grad_feed_out,
    )


def fits_fast(tokens, feed_out):
    chips = lax.axis_size("seq") // 2
    return (
        lax.axis_size("col") == 4
        and lax.axis_size("seq") == 8
        and tokens.shape[0] == 1
        and tokens.shape[1] == chips * WINDOW
        and tokens.shape[2] == HEADS * HEAD_DIM
        and feed_out.shape[0] * 2 == tokens.shape[2]
    )


def on_device(tokens, offsets, band, col_counts, *rest):
    if not fits_fast(tokens, rest[15]):
        return general_plan(tokens, offsets, band, col_counts, *rest)
    return fast_plan(
        tokens,
        offsets,
        band,
        col_counts,
        rest[0:6],
        rest[6:10],
        rest[10:14],
        rest[14],
        rest[15],
        rest[16],
    )


def solution(mesh):
    return jax.shard_map(
        on_device,
        mesh=mesh,
        in_specs=(
            P("seq", "col", None),
            P(),
            P("col", None),
            P("col"),
            P("seq"),
            P("seq"),
            P("seq"),
            P("seq"),
            P("seq"),
            P("seq"),
            P("seq", None),
            P("seq", None),
            P("seq", None),
            P("seq", None),
            P("seq", None),
            P("seq", None),
            P("seq", None),
            P("seq", None),
            P("seq", None),
            P("seq", None),
            P("seq", "col", None),
        ),
        out_specs=(
            P("seq", "col", None),
            P(),
            P("seq", "col", None),
            P("seq"),
            P("seq"),
            P("seq"),
            P("seq"),
            P("seq"),
            P("seq"),
            P("seq", None),
            P("seq", None),
            P("seq", None),
            P("seq", None),
            P("seq", None),
            P("seq", None),
            P("seq", None),
            P("seq", None),
            P("seq", None),
            P("seq", None),
        ),
        check_vma=False,
    )
```

```python
from functools import partial
import math

import jax
import jax.numpy as jnp
from jax import lax
from jax.experimental import pallas as pl
from jax.experimental.pallas import tpu as pltpu
from jax.sharding import PartitionSpec as P

HEADS = 12
HEAD_DIM = 64
WINDOW = 32


entropy_weight = 8192.0
norm_eps = 1e-05


def with_halo(cells, sides, width):
    for axis, dim in sides:
        count = lax.axis_size(axis)
        ends = count - 1
        head = lax.slice_in_dim(cells, 0, width, axis=dim)
        tail = lax.slice_in_dim(cells, cells.shape[dim] - width, cells.shape[dim], axis=dim)
        cells = jnp.concatenate(
            [
                lax.ppermute(tail, axis, [(i, (i + 1) % count) for i in range(ends)]),
                cells,
                lax.ppermute(head, axis, [((i + 1) % count, i) for i in range(ends)]),
            ],
            axis=dim,
        )
    return cells


def layer_norm(inputs, norm_gain, norm_shift):
    average = jnp.mean(inputs, axis=-1, keepdims=True)
    centred = inputs - average
    variance = jnp.mean(centred * centred, axis=-1, keepdims=True)
    return centred * lax.rsqrt(variance + norm_eps) * norm_gain + norm_shift


def position_table(offsets, row_first, col_first, row_count, col_count, model_width):
    half_width = model_width // 2
    frequency = jnp.exp(-math.log(1000.0) * jnp.arange(half_width, dtype=jnp.float32) / half_width)
    col_place = (jnp.arange(col_count, dtype=jnp.int32) + col_first + offsets[1]).astype(
        jnp.float32
    )
    row_place = (jnp.arange(row_count, dtype=jnp.int32) + row_first + offsets[0]).astype(
        jnp.float32
    )
    col_wave = jnp.sin(col_place[:, None] * frequency[None, :])
    row_wave = jnp.sin(row_place[:, None] * frequency[None, :])
    col_full = jnp.broadcast_to(col_wave[None, :, :], (row_count, col_count, half_width))
    row_full = jnp.broadcast_to(row_wave[:, None, :], (row_count, col_count, half_width))
    return 0.5 * jnp.concatenate([col_full, row_full], axis=-1)


def softmax_entropy(scores, allowed, valid):
    masked = jnp.where(allowed[None], scores, -1000000000.0)
    largest = jnp.max(masked, axis=-1, keepdims=True)
    powers = jnp.exp(masked - largest)
    row_total = jnp.sum(powers, axis=-1, keepdims=True)
    probs_out = powers / row_total
    log_total = largest[..., 0] + jnp.log(row_total[..., 0])
    entropies = log_total - jnp.sum(probs_out * jnp.where(allowed[None], scores, 0.0), axis=-1)
    return (probs_out, jnp.sum(entropies * valid[None, :]))


def plain_softmax(scores):
    largest = jnp.max(scores, axis=-1, keepdims=True)
    powers = jnp.exp(scores - largest)
    return powers / jnp.sum(powers, axis=-1, keepdims=True)


def project(activations, weight):
    return jnp.einsum("rci,ij->rcj", activations, weight, preferred_element_type=jnp.float32)


def project_back(gradient, weight):
    return jnp.einsum("rcj,ij->rci", gradient, weight, preferred_element_type=jnp.float32)


def weight_grad(activations, gradient):
    return jnp.einsum("rci,rcj->ij", activations, gradient, preferred_element_type=jnp.float32)


def general_plan(
    tokens,
    offsets,
    band,
    col_counts,
    norm1_gain,
    norm1_shift,
    norm2_gain,
    norm2_shift,
    norm3_gain,
    norm3_shift,
    row_query,
    row_key,
    row_value,
    row_output,
    col_query,
    col_key,
    col_value,
    col_output,
    feed_in,
    feed_out,
    cotangent,
):
    rows_dev, cols_dev, model_width = tokens.shape
    total_rows = rows_dev * lax.axis_size("seq")
    total_cols = cols_dev * lax.axis_size("col")
    row_first = lax.axis_index("seq") * rows_dev
    col_first = lax.axis_index("col") * cols_dev
    count_here = col_counts[0].astype(jnp.float32)
    count_early = lax.psum(count_here, "col")
    params = (
        lax.all_gather(norm1_gain, "seq", axis=0, tiled=True),
        lax.all_gather(norm1_shift, "seq", axis=0, tiled=True),
        lax.all_gather(norm2_gain, "seq", axis=0, tiled=True),
        lax.all_gather(norm2_shift, "seq", axis=0, tiled=True),
        lax.all_gather(norm3_gain, "seq", axis=0, tiled=True),
        lax.all_gather(norm3_shift, "seq", axis=0, tiled=True),
        lax.all_gather(row_query, "seq", axis=0, tiled=True),
        lax.all_gather(row_key, "seq", axis=0, tiled=True),
        lax.all_gather(row_value, "seq", axis=0, tiled=True),
        lax.all_gather(row_output, "seq", axis=0, tiled=True),
        lax.all_gather(col_query, "seq", axis=0, tiled=True),
        lax.all_gather(col_key, "seq", axis=0, tiled=True),
        lax.all_gather(col_value, "seq", axis=0, tiled=True),
        lax.all_gather(col_output, "seq", axis=0, tiled=True),
        lax.all_gather(feed_in, "seq", axis=0, tiled=True),
        lax.all_gather(feed_out, "seq", axis=0, tiled=True),
    )
    gain_one = params[0].astype(jnp.float32)
    shift_one = params[1].astype(jnp.float32)
    gain_two = params[2].astype(jnp.float32)
    shift_two = params[3].astype(jnp.float32)
    gain_three = params[4].astype(jnp.float32)
    shift_three = params[5].astype(jnp.float32)
    query_row, key_row, value_row, output_row = (params[6], params[7], params[8], params[9])
    query_col, key_col, value_col, output_col = (params[10], params[11], params[12], params[13])
    feed_up, feed_down = (params[14], params[15])
    stream_zero = tokens.astype(jnp.float32) + position_table(
        offsets, row_first, col_first, rows_dev, cols_dev, model_width
    )
    normed_one, norm_back_one = jax.vjp(layer_norm, stream_zero, gain_one, shift_one)
    normed_one = normed_one.astype(jnp.bfloat16)
    row_queries = project(normed_one, query_row).astype(jnp.bfloat16)
    row_keys = project(normed_one, key_row).astype(jnp.bfloat16)
    row_values = project(normed_one, value_row).astype(jnp.bfloat16)
    extended = with_halo(jnp.stack([row_keys, row_values]), (("col", 2),), WINDOW)
    ext_cols = cols_dev + 2 * WINDOW
    queries_heads = row_queries.reshape(rows_dev, cols_dev, HEADS, HEAD_DIM)
    keys_ext = extended[0].reshape(rows_dev, ext_cols, HEADS, HEAD_DIM)
    values_ext = extended[1].reshape(rows_dev, ext_cols, HEADS, HEAD_DIM)
    partial_logits = jnp.einsum(
        "rchd,rehd->hce", queries_heads, keys_ext, preferred_element_type=jnp.float32
    )
    row_scale = 1.0 / math.sqrt(HEAD_DIM * total_rows)
    row_scores = lax.psum(partial_logits, "seq") * row_scale
    query_index = jnp.arange(cols_dev, dtype=jnp.int32)[:, None]
    key_index = jnp.arange(ext_cols, dtype=jnp.int32)[None, :]
    distance = key_index - query_index
    choose = jnp.arange(2 * WINDOW + 1, dtype=jnp.int32)
    matches = (distance[:, None, :] == choose[None, :, None]) & (band[:, :, None] == 1)
    key_global = col_first - WINDOW + key_index
    inside = (key_global >= 0) & (key_global < total_cols)
    allowed = (jnp.any(matches, axis=1) | (distance == WINDOW)) & inside
    valid = (jnp.arange(cols_dev, dtype=jnp.int32) < col_counts[0]).astype(jnp.float32)
    (row_probs, ent_part), ent_back = jax.vjp(
        lambda given: softmax_entropy(given, allowed, valid), row_scores
    )
    payload = ent_part[None]
    sums = lax.psum(payload, "col")
    entropy = sums[0] / (HEADS * count_early)
    row_probs_low = row_probs.astype(jnp.bfloat16)
    row_mix = jnp.einsum(
        "hce,rehd->rchd", row_probs_low, values_ext, preferred_element_type=jnp.float32
    )
    row_mix = row_mix.reshape(rows_dev, cols_dev, model_width).astype(jnp.bfloat16)
    stream_one = stream_zero + project(row_mix, output_row)
    normed_two, norm_back_two = jax.vjp(layer_norm, stream_one, gain_two, shift_two)
    normed_two = normed_two.astype(jnp.bfloat16)
    col_queries = project(normed_two, query_col).astype(jnp.bfloat16)
    col_keys = project(normed_two, key_col).astype(jnp.bfloat16)
    col_values = project(normed_two, value_col).astype(jnp.bfloat16)
    col_scale = 1.0 / math.sqrt(HEAD_DIM)
    keys_all, values_all = (
        lax.all_gather(col_keys, "seq", axis=0, tiled=True),
        lax.all_gather(col_values, "seq", axis=0, tiled=True),
    )
    col_heads_q = col_queries.reshape(rows_dev, cols_dev, HEADS, HEAD_DIM)
    keys_heads = keys_all.reshape(total_rows, cols_dev, HEADS, HEAD_DIM)
    values_heads = values_all.reshape(total_rows, cols_dev, HEADS, HEAD_DIM)
    col_raw = jnp.einsum(
        "rchd,schd->chrs", col_heads_q, keys_heads, preferred_element_type=jnp.float32
    )
    col_probs = plain_softmax(col_raw * col_scale)
    col_probs_low = col_probs.astype(jnp.bfloat16)
    col_mix = jnp.einsum(
        "chrs,schd->rchd", col_probs_low, values_heads, preferred_element_type=jnp.float32
    )
    col_mix = col_mix.reshape(rows_dev, cols_dev, model_width).astype(jnp.bfloat16)
    stream_two = stream_one + project(col_mix, output_col)
    normed_three, norm_back_three = jax.vjp(layer_norm, stream_two, gain_three, shift_three)
    normed_three = normed_three.astype(jnp.bfloat16)
    hidden_pre = project(normed_three, feed_up)
    hidden_act, gelu_back = jax.vjp(partial(jax.nn.gelu, approximate=False), hidden_pre)
    hidden_low = hidden_act.astype(jnp.bfloat16)
    output = (stream_two + project(hidden_low, feed_down)).astype(jnp.bfloat16)
    grad_feed_down = weight_grad(hidden_low, cotangent)
    grad_hidden = gelu_back(project_back(cotangent, feed_down))[0].astype(jnp.bfloat16)
    grad_feed_up = weight_grad(normed_three, grad_hidden)
    back_stream, grad_gain_three, grad_shift_three = norm_back_three(
        project_back(grad_hidden, feed_up)
    )
    grad_two = cotangent.astype(jnp.float32) + back_stream
    grad_two_low = grad_two.astype(jnp.bfloat16)
    grad_output_col = weight_grad(col_mix, grad_two_low)
    grad_mix_flat = project_back(grad_two_low, output_col).astype(jnp.bfloat16)
    grad_col_mix = grad_mix_flat.reshape(rows_dev, cols_dev, HEADS, HEAD_DIM)
    col_dprobs = jnp.einsum(
        "rchd,schd->chrs", grad_col_mix, values_heads, preferred_element_type=jnp.float32
    )
    col_dscores = col_probs * (col_dprobs - jnp.sum(col_probs * col_dprobs, axis=-1, keepdims=True))
    col_dscores = col_dscores.astype(jnp.bfloat16)
    grad_col_q = (
        jnp.einsum("chrs,schd->rchd", col_dscores, keys_heads, preferred_element_type=jnp.float32)
        * col_scale
    )
    grad_col_q = grad_col_q.reshape(rows_dev, cols_dev, model_width).astype(jnp.bfloat16)
    row_count = lax.axis_size("seq") * rows_dev
    key_part = (
        jnp.einsum("chrs,rchd->schd", col_dscores, col_heads_q, preferred_element_type=jnp.float32)
        * col_scale
    )
    value_part = jnp.einsum(
        "chrs,rchd->schd", col_probs_low, grad_col_mix, preferred_element_type=jnp.float32
    )
    key_value_grads = lax.psum_scatter(
        jnp.concatenate(
            [
                key_part.reshape(row_count, cols_dev, model_width),
                value_part.reshape(row_count, cols_dev, model_width),
            ],
            axis=-1,
        ),
        "seq",
        scatter_dimension=0,
        tiled=True,
    )
    grad_col_k = key_value_grads[..., :model_width].astype(jnp.bfloat16)
    grad_col_v = key_value_grads[..., model_width:].astype(jnp.bfloat16)
    grad_query_col = weight_grad(normed_two, grad_col_q)
    grad_key_col = weight_grad(normed_two, grad_col_k)
    grad_value_col = weight_grad(normed_two, grad_col_v)
    back_input = (
        project_back(grad_col_q, query_col)
        + project_back(grad_col_k, key_col)
        + project_back(grad_col_v, value_col)
    )
    back_stream, grad_gain_two, grad_shift_two = norm_back_two(back_input)
    grad_one = grad_two + back_stream
    grad_one_low = grad_one.astype(jnp.bfloat16)
    grad_output_row = weight_grad(row_mix, grad_one_low)
    grad_row_mix = project_back(grad_one_low, output_row).astype(jnp.bfloat16)
    grad_row_mix = grad_row_mix.reshape(rows_dev, cols_dev, HEADS, HEAD_DIM)
    dprobs_part = jnp.einsum(
        "rchd,rehd->hce", grad_row_mix, values_ext, preferred_element_type=jnp.float32
    )
    row_dprobs = lax.psum(dprobs_part.astype(jnp.bfloat16), "seq").astype(jnp.float32)
    ent_cot = jnp.asarray(entropy_weight, dtype=jnp.float32) / (HEADS * count_early)
    row_dscores = ent_back((row_dprobs, ent_cot))[0].astype(jnp.bfloat16)
    grad_row_q = (
        jnp.einsum("hce,rehd->rchd", row_dscores, keys_ext, preferred_element_type=jnp.float32)
        * row_scale
    )
    grad_row_q = grad_row_q.reshape(rows_dev, cols_dev, model_width).astype(jnp.bfloat16)
    grad_keys_ext = (
        jnp.einsum("hce,rchd->rehd", row_dscores, queries_heads, preferred_element_type=jnp.float32)
        * row_scale
    )
    grad_values_ext = jnp.einsum(
        "hce,rchd->rehd", row_probs_low, grad_row_mix, preferred_element_type=jnp.float32
    )
    grad_ext = jnp.stack([grad_keys_ext, grad_values_ext]).reshape(
        2, rows_dev, ext_cols, model_width
    )
    rims = jnp.concatenate([grad_ext[:, :, :WINDOW], grad_ext[:, :, WINDOW + cols_dev :]], axis=2)
    returned = with_halo(rims.astype(jnp.bfloat16), (("col", 2),), WINDOW).astype(rims.dtype)
    interior = grad_ext[:, :, WINDOW : WINDOW + cols_dev]
    interior = interior.at[:, :, :WINDOW].add(returned[:, :, :WINDOW])
    interior = interior.at[:, :, cols_dev - WINDOW :].add(returned[:, :, 3 * WINDOW :])
    grad_row_k = interior[0].astype(jnp.bfloat16)
    grad_row_v = interior[1].astype(jnp.bfloat16)
    grad_query_row = weight_grad(normed_one, grad_row_q)
    grad_key_row = weight_grad(normed_one, grad_row_k)
    grad_value_row = weight_grad(normed_one, grad_row_v)
    back_input = (
        project_back(grad_row_q, query_row)
        + project_back(grad_row_k, key_row)
        + project_back(grad_row_v, value_row)
    )
    back_stream, grad_gain_one, grad_shift_one = norm_back_one(back_input)
    input_grad = (grad_one + back_stream).astype(jnp.bfloat16)
    shares = (
        lax.psum_scatter(
            grad_gain_one.astype(jnp.bfloat16), "seq", scatter_dimension=0, tiled=True
        ).astype(jnp.float32),
        lax.psum_scatter(
            grad_shift_one.astype(jnp.bfloat16), "seq", scatter_dimension=0, tiled=True
        ).astype(jnp.float32),
        lax.psum_scatter(
            grad_gain_two.astype(jnp.bfloat16), "seq", scatter_dimension=0, tiled=True
        ).astype(jnp.float32),
        lax.psum_scatter(
            grad_shift_two.astype(jnp.bfloat16), "seq", scatter_dimension=0, tiled=True
        ).astype(jnp.float32),
        lax.psum_scatter(
            grad_gain_three.astype(jnp.bfloat16), "seq", scatter_dimension=0, tiled=True
        ).astype(jnp.float32),
        lax.psum_scatter(
            grad_shift_three.astype(jnp.bfloat16), "seq", scatter_dimension=0, tiled=True
        ).astype(jnp.float32),
        lax.psum_scatter(
            grad_query_row.astype(jnp.bfloat16), "seq", scatter_dimension=0, tiled=True
        ).astype(jnp.float32),
        lax.psum_scatter(
            grad_key_row.astype(jnp.bfloat16), "seq", scatter_dimension=0, tiled=True
        ).astype(jnp.float32),
        lax.psum_scatter(
            grad_value_row.astype(jnp.bfloat16), "seq", scatter_dimension=0, tiled=True
        ).astype(jnp.float32),
        lax.psum_scatter(
            grad_output_row.astype(jnp.bfloat16), "seq", scatter_dimension=0, tiled=True
        ).astype(jnp.float32),
        lax.psum_scatter(
            grad_query_col.astype(jnp.bfloat16), "seq", scatter_dimension=0, tiled=True
        ).astype(jnp.float32),
        lax.psum_scatter(
            grad_key_col.astype(jnp.bfloat16), "seq", scatter_dimension=0, tiled=True
        ).astype(jnp.float32),
        lax.psum_scatter(
            grad_value_col.astype(jnp.bfloat16), "seq", scatter_dimension=0, tiled=True
        ).astype(jnp.float32),
        lax.psum_scatter(
            grad_output_col.astype(jnp.bfloat16), "seq", scatter_dimension=0, tiled=True
        ).astype(jnp.float32),
        lax.psum_scatter(
            grad_feed_up.astype(jnp.bfloat16), "seq", scatter_dimension=0, tiled=True
        ).astype(jnp.float32),
        lax.psum_scatter(
            grad_feed_down.astype(jnp.bfloat16), "seq", scatter_dimension=0, tiled=True
        ).astype(jnp.float32),
    )
    totals = (
        lax.psum(shares[0].astype(jnp.bfloat16), "col").astype(jnp.float32),
        lax.psum(shares[1].astype(jnp.bfloat16), "col").astype(jnp.float32),
        lax.psum(shares[2].astype(jnp.bfloat16), "col").astype(jnp.float32),
        lax.psum(shares[3].astype(jnp.bfloat16), "col").astype(jnp.float32),
        lax.psum(shares[4].astype(jnp.bfloat16), "col").astype(jnp.float32),
        lax.psum(shares[5].astype(jnp.bfloat16), "col").astype(jnp.float32),
        lax.psum(shares[6].astype(jnp.bfloat16), "col").astype(jnp.float32),
        lax.psum(shares[7].astype(jnp.bfloat16), "col").astype(jnp.float32),
        lax.psum(shares[8].astype(jnp.bfloat16), "col").astype(jnp.float32),
        lax.psum(shares[9].astype(jnp.bfloat16), "col").astype(jnp.float32),
        lax.psum(shares[10].astype(jnp.bfloat16), "col").astype(jnp.float32),
        lax.psum(shares[11].astype(jnp.bfloat16), "col").astype(jnp.float32),
        lax.psum(shares[12].astype(jnp.bfloat16), "col").astype(jnp.float32),
        lax.psum(shares[13].astype(jnp.bfloat16), "col").astype(jnp.float32),
        lax.psum(shares[14].astype(jnp.bfloat16), "col").astype(jnp.float32),
        lax.psum(shares[15].astype(jnp.bfloat16), "col").astype(jnp.float32),
    )
    return (
        output,
        entropy,
        input_grad,
        totals[0],
        totals[1],
        totals[2],
        totals[3],
        totals[4],
        totals[5],
        totals[6],
        totals[7],
        totals[8],
        totals[9],
        totals[10],
        totals[11],
        totals[12],
        totals[13],
        totals[14],
        totals[15],
    )


def after(values, *needed):
    return lax.optimization_barrier((values, needed))[0]


def kernel_call(
    body, outs, args, smem=(), scratch=(), flops=1, moved=1, stream=False, room=16
):
    out_shapes = [jax.ShapeDtypeStruct(shape, kind) for shape, kind in outs]

    def whole(item):
        if not stream:
            return pl.BlockSpec(memory_space=pltpu.VMEM)
        rank = len(item.shape)
        return pl.BlockSpec(item.shape, lambda step: (0,) * rank, pipeline_mode=pl.Buffered(1))

    return pl.pallas_call(
        body,
        grid=(1,) if stream else (),
        out_shape=out_shapes,
        in_specs=[
            pl.BlockSpec(memory_space=pltpu.SMEM) if place in smem else whole(item)
            for place, item in enumerate(args)
        ],
        out_specs=[whole(item) for item in out_shapes],
        scratch_shapes=list(scratch),
        compiler_params=pltpu.CompilerParams(vmem_limit_bytes=(56 if stream else room) << 20),
        cost_estimate=pl.CostEstimate(
            flops=int(flops), bytes_accessed=int(moved), transcendentals=0
        ),
        name=body.__name__,
    )(*args)


def dot(left, right):
    return jnp.dot(left, right, preferred_element_type=jnp.float32)


def dot_back(left, right):
    return lax.dot_general(
        left, right, (((1,), (1,)), ((), ())), preferred_element_type=jnp.float32
    )


def dot_tokens(left, right):
    return lax.dot_general(
        left, right, (((0,), (0,)), ((), ())), preferred_element_type=jnp.float32
    )


def unit_norm(inputs):
    centred = inputs - jnp.mean(inputs, axis=-1, keepdims=True)
    scale = lax.rsqrt(jnp.mean(centred * centred, axis=-1, keepdims=True) + norm_eps)
    return centred * scale, scale


def unit_norm_back(given, unit, scale, gain):
    scaled = given * gain
    first = jnp.mean(scaled, axis=-1, keepdims=True)
    second = jnp.mean(scaled * unit, axis=-1, keepdims=True)
    return scale * (scaled - first - unit * second)


def norm_sums(given, unit):
    return jnp.concatenate(
        [
            jnp.sum(given * unit, axis=0, keepdims=True),
            jnp.sum(given, axis=0, keepdims=True),
        ],
        axis=0,
    )


def head_mask(width, model_width):
    rows = lax.broadcasted_iota(jnp.int32, (HEADS * width, model_width), 0) // width
    lanes = lax.broadcasted_iota(jnp.int32, (HEADS * width, model_width), 1) // HEAD_DIM
    return rows == lanes


def spread_heads(block, mask):
    tiled = jnp.concatenate([block] * HEADS, axis=0)
    return jnp.where(mask, tiled, jnp.zeros_like(tiled))


def fold_heads(product, mask, width):
    kept = jnp.where(mask, product, 0.0)
    total = kept[:width]
    for head in range(1, HEADS):
        total = total + kept[head * width : (head + 1) * width]
    return total


def head_of_lane(model_width):
    rows = lax.broadcasted_iota(jnp.int32, (model_width, 128), 0) // HEAD_DIM
    lanes = lax.broadcasted_iota(jnp.int32, (model_width, 128), 1)
    return (rows == lanes).astype(jnp.bfloat16)


def per_head_sum(product, lane_heads):
    return dot(product.astype(jnp.bfloat16), lane_heads)


def slot_span(spot_ref, side, slot, width):
    return pl.ds(pl.multiple_of((slot ^ spot_ref[side]) * width, width), width)


def window_rows(spot_ref, near_ref, left_ref, right_ref, which, slot, width):
    return jnp.concatenate(
        [
            left_ref[which, slot_span(spot_ref, 5, slot, width)],
            near_ref[which, slot * width : (slot + 1) * width],
            right_ref[which, slot_span(spot_ref, 6, slot, width)],
        ],
        axis=0,
    )


def half_of(values, core, width):
    return jnp.where(core == 0, values[:, :width], values[:, width:])


def fast_plan(
    tokens,
    offsets,
    band,
    col_counts,
    norms,
    row_weights,
    col_weights,
    feed_in,
    feed_out,
    cotangent,
):
    f32, bf16 = jnp.float32, jnp.bfloat16
    cols_dev, model = tokens.shape[1:]
    cols_axis, seqs = lax.axis_size("col"), lax.axis_size("seq")
    chips = seqs // 2
    width = cols_dev // chips
    toks = chips * width
    shard = model // seqs
    half = model // 2
    hidden = feed_out.shape[0] * seqs // cols_axis
    fold = HEADS * width
    span = 3 * width
    col_at = lax.axis_index("col")
    seq_at = lax.axis_index("seq")
    chip, core = seq_at // 2, seq_at % 2
    flip = col_at % 2

    def chunk_of(chip_index):
        return jnp.where(flip == 0, chip_index, chips - 1 - chip_index)

    chunk = chunk_of(chip)
    piece = col_at * chips + chunk

    def along_chips(values, step):
        return lax.ppermute(values, "seq", [(i, i ^ (2 * step)) for i in range(seqs)])

    def along_core(values):
        return lax.ppermute(values, "seq", [(i, i ^ 1) for i in range(seqs)])

    def along_cols(values, step):
        return lax.ppermute(values, "col", [(i, i ^ step) for i in range(cols_axis)])

    def pair_cols(values):
        pairs = [
            (c * seqs + i, (c ^ (1 + i % 2)) * seqs + i)
            for c in range(cols_axis)
            for i in range(seqs)
        ]
        return lax.ppermute(values, ("col", "seq"), pairs)

    def pair_chips(values):
        pairs = [(i, (i // 2 ^ (1 + i % 2)) * 2 + i % 2) for i in range(seqs)]
        return lax.ppermute(values, "seq", pairs)

    def place_of(piece_index, core_index):
        block, part = divmod(piece_index, chips)
        chip_index = part if block % 2 == 0 else chips - 1 - part
        return block * seqs + chip_index * 2 + core_index

    rightward = [
        (place_of(i, k), place_of(i + 1, k)) for i in range(cols_axis * chips - 1) for k in (0, 1)
    ]
    leftward = [(target, source) for source, target in rightward]

    def to_right(values):
        return lax.ppermute(values, ("col", "seq"), rightward)

    def to_left(values):
        return lax.ppermute(values, ("col", "seq"), leftward)

    steps = range(1, chips)
    col_steps = range(1, cols_axis)

    def turn_to(other):
        block, rest = other // chips, other % chips
        return chip ^ jnp.where(block % 2 == 0, rest, chips - 1 - rest)

    to_left_turn = turn_to(jnp.maximum(piece - 1, 0))
    to_right_turn = turn_to(jnp.minimum(piece + 1, cols_axis * chips - 1))
    spot = jnp.stack(
        [col_at, chip, core, chunk, col_counts[0], to_left_turn, to_right_turn]
    ).astype(jnp.int32)

    half_width = model // 2
    frequency = jnp.exp(-math.log(1000.0) * jnp.arange(half_width, dtype=f32) / half_width)
    col_place = (jnp.arange(width, dtype=jnp.int32) + piece * width + offsets[1]).astype(f32)
    seq_slots = jnp.stack([(chip ^ step) * 2 + core for step in range(chips)])
    row_place = (seq_slots + offsets[0]).astype(f32)
    waves = 0.5 * jnp.sin(
        jnp.concatenate([col_place, row_place])[:, None] * frequency[None, :]
    )
    band_here = lax.dynamic_slice_in_dim(band, chunk * width, width, axis=0)
    query_index = jnp.arange(width, dtype=jnp.int32)[:, None]
    key_index = jnp.arange(span, dtype=jnp.int32)[None, :]
    distance = key_index - query_index
    choose = jnp.arange(2 * WINDOW + 1, dtype=jnp.int32)
    matches = (distance[:, None, :] == choose[None, :, None]) & (band_here[:, :, None] == 1)
    key_global = (piece - 1) * width + key_index
    inside = (key_global >= 0) & (key_global < cols_axis * cols_dev)
    allowed = ((jnp.any(matches, axis=1) | (distance == WINDOW)) & inside).astype(f32)

    quarter = shard // cols_axis
    lines = 8
    hops = chips - 1
    col_rows = cols_axis * quarter
    row_rows = col_rows + lines

    def chunk_at(spot_ref, chip_index):
        at = jnp.where(spot_ref[0] % 2 == 0, chip_index, chips - 1 - chip_index)
        return pl.ds(pl.multiple_of(at * width, width), width)

    def pack(spot_ref, weights, own_ref, send_refs, block):
        at = pl.multiple_of(spot_ref[0] * quarter, quarter)
        size = len(weights) * quarter
        for index, ref in enumerate(weights):
            own_ref[index * shard : (index + 1) * shard] = ref[...]
            for send_ref in send_refs:
                send_ref[index * quarter : (index + 1) * quarter] = ref[pl.ds(at, quarter)]
        if block is not None:
            for ref, row in [(own_ref, len(weights) * shard)] + [
                (ref, size) for ref in send_refs
            ]:
                ref[row : row + lines] = jnp.zeros((lines, model), bf16)
                ref[row : row + lines, :128] = block

    def pack_row(spot_ref, *refs):
        norm_refs, own_ref, send_ref = refs[4:10], refs[10], refs[11]
        block = jnp.zeros((lines, 128), f32)
        rows = lax.broadcasted_iota(jnp.int32, (lines, 128), 0)
        for index, ref in enumerate(norm_refs):
            line = jnp.pad(ref[...].astype(f32), ((0, 0), (0, 128 - shard)))
            block = jnp.where(rows == index, line, block)
        block = jnp.where(rows == 6, spot_ref[4].astype(f32), block).astype(bf16)
        pack(spot_ref, refs[:4], own_ref, [send_ref], block)

    part = feed_out.shape[0] // cols_axis
    block_cols = feed_out.shape[0]

    def pack_rest(spot_ref, *refs):
        token_refs, in_ref, out_ref = refs[4:6], refs[6], refs[7]
        own_ref, chunk_ref, send_refs = refs[8], refs[10], refs[11:]
        pack(spot_ref, refs[:4], refs[9], send_refs, None)
        for index, ref in enumerate(token_refs):
            chunk_ref[index * width : (index + 1) * width] = ref[0, chunk_at(spot_ref, spot_ref[1])]
            for hop, send_ref in enumerate(send_refs):
                at = col_rows + index * width
                send_ref[at : at + width] = ref[0, chunk_at(spot_ref, spot_ref[1] ^ (hop + 1))]
        first = lax.broadcasted_iota(jnp.int32, (block_cols, 128), 0)
        lanes = lax.broadcasted_iota(jnp.int32, (block_cols, 128), 1)
        chosen = ((first == lanes + spot_ref[0] * part) & (lanes < part)).astype(bf16)
        for index in range(seqs):
            block = in_ref[:, index * block_cols : (index + 1) * block_cols]
            own_ref[0, :, index * part : (index + 1) * part] = dot(block, chosen)[
                :, :part
            ].astype(bf16)
        own_ref[1] = out_ref[pl.ds(pl.multiple_of(spot_ref[0] * part, part), part)]

    def stack_row(*refs):
        for hop, ref in enumerate(refs[:-1]):
            refs[-1][hop * row_rows : (hop + 1) * row_rows] = ref[...]

    def stack_col(own_ref, *refs):
        ins, (out_ref, given_ref) = refs[:-2], refs[-2:]
        for slot, ref in enumerate((own_ref, *ins)):
            at = 0 if slot == 0 else col_rows
            given_ref[slot * width : (slot + 1) * width] = ref[at + width : at + 2 * width]
            if slot:
                out_ref[(slot - 1) * col_rows : slot * col_rows] = ref[:col_rows]

    def spread_plane(near, far):
        def join_cores(near_ref, far_ref, out_ref):
            rows = near_ref.shape[0]
            out_ref[:rows] = near_ref[...]
            out_ref[rows:] = far_ref[...]

        both_cores = kernel_call(join_cores, [((2 * near.shape[0], model), bf16)], [near, far])[0]
        return both_cores, pair_cols(both_cores), along_cols(near, cols_axis - 1)

    def place_rows(spot_ref, refs, outs, rows, unit):
        at_col, at_chip, at_core = spot_ref[0], spot_ref[1], spot_ref[2]
        other = 1 - at_core

        def row_of(from_chip, from_core, offset, size):
            return pl.ds(
                pl.multiple_of((from_chip * 2 + from_core) * shard + offset, quarter), size
            )

        pieces = (
            (refs[2], at_col, at_core, 2),
            (refs[3], at_col ^ (1 + at_core), at_core, 2),
            (refs[4], at_col ^ 3, at_core, 1),
            (refs[5], at_col ^ (1 + other), other, 2),
            (refs[6], at_col ^ 3, other, 1),
        )
        for index, (out_ref, lead) in enumerate(outs):
            for ref, core_at in ((refs[0], at_core), (refs[1], other)):
                out_ref[lead + (row_of(at_chip, core_at, 0, shard),)] = ref[
                    index * shard : (index + 1) * shard
                ]
            for ref, col, core_at, sides in pieces:
                for side in range(sides):
                    for hop in steps:
                        at = row_of(at_chip ^ hop, core_at ^ side, col * quarter, quarter)
                        start = side * unit + (hop - 1) * rows + index * quarter
                        out_ref[lead + (at,)] = ref[start : start + quarter]

    row_own, row_send = kernel_call(
        pack_row,
        [((cols_axis * shard + lines, model), bf16), ((row_rows, model), bf16)],
        [spot, *row_weights, *[item[None] for item in norms]],
        smem=(0,),
        stream=True,
    )
    row_got = [along_chips(row_send, step) for step in steps]
    feed_own, col_own, chunks_own, *col_sends = kernel_call(
        pack_rest,
        [
            ((2, shard, hidden), bf16),
            ((cols_axis * shard, model), bf16),
            ((2 * width, model), bf16),
        ]
        + [((col_rows + 2 * width, model), bf16)] * hops,
        [spot, *col_weights, tokens, cotangent, feed_in, feed_out],
        smem=(0,),
        stream=True,
    )
    row_got = after(row_got, waves, allowed, col_sends)
    feed_other = along_core(feed_own)
    row_hops = kernel_call(stack_row, [((hops * row_rows, model), bf16)], row_got)[0]
    row_far_own = along_core(row_own)
    row_plane, row_pair, row_diagonal = spread_plane(row_hops, along_core(row_hops))
    col_sends = after(col_sends, row_plane)
    col_got = [along_chips(col_sends[step - 1], step) for step in steps]

    def pair_feed(own_ref, other_ref, out_ref):
        out_ref[0] = own_ref[...]
        out_ref[1] = other_ref[...]

    feed_both = kernel_call(
        pair_feed, [((2, 2, shard, hidden), bf16)], [feed_own, after(feed_other, row_plane)]
    )[0]
    row_last = after((row_pair, row_diagonal), row_pair, row_diagonal, col_got, feed_both)
    row_pieces = [row_own, row_far_own, row_plane, row_pair, row_diagonal] + [
        along_core(item) for item in row_last
    ]
    def project_row(spot_ref, waves_ref, *refs):
        token_refs, pieces, outs = refs[:chips], refs[chips : chips + 7], refs[chips + 7 :]
        zero_ref, low_ref, q_ref, kv_ref, weight_ref, last_ref, norm_ref = outs
        place_rows(
            spot_ref,
            pieces,
            [(weight_ref, (index,)) for index in range(3)] + [(last_ref, ())],
            row_rows,
            hops * row_rows,
        )
        first = lax.broadcasted_iota(jnp.int32, (128, model), 0)
        lanes = lax.broadcasted_iota(jnp.int32, (128, model), 1)
        total = jnp.zeros((lines, model), f32)
        for side in (0, 1):
            for hop in range(chips):
                if hop == 0:
                    block = pieces[side][cols_axis * shard : cols_axis * shard + lines, :128]
                else:
                    at = (side * hops + hop) * row_rows - lines
                    block = pieces[2][at : at + lines, :128]
                start = ((spot_ref[1] ^ hop) * 2 + (spot_ref[2] ^ side)) * shard
                chosen = ((lanes == first + start) & (first < shard)).astype(bf16)
                total = total + dot(block, chosen)
        count = spot_ref[4].astype(f32)
        for ref in pieces[3:6]:
            count = count + ref[row_rows - lines : row_rows, :128][6:7, 0:1].astype(f32)
        rows = lax.broadcasted_iota(jnp.int32, (lines, model), 0)
        norm_ref[...] = jnp.where(rows == 6, count, total)
        for slot in range(chips):
            rows = slice(slot * width, (slot + 1) * width)
            at = 0 if slot == 0 else col_rows
            stream = token_refs[slot][at : at + width].astype(f32)
            zero_ref[rows, :half] = stream[:, :half] + waves_ref[:width]
            zero_ref[rows, half:] = stream[:, half:] + waves_ref[width + slot : width + slot + 1]
        unit, _ = unit_norm(zero_ref[...])
        low = (unit * norm_ref[0:1] + norm_ref[1:2]).astype(bf16)
        low_ref[...] = low
        q_ref[...] = dot(low, weight_ref[0]).astype(bf16)
        kv_ref[0] = dot(low, weight_ref[1]).astype(bf16)
        kv_ref[1] = dot(low, weight_ref[2]).astype(bf16)

    big = 2.0 * toks * model * model
    stream_zero, normed_one, row_q, row_kv, weights_row, weights_out, norm_rows = kernel_call(
        project_row,
        [
            ((toks, model), f32),
            ((toks, model), bf16),
            ((toks, model), bf16),
            ((2, toks, model), bf16),
            ((3, model, model), bf16),
            ((model, model), bf16),
            ((lines, model), f32),
        ],
        [spot, waves, chunks_own, *col_got, *row_pieces],
        smem=(0,),
    )
    kv_left = to_right(row_kv)
    kv_right = to_left(row_kv)
    col_unit = hops * col_rows
    col_hops, given_out = kernel_call(
        stack_col,
        [((col_unit, model), bf16), ((toks, model), bf16)],
        [after(chunks_own, row_q), *col_got],
    )
    col_far_own = along_core(col_own)
    col_plane, col_pair, col_diagonal = spread_plane(col_hops, along_core(col_hops))

    feed_pair = pair_chips(after(feed_both, row_q))
    kv_left = after(kv_left, feed_pair, col_pair, col_diagonal)

    def tied_logits(spot_ref, q_ref, near_ref, left_ref, right_ref, out_ref):
        mask = head_mask(width, model)
        total = None
        for slot in range(chips):
            keys = window_rows(spot_ref, near_ref, left_ref, right_ref, 0, slot, width)
            spread = spread_heads(q_ref[slot * width : (slot + 1) * width], mask)
            term = dot_back(spread, keys)
            total = term if total is None else total + term
        out_ref[...] = total

    logits = kernel_call(
        tied_logits,
        [((fold, span), f32)],
        [spot, row_q, row_kv, kv_left, kv_right],
        smem=(0,),
    )[0]
    logits_other = along_core(logits)
    feed_diagonal = along_chips(after(feed_own, logits), chips - 1)
    given_far = after(along_core(given_out), logits)
    row_scale = 1.0 / math.sqrt(HEAD_DIM * seqs)
    col_scale = 1.0 / math.sqrt(HEAD_DIM)

    def attend_row(
        spot_ref,
        logits_ref,
        other_ref,
        allowed_ref,
        near_ref,
        left_ref,
        right_ref,
        zero_ref,
        norm_ref,
        weight_ref,
        scores_ref,
        probs_ref,
        mix_ref,
        stream_ref,
        low_ref,
        entropy_ref,
    ):
        mask = head_mask(width, model)
        scores = (logits_ref[...] + other_ref[...]) * row_scale
        open_here = jnp.concatenate([allowed_ref[...]] * HEADS, axis=0) > 0.5
        masked = jnp.where(open_here, scores, -1000000000.0)
        largest = jnp.max(masked, axis=-1, keepdims=True)
        powers = jnp.exp(masked - largest)
        total = jnp.sum(powers, axis=-1, keepdims=True)
        probs = powers / total
        kept = jnp.where(open_here, scores, 0.0)
        entropies = largest + jnp.log(total) - jnp.sum(probs * kept, axis=-1, keepdims=True)
        rows = lax.broadcasted_iota(jnp.int32, (fold, 1), 0) % width
        entropies = jnp.where(rows + spot_ref[3] * width < spot_ref[4], entropies, 0.0)
        lanes = lax.broadcasted_iota(jnp.int32, (1, model), 1)
        found = jnp.sum(entropies, axis=0, keepdims=True)
        entropy_ref[...] = jnp.where((lanes == 0) & (spot_ref[2] == 0), found, 0.0)
        scores_ref[...] = kept
        probs_ref[...] = probs
        low_probs = probs.astype(bf16)
        for slot in range(chips):
            values = window_rows(spot_ref, near_ref, left_ref, right_ref, 1, slot, width)
            mix_ref[slot * width : (slot + 1) * width] = fold_heads(
                dot(low_probs, values), mask, width
            ).astype(bf16)
        stream = zero_ref[...] + dot(mix_ref[...], weight_ref[...])
        stream_ref[...] = stream
        unit, _ = unit_norm(stream)
        low_ref[...] = (unit * norm_ref[2:3] + norm_ref[3:4]).astype(bf16)

    scores, probs, row_mix, stream_one, normed_two, entropy_row = kernel_call(
        attend_row,
        [
            ((fold, span), f32),
            ((fold, span), f32),
            ((toks, model), bf16),
            ((toks, model), f32),
            ((toks, model), bf16),
            ((1, model), f32),
        ],
        [
            spot,
            logits,
            logits_other,
            allowed,
            row_kv,
            kv_left,
            kv_right,
            stream_zero,
            norm_rows,
            weights_out,
        ],
        smem=(0,),
    )

    col_last = after((col_pair, col_diagonal), normed_two)
    col_pieces = [col_own, col_far_own, col_plane, col_pair, col_diagonal] + [
        along_core(item) for item in col_last
    ]

    def assemble_col(spot_ref, *refs):
        three_ref, last_ref = refs[7:]
        outs = [(three_ref, (index,)) for index in range(3)] + [(last_ref, ())]
        place_rows(spot_ref, refs[:7], outs, col_rows, col_unit)

    weights_three, weights_last = kernel_call(
        assemble_col,
        [((3, model, model), bf16), ((model, model), bf16)],
        [spot, *col_pieces],
        smem=(0,),
    )

    def project_col(low_ref, weight_ref, q_ref, kv_ref):
        low = low_ref[...]
        q_ref[...] = dot(low, weight_ref[0]).astype(bf16)
        kv_ref[0] = dot(low, weight_ref[1]).astype(bf16)
        kv_ref[1] = dot(low, weight_ref[2]).astype(bf16)

    col_q, col_kv = kernel_call(
        project_col,
        [((toks, model), bf16), ((2, toks, model), bf16)],
        [normed_two, weights_three],
    )
    kv_other = along_core(col_kv)

    def join_given(near_ref, far_ref, out_ref):
        out_ref[:toks] = near_ref[...]
        out_ref[toks:] = far_ref[...]

    given_both = kernel_call(join_given, [((2 * toks, model), bf16)], [given_out, given_far])[0]
    given_pair = pair_cols(given_both)

    def slot_rows(slot):
        return slice(slot * width, (slot + 1) * width)

    def attend_col(
        q_ref,
        near_ref,
        far_ref,
        one_ref,
        norm_ref,
        weight_ref,
        given_ref,
        probs_ref,
        mix_ref,
        stream_ref,
        low_ref,
        message_ref,
    ):
        lane_heads = head_of_lane(model)
        sides = (near_ref, far_ref)
        for slot in range(chips):
            query = q_ref[slot_rows(slot)].astype(f32)
            products = jnp.concatenate(
                [
                    query * sides[s // chips][0, slot_rows(s % chips)].astype(f32)
                    for s in range(seqs)
                ],
                axis=0,
            )
            found = per_head_sum(products, lane_heads) * col_scale
            parts = [found[s * width : (s + 1) * width] for s in range(seqs)]
            largest = parts[0]
            for item in parts[1:]:
                largest = jnp.maximum(largest, item)
            powers = [jnp.exp(item - largest) for item in parts]
            total = powers[0]
            for item in powers[1:]:
                total = total + item
            weights = jnp.concatenate([item / total for item in powers], axis=0)
            probs_ref[slot] = weights
            wide = dot_back(weights.astype(bf16), lane_heads)
            mixed = None
            for s in range(seqs):
                term = wide[s * width : (s + 1) * width] * sides[s // chips][
                    1, slot_rows(s % chips)
                ].astype(f32)
                mixed = term if mixed is None else mixed + term
            mix_ref[slot_rows(slot)] = mixed.astype(bf16)
        stream = one_ref[...] + dot(mix_ref[...], weight_ref[...])
        stream_ref[...] = stream
        unit, _ = unit_norm(stream)
        low = (unit * norm_ref[4:5] + norm_ref[5:6]).astype(bf16)
        low_ref[...] = low
        message_ref[:toks] = low
        message_ref[toks:] = given_ref[...]

    col_probs, col_mix, stream_two, normed_three, message = kernel_call(
        attend_col,
        [
            ((chips, seqs * width, 128), f32),
            ((toks, model), bf16),
            ((toks, model), f32),
            ((toks, model), bf16),
            ((2 * toks, model), bf16),
        ],
        [col_q, col_kv, kv_other, stream_one, norm_rows, weights_last, given_out],
    )
    low_near = [
        normed_three,
        along_cols(normed_three, 1),
        along_cols(normed_three, 2),
        along_cols(message, 3),
    ]

    feed_last = after((feed_pair, feed_diagonal, given_pair), low_near)
    feed_far = [along_core(item) for item in feed_last]

    def assemble_feed(
        spot_ref,
        both_ref,
        pair_ref,
        last_ref,
        pair2_ref,
        last2_ref,
        d0_ref,
        d1_ref,
        d2_ref,
        d3_ref,
        out_ref,
        given_ref,
    ):
        at_chip, at_core = spot_ref[1], spot_ref[2]
        other = 1 - at_core

        def move(rows, from_chip, from_core):
            at = pl.multiple_of((from_chip * 2 + from_core) * shard, shard)
            out_ref[:, pl.ds(at, shard)] = rows

        for side in (0, 1):
            move(both_ref[side], at_chip, at_core ^ side)
            move(pair_ref[side], at_chip ^ (1 + at_core), at_core ^ side)
            move(pair2_ref[side], at_chip ^ (1 + other), other ^ side)
        move(last_ref[...], at_chip ^ 3, at_core)
        move(last2_ref[...], at_chip ^ 3, other)
        given_ref[0] = d0_ref[...]
        given_ref[1 + at_core] = d1_ref[:toks]
        given_ref[2 - at_core] = d2_ref[toks:]
        given_ref[3] = d3_ref[toks:]

    weights_feed, given_all = kernel_call(
        assemble_feed,
        [((2, model, hidden), bf16), ((cols_axis, toks, model), bf16)],
        [
            spot,
            feed_both,
            feed_pair,
            feed_diagonal,
            feed_far[0],
            feed_far[1],
            given_out,
            given_pair,
            feed_far[2],
            low_near[3],
        ],
        smem=(0,),
    )

    def feed_main(a0, a1, a2, a3, given_ref, weight_ref, act_ref, grad_ref, *back_refs):
        up, down = weight_ref[0], weight_ref[1]
        for step, low_ref in enumerate((a0, a1, a2, a3)):
            pre = dot(low_ref[:toks], up)
            bell = 0.5 * (1.0 + lax.erf(pre * (0.5**0.5)))
            slope = bell + pre * jnp.exp(-0.5 * pre * pre) * ((0.5 / math.pi) ** 0.5)
            act_ref[step] = (pre * bell).astype(bf16)
            grad = (slope * dot_back(given_ref[step], down)).astype(bf16)
            grad_ref[step] = grad
            back_refs[step][...] = dot_back(grad, up).astype(bf16)

    feed_big = 2.0 * toks * cols_axis * model * hidden
    feed_results = kernel_call(
        feed_main,
        [((cols_axis, toks, hidden), bf16)] * 2 + [((toks, model), bf16)] * cols_axis,
        [*low_near, given_all, weights_feed],
    )
    act, grad_hidden, back_parts = feed_results[0], feed_results[1], feed_results[2:]
    back_near = [back_parts[0]] + [along_cols(back_parts[step], step) for step in col_steps]

    def feed_weights(
        spot_ref, a0, a1, a2, a3, given_ref, act_ref, grad_ref, weight_ref, mine_ref, give_ref, *outs
    ):
        at_core = spot_ref[2]
        low = jnp.concatenate([a0[...], a1[...], a2[...], a3[:toks]], axis=0)
        given = given_ref[...].reshape(cols_axis * toks, model)
        rows = cols_axis * toks
        acts = act_ref[...].reshape(rows, hidden)
        grads = grad_ref[...].reshape(rows, hidden)
        for step in range(cols_axis):
            outs[step][...] = dot(act_ref[step], weight_ref[1]).astype(bf16)
        for ref, at in ((mine_ref, at_core), (give_ref, 1 - at_core)):
            ref[:model] = dot_tokens(low, half_of(grads, at, half)).astype(bf16)
            ref[model:] = dot_tokens(acts, half_of(given, at, half)).astype(bf16)

    feed_grads = kernel_call(
        feed_weights,
        [((2 * model, half), bf16)] * 2 + [((toks, model), bf16)] * cols_axis,
        [spot, *low_near, given_all, act, grad_hidden, weights_feed],
        smem=(0,),
        flops=6.0 * toks * cols_axis * model * hidden,
        moved=16 << 20,
        room=24,
    )
    feed_mine, feed_give, out_parts = feed_grads[0], feed_grads[1], feed_grads[2:]

    block = 2 * shard
    extra = 2 * lines

    def renew(total, at):
        line = total[at : at + 1]
        whole = line[:, 0:1] + line[:, 1:2]
        high = whole.astype(bf16).astype(f32)
        lanes = lax.broadcasted_iota(jnp.int32, total.shape, 1)
        rows = lax.broadcasted_iota(jnp.int32, total.shape, 0)
        total = jnp.where((rows == at) & (lanes == 0), high, total)
        return jnp.where((rows == at) & (lanes == 1), whole - high, total)

    def layer_grads(low, mix, low_far, mix_far, mine, got, more):
        rows = model + (extra if len(more) == 1 else 2 * toks)

        def weight_sums(spot_ref, low_ref, mix_ref, low2_ref, mix2_ref, mine_ref, got_ref, *refs):
            more_refs, outs = refs[: len(more)], refs[len(more) : -2]
            left_ref, right_ref = refs[-2:]
            left_ref[0, :toks] = low_ref[...]
            left_ref[0, toks:] = low2_ref[...]
            left_ref[1, :toks] = mix_ref[...]
            left_ref[1, toks:] = mix2_ref[...]
            right_ref[:, :toks] = mine_ref[...]
            right_ref[:, toks:] = got_ref[...]
            for step in range(cols_axis):
                matrix = spot_ref[0] ^ step
                left = left_ref[matrix // 3]
                outs[step][:model] = dot_tokens(left, right_ref[matrix]).astype(bf16)
                if len(more) == 1:
                    sums_ref = more_refs[0]
                    tail = jnp.concatenate([sums_ref[:, :half], sums_ref[:, half:]], axis=0)
                    outs[step][model:] = renew(tail, 6).astype(bf16)
                else:
                    outs[step][model : model + toks] = more_refs[step][:, :half]
                    outs[step][model + toks :] = more_refs[step][:, half:]

        return kernel_call(
            weight_sums,
            [((rows, half), bf16)] * cols_axis,
            [spot, low, mix, low_far, mix_far, mine, got, *more],
            smem=(0,),
            scratch=[
                pltpu.VMEM((2, 2 * toks, model), bf16),
                pltpu.VMEM((4, 2 * toks, half), bf16),
            ],
        )

    def split_chips(items, count, tail, stream=None, slots=()):
        slot_rows_out = 2 * width * ((stream is not None) + bool(slots))

        def chip_parts(spot_ref, *refs):
            ins, outs, total_ref = refs[: len(items)], refs[-chips - 1 : -1], refs[-1]
            more = refs[len(items) : -chips - 1]
            total = ins[0][...].astype(f32)
            for ref in ins[1:]:
                total = total + ref[...].astype(f32)
            total_ref[...] = total.astype(bf16)
            if stream is not None:
                result = more[0][...] + jnp.concatenate(
                    [total[model : model + toks], total[model + toks :]], axis=1
                )
            for hop in range(chips):
                at = pl.multiple_of((spot_ref[1] ^ hop) * block, block)
                for index in range(count):
                    outs[hop][index * block : (index + 1) * block] = total_ref[
                        pl.ds(index * model + at, block)
                    ]
                row = count * block
                if tail:
                    outs[hop][row : row + tail] = renew(total[count * model :], 6).astype(bf16)
                    row = row + tail
                sent = []
                if stream is not None:
                    sent.append(result[slot_rows(hop)].astype(bf16))
                if slots:
                    sent.append(more[hop - chips][...])
                for slot in sent:
                    outs[hop][row : row + width] = slot[:, :half]
                    outs[hop][row + width : row + 2 * width] = slot[:, half:]
                    row = row + 2 * width

        size = count * block + tail + slot_rows_out
        return kernel_call(
            chip_parts,
            [((size, half), bf16)] * chips,
            [spot, *items] + ([] if stream is None else [stream]) + list(slots),
            smem=(0,),
            scratch=[pltpu.VMEM(items[0].shape, bf16)],
        )

    def split_cores(items, count, tail):
        rows_in = count * block + tail

        def core_parts(spot_ref, *refs):
            ins, (keep_ref, give_ref, total_ref) = refs[: len(items)], refs[len(items) :]
            total = ins[0][:rows_in].astype(f32)
            for ref in ins[1:]:
                total = total + ref[:rows_in].astype(f32)
            total_ref[...] = total.astype(bf16)
            for ref, at in ((keep_ref, spot_ref[2]), (give_ref, 1 - spot_ref[2])):
                for index in range(count):
                    row = pl.multiple_of(index * block + at * shard, shard)
                    ref[index * shard : (index + 1) * shard] = total_ref[pl.ds(row, shard)]
                if tail:
                    ref[count * shard :] = renew(total[count * block :], 6).astype(bf16)

        size = count * shard + tail
        return kernel_call(
            core_parts,
            [((size, half), bf16)] * 2,
            [spot, *items],
            smem=(0,),
            scratch=[pltpu.VMEM((rows_in, half), bf16)],
        )

    def over_chips(parts):
        return [parts[0]] + [along_chips(parts[step], step) for step in steps]

    back_near = after(back_near, feed_mine)

    def attend_col_back(
        spot_ref,
        b0,
        b1,
        b2,
        b3,
        given_ref,
        two_ref,
        norm_ref,
        weight_ref,
        q_ref,
        near_ref,
        far_ref,
        probs_ref,
        dtwo_ref,
        low_ref,
        dq_ref,
        dkv_ref,
        send_ref,
        sums_ref,
        wide_ref,
    ):
        lane_heads = head_of_lane(model)
        back = b0[...].astype(f32) + b1[...].astype(f32) + b2[...].astype(f32) + b3[...].astype(f32)
        unit, scale = unit_norm(two_ref[...])
        sums_ref[...] = norm_sums(back, unit)
        dtwo = given_ref[0].astype(f32) + unit_norm_back(back, unit, scale, norm_ref[4:5])
        dtwo_ref[...] = dtwo
        low = dtwo.astype(bf16)
        low_ref[...] = low
        dmix = dot_back(low, weight_ref[...]).astype(bf16).astype(f32)
        wide_ref[...] = jnp.zeros_like(wide_ref)
        sides = (near_ref, far_ref)
        for slot in range(chips):
            dout = dmix[slot_rows(slot)]
            query = q_ref[slot_rows(slot)].astype(f32)
            products = jnp.concatenate(
                [
                    dout * sides[s // chips][1, slot_rows(s % chips)].astype(f32)
                    for s in range(seqs)
                ],
                axis=0,
            )
            found = per_head_sum(products, lane_heads)
            weights = probs_ref[slot]
            mean = None
            for s in range(seqs):
                rows = slice(s * width, (s + 1) * width)
                term = weights[rows] * found[rows]
                mean = term if mean is None else mean + term
            dscores = (weights * (found - jnp.concatenate([mean] * seqs, axis=0))).astype(bf16)
            wide_d = dot_back(dscores, lane_heads)
            wide_p = dot_back(weights.astype(bf16), lane_heads)
            dquery = None
            for s in range(seqs):
                rows = slice(s * width, (s + 1) * width)
                term = wide_d[rows] * sides[s // chips][0, slot_rows(s % chips)].astype(f32)
                dquery = term if dquery is None else dquery + term
                wide_ref[0, rows] += wide_d[rows] * query
                wide_ref[1, rows] += wide_p[rows] * dout
            dq_ref[slot_rows(slot)] = (dquery * col_scale).astype(bf16)
        dkv_ref[0] = wide_ref[0, :toks] * col_scale
        dkv_ref[1] = wide_ref[1, :toks]
        send_ref[0] = (wide_ref[0, toks:] * col_scale).astype(bf16)
        send_ref[1] = wide_ref[1, toks:].astype(bf16)

    grad_two, grad_two_low, col_dq, col_dkv, col_send, sums_three = kernel_call(
        attend_col_back,
        [
            ((toks, model), f32),
            ((toks, model), bf16),
            ((toks, model), bf16),
            ((2, toks, model), f32),
            ((2, toks, model), bf16),
            ((2, model), f32),
        ],
        [
            spot,
            *back_near,
            given_all,
            stream_two,
            norm_rows,
            weights_last,
            col_q,
            col_kv,
            kv_other,
            col_probs,
        ],
        smem=(0,),
        scratch=[pltpu.VMEM((2, 2 * toks, model), f32)],
    )
    row_low_far, row_mix_far = along_core(normed_one), along_core(row_mix)
    col_low_far, col_mix_far = along_core(normed_two), along_core(col_mix)
    dkv_got = after(along_core(col_send), row_low_far, row_mix_far)

    def row_entry_back(
        spot_ref,
        dq_ref,
        dkv_ref,
        got_ref,
        low_two_ref,
        dtwo_ref,
        one_ref,
        norm_ref,
        col_ref,
        row_ref,
        near_ref,
        left_ref,
        right_ref,
        mine_ref,
        give_ref,
        done_ref,
        low_ref,
        dmix_ref,
        dprobs_ref,
        sums_ref,
    ):
        at_core = spot_ref[2]
        dq = dq_ref[...]
        dk = (dkv_ref[0] + got_ref[0].astype(f32)).astype(bf16)
        dv = (dkv_ref[1] + got_ref[1].astype(f32)).astype(bf16)
        for index, item in enumerate((dq, dk, dv, low_two_ref[...])):
            mine_ref[index] = half_of(item, at_core, half)
            give_ref[index] = half_of(item, 1 - at_core, half)
        back = dot_back(dq, col_ref[0]) + dot_back(dk, col_ref[1]) + dot_back(dv, col_ref[2])
        unit, scale = unit_norm(one_ref[...])
        sums_ref[...] = norm_sums(back, unit)
        done = dtwo_ref[...] + unit_norm_back(back, unit, scale, norm_ref[2:3])
        done_ref[...] = done
        low = done.astype(bf16)
        low_ref[...] = low
        dmix = dot_back(low, row_ref[...]).astype(bf16)
        dmix_ref[...] = dmix
        mask = head_mask(width, model)
        total = None
        for slot in range(chips):
            values = window_rows(spot_ref, near_ref, left_ref, right_ref, 1, slot, width)
            term = dot_back(spread_heads(dmix[slot_rows(slot)], mask), values)
            total = term if total is None else total + term
        dprobs_ref[...] = total

    (
        col_mine,
        col_give,
        grad_one,
        grad_one_low,
        row_dmix,
        dprobs,
        sums_two,
    ) = kernel_call(
        row_entry_back,
        [
            ((4, toks, half), bf16),
            ((4, toks, half), bf16),
            ((toks, model), f32),
            ((toks, model), bf16),
            ((toks, model), bf16),
            ((fold, span), f32),
            ((2, model), f32),
        ],
        [
            spot,
            col_dq,
            col_dkv,
            dkv_got,
            grad_two_low,
            grad_two,
            stream_one,
            norm_rows,
            weights_three,
            weights_out,
            row_kv,
            kv_left,
            kv_right,
        ],
        smem=(0,),
    )
    dprobs_other = along_core(dprobs)
    col_sums = layer_grads(
        normed_two,
        col_mix,
        col_low_far,
        col_mix_far,
        col_mine,
        along_core(col_give),
        out_parts,
    )
    dprobs_other = after(dprobs_other, col_sums)

    def attend_row_back(
        spot_ref,
        weight_ref,
        dprobs_ref,
        other_ref,
        scores_ref,
        probs_ref,
        q_ref,
        near_ref,
        left_ref,
        right_ref,
        dmix_ref,
        dq_ref,
        dkv_ref,
        to_left_ref,
        to_right_ref,
    ):
        mask = head_mask(width, model)
        dprob = dprobs_ref[...] + other_ref[...]
        probs_here, scores_here = probs_ref[...], scores_ref[...]
        rows = lax.broadcasted_iota(jnp.int32, (fold, 1), 0) % width
        weight = jnp.where(rows + spot_ref[3] * width < spot_ref[4], entropy_weight / (HEADS * weight_ref[6:7, 0:1]), 0.0)
        first = dprob - jnp.sum(probs_here * dprob, axis=-1, keepdims=True)
        second = scores_here - jnp.sum(probs_here * scores_here, axis=-1, keepdims=True)
        dscores = (probs_here * (first - weight * second)).astype(bf16)
        low_probs = probs_here.astype(bf16)
        for slot in range(chips):
            at = slot_rows(slot)
            keys = window_rows(spot_ref, near_ref, left_ref, right_ref, 0, slot, width)
            dq_ref[at] = (
                fold_heads(dot(dscores, keys), mask, width) * row_scale
            ).astype(bf16)
            dkeys = dot_tokens(dscores, spread_heads(q_ref[at], mask)) * row_scale
            dvalues = dot_tokens(low_probs, spread_heads(dmix_ref[at], mask))
            for index, item in enumerate((dkeys, dvalues)):
                to_left_ref[index, at] = item[:width].astype(bf16)
                dkv_ref[index, at] = item[width : 2 * width]
                to_right_ref[index, at] = item[2 * width :].astype(bf16)

    row_dq, row_dkv, edge_left, edge_right = kernel_call(
        attend_row_back,
        [
            ((toks, model), bf16),
            ((2, toks, model), f32),
            ((2, toks, model), bf16),
            ((2, toks, model), bf16),
        ],
        [
            spot,
            norm_rows,
            dprobs,
            dprobs_other,
            scores,
            probs,
            row_q,
            row_kv,
            kv_left,
            kv_right,
            row_dmix,
        ],
        smem=(0,),
    )
    edge_from_right = to_left(edge_left)
    edge_from_left = to_right(edge_right)
    feed_slices = split_chips([feed_mine, along_core(after(feed_give, edge_left))], 2, 0)
    feed_keep, feed_swap = split_cores(over_chips(feed_slices), 2, 0)

    def input_back(
        spot_ref,
        dq_ref,
        dkv_ref,
        from_right_ref,
        from_left_ref,
        low_one_ref,
        done_ref,
        zero_ref,
        norm_ref,
        row_ref,
        two_ref,
        three_ref,
        entropy_ref,
        mine_ref,
        give_ref,
        sums_ref,
        *slot_refs,
    ):
        at_core = spot_ref[2]
        dq = dq_ref[...]
        dk, dv = (
            jnp.concatenate(
                [
                    (
                        dkv_ref[index, slot_rows(slot)]
                        + from_left_ref[index, slot_span(spot_ref, 5, slot, width)].astype(f32)
                        + from_right_ref[index, slot_span(spot_ref, 6, slot, width)].astype(f32)
                    ).astype(bf16)
                    for slot in range(chips)
                ],
                axis=0,
            )
            for index in (0, 1)
        )
        for index, item in enumerate((dq, dk, dv, low_one_ref[...])):
            mine_ref[index] = half_of(item, at_core, half)
            give_ref[index] = half_of(item, 1 - at_core, half)
        back = dot_back(dq, row_ref[0]) + dot_back(dk, row_ref[1]) + dot_back(dv, row_ref[2])
        unit, scale = unit_norm(zero_ref[...])
        sums_ref[0:2] = norm_sums(back, unit)
        sums_ref[2:4] = two_ref[...]
        sums_ref[4:6] = three_ref[...]
        sums_ref[6:7] = entropy_ref[...]
        sums_ref[7:8] = jnp.zeros((1, model), f32)
        result = (done_ref[...] + unit_norm_back(back, unit, scale, norm_ref[0:1])).astype(bf16)
        for slot in range(chips):
            slot_refs[slot][...] = result[slot_rows(slot)]

    row_mine, row_give, sums, *grad_slots = kernel_call(
        input_back,
        [
            ((4, toks, half), bf16),
            ((4, toks, half), bf16),
            ((lines, model), f32),
        ]
        + [((width, model), bf16)] * chips,
        [
            spot,
            row_dq,
            row_dkv,
            edge_from_right,
            edge_from_left,
            grad_one_low,
            grad_one,
            stream_zero,
            norm_rows,
            weights_row,
            sums_two,
            sums_three,
            entropy_row,
        ],
        smem=(0,),
    )

    def join_halves(spot_ref, keep_rows, got_rows):
        first = spot_ref[2] == 0
        return jnp.concatenate(
            [jnp.where(first, keep_rows, got_rows), jnp.where(first, got_rows, keep_rows)], axis=1
        )

    def over_cols(whole):
        return [whole] + [along_cols(whole, step) for step in col_steps]

    def order_rows(slices, at):
        def order_slots(spot_ref, *refs):
            for hop, ref in enumerate(refs[:-1]):
                refs[-1][0, chunk_at(spot_ref, spot_ref[1] ^ hop)] = jnp.concatenate(
                    [ref[at : at + width], ref[at + width : at + 2 * width]], axis=1
                )

        return kernel_call(order_slots, [(tokens.shape, bf16)], [spot, *slices], smem=(0,))[0]

    feed_back = along_core(feed_swap)
    col_parts = [col_sums[0]] + [along_cols(col_sums[step], step) for step in col_steps]
    col_slices = split_chips(col_parts, 1, 0, stream=stream_two, slots=grad_slots)
    col_reached = over_chips(col_slices)
    col_keep, col_swap = split_cores(col_reached, 1, 0)

    def join_two(spot_ref, keep_ref, got_ref, keep2_ref, got2_ref, out_ref):
        rows = 2 * shard
        out_ref[:rows] = join_halves(spot_ref, keep_ref[...], got_ref[...])
        out_ref[rows:] = join_halves(spot_ref, keep2_ref[...], got2_ref[...])

    (pair,) = kernel_call(
        join_two,
        [((3 * shard, model), bf16)],
        [spot, feed_keep, feed_back, col_keep, along_core(col_swap)],
        smem=(0,),
    )
    pair_ends = over_cols(pair)

    def spread_pair(spot_ref, u0, u1, u2, u3, in_ref, out_ref, g0, g1, g2, g3, all_ref):
        for step, ref in enumerate((u0, u1, u2, u3)):
            all_ref[spot_ref[0] ^ step] = ref[...]
        for source, grad_ref in enumerate((g0, g1, g2, g3)):
            wide = all_ref[source, :shard].astype(f32)
            for index in range(seqs):
                at = index * block_cols + source * part
                in_ref[:, at : at + part] = wide[:, index * part : (index + 1) * part]
            out_ref[source * part : (source + 1) * part] = all_ref[
                source, shard : 2 * shard
            ].astype(f32)
            grad_ref[...] = all_ref[source, 2 * shard :].astype(f32)

    row_parts = layer_grads(
        normed_one,
        row_mix,
        row_low_far,
        row_mix_far,
        row_mine,
        along_core(row_give),
        [sums],
    )
    row_sends = after(row_parts, col_parts, feed_keep)
    row_parts = [row_parts[0]] + [along_cols(row_sends[step], step) for step in col_steps]
    row_slices = split_chips(row_parts, 1, extra)
    row_reached = over_chips(row_slices)
    row_keep, row_swap = split_cores(row_reached, 1, extra)

    def join_row(spot_ref, keep_ref, got_ref, out_ref, norm_ref, entropy_ref):
        out_ref[...] = join_halves(spot_ref, keep_ref[:shard], got_ref[:shard])
        total = keep_ref[shard:].astype(f32) + got_ref[shard:].astype(f32)
        line = total[6:7]
        entropy_ref[...] = line[:, 0:1] + line[:, 1:2]
        wide = jnp.concatenate([total[:lines], total[lines:]], axis=1)
        at = spot_ref[1] * 2 + spot_ref[2]
        found = wide[:, :shard]
        for index in range(1, seqs):
            here = wide[:, index * shard : (index + 1) * shard]
            found = jnp.where(at == index, here, found)
        norm_ref[...] = found

    row_join, norm_here, entropy_sum = kernel_call(
        join_row,
        [((shard, model), bf16), ((lines, shard), f32), ((1, 1), f32)],
        [spot, row_keep, along_core(row_swap)],
        smem=(0,),
    )
    row_ends = over_cols(row_join)
    result = order_rows(after(col_reached, row_join), block)
    grad_in = order_rows(after(col_reached, row_join), block + 2 * width)
    grad_feed_in, grad_feed_out, *col_grads = kernel_call(
        spread_pair,
        [(feed_in.shape, f32), (feed_out.shape, f32)] + [((shard, model), f32)] * cols_axis,
        [spot, *after(pair_ends, row_join)],
        smem=(0,),
        scratch=[pltpu.VMEM((cols_axis, 3 * shard, model), bf16)],
        room=24,
    )

    def spread_row(spot_ref, *refs):
        ins, outs, all_ref = refs[:cols_axis], refs[cols_axis:-1], refs[-1]
        for step, ref in enumerate(ins):
            all_ref[spot_ref[0] ^ step] = ref[...]
        for matrix in range(cols_axis):
            outs[matrix][...] = all_ref[matrix].astype(f32)

    row_grads = kernel_call(
        spread_row,
        [((shard, model), f32)] * cols_axis,
        [spot, *row_ends],
        smem=(0,),
        scratch=[pltpu.VMEM((cols_axis, shard, model), bf16)],
    )
    entropy = entropy_sum[0, 0] / (HEADS * norm_rows[6, 0])

    return (
        result,
        entropy,
        grad_in,
        *[norm_here[index] for index in range(6)],
        *row_grads,
        *col_grads,
        grad_feed_in,
        grad_feed_out,
    )


def fits_fast(tokens, feed_out):
    chips = lax.axis_size("seq") // 2
    return (
        lax.axis_size("col") == 4
        and lax.axis_size("seq") == 8
        and tokens.shape[0] == 1
        and tokens.shape[1] == chips * WINDOW
        and tokens.shape[2] == HEADS * HEAD_DIM
        and feed_out.shape[0] * 2 == tokens.shape[2]
    )


def on_device(tokens, offsets, band, col_counts, *rest):
    if not fits_fast(tokens, rest[15]):
        return general_plan(tokens, offsets, band, col_counts, *rest)
    return fast_plan(
        tokens,
        offsets,
        band,
        col_counts,
        rest[0:6],
        rest[6:10],
        rest[10:14],
        rest[14],
        rest[15],
        rest[16],
    )


def solution(mesh):
    return jax.shard_map(
        on_device,
        mesh=mesh,
        in_specs=(
            P("seq", "col", None),
            P(),
            P("col", None),
            P("col"),
            P("seq"),
            P("seq"),
            P("seq"),
            P("seq"),
            P("seq"),
            P("seq"),
            P("seq", None),
            P("seq", None),
            P("seq", None),
            P("seq", None),
            P("seq", None),
            P("seq", None),
            P("seq", None),
            P("seq", None),
            P("seq", None),
            P("seq", None),
            P("seq", "col", None),
        ),
        out_specs=(
            P("seq", "col", None),
            P(),
            P("seq", "col", None),
            P("seq"),
            P("seq"),
            P("seq"),
            P("seq"),
            P("seq"),
            P("seq"),
            P("seq", None),
            P("seq", None),
            P("seq", None),
            P("seq", None),
            P("seq", None),
            P("seq", None),
            P("seq", None),
            P("seq", None),
            P("seq", None),
            P("seq", None),
        ),
        check_vma=False,
    )
```

```python
from functools import partial
import math

import jax
import jax.numpy as jnp
from jax import lax
from jax.experimental import pallas as pl
from jax.experimental.pallas import tpu as pltpu
from jax.sharding import PartitionSpec as P

HEADS = 12
HEAD_DIM = 64
WINDOW = 32


entropy_weight = 8192.0
norm_eps = 1e-05


def with_halo(cells, sides, width):
    for axis, dim in sides:
        count = lax.axis_size(axis)
        ends = count - 1
        head = lax.slice_in_dim(cells, 0, width, axis=dim)
        tail = lax.slice_in_dim(cells, cells.shape[dim] - width, cells.shape[dim], axis=dim)
        cells = jnp.concatenate(
            [
                lax.ppermute(tail, axis, [(i, (i + 1) % count) for i in range(ends)]),
                cells,
                lax.ppermute(head, axis, [((i + 1) % count, i) for i in range(ends)]),
            ],
            axis=dim,
        )
    return cells


def layer_norm(inputs, norm_gain, norm_shift):
    average = jnp.mean(inputs, axis=-1, keepdims=True)
    centred = inputs - average
    variance = jnp.mean(centred * centred, axis=-1, keepdims=True)
    return centred * lax.rsqrt(variance + norm_eps) * norm_gain + norm_shift


def position_table(offsets, row_first, col_first, row_count, col_count, model_width):
    half_width = model_width // 2
    frequency = jnp.exp(-math.log(1000.0) * jnp.arange(half_width, dtype=jnp.float32) / half_width)
    col_place = (jnp.arange(col_count, dtype=jnp.int32) + col_first + offsets[1]).astype(
        jnp.float32
    )
    row_place = (jnp.arange(row_count, dtype=jnp.int32) + row_first + offsets[0]).astype(
        jnp.float32
    )
    col_wave = jnp.sin(col_place[:, None] * frequency[None, :])
    row_wave = jnp.sin(row_place[:, None] * frequency[None, :])
    col_full = jnp.broadcast_to(col_wave[None, :, :], (row_count, col_count, half_width))
    row_full = jnp.broadcast_to(row_wave[:, None, :], (row_count, col_count, half_width))
    return 0.5 * jnp.concatenate([col_full, row_full], axis=-1)


def softmax_entropy(scores, allowed, valid):
    masked = jnp.where(allowed[None], scores, -1000000000.0)
    largest = jnp.max(masked, axis=-1, keepdims=True)
    powers = jnp.exp(masked - largest)
    row_total = jnp.sum(powers, axis=-1, keepdims=True)
    probs_out = powers / row_total
    log_total = largest[..., 0] + jnp.log(row_total[..., 0])
    entropies = log_total - jnp.sum(probs_out * jnp.where(allowed[None], scores, 0.0), axis=-1)
    return (probs_out, jnp.sum(entropies * valid[None, :]))


def plain_softmax(scores):
    largest = jnp.max(scores, axis=-1, keepdims=True)
    powers = jnp.exp(scores - largest)
    return powers / jnp.sum(powers, axis=-1, keepdims=True)


def project(activations, weight):
    return jnp.einsum("rci,ij->rcj", activations, weight, preferred_element_type=jnp.float32)


def project_back(gradient, weight):
    return jnp.einsum("rcj,ij->rci", gradient, weight, preferred_element_type=jnp.float32)


def weight_grad(activations, gradient):
    return jnp.einsum("rci,rcj->ij", activations, gradient, preferred_element_type=jnp.float32)


def general_plan(
    tokens,
    offsets,
    band,
    col_counts,
    norm1_gain,
    norm1_shift,
    norm2_gain,
    norm2_shift,
    norm3_gain,
    norm3_shift,
    row_query,
    row_key,
    row_value,
    row_output,
    col_query,
    col_key,
    col_value,
    col_output,
    feed_in,
    feed_out,
    cotangent,
):
    rows_dev, cols_dev, model_width = tokens.shape
    total_rows = rows_dev * lax.axis_size("seq")
    total_cols = cols_dev * lax.axis_size("col")
    row_first = lax.axis_index("seq") * rows_dev
    col_first = lax.axis_index("col") * cols_dev
    count_here = col_counts[0].astype(jnp.float32)
    count_early = lax.psum(count_here, "col")
    params = (
        lax.all_gather(norm1_gain, "seq", axis=0, tiled=True),
        lax.all_gather(norm1_shift, "seq", axis=0, tiled=True),
        lax.all_gather(norm2_gain, "seq", axis=0, tiled=True),
        lax.all_gather(norm2_shift, "seq", axis=0, tiled=True),
        lax.all_gather(norm3_gain, "seq", axis=0, tiled=True),
        lax.all_gather(norm3_shift, "seq", axis=0, tiled=True),
        lax.all_gather(row_query, "seq", axis=0, tiled=True),
        lax.all_gather(row_key, "seq", axis=0, tiled=True),
        lax.all_gather(row_value, "seq", axis=0, tiled=True),
        lax.all_gather(row_output, "seq", axis=0, tiled=True),
        lax.all_gather(col_query, "seq", axis=0, tiled=True),
        lax.all_gather(col_key, "seq", axis=0, tiled=True),
        lax.all_gather(col_value, "seq", axis=0, tiled=True),
        lax.all_gather(col_output, "seq", axis=0, tiled=True),
        lax.all_gather(feed_in, "seq", axis=0, tiled=True),
        lax.all_gather(feed_out, "seq", axis=0, tiled=True),
    )
    gain_one = params[0].astype(jnp.float32)
    shift_one = params[1].astype(jnp.float32)
    gain_two = params[2].astype(jnp.float32)
    shift_two = params[3].astype(jnp.float32)
    gain_three = params[4].astype(jnp.float32)
    shift_three = params[5].astype(jnp.float32)
    query_row, key_row, value_row, output_row = (params[6], params[7], params[8], params[9])
    query_col, key_col, value_col, output_col = (params[10], params[11], params[12], params[13])
    feed_up, feed_down = (params[14], params[15])
    stream_zero = tokens.astype(jnp.float32) + position_table(
        offsets, row_first, col_first, rows_dev, cols_dev, model_width
    )
    normed_one, norm_back_one = jax.vjp(layer_norm, stream_zero, gain_one, shift_one)
    normed_one = normed_one.astype(jnp.bfloat16)
    row_queries = project(normed_one, query_row).astype(jnp.bfloat16)
    row_keys = project(normed_one, key_row).astype(jnp.bfloat16)
    row_values = project(normed_one, value_row).astype(jnp.bfloat16)
    extended = with_halo(jnp.stack([row_keys, row_values]), (("col", 2),), WINDOW)
    ext_cols = cols_dev + 2 * WINDOW
    queries_heads = row_queries.reshape(rows_dev, cols_dev, HEADS, HEAD_DIM)
    keys_ext = extended[0].reshape(rows_dev, ext_cols, HEADS, HEAD_DIM)
    values_ext = extended[1].reshape(rows_dev, ext_cols, HEADS, HEAD_DIM)
    partial_logits = jnp.einsum(
        "rchd,rehd->hce", queries_heads, keys_ext, preferred_element_type=jnp.float32
    )
    row_scale = 1.0 / math.sqrt(HEAD_DIM * total_rows)
    row_scores = lax.psum(partial_logits, "seq") * row_scale
    query_index = jnp.arange(cols_dev, dtype=jnp.int32)[:, None]
    key_index = jnp.arange(ext_cols, dtype=jnp.int32)[None, :]
    distance = key_index - query_index
    choose = jnp.arange(2 * WINDOW + 1, dtype=jnp.int32)
    matches = (distance[:, None, :] == choose[None, :, None]) & (band[:, :, None] == 1)
    key_global = col_first - WINDOW + key_index
    inside = (key_global >= 0) & (key_global < total_cols)
    allowed = (jnp.any(matches, axis=1) | (distance == WINDOW)) & inside
    valid = (jnp.arange(cols_dev, dtype=jnp.int32) < col_counts[0]).astype(jnp.float32)
    (row_probs, ent_part), ent_back = jax.vjp(
        lambda given: softmax_entropy(given, allowed, valid), row_scores
    )
    payload = ent_part[None]
    sums = lax.psum(payload, "col")
    entropy = sums[0] / (HEADS * count_early)
    row_probs_low = row_probs.astype(jnp.bfloat16)
    row_mix = jnp.einsum(
        "hce,rehd->rchd", row_probs_low, values_ext, preferred_element_type=jnp.float32
    )
    row_mix = row_mix.reshape(rows_dev, cols_dev, model_width).astype(jnp.bfloat16)
    stream_one = stream_zero + project(row_mix, output_row)
    normed_two, norm_back_two = jax.vjp(layer_norm, stream_one, gain_two, shift_two)
    normed_two = normed_two.astype(jnp.bfloat16)
    col_queries = project(normed_two, query_col).astype(jnp.bfloat16)
    col_keys = project(normed_two, key_col).astype(jnp.bfloat16)
    col_values = project(normed_two, value_col).astype(jnp.bfloat16)
    col_scale = 1.0 / math.sqrt(HEAD_DIM)
    keys_all, values_all = (
        lax.all_gather(col_keys, "seq", axis=0, tiled=True),
        lax.all_gather(col_values, "seq", axis=0, tiled=True),
    )
    col_heads_q = col_queries.reshape(rows_dev, cols_dev, HEADS, HEAD_DIM)
    keys_heads = keys_all.reshape(total_rows, cols_dev, HEADS, HEAD_DIM)
    values_heads = values_all.reshape(total_rows, cols_dev, HEADS, HEAD_DIM)
    col_raw = jnp.einsum(
        "rchd,schd->chrs", col_heads_q, keys_heads, preferred_element_type=jnp.float32
    )
    col_probs = plain_softmax(col_raw * col_scale)
    col_probs_low = col_probs.astype(jnp.bfloat16)
    col_mix = jnp.einsum(
        "chrs,schd->rchd", col_probs_low, values_heads, preferred_element_type=jnp.float32
    )
    col_mix = col_mix.reshape(rows_dev, cols_dev, model_width).astype(jnp.bfloat16)
    stream_two = stream_one + project(col_mix, output_col)
    normed_three, norm_back_three = jax.vjp(layer_norm, stream_two, gain_three, shift_three)
    normed_three = normed_three.astype(jnp.bfloat16)
    hidden_pre = project(normed_three, feed_up)
    hidden_act, gelu_back = jax.vjp(partial(jax.nn.gelu, approximate=False), hidden_pre)
    hidden_low = hidden_act.astype(jnp.bfloat16)
    output = (stream_two + project(hidden_low, feed_down)).astype(jnp.bfloat16)
    grad_feed_down = weight_grad(hidden_low, cotangent)
    grad_hidden = gelu_back(project_back(cotangent, feed_down))[0].astype(jnp.bfloat16)
    grad_feed_up = weight_grad(normed_three, grad_hidden)
    back_stream, grad_gain_three, grad_shift_three = norm_back_three(
        project_back(grad_hidden, feed_up)
    )
    grad_two = cotangent.astype(jnp.float32) + back_stream
    grad_two_low = grad_two.astype(jnp.bfloat16)
    grad_output_col = weight_grad(col_mix, grad_two_low)
    grad_mix_flat = project_back(grad_two_low, output_col).astype(jnp.bfloat16)
    grad_col_mix = grad_mix_flat.reshape(rows_dev, cols_dev, HEADS, HEAD_DIM)
    col_dprobs = jnp.einsum(
        "rchd,schd->chrs", grad_col_mix, values_heads, preferred_element_type=jnp.float32
    )
    col_dscores = col_probs * (col_dprobs - jnp.sum(col_probs * col_dprobs, axis=-1, keepdims=True))
    col_dscores = col_dscores.astype(jnp.bfloat16)
    grad_col_q = (
        jnp.einsum("chrs,schd->rchd", col_dscores, keys_heads, preferred_element_type=jnp.float32)
        * col_scale
    )
    grad_col_q = grad_col_q.reshape(rows_dev, cols_dev, model_width).astype(jnp.bfloat16)
    row_count = lax.axis_size("seq") * rows_dev
    key_part = (
        jnp.einsum("chrs,rchd->schd", col_dscores, col_heads_q, preferred_element_type=jnp.float32)
        * col_scale
    )
    value_part = jnp.einsum(
        "chrs,rchd->schd", col_probs_low, grad_col_mix, preferred_element_type=jnp.float32
    )
    key_value_grads = lax.psum_scatter(
        jnp.concatenate(
            [
                key_part.reshape(row_count, cols_dev, model_width),
                value_part.reshape(row_count, cols_dev, model_width),
            ],
            axis=-1,
        ),
        "seq",
        scatter_dimension=0,
        tiled=True,
    )
    grad_col_k = key_value_grads[..., :model_width].astype(jnp.bfloat16)
    grad_col_v = key_value_grads[..., model_width:].astype(jnp.bfloat16)
    grad_query_col = weight_grad(normed_two, grad_col_q)
    grad_key_col = weight_grad(normed_two, grad_col_k)
    grad_value_col = weight_grad(normed_two, grad_col_v)
    back_input = (
        project_back(grad_col_q, query_col)
        + project_back(grad_col_k, key_col)
        + project_back(grad_col_v, value_col)
    )
    back_stream, grad_gain_two, grad_shift_two = norm_back_two(back_input)
    grad_one = grad_two + back_stream
    grad_one_low = grad_one.astype(jnp.bfloat16)
    grad_output_row = weight_grad(row_mix, grad_one_low)
    grad_row_mix = project_back(grad_one_low, output_row).astype(jnp.bfloat16)
    grad_row_mix = grad_row_mix.reshape(rows_dev, cols_dev, HEADS, HEAD_DIM)
    dprobs_part = jnp.einsum(
        "rchd,rehd->hce", grad_row_mix, values_ext, preferred_element_type=jnp.float32
    )
    row_dprobs = lax.psum(dprobs_part.astype(jnp.bfloat16), "seq").astype(jnp.float32)
    ent_cot = jnp.asarray(entropy_weight, dtype=jnp.float32) / (HEADS * count_early)
    row_dscores = ent_back((row_dprobs, ent_cot))[0].astype(jnp.bfloat16)
    grad_row_q = (
        jnp.einsum("hce,rehd->rchd", row_dscores, keys_ext, preferred_element_type=jnp.float32)
        * row_scale
    )
    grad_row_q = grad_row_q.reshape(rows_dev, cols_dev, model_width).astype(jnp.bfloat16)
    grad_keys_ext = (
        jnp.einsum("hce,rchd->rehd", row_dscores, queries_heads, preferred_element_type=jnp.float32)
        * row_scale
    )
    grad_values_ext = jnp.einsum(
        "hce,rchd->rehd", row_probs_low, grad_row_mix, preferred_element_type=jnp.float32
    )
    grad_ext = jnp.stack([grad_keys_ext, grad_values_ext]).reshape(
        2, rows_dev, ext_cols, model_width
    )
    rims = jnp.concatenate([grad_ext[:, :, :WINDOW], grad_ext[:, :, WINDOW + cols_dev :]], axis=2)
    returned = with_halo(rims.astype(jnp.bfloat16), (("col", 2),), WINDOW).astype(rims.dtype)
    interior = grad_ext[:, :, WINDOW : WINDOW + cols_dev]
    interior = interior.at[:, :, :WINDOW].add(returned[:, :, :WINDOW])
    interior = interior.at[:, :, cols_dev - WINDOW :].add(returned[:, :, 3 * WINDOW :])
    grad_row_k = interior[0].astype(jnp.bfloat16)
    grad_row_v = interior[1].astype(jnp.bfloat16)
    grad_query_row = weight_grad(normed_one, grad_row_q)
    grad_key_row = weight_grad(normed_one, grad_row_k)
    grad_value_row = weight_grad(normed_one, grad_row_v)
    back_input = (
        project_back(grad_row_q, query_row)
        + project_back(grad_row_k, key_row)
        + project_back(grad_row_v, value_row)
    )
    back_stream, grad_gain_one, grad_shift_one = norm_back_one(back_input)
    input_grad = (grad_one + back_stream).astype(jnp.bfloat16)
    shares = (
        lax.psum_scatter(
            grad_gain_one.astype(jnp.bfloat16), "seq", scatter_dimension=0, tiled=True
        ).astype(jnp.float32),
        lax.psum_scatter(
            grad_shift_one.astype(jnp.bfloat16), "seq", scatter_dimension=0, tiled=True
        ).astype(jnp.float32),
        lax.psum_scatter(
            grad_gain_two.astype(jnp.bfloat16), "seq", scatter_dimension=0, tiled=True
        ).astype(jnp.float32),
        lax.psum_scatter(
            grad_shift_two.astype(jnp.bfloat16), "seq", scatter_dimension=0, tiled=True
        ).astype(jnp.float32),
        lax.psum_scatter(
            grad_gain_three.astype(jnp.bfloat16), "seq", scatter_dimension=0, tiled=True
        ).astype(jnp.float32),
        lax.psum_scatter(
            grad_shift_three.astype(jnp.bfloat16), "seq", scatter_dimension=0, tiled=True
        ).astype(jnp.float32),
        lax.psum_scatter(
            grad_query_row.astype(jnp.bfloat16), "seq", scatter_dimension=0, tiled=True
        ).astype(jnp.float32),
        lax.psum_scatter(
            grad_key_row.astype(jnp.bfloat16), "seq", scatter_dimension=0, tiled=True
        ).astype(jnp.float32),
        lax.psum_scatter(
            grad_value_row.astype(jnp.bfloat16), "seq", scatter_dimension=0, tiled=True
        ).astype(jnp.float32),
        lax.psum_scatter(
            grad_output_row.astype(jnp.bfloat16), "seq", scatter_dimension=0, tiled=True
        ).astype(jnp.float32),
        lax.psum_scatter(
            grad_query_col.astype(jnp.bfloat16), "seq", scatter_dimension=0, tiled=True
        ).astype(jnp.float32),
        lax.psum_scatter(
            grad_key_col.astype(jnp.bfloat16), "seq", scatter_dimension=0, tiled=True
        ).astype(jnp.float32),
        lax.psum_scatter(
            grad_value_col.astype(jnp.bfloat16), "seq", scatter_dimension=0, tiled=True
        ).astype(jnp.float32),
        lax.psum_scatter(
            grad_output_col.astype(jnp.bfloat16), "seq", scatter_dimension=0, tiled=True
        ).astype(jnp.float32),
        lax.psum_scatter(
            grad_feed_up.astype(jnp.bfloat16), "seq", scatter_dimension=0, tiled=True
        ).astype(jnp.float32),
        lax.psum_scatter(
            grad_feed_down.astype(jnp.bfloat16), "seq", scatter_dimension=0, tiled=True
        ).astype(jnp.float32),
    )
    totals = (
        lax.psum(shares[0].astype(jnp.bfloat16), "col").astype(jnp.float32),
        lax.psum(shares[1].astype(jnp.bfloat16), "col").astype(jnp.float32),
        lax.psum(shares[2].astype(jnp.bfloat16), "col").astype(jnp.float32),
        lax.psum(shares[3].astype(jnp.bfloat16), "col").astype(jnp.float32),
        lax.psum(shares[4].astype(jnp.bfloat16), "col").astype(jnp.float32),
        lax.psum(shares[5].astype(jnp.bfloat16), "col").astype(jnp.float32),
        lax.psum(shares[6].astype(jnp.bfloat16), "col").astype(jnp.float32),
        lax.psum(shares[7].astype(jnp.bfloat16), "col").astype(jnp.float32),
        lax.psum(shares[8].astype(jnp.bfloat16), "col").astype(jnp.float32),
        lax.psum(shares[9].astype(jnp.bfloat16), "col").astype(jnp.float32),
        lax.psum(shares[10].astype(jnp.bfloat16), "col").astype(jnp.float32),
        lax.psum(shares[11].astype(jnp.bfloat16), "col").astype(jnp.float32),
        lax.psum(shares[12].astype(jnp.bfloat16), "col").astype(jnp.float32),
        lax.psum(shares[13].astype(jnp.bfloat16), "col").astype(jnp.float32),
        lax.psum(shares[14].astype(jnp.bfloat16), "col").astype(jnp.float32),
        lax.psum(shares[15].astype(jnp.bfloat16), "col").astype(jnp.float32),
    )
    return (
        output,
        entropy,
        input_grad,
        totals[0],
        totals[1],
        totals[2],
        totals[3],
        totals[4],
        totals[5],
        totals[6],
        totals[7],
        totals[8],
        totals[9],
        totals[10],
        totals[11],
        totals[12],
        totals[13],
        totals[14],
        totals[15],
    )


def after(values, *needed):
    return lax.optimization_barrier((values, needed))[0]


def kernel_call(
    body, outs, args, smem=(), scratch=(), flops=1, moved=1, stream=False, room=16
):
    out_shapes = [jax.ShapeDtypeStruct(shape, kind) for shape, kind in outs]

    def whole(item):
        if not stream:
            return pl.BlockSpec(memory_space=pltpu.VMEM)
        rank = len(item.shape)
        return pl.BlockSpec(item.shape, lambda step: (0,) * rank, pipeline_mode=pl.Buffered(1))

    return pl.pallas_call(
        body,
        grid=(1,) if stream else (),
        out_shape=out_shapes,
        in_specs=[
            pl.BlockSpec(memory_space=pltpu.SMEM) if place in smem else whole(item)
            for place, item in enumerate(args)
        ],
        out_specs=[whole(item) for item in out_shapes],
        scratch_shapes=list(scratch),
        compiler_params=pltpu.CompilerParams(vmem_limit_bytes=(56 if stream else room) << 20),
        cost_estimate=pl.CostEstimate(
            flops=int(flops), bytes_accessed=int(moved), transcendentals=0
        ),
        name=body.__name__,
    )(*args)


def dot(left, right):
    return jnp.dot(left, right, preferred_element_type=jnp.float32)


def dot_back(left, right):
    return lax.dot_general(
        left, right, (((1,), (1,)), ((), ())), preferred_element_type=jnp.float32
    )


def dot_tokens(left, right):
    return lax.dot_general(
        left, right, (((0,), (0,)), ((), ())), preferred_element_type=jnp.float32
    )


def unit_norm(inputs):
    centred = inputs - jnp.mean(inputs, axis=-1, keepdims=True)
    scale = lax.rsqrt(jnp.mean(centred * centred, axis=-1, keepdims=True) + norm_eps)
    return centred * scale, scale


def unit_norm_back(given, unit, scale, gain):
    scaled = given * gain
    first = jnp.mean(scaled, axis=-1, keepdims=True)
    second = jnp.mean(scaled * unit, axis=-1, keepdims=True)
    return scale * (scaled - first - unit * second)


def norm_sums(given, unit):
    return jnp.concatenate(
        [
            jnp.sum(given * unit, axis=0, keepdims=True),
            jnp.sum(given, axis=0, keepdims=True),
        ],
        axis=0,
    )


def head_mask(width, model_width):
    rows = lax.broadcasted_iota(jnp.int32, (HEADS * width, model_width), 0) // width
    lanes = lax.broadcasted_iota(jnp.int32, (HEADS * width, model_width), 1) // HEAD_DIM
    return rows == lanes


def spread_heads(block, mask):
    tiled = jnp.concatenate([block] * HEADS, axis=0)
    return jnp.where(mask, tiled, jnp.zeros_like(tiled))


def fold_heads(product, mask, width):
    kept = jnp.where(mask, product, 0.0)
    total = kept[:width]
    for head in range(1, HEADS):
        total = total + kept[head * width : (head + 1) * width]
    return total


def head_of_lane(model_width):
    rows = lax.broadcasted_iota(jnp.int32, (model_width, 128), 0) // HEAD_DIM
    lanes = lax.broadcasted_iota(jnp.int32, (model_width, 128), 1)
    return (rows == lanes).astype(jnp.bfloat16)


def per_head_sum(product, lane_heads):
    return dot(product.astype(jnp.bfloat16), lane_heads)


def slot_span(spot_ref, side, slot, width):
    return pl.ds(pl.multiple_of((slot ^ spot_ref[side]) * width, width), width)


def window_rows(spot_ref, near_ref, left_ref, right_ref, which, slot, width):
    return jnp.concatenate(
        [
            left_ref[which, slot_span(spot_ref, 5, slot, width)],
            near_ref[which, slot * width : (slot + 1) * width],
            right_ref[which, slot_span(spot_ref, 6, slot, width)],
        ],
        axis=0,
    )


def half_of(values, core, width):
    return jnp.where(core == 0, values[:, :width], values[:, width:])


def fast_plan(
    tokens,
    offsets,
    band,
    col_counts,
    norms,
    row_weights,
    col_weights,
    feed_in,
    feed_out,
    cotangent,
):
    f32, bf16 = jnp.float32, jnp.bfloat16
    cols_dev, model = tokens.shape[1:]
    cols_axis, seqs = lax.axis_size("col"), lax.axis_size("seq")
    chips = seqs // 2
    width = cols_dev // chips
    toks = chips * width
    shard = model // seqs
    half = model // 2
    hidden = feed_out.shape[0] * seqs // cols_axis
    fold = HEADS * width
    span = 3 * width
    col_at = lax.axis_index("col")
    seq_at = lax.axis_index("seq")
    chip, core = seq_at // 2, seq_at % 2
    flip = col_at % 2

    def chunk_of(chip_index):
        return jnp.where(flip == 0, chip_index, chips - 1 - chip_index)

    chunk = chunk_of(chip)
    piece = col_at * chips + chunk

    def along_chips(values, step):
        return lax.ppermute(values, "seq", [(i, i ^ (2 * step)) for i in range(seqs)])

    def along_core(values):
        return lax.ppermute(values, "seq", [(i, i ^ 1) for i in range(seqs)])

    def along_cols(values, step):
        return lax.ppermute(values, "col", [(i, i ^ step) for i in range(cols_axis)])

    def pair_cols(values):
        pairs = [
            (c * seqs + i, (c ^ (1 + i % 2)) * seqs + i)
            for c in range(cols_axis)
            for i in range(seqs)
        ]
        return lax.ppermute(values, ("col", "seq"), pairs)

    def pair_chips(values):
        pairs = [(i, (i // 2 ^ (1 + i % 2)) * 2 + i % 2) for i in range(seqs)]
        return lax.ppermute(values, "seq", pairs)

    def place_of(piece_index, core_index):
        block, part = divmod(piece_index, chips)
        chip_index = part if block % 2 == 0 else chips - 1 - part
        return block * seqs + chip_index * 2 + core_index

    rightward = [
        (place_of(i, k), place_of(i + 1, k)) for i in range(cols_axis * chips - 1) for k in (0, 1)
    ]
    leftward = [(target, source) for source, target in rightward]

    def to_right(values):
        return lax.ppermute(values, ("col", "seq"), rightward)

    def to_left(values):
        return lax.ppermute(values, ("col", "seq"), leftward)

    steps = range(1, chips)
    col_steps = range(1, cols_axis)

    def turn_to(other):
        block, rest = other // chips, other % chips
        return chip ^ jnp.where(block % 2 == 0, rest, chips - 1 - rest)

    to_left_turn = turn_to(jnp.maximum(piece - 1, 0))
    to_right_turn = turn_to(jnp.minimum(piece + 1, cols_axis * chips - 1))
    spot = jnp.stack(
        [col_at, chip, core, chunk, col_counts[0], to_left_turn, to_right_turn]
    ).astype(jnp.int32)

    half_width = model // 2
    frequency = jnp.exp(-math.log(1000.0) * jnp.arange(half_width, dtype=f32) / half_width)
    col_place = (jnp.arange(width, dtype=jnp.int32) + piece * width + offsets[1]).astype(f32)
    seq_slots = jnp.stack([(chip ^ step) * 2 + core for step in range(chips)])
    row_place = (seq_slots + offsets[0]).astype(f32)
    waves = 0.5 * jnp.sin(
        jnp.concatenate([col_place, row_place])[:, None] * frequency[None, :]
    )
    band_here = lax.dynamic_slice_in_dim(band, chunk * width, width, axis=0)
    query_index = jnp.arange(width, dtype=jnp.int32)[:, None]
    key_index = jnp.arange(span, dtype=jnp.int32)[None, :]
    distance = key_index - query_index
    choose = jnp.arange(2 * WINDOW + 1, dtype=jnp.int32)
    matches = (distance[:, None, :] == choose[None, :, None]) & (band_here[:, :, None] == 1)
    key_global = (piece - 1) * width + key_index
    inside = (key_global >= 0) & (key_global < cols_axis * cols_dev)
    allowed = ((jnp.any(matches, axis=1) | (distance == WINDOW)) & inside).astype(f32)

    quarter = shard // cols_axis
    lines = 8
    hops = chips - 1
    col_rows = cols_axis * quarter
    row_rows = col_rows + lines

    def chunk_at(spot_ref, chip_index):
        at = jnp.where(spot_ref[0] % 2 == 0, chip_index, chips - 1 - chip_index)
        return pl.ds(pl.multiple_of(at * width, width), width)

    def pack(spot_ref, weights, own_ref, send_refs, block):
        at = pl.multiple_of(spot_ref[0] * quarter, quarter)
        size = len(weights) * quarter
        for index, ref in enumerate(weights):
            own_ref[index * shard : (index + 1) * shard] = ref[...]
            for send_ref in send_refs:
                send_ref[index * quarter : (index + 1) * quarter] = ref[pl.ds(at, quarter)]
        if block is not None:
            for ref, row in [(own_ref, len(weights) * shard)] + [
                (ref, size) for ref in send_refs
            ]:
                ref[row : row + lines] = jnp.zeros((lines, model), bf16)
                ref[row : row + lines, :128] = block

    def pack_row(spot_ref, *refs):
        norm_refs, own_ref, send_ref = refs[4:10], refs[10], refs[11]
        block = jnp.zeros((lines, 128), f32)
        rows = lax.broadcasted_iota(jnp.int32, (lines, 128), 0)
        for index, ref in enumerate(norm_refs):
            line = jnp.pad(ref[...].astype(f32), ((0, 0), (0, 128 - shard)))
            block = jnp.where(rows == index, line, block)
        block = jnp.where(rows == 6, spot_ref[4].astype(f32), block).astype(bf16)
        pack(spot_ref, refs[:4], own_ref, [send_ref], block)

    part = feed_out.shape[0] // cols_axis
    block_cols = feed_out.shape[0]

    def pack_rest(spot_ref, *refs):
        token_refs, in_ref, out_ref = refs[4:6], refs[6], refs[7]
        own_ref, chunk_ref, send_refs = refs[8], refs[10], refs[11:]
        pack(spot_ref, refs[:4], refs[9], send_refs, None)
        for index, ref in enumerate(token_refs):
            chunk_ref[index * width : (index + 1) * width] = ref[0, chunk_at(spot_ref, spot_ref[1])]
            for hop, send_ref in enumerate(send_refs):
                at = col_rows + index * width
                send_ref[at : at + width] = ref[0, chunk_at(spot_ref, spot_ref[1] ^ (hop + 1))]
        first = lax.broadcasted_iota(jnp.int32, (block_cols, 128), 0)
        lanes = lax.broadcasted_iota(jnp.int32, (block_cols, 128), 1)
        chosen = ((first == lanes + spot_ref[0] * part) & (lanes < part)).astype(bf16)
        for index in range(seqs):
            block = in_ref[:, index * block_cols : (index + 1) * block_cols]
            own_ref[0, :, index * part : (index + 1) * part] = dot(block, chosen)[
                :, :part
            ].astype(bf16)
        own_ref[1] = out_ref[pl.ds(pl.multiple_of(spot_ref[0] * part, part), part)]

    def stack_row(*refs):
        for hop, ref in enumerate(refs[:-1]):
            refs[-1][hop * row_rows : (hop + 1) * row_rows] = ref[...]

    def stack_col(own_ref, *refs):
        ins, (out_ref, given_ref) = refs[:-2], refs[-2:]
        for slot, ref in enumerate((own_ref, *ins)):
            at = 0 if slot == 0 else col_rows
            given_ref[slot * width : (slot + 1) * width] = ref[at + width : at + 2 * width]
            if slot:
                out_ref[(slot - 1) * col_rows : slot * col_rows] = ref[:col_rows]

    def spread_plane(near, far):
        def join_cores(near_ref, far_ref, out_ref):
            rows = near_ref.shape[0]
            out_ref[:rows] = near_ref[...]
            out_ref[rows:] = far_ref[...]

        both_cores = kernel_call(join_cores, [((2 * near.shape[0], model), bf16)], [near, far])[0]
        return both_cores, pair_cols(both_cores), along_cols(near, cols_axis - 1)

    def place_rows(spot_ref, refs, outs, rows, unit):
        at_col, at_chip, at_core = spot_ref[0], spot_ref[1], spot_ref[2]
        other = 1 - at_core

        def row_of(from_chip, from_core, offset, size):
            return pl.ds(
                pl.multiple_of((from_chip * 2 + from_core) * shard + offset, quarter), size
            )

        pieces = (
            (refs[2], at_col, at_core, 2),
            (refs[3], at_col ^ (1 + at_core), at_core, 2),
            (refs[4], at_col ^ 3, at_core, 1),
            (refs[5], at_col ^ (1 + other), other, 2),
            (refs[6], at_col ^ 3, other, 1),
        )
        for index, (out_ref, lead) in enumerate(outs):
            for ref, core_at in ((refs[0], at_core), (refs[1], other)):
                out_ref[lead + (row_of(at_chip, core_at, 0, shard),)] = ref[
                    index * shard : (index + 1) * shard
                ]
            for ref, col, core_at, sides in pieces:
                for side in range(sides):
                    for hop in steps:
                        at = row_of(at_chip ^ hop, core_at ^ side, col * quarter, quarter)
                        start = side * unit + (hop - 1) * rows + index * quarter
                        out_ref[lead + (at,)] = ref[start : start + quarter]

    row_own, row_send = kernel_call(
        pack_row,
        [((cols_axis * shard + lines, model), bf16), ((row_rows, model), bf16)],
        [spot, *row_weights, *[item[None] for item in norms]],
        smem=(0,),
        stream=True,
    )
    row_got = [along_chips(row_send, step) for step in steps]
    feed_own, col_own, chunks_own, *col_sends = kernel_call(
        pack_rest,
        [
            ((2, shard, hidden), bf16),
            ((cols_axis * shard, model), bf16),
            ((2 * width, model), bf16),
        ]
        + [((col_rows + 2 * width, model), bf16)] * hops,
        [spot, *col_weights, tokens, cotangent, feed_in, feed_out],
        smem=(0,),
        stream=True,
    )
    row_got = after(row_got, waves, allowed, col_sends)
    feed_other = along_core(feed_own)
    row_hops = kernel_call(stack_row, [((hops * row_rows, model), bf16)], row_got)[0]
    row_far_own = along_core(row_own)
    row_plane, row_pair, row_diagonal = spread_plane(row_hops, along_core(row_hops))
    col_sends = after(col_sends, row_plane)
    col_got = [along_chips(col_sends[step - 1], step) for step in steps]

    def pair_feed(own_ref, other_ref, out_ref):
        out_ref[0] = own_ref[...]
        out_ref[1] = other_ref[...]

    feed_both = kernel_call(
        pair_feed, [((2, 2, shard, hidden), bf16)], [feed_own, after(feed_other, row_plane)]
    )[0]
    row_last = after((row_pair, row_diagonal), row_pair, row_diagonal, col_got, feed_both)
    row_pieces = [row_own, row_far_own, row_plane, row_pair, row_diagonal] + [
        along_core(item) for item in row_last
    ]
    def project_row(spot_ref, waves_ref, *refs):
        token_refs, pieces, outs = refs[:chips], refs[chips : chips + 7], refs[chips + 7 :]
        zero_ref, low_ref, q_ref, kv_ref, weight_ref, last_ref, norm_ref = outs
        place_rows(
            spot_ref,
            pieces,
            [(weight_ref, (index,)) for index in range(3)] + [(last_ref, ())],
            row_rows,
            hops * row_rows,
        )
        first = lax.broadcasted_iota(jnp.int32, (128, model), 0)
        lanes = lax.broadcasted_iota(jnp.int32, (128, model), 1)
        total = jnp.zeros((lines, model), f32)
        for side in (0, 1):
            for hop in range(chips):
                if hop == 0:
                    block = pieces[side][cols_axis * shard : cols_axis * shard + lines, :128]
                else:
                    at = (side * hops + hop) * row_rows - lines
                    block = pieces[2][at : at + lines, :128]
                start = ((spot_ref[1] ^ hop) * 2 + (spot_ref[2] ^ side)) * shard
                chosen = ((lanes == first + start) & (first < shard)).astype(bf16)
                total = total + dot(block, chosen)
        count = spot_ref[4].astype(f32)
        for ref in pieces[3:6]:
            count = count + ref[row_rows - lines : row_rows, :128][6:7, 0:1].astype(f32)
        rows = lax.broadcasted_iota(jnp.int32, (lines, model), 0)
        norm_ref[...] = jnp.where(rows == 6, count, total)
        for slot in range(chips):
            rows = slice(slot * width, (slot + 1) * width)
            at = 0 if slot == 0 else col_rows
            stream = token_refs[slot][at : at + width].astype(f32)
            zero_ref[rows, :half] = stream[:, :half] + waves_ref[:width]
            zero_ref[rows, half:] = stream[:, half:] + waves_ref[width + slot : width + slot + 1]
        unit, _ = unit_norm(zero_ref[...])
        low = (unit * norm_ref[0:1] + norm_ref[1:2]).astype(bf16)
        low_ref[...] = low
        q_ref[...] = dot(low, weight_ref[0]).astype(bf16)
        kv_ref[0] = dot(low, weight_ref[1]).astype(bf16)
        kv_ref[1] = dot(low, weight_ref[2]).astype(bf16)

    big = 2.0 * toks * model * model
    stream_zero, normed_one, row_q, row_kv, weights_row, weights_out, norm_rows = kernel_call(
        project_row,
        [
            ((toks, model), f32),
            ((toks, model), bf16),
            ((toks, model), bf16),
            ((2, toks, model), bf16),
            ((3, model, model), bf16),
            ((model, model), bf16),
            ((lines, model), f32),
        ],
        [spot, waves, chunks_own, *col_got, *row_pieces],
        smem=(0,),
    )
    kv_left = to_right(row_kv)
    kv_right = to_left(row_kv)
    col_unit = hops * col_rows
    col_hops, given_out = kernel_call(
        stack_col,
        [((col_unit, model), bf16), ((toks, model), bf16)],
        [after(chunks_own, row_q), *col_got],
    )
    col_far_own = along_core(col_own)
    col_plane, col_pair, col_diagonal = spread_plane(col_hops, along_core(col_hops))

    feed_pair = pair_chips(after(feed_both, row_q))

    def tied_logits(spot_ref, q_ref, near_ref, left_ref, right_ref, out_ref):
        mask = head_mask(width, model)
        total = None
        for slot in range(chips):
            keys = window_rows(spot_ref, near_ref, left_ref, right_ref, 0, slot, width)
            spread = spread_heads(q_ref[slot * width : (slot + 1) * width], mask)
            term = dot_back(spread, keys)
            total = term if total is None else total + term
        out_ref[...] = total

    logits = kernel_call(
        tied_logits,
        [((fold, span), f32)],
        [spot, row_q, row_kv, kv_left, kv_right],
        smem=(0,),
    )[0]
    logits_other = along_core(logits)
    feed_diagonal = along_chips(after(feed_own, logits), chips - 1)
    given_far = after(along_core(given_out), logits)
    row_scale = 1.0 / math.sqrt(HEAD_DIM * seqs)
    col_scale = 1.0 / math.sqrt(HEAD_DIM)

    def attend_row(
        spot_ref,
        logits_ref,
        other_ref,
        allowed_ref,
        near_ref,
        left_ref,
        right_ref,
        zero_ref,
        norm_ref,
        weight_ref,
        scores_ref,
        probs_ref,
        mix_ref,
        stream_ref,
        low_ref,
        entropy_ref,
    ):
        mask = head_mask(width, model)
        scores = (logits_ref[...] + other_ref[...]) * row_scale
        open_here = jnp.concatenate([allowed_ref[...]] * HEADS, axis=0) > 0.5
        masked = jnp.where(open_here, scores, -1000000000.0)
        largest = jnp.max(masked, axis=-1, keepdims=True)
        powers = jnp.exp(masked - largest)
        total = jnp.sum(powers, axis=-1, keepdims=True)
        probs = powers / total
        kept = jnp.where(open_here, scores, 0.0)
        entropies = largest + jnp.log(total) - jnp.sum(probs * kept, axis=-1, keepdims=True)
        rows = lax.broadcasted_iota(jnp.int32, (fold, 1), 0) % width
        entropies = jnp.where(rows + spot_ref[3] * width < spot_ref[4], entropies, 0.0)
        lanes = lax.broadcasted_iota(jnp.int32, (1, model), 1)
        found = jnp.sum(entropies, axis=0, keepdims=True)
        entropy_ref[...] = jnp.where((lanes == 0) & (spot_ref[2] == 0), found, 0.0)
        scores_ref[...] = kept
        probs_ref[...] = probs
        low_probs = probs.astype(bf16)
        for slot in range(chips):
            values = window_rows(spot_ref, near_ref, left_ref, right_ref, 1, slot, width)
            mix_ref[slot * width : (slot + 1) * width] = fold_heads(
                dot(low_probs, values), mask, width
            ).astype(bf16)
        stream = zero_ref[...] + dot(mix_ref[...], weight_ref[...])
        stream_ref[...] = stream
        unit, _ = unit_norm(stream)
        low_ref[...] = (unit * norm_ref[2:3] + norm_ref[3:4]).astype(bf16)

    scores, probs, row_mix, stream_one, normed_two, entropy_row = kernel_call(
        attend_row,
        [
            ((fold, span), f32),
            ((fold, span), f32),
            ((toks, model), bf16),
            ((toks, model), f32),
            ((toks, model), bf16),
            ((1, model), f32),
        ],
        [
            spot,
            logits,
            logits_other,
            allowed,
            row_kv,
            kv_left,
            kv_right,
            stream_zero,
            norm_rows,
            weights_out,
        ],
        smem=(0,),
    )

    col_last = after((col_pair, col_diagonal), normed_two, feed_pair)
    col_pieces = [col_own, col_far_own, col_plane, col_pair, col_diagonal] + [
        along_core(item) for item in col_last
    ]

    def assemble_col(spot_ref, *refs):
        three_ref, last_ref = refs[7:]
        outs = [(three_ref, (index,)) for index in range(3)] + [(last_ref, ())]
        place_rows(spot_ref, refs[:7], outs, col_rows, col_unit)

    weights_three, weights_last = kernel_call(
        assemble_col,
        [((3, model, model), bf16), ((model, model), bf16)],
        [spot, *col_pieces],
        smem=(0,),
    )

    def project_col(low_ref, weight_ref, q_ref, k_ref, v_ref):
        low = low_ref[...]
        q_ref[...] = dot(low, weight_ref[0]).astype(bf16)
        k_ref[...] = dot(low, weight_ref[1]).astype(bf16)
        v_ref[...] = dot(low, weight_ref[2]).astype(bf16)

    col_q, col_k, col_v = kernel_call(
        project_col,
        [((toks, model), bf16)] * 3,
        [normed_two, weights_three],
    )
    k_other, v_other = along_core(col_k), along_core(col_v)

    def join_given(near_ref, far_ref, out_ref):
        out_ref[:toks] = near_ref[...]
        out_ref[toks:] = far_ref[...]

    given_both = kernel_call(join_given, [((2 * toks, model), bf16)], [given_out, given_far])[0]
    given_pair = pair_cols(given_both)

    def slot_rows(slot):
        return slice(slot * width, (slot + 1) * width)

    def attend_col(
        q_ref,
        k_ref,
        v_ref,
        k2_ref,
        v2_ref,
        one_ref,
        norm_ref,
        weight_ref,
        given_ref,
        probs_ref,
        mix_ref,
        stream_ref,
        low_ref,
        message_ref,
    ):
        lane_heads = head_of_lane(model)
        sides = ((k_ref, v_ref), (k2_ref, v2_ref))
        for slot in range(chips):
            query = q_ref[slot_rows(slot)].astype(f32)
            products = jnp.concatenate(
                [
                    query * sides[s // chips][0][slot_rows(s % chips)].astype(f32)
                    for s in range(seqs)
                ],
                axis=0,
            )
            found = per_head_sum(products, lane_heads) * col_scale
            parts = [found[s * width : (s + 1) * width] for s in range(seqs)]
            largest = parts[0]
            for item in parts[1:]:
                largest = jnp.maximum(largest, item)
            powers = [jnp.exp(item - largest) for item in parts]
            total = powers[0]
            for item in powers[1:]:
                total = total + item
            weights = jnp.concatenate([item / total for item in powers], axis=0)
            probs_ref[slot] = weights
            wide = dot_back(weights.astype(bf16), lane_heads)
            mixed = None
            for s in range(seqs):
                term = wide[s * width : (s + 1) * width] * sides[s // chips][1][
                    slot_rows(s % chips)
                ].astype(f32)
                mixed = term if mixed is None else mixed + term
            mix_ref[slot_rows(slot)] = mixed.astype(bf16)
        stream = one_ref[...] + dot(mix_ref[...], weight_ref[...])
        stream_ref[...] = stream
        unit, _ = unit_norm(stream)
        low = (unit * norm_ref[4:5] + norm_ref[5:6]).astype(bf16)
        low_ref[...] = low
        message_ref[:toks] = low
        message_ref[toks:] = given_ref[...]

    col_probs, col_mix, stream_two, normed_three, message = kernel_call(
        attend_col,
        [
            ((chips, seqs * width, 128), f32),
            ((toks, model), bf16),
            ((toks, model), f32),
            ((toks, model), bf16),
            ((2 * toks, model), bf16),
        ],
        [col_q, col_k, col_v, k_other, v_other, stream_one, norm_rows, weights_last, given_out],
    )
    low_near = [
        normed_three,
        along_cols(normed_three, 1),
        along_cols(normed_three, 2),
        along_cols(message, 3),
    ]

    feed_last = after((feed_pair, feed_diagonal, given_pair), low_near)
    feed_far = [along_core(item) for item in feed_last]

    def assemble_feed(
        spot_ref,
        both_ref,
        pair_ref,
        last_ref,
        pair2_ref,
        last2_ref,
        d0_ref,
        d1_ref,
        d2_ref,
        d3_ref,
        out_ref,
        given_ref,
    ):
        at_chip, at_core = spot_ref[1], spot_ref[2]
        other = 1 - at_core

        def move(rows, from_chip, from_core):
            at = pl.multiple_of((from_chip * 2 + from_core) * shard, shard)
            out_ref[:, pl.ds(at, shard)] = rows

        for side in (0, 1):
            move(both_ref[side], at_chip, at_core ^ side)
            move(pair_ref[side], at_chip ^ (1 + at_core), at_core ^ side)
            move(pair2_ref[side], at_chip ^ (1 + other), other ^ side)
        move(last_ref[...], at_chip ^ 3, at_core)
        move(last2_ref[...], at_chip ^ 3, other)
        given_ref[0] = d0_ref[...]
        given_ref[1 + at_core] = d1_ref[:toks]
        given_ref[2 - at_core] = d2_ref[toks:]
        given_ref[3] = d3_ref[toks:]

    weights_feed, given_all = kernel_call(
        assemble_feed,
        [((2, model, hidden), bf16), ((cols_axis, toks, model), bf16)],
        [
            spot,
            feed_both,
            feed_pair,
            feed_diagonal,
            feed_far[0],
            feed_far[1],
            given_out,
            given_pair,
            feed_far[2],
            low_near[3],
        ],
        smem=(0,),
    )

    def feed_main(a0, a1, a2, a3, given_ref, weight_ref, act_ref, grad_ref, *back_refs):
        up, down = weight_ref[0], weight_ref[1]
        for step, low_ref in enumerate((a0, a1, a2, a3)):
            pre = dot(low_ref[:toks], up)
            bell = 0.5 * (1.0 + lax.erf(pre * (0.5**0.5)))
            slope = bell + pre * jnp.exp(-0.5 * pre * pre) * ((0.5 / math.pi) ** 0.5)
            act_ref[step] = (pre * bell).astype(bf16)
            grad = (slope * dot_back(given_ref[step], down)).astype(bf16)
            grad_ref[step] = grad
            back_refs[step][...] = dot_back(grad, up).astype(bf16)

    feed_big = 2.0 * toks * cols_axis * model * hidden
    feed_results = kernel_call(
        feed_main,
        [((cols_axis, toks, hidden), bf16)] * 2 + [((toks, model), bf16)] * cols_axis,
        [*low_near, given_all, weights_feed],
    )
    act, grad_hidden, back_parts = feed_results[0], feed_results[1], feed_results[2:]
    back_near = [back_parts[0]] + [along_cols(back_parts[step], step) for step in col_steps]

    def feed_weights(
        spot_ref, a0, a1, a2, a3, given_ref, act_ref, grad_ref, weight_ref, mine_ref, give_ref, *outs
    ):
        at_core = spot_ref[2]
        low = jnp.concatenate([a0[...], a1[...], a2[...], a3[:toks]], axis=0)
        given = given_ref[...].reshape(cols_axis * toks, model)
        rows = cols_axis * toks
        acts = act_ref[...].reshape(rows, hidden)
        grads = grad_ref[...].reshape(rows, hidden)
        for step in range(cols_axis):
            outs[step][...] = dot(act_ref[step], weight_ref[1]).astype(bf16)
        for ref, at in ((mine_ref, at_core), (give_ref, 1 - at_core)):
            ref[:model] = dot_tokens(low, half_of(grads, at, half)).astype(bf16)
            ref[model:] = dot_tokens(acts, half_of(given, at, half)).astype(bf16)

    feed_grads = kernel_call(
        feed_weights,
        [((2 * model, half), bf16)] * 2 + [((toks, model), bf16)] * cols_axis,
        [spot, *low_near, given_all, act, grad_hidden, weights_feed],
        smem=(0,),
        flops=6.0 * toks * cols_axis * model * hidden,
        moved=16 << 20,
        room=24,
    )
    feed_mine, feed_give, out_parts = feed_grads[0], feed_grads[1], feed_grads[2:]

    block = 2 * shard
    extra = 2 * lines

    def renew(total, at):
        line = total[at : at + 1]
        whole = line[:, 0:1] + line[:, 1:2]
        high = whole.astype(bf16).astype(f32)
        lanes = lax.broadcasted_iota(jnp.int32, total.shape, 1)
        rows = lax.broadcasted_iota(jnp.int32, total.shape, 0)
        total = jnp.where((rows == at) & (lanes == 0), high, total)
        return jnp.where((rows == at) & (lanes == 1), whole - high, total)

    def layer_grads(low, mix, low_far, mix_far, mine, got, more):
        rows = model + (extra if len(more) == 1 else 2 * toks)

        def weight_sums(spot_ref, low_ref, mix_ref, low2_ref, mix2_ref, mine_ref, got_ref, *refs):
            more_refs, outs = refs[: len(more)], refs[len(more) : -2]
            left_ref, right_ref = refs[-2:]
            left_ref[0, :toks] = low_ref[...]
            left_ref[0, toks:] = low2_ref[...]
            left_ref[1, :toks] = mix_ref[...]
            left_ref[1, toks:] = mix2_ref[...]
            right_ref[:, :toks] = mine_ref[...]
            right_ref[:, toks:] = got_ref[...]
            for step in range(cols_axis):
                matrix = spot_ref[0] ^ step
                left = left_ref[matrix // 3]
                outs[step][:model] = dot_tokens(left, right_ref[matrix]).astype(bf16)
                if len(more) == 1:
                    sums_ref = more_refs[0]
                    tail = jnp.concatenate([sums_ref[:, :half], sums_ref[:, half:]], axis=0)
                    outs[step][model:] = renew(tail, 6).astype(bf16)
                else:
                    outs[step][model : model + toks] = more_refs[step][:, :half]
                    outs[step][model + toks :] = more_refs[step][:, half:]

        return kernel_call(
            weight_sums,
            [((rows, half), bf16)] * cols_axis,
            [spot, low, mix, low_far, mix_far, mine, got, *more],
            smem=(0,),
            scratch=[
                pltpu.VMEM((2, 2 * toks, model), bf16),
                pltpu.VMEM((4, 2 * toks, half), bf16),
            ],
        )

    def split_chips(items, count, tail, stream=None, slots=()):
        slot_rows_out = 2 * width * ((stream is not None) + bool(slots))

        def chip_parts(spot_ref, *refs):
            ins, outs, total_ref = refs[: len(items)], refs[-chips - 1 : -1], refs[-1]
            more = refs[len(items) : -chips - 1]
            total = ins[0][...].astype(f32)
            for ref in ins[1:]:
                total = total + ref[...].astype(f32)
            total_ref[...] = total.astype(bf16)
            if stream is not None:
                result = more[0][...] + jnp.concatenate(
                    [total[model : model + toks], total[model + toks :]], axis=1
                )
            for hop in range(chips):
                at = pl.multiple_of((spot_ref[1] ^ hop) * block, block)
                for index in range(count):
                    outs[hop][index * block : (index + 1) * block] = total_ref[
                        pl.ds(index * model + at, block)
                    ]
                row = count * block
                if tail:
                    outs[hop][row : row + tail] = renew(total[count * model :], 6).astype(bf16)
                    row = row + tail
                sent = []
                if stream is not None:
                    sent.append(result[slot_rows(hop)].astype(bf16))
                if slots:
                    sent.append(more[hop - chips][...])
                for slot in sent:
                    outs[hop][row : row + width] = slot[:, :half]
                    outs[hop][row + width : row + 2 * width] = slot[:, half:]
                    row = row + 2 * width

        size = count * block + tail + slot_rows_out
        return kernel_call(
            chip_parts,
            [((size, half), bf16)] * chips,
            [spot, *items] + ([] if stream is None else [stream]) + list(slots),
            smem=(0,),
            scratch=[pltpu.VMEM(items[0].shape, bf16)],
        )

    def split_cores(items, count, tail):
        rows_in = count * block + tail

        def core_parts(spot_ref, *refs):
            ins, (keep_ref, give_ref, total_ref) = refs[: len(items)], refs[len(items) :]
            total = ins[0][:rows_in].astype(f32)
            for ref in ins[1:]:
                total = total + ref[:rows_in].astype(f32)
            total_ref[...] = total.astype(bf16)
            for ref, at in ((keep_ref, spot_ref[2]), (give_ref, 1 - spot_ref[2])):
                for index in range(count):
                    row = pl.multiple_of(index * block + at * shard, shard)
                    ref[index * shard : (index + 1) * shard] = total_ref[pl.ds(row, shard)]
                if tail:
                    ref[count * shard :] = renew(total[count * block :], 6).astype(bf16)

        size = count * shard + tail
        return kernel_call(
            core_parts,
            [((size, half), bf16)] * 2,
            [spot, *items],
            smem=(0,),
            scratch=[pltpu.VMEM((rows_in, half), bf16)],
        )

    def over_chips(parts):
        return [parts[0]] + [along_chips(parts[step], step) for step in steps]

    back_near = after(back_near, feed_mine)

    def attend_col_back(
        spot_ref,
        b0,
        b1,
        b2,
        b3,
        given_ref,
        two_ref,
        norm_ref,
        weight_ref,
        q_ref,
        k_ref,
        v_ref,
        k2_ref,
        v2_ref,
        probs_ref,
        dtwo_ref,
        low_ref,
        dq_ref,
        dkv_ref,
        send_ref,
        sums_ref,
        wide_ref,
    ):
        lane_heads = head_of_lane(model)
        back = b0[...].astype(f32) + b1[...].astype(f32) + b2[...].astype(f32) + b3[...].astype(f32)
        unit, scale = unit_norm(two_ref[...])
        sums_ref[...] = norm_sums(back, unit)
        dtwo = given_ref[0].astype(f32) + unit_norm_back(back, unit, scale, norm_ref[4:5])
        dtwo_ref[...] = dtwo
        low = dtwo.astype(bf16)
        low_ref[...] = low
        dmix = dot_back(low, weight_ref[...]).astype(bf16).astype(f32)
        wide_ref[...] = jnp.zeros_like(wide_ref)
        sides = ((k_ref, v_ref), (k2_ref, v2_ref))
        for slot in range(chips):
            dout = dmix[slot_rows(slot)]
            query = q_ref[slot_rows(slot)].astype(f32)
            products = jnp.concatenate(
                [
                    dout * sides[s // chips][1][slot_rows(s % chips)].astype(f32)
                    for s in range(seqs)
                ],
                axis=0,
            )
            found = per_head_sum(products, lane_heads)
            weights = probs_ref[slot]
            mean = None
            for s in range(seqs):
                rows = slice(s * width, (s + 1) * width)
                term = weights[rows] * found[rows]
                mean = term if mean is None else mean + term
            dscores = (weights * (found - jnp.concatenate([mean] * seqs, axis=0))).astype(bf16)
            wide_d = dot_back(dscores, lane_heads)
            wide_p = dot_back(weights.astype(bf16), lane_heads)
            dquery = None
            for s in range(seqs):
                rows = slice(s * width, (s + 1) * width)
                term = wide_d[rows] * sides[s // chips][0][slot_rows(s % chips)].astype(f32)
                dquery = term if dquery is None else dquery + term
                wide_ref[0, rows] += wide_d[rows] * query
                wide_ref[1, rows] += wide_p[rows] * dout
            dq_ref[slot_rows(slot)] = (dquery * col_scale).astype(bf16)
        dkv_ref[0] = wide_ref[0, :toks] * col_scale
        dkv_ref[1] = wide_ref[1, :toks]
        send_ref[0] = (wide_ref[0, toks:] * col_scale).astype(bf16)
        send_ref[1] = wide_ref[1, toks:].astype(bf16)

    grad_two, grad_two_low, col_dq, col_dkv, col_send, sums_three = kernel_call(
        attend_col_back,
        [
            ((toks, model), f32),
            ((toks, model), bf16),
            ((toks, model), bf16),
            ((2, toks, model), f32),
            ((2, toks, model), bf16),
            ((2, model), f32),
        ],
        [
            spot,
            *back_near,
            given_all,
            stream_two,
            norm_rows,
            weights_last,
            col_q,
            col_k,
            col_v,
            k_other,
            v_other,
            col_probs,
        ],
        smem=(0,),
        scratch=[pltpu.VMEM((2, 2 * toks, model), f32)],
    )
    row_low_far, row_mix_far = along_core(normed_one), along_core(row_mix)
    col_low_far, col_mix_far = along_core(normed_two), along_core(col_mix)
    dkv_got = after(along_core(col_send), row_low_far, row_mix_far)

    def row_entry_back(
        spot_ref,
        dq_ref,
        dkv_ref,
        got_ref,
        low_two_ref,
        dtwo_ref,
        one_ref,
        norm_ref,
        col_ref,
        row_ref,
        near_ref,
        left_ref,
        right_ref,
        mine_ref,
        give_ref,
        done_ref,
        low_ref,
        dmix_ref,
        dprobs_ref,
        sums_ref,
    ):
        at_core = spot_ref[2]
        dq = dq_ref[...]
        dk = (dkv_ref[0] + got_ref[0].astype(f32)).astype(bf16)
        dv = (dkv_ref[1] + got_ref[1].astype(f32)).astype(bf16)
        for index, item in enumerate((dq, dk, dv, low_two_ref[...])):
            mine_ref[index] = half_of(item, at_core, half)
            give_ref[index] = half_of(item, 1 - at_core, half)
        back = dot_back(dq, col_ref[0]) + dot_back(dk, col_ref[1]) + dot_back(dv, col_ref[2])
        unit, scale = unit_norm(one_ref[...])
        sums_ref[...] = norm_sums(back, unit)
        done = dtwo_ref[...] + unit_norm_back(back, unit, scale, norm_ref[2:3])
        done_ref[...] = done
        low = done.astype(bf16)
        low_ref[...] = low
        dmix = dot_back(low, row_ref[...]).astype(bf16)
        dmix_ref[...] = dmix
        mask = head_mask(width, model)
        total = None
        for slot in range(chips):
            values = window_rows(spot_ref, near_ref, left_ref, right_ref, 1, slot, width)
            term = dot_back(spread_heads(dmix[slot_rows(slot)], mask), values)
            total = term if total is None else total + term
        dprobs_ref[...] = total

    (
        col_mine,
        col_give,
        grad_one,
        grad_one_low,
        row_dmix,
        dprobs,
        sums_two,
    ) = kernel_call(
        row_entry_back,
        [
            ((4, toks, half), bf16),
            ((4, toks, half), bf16),
            ((toks, model), f32),
            ((toks, model), bf16),
            ((toks, model), bf16),
            ((fold, span), f32),
            ((2, model), f32),
        ],
        [
            spot,
            col_dq,
            col_dkv,
            dkv_got,
            grad_two_low,
            grad_two,
            stream_one,
            norm_rows,
            weights_three,
            weights_out,
            row_kv,
            kv_left,
            kv_right,
        ],
        smem=(0,),
    )
    dprobs_other = along_core(dprobs)

    def attend_row_back(
        spot_ref,
        weight_ref,
        dprobs_ref,
        other_ref,
        scores_ref,
        probs_ref,
        q_ref,
        near_ref,
        left_ref,
        right_ref,
        dmix_ref,
        dq_ref,
        dkv_ref,
        to_left_ref,
        to_right_ref,
    ):
        mask = head_mask(width, model)
        dprob = dprobs_ref[...] + other_ref[...]
        probs_here, scores_here = probs_ref[...], scores_ref[...]
        rows = lax.broadcasted_iota(jnp.int32, (fold, 1), 0) % width
        weight = jnp.where(rows + spot_ref[3] * width < spot_ref[4], entropy_weight / (HEADS * weight_ref[6:7, 0:1]), 0.0)
        first = dprob - jnp.sum(probs_here * dprob, axis=-1, keepdims=True)
        second = scores_here - jnp.sum(probs_here * scores_here, axis=-1, keepdims=True)
        dscores = (probs_here * (first - weight * second)).astype(bf16)
        low_probs = probs_here.astype(bf16)
        for slot in range(chips):
            at = slot_rows(slot)
            keys = window_rows(spot_ref, near_ref, left_ref, right_ref, 0, slot, width)
            dq_ref[at] = (
                fold_heads(dot(dscores, keys), mask, width) * row_scale
            ).astype(bf16)
            dkeys = dot_tokens(dscores, spread_heads(q_ref[at], mask)) * row_scale
            dvalues = dot_tokens(low_probs, spread_heads(dmix_ref[at], mask))
            for index, item in enumerate((dkeys, dvalues)):
                to_left_ref[index, at] = item[:width].astype(bf16)
                dkv_ref[index, at] = item[width : 2 * width]
                to_right_ref[index, at] = item[2 * width :].astype(bf16)

    row_dq, row_dkv, edge_left, edge_right = kernel_call(
        attend_row_back,
        [
            ((toks, model), bf16),
            ((2, toks, model), f32),
            ((2, toks, model), bf16),
            ((2, toks, model), bf16),
        ],
        [
            spot,
            norm_rows,
            dprobs,
            dprobs_other,
            scores,
            probs,
            row_q,
            row_kv,
            kv_left,
            kv_right,
            row_dmix,
        ],
        smem=(0,),
    )
    col_sums = layer_grads(
        normed_two,
        col_mix,
        col_low_far,
        col_mix_far,
        col_mine,
        after(along_core(col_give), edge_left),
        out_parts,
    )
    edge_from_right = to_left(edge_left)
    edge_from_left = to_right(edge_right)
    feed_slices = split_chips([feed_mine, along_core(after(feed_give, edge_left))], 2, 0)
    feed_keep, feed_swap = split_cores(over_chips(feed_slices), 2, 0)

    def input_back(
        spot_ref,
        dq_ref,
        dkv_ref,
        from_right_ref,
        from_left_ref,
        low_one_ref,
        done_ref,
        zero_ref,
        norm_ref,
        row_ref,
        two_ref,
        three_ref,
        entropy_ref,
        mine_ref,
        give_ref,
        sums_ref,
        *slot_refs,
    ):
        at_core = spot_ref[2]
        dq = dq_ref[...]
        dk, dv = (
            jnp.concatenate(
                [
                    (
                        dkv_ref[index, slot_rows(slot)]
                        + from_left_ref[index, slot_span(spot_ref, 5, slot, width)].astype(f32)
                        + from_right_ref[index, slot_span(spot_ref, 6, slot, width)].astype(f32)
                    ).astype(bf16)
                    for slot in range(chips)
                ],
                axis=0,
            )
            for index in (0, 1)
        )
        for index, item in enumerate((dq, dk, dv, low_one_ref[...])):
            mine_ref[index] = half_of(item, at_core, half)
            give_ref[index] = half_of(item, 1 - at_core, half)
        back = dot_back(dq, row_ref[0]) + dot_back(dk, row_ref[1]) + dot_back(dv, row_ref[2])
        unit, scale = unit_norm(zero_ref[...])
        sums_ref[0:2] = norm_sums(back, unit)
        sums_ref[2:4] = two_ref[...]
        sums_ref[4:6] = three_ref[...]
        sums_ref[6:7] = entropy_ref[...]
        sums_ref[7:8] = jnp.zeros((1, model), f32)
        result = (done_ref[...] + unit_norm_back(back, unit, scale, norm_ref[0:1])).astype(bf16)
        for slot in range(chips):
            slot_refs[slot][...] = result[slot_rows(slot)]

    row_mine, row_give, sums, *grad_slots = kernel_call(
        input_back,
        [
            ((4, toks, half), bf16),
            ((4, toks, half), bf16),
            ((lines, model), f32),
        ]
        + [((width, model), bf16)] * chips,
        [
            spot,
            row_dq,
            row_dkv,
            edge_from_right,
            edge_from_left,
            grad_one_low,
            grad_one,
            stream_zero,
            norm_rows,
            weights_row,
            sums_two,
            sums_three,
            entropy_row,
        ],
        smem=(0,),
    )

    def join_halves(spot_ref, keep_rows, got_rows):
        first = spot_ref[2] == 0
        return jnp.concatenate(
            [jnp.where(first, keep_rows, got_rows), jnp.where(first, got_rows, keep_rows)], axis=1
        )

    def over_cols(whole):
        return [whole] + [along_cols(whole, step) for step in col_steps]

    def order_rows(slices, at):
        def order_slots(spot_ref, *refs):
            for hop, ref in enumerate(refs[:-1]):
                refs[-1][0, chunk_at(spot_ref, spot_ref[1] ^ hop)] = jnp.concatenate(
                    [ref[at : at + width], ref[at + width : at + 2 * width]], axis=1
                )

        return kernel_call(order_slots, [(tokens.shape, bf16)], [spot, *slices], smem=(0,))[0]

    feed_back = along_core(feed_swap)
    col_parts = [col_sums[0]] + [along_cols(col_sums[step], step) for step in col_steps]
    col_slices = split_chips(col_parts, 1, 0, stream=stream_two, slots=grad_slots)
    col_reached = over_chips(col_slices)
    col_keep, col_swap = split_cores(col_reached, 1, 0)

    def join_two(spot_ref, keep_ref, got_ref, keep2_ref, got2_ref, out_ref):
        rows = 2 * shard
        out_ref[:rows] = join_halves(spot_ref, keep_ref[...], got_ref[...])
        out_ref[rows:] = join_halves(spot_ref, keep2_ref[...], got2_ref[...])

    (pair,) = kernel_call(
        join_two,
        [((3 * shard, model), bf16)],
        [spot, feed_keep, feed_back, col_keep, along_core(col_swap)],
        smem=(0,),
    )
    pair_ends = over_cols(pair)

    def spread_pair(spot_ref, u0, u1, u2, u3, in_ref, out_ref, g0, g1, g2, g3, all_ref):
        for step, ref in enumerate((u0, u1, u2, u3)):
            all_ref[spot_ref[0] ^ step] = ref[...]
        for source, grad_ref in enumerate((g0, g1, g2, g3)):
            wide = all_ref[source, :shard].astype(f32)
            for index in range(seqs):
                at = index * block_cols + source * part
                in_ref[:, at : at + part] = wide[:, index * part : (index + 1) * part]
            out_ref[source * part : (source + 1) * part] = all_ref[
                source, shard : 2 * shard
            ].astype(f32)
            grad_ref[...] = all_ref[source, 2 * shard :].astype(f32)

    row_parts = layer_grads(
        normed_one,
        row_mix,
        row_low_far,
        row_mix_far,
        row_mine,
        along_core(row_give),
        [sums],
    )
    row_sends = after(row_parts, col_parts, feed_keep)
    row_parts = [row_parts[0]] + [along_cols(row_sends[step], step) for step in col_steps]
    row_slices = split_chips(row_parts, 1, extra)
    row_reached = over_chips(row_slices)
    row_keep, row_swap = split_cores(row_reached, 1, extra)

    def join_row(spot_ref, keep_ref, got_ref, out_ref, norm_ref, entropy_ref):
        out_ref[...] = join_halves(spot_ref, keep_ref[:shard], got_ref[:shard])
        total = keep_ref[shard:].astype(f32) + got_ref[shard:].astype(f32)
        line = total[6:7]
        entropy_ref[...] = line[:, 0:1] + line[:, 1:2]
        wide = jnp.concatenate([total[:lines], total[lines:]], axis=1)
        at = spot_ref[1] * 2 + spot_ref[2]
        found = wide[:, :shard]
        for index in range(1, seqs):
            here = wide[:, index * shard : (index + 1) * shard]
            found = jnp.where(at == index, here, found)
        norm_ref[...] = found

    row_join, norm_here, entropy_sum = kernel_call(
        join_row,
        [((shard, model), bf16), ((lines, shard), f32), ((1, 1), f32)],
        [spot, row_keep, along_core(row_swap)],
        smem=(0,),
    )
    row_ends = over_cols(after(row_join, pair_ends))
    result = order_rows(after(col_reached, row_join), block)
    grad_in = order_rows(after(col_reached, row_join), block + 2 * width)
    grad_feed_in, grad_feed_out, *col_grads = kernel_call(
        spread_pair,
        [(feed_in.shape, f32), (feed_out.shape, f32)] + [((shard, model), f32)] * cols_axis,
        [spot, *after(pair_ends, row_join)],
        smem=(0,),
        scratch=[pltpu.VMEM((cols_axis, 3 * shard, model), bf16)],
        room=24,
    )

    def spread_row(spot_ref, *refs):
        ins, outs, all_ref = refs[:cols_axis], refs[cols_axis:-1], refs[-1]
        for step, ref in enumerate(ins):
            all_ref[spot_ref[0] ^ step] = ref[...]
        for matrix in range(cols_axis):
            outs[matrix][...] = all_ref[matrix].astype(f32)

    row_grads = kernel_call(
        spread_row,
        [((shard, model), f32)] * cols_axis,
        [spot, *row_ends],
        smem=(0,),
        scratch=[pltpu.VMEM((cols_axis, shard, model), bf16)],
    )
    entropy = entropy_sum[0, 0] / (HEADS * norm_rows[6, 0])

    return (
        result,
        entropy,
        grad_in,
        *[norm_here[index] for index in range(6)],
        *row_grads,
        *col_grads,
        grad_feed_in,
        grad_feed_out,
    )


def fits_fast(tokens, feed_out):
    chips = lax.axis_size("seq") // 2
    return (
        lax.axis_size("col") == 4
        and lax.axis_size("seq") == 8
        and tokens.shape[0] == 1
        and tokens.shape[1] == chips * WINDOW
        and tokens.shape[2] == HEADS * HEAD_DIM
        and feed_out.shape[0] * 2 == tokens.shape[2]
    )


def on_device(tokens, offsets, band, col_counts, *rest):
    if not fits_fast(tokens, rest[15]):
        return general_plan(tokens, offsets, band, col_counts, *rest)
    return fast_plan(
        tokens,
        offsets,
        band,
        col_counts,
        rest[0:6],
        rest[6:10],
        rest[10:14],
        rest[14],
        rest[15],
        rest[16],
    )


def solution(mesh):
    return jax.shard_map(
        on_device,
        mesh=mesh,
        in_specs=(
            P("seq", "col", None),
            P(),
            P("col", None),
            P("col"),
            P("seq"),
            P("seq"),
            P("seq"),
            P("seq"),
            P("seq"),
            P("seq"),
            P("seq", None),
            P("seq", None),
            P("seq", None),
            P("seq", None),
            P("seq", None),
            P("seq", None),
            P("seq", None),
            P("seq", None),
            P("seq", None),
            P("seq", None),
            P("seq", "col", None),
        ),
        out_specs=(
            P("seq", "col", None),
            P(),
            P("seq", "col", None),
            P("seq"),
            P("seq"),
            P("seq"),
            P("seq"),
            P("seq"),
            P("seq"),
            P("seq", None),
            P("seq", None),
            P("seq", None),
            P("seq", None),
            P("seq", None),
            P("seq", None),
            P("seq", None),
            P("seq", None),
            P("seq", None),
            P("seq", None),
        ),
        check_vma=False,
    )
```

```python
from functools import partial
import math

import jax
import jax.numpy as jnp
from jax import lax
from jax.experimental import pallas as pl
from jax.experimental.pallas import tpu as pltpu
from jax.sharding import PartitionSpec as P

HEADS = 12
HEAD_DIM = 64
WINDOW = 32


entropy_weight = 8192.0
norm_eps = 1e-05


def with_halo(cells, sides, width):
    for axis, dim in sides:
        count = lax.axis_size(axis)
        ends = count - 1
        head = lax.slice_in_dim(cells, 0, width, axis=dim)
        tail = lax.slice_in_dim(cells, cells.shape[dim] - width, cells.shape[dim], axis=dim)
        cells = jnp.concatenate(
            [
                lax.ppermute(tail, axis, [(i, (i + 1) % count) for i in range(ends)]),
                cells,
                lax.ppermute(head, axis, [((i + 1) % count, i) for i in range(ends)]),
            ],
            axis=dim,
        )
    return cells


def layer_norm(inputs, norm_gain, norm_shift):
    average = jnp.mean(inputs, axis=-1, keepdims=True)
    centred = inputs - average
    variance = jnp.mean(centred * centred, axis=-1, keepdims=True)
    return centred * lax.rsqrt(variance + norm_eps) * norm_gain + norm_shift


def position_table(offsets, row_first, col_first, row_count, col_count, model_width):
    half_width = model_width // 2
    frequency = jnp.exp(-math.log(1000.0) * jnp.arange(half_width, dtype=jnp.float32) / half_width)
    col_place = (jnp.arange(col_count, dtype=jnp.int32) + col_first + offsets[1]).astype(
        jnp.float32
    )
    row_place = (jnp.arange(row_count, dtype=jnp.int32) + row_first + offsets[0]).astype(
        jnp.float32
    )
    col_wave = jnp.sin(col_place[:, None] * frequency[None, :])
    row_wave = jnp.sin(row_place[:, None] * frequency[None, :])
    col_full = jnp.broadcast_to(col_wave[None, :, :], (row_count, col_count, half_width))
    row_full = jnp.broadcast_to(row_wave[:, None, :], (row_count, col_count, half_width))
    return 0.5 * jnp.concatenate([col_full, row_full], axis=-1)


def softmax_entropy(scores, allowed, valid):
    masked = jnp.where(allowed[None], scores, -1000000000.0)
    largest = jnp.max(masked, axis=-1, keepdims=True)
    powers = jnp.exp(masked - largest)
    row_total = jnp.sum(powers, axis=-1, keepdims=True)
    probs_out = powers / row_total
    log_total = largest[..., 0] + jnp.log(row_total[..., 0])
    entropies = log_total - jnp.sum(probs_out * jnp.where(allowed[None], scores, 0.0), axis=-1)
    return (probs_out, jnp.sum(entropies * valid[None, :]))


def plain_softmax(scores):
    largest = jnp.max(scores, axis=-1, keepdims=True)
    powers = jnp.exp(scores - largest)
    return powers / jnp.sum(powers, axis=-1, keepdims=True)


def project(activations, weight):
    return jnp.einsum("rci,ij->rcj", activations, weight, preferred_element_type=jnp.float32)


def project_back(gradient, weight):
    return jnp.einsum("rcj,ij->rci", gradient, weight, preferred_element_type=jnp.float32)


def weight_grad(activations, gradient):
    return jnp.einsum("rci,rcj->ij", activations, gradient, preferred_element_type=jnp.float32)


def general_plan(
    tokens,
    offsets,
    band,
    col_counts,
    norm1_gain,
    norm1_shift,
    norm2_gain,
    norm2_shift,
    norm3_gain,
    norm3_shift,
    row_query,
    row_key,
    row_value,
    row_output,
    col_query,
    col_key,
    col_value,
    col_output,
    feed_in,
    feed_out,
    cotangent,
):
    rows_dev, cols_dev, model_width = tokens.shape
    total_rows = rows_dev * lax.axis_size("seq")
    total_cols = cols_dev * lax.axis_size("col")
    row_first = lax.axis_index("seq") * rows_dev
    col_first = lax.axis_index("col") * cols_dev
    count_here = col_counts[0].astype(jnp.float32)
    count_early = lax.psum(count_here, "col")
    params = (
        lax.all_gather(norm1_gain, "seq", axis=0, tiled=True),
        lax.all_gather(norm1_shift, "seq", axis=0, tiled=True),
        lax.all_gather(norm2_gain, "seq", axis=0, tiled=True),
        lax.all_gather(norm2_shift, "seq", axis=0, tiled=True),
        lax.all_gather(norm3_gain, "seq", axis=0, tiled=True),
        lax.all_gather(norm3_shift, "seq", axis=0, tiled=True),
        lax.all_gather(row_query, "seq", axis=0, tiled=True),
        lax.all_gather(row_key, "seq", axis=0, tiled=True),
        lax.all_gather(row_value, "seq", axis=0, tiled=True),
        lax.all_gather(row_output, "seq", axis=0, tiled=True),
        lax.all_gather(col_query, "seq", axis=0, tiled=True),
        lax.all_gather(col_key, "seq", axis=0, tiled=True),
        lax.all_gather(col_value, "seq", axis=0, tiled=True),
        lax.all_gather(col_output, "seq", axis=0, tiled=True),
        lax.all_gather(feed_in, "seq", axis=0, tiled=True),
        lax.all_gather(feed_out, "seq", axis=0, tiled=True),
    )
    gain_one = params[0].astype(jnp.float32)
    shift_one = params[1].astype(jnp.float32)
    gain_two = params[2].astype(jnp.float32)
    shift_two = params[3].astype(jnp.float32)
    gain_three = params[4].astype(jnp.float32)
    shift_three = params[5].astype(jnp.float32)
    query_row, key_row, value_row, output_row = (params[6], params[7], params[8], params[9])
    query_col, key_col, value_col, output_col = (params[10], params[11], params[12], params[13])
    feed_up, feed_down = (params[14], params[15])
    stream_zero = tokens.astype(jnp.float32) + position_table(
        offsets, row_first, col_first, rows_dev, cols_dev, model_width
    )
    normed_one, norm_back_one = jax.vjp(layer_norm, stream_zero, gain_one, shift_one)
    normed_one = normed_one.astype(jnp.bfloat16)
    row_queries = project(normed_one, query_row).astype(jnp.bfloat16)
    row_keys = project(normed_one, key_row).astype(jnp.bfloat16)
    row_values = project(normed_one, value_row).astype(jnp.bfloat16)
    extended = with_halo(jnp.stack([row_keys, row_values]), (("col", 2),), WINDOW)
    ext_cols = cols_dev + 2 * WINDOW
    queries_heads = row_queries.reshape(rows_dev, cols_dev, HEADS, HEAD_DIM)
    keys_ext = extended[0].reshape(rows_dev, ext_cols, HEADS, HEAD_DIM)
    values_ext = extended[1].reshape(rows_dev, ext_cols, HEADS, HEAD_DIM)
    partial_logits = jnp.einsum(
        "rchd,rehd->hce", queries_heads, keys_ext, preferred_element_type=jnp.float32
    )
    row_scale = 1.0 / math.sqrt(HEAD_DIM * total_rows)
    row_scores = lax.psum(partial_logits, "seq") * row_scale
    query_index = jnp.arange(cols_dev, dtype=jnp.int32)[:, None]
    key_index = jnp.arange(ext_cols, dtype=jnp.int32)[None, :]
    distance = key_index - query_index
    choose = jnp.arange(2 * WINDOW + 1, dtype=jnp.int32)
    matches = (distance[:, None, :] == choose[None, :, None]) & (band[:, :, None] == 1)
    key_global = col_first - WINDOW + key_index
    inside = (key_global >= 0) & (key_global < total_cols)
    allowed = (jnp.any(matches, axis=1) | (distance == WINDOW)) & inside
    valid = (jnp.arange(cols_dev, dtype=jnp.int32) < col_counts[0]).astype(jnp.float32)
    (row_probs, ent_part), ent_back = jax.vjp(
        lambda given: softmax_entropy(given, allowed, valid), row_scores
    )
    payload = ent_part[None]
    sums = lax.psum(payload, "col")
    entropy = sums[0] / (HEADS * count_early)
    row_probs_low = row_probs.astype(jnp.bfloat16)
    row_mix = jnp.einsum(
        "hce,rehd->rchd", row_probs_low, values_ext, preferred_element_type=jnp.float32
    )
    row_mix = row_mix.reshape(rows_dev, cols_dev, model_width).astype(jnp.bfloat16)
    stream_one = stream_zero + project(row_mix, output_row)
    normed_two, norm_back_two = jax.vjp(layer_norm, stream_one, gain_two, shift_two)
    normed_two = normed_two.astype(jnp.bfloat16)
    col_queries = project(normed_two, query_col).astype(jnp.bfloat16)
    col_keys = project(normed_two, key_col).astype(jnp.bfloat16)
    col_values = project(normed_two, value_col).astype(jnp.bfloat16)
    col_scale = 1.0 / math.sqrt(HEAD_DIM)
    keys_all, values_all = (
        lax.all_gather(col_keys, "seq", axis=0, tiled=True),
        lax.all_gather(col_values, "seq", axis=0, tiled=True),
    )
    col_heads_q = col_queries.reshape(rows_dev, cols_dev, HEADS, HEAD_DIM)
    keys_heads = keys_all.reshape(total_rows, cols_dev, HEADS, HEAD_DIM)
    values_heads = values_all.reshape(total_rows, cols_dev, HEADS, HEAD_DIM)
    col_raw = jnp.einsum(
        "rchd,schd->chrs", col_heads_q, keys_heads, preferred_element_type=jnp.float32
    )
    col_probs = plain_softmax(col_raw * col_scale)
    col_probs_low = col_probs.astype(jnp.bfloat16)
    col_mix = jnp.einsum(
        "chrs,schd->rchd", col_probs_low, values_heads, preferred_element_type=jnp.float32
    )
    col_mix = col_mix.reshape(rows_dev, cols_dev, model_width).astype(jnp.bfloat16)
    stream_two = stream_one + project(col_mix, output_col)
    normed_three, norm_back_three = jax.vjp(layer_norm, stream_two, gain_three, shift_three)
    normed_three = normed_three.astype(jnp.bfloat16)
    hidden_pre = project(normed_three, feed_up)
    hidden_act, gelu_back = jax.vjp(partial(jax.nn.gelu, approximate=False), hidden_pre)
    hidden_low = hidden_act.astype(jnp.bfloat16)
    output = (stream_two + project(hidden_low, feed_down)).astype(jnp.bfloat16)
    grad_feed_down = weight_grad(hidden_low, cotangent)
    grad_hidden = gelu_back(project_back(cotangent, feed_down))[0].astype(jnp.bfloat16)
    grad_feed_up = weight_grad(normed_three, grad_hidden)
    back_stream, grad_gain_three, grad_shift_three = norm_back_three(
        project_back(grad_hidden, feed_up)
    )
    grad_two = cotangent.astype(jnp.float32) + back_stream
    grad_two_low = grad_two.astype(jnp.bfloat16)
    grad_output_col = weight_grad(col_mix, grad_two_low)
    grad_mix_flat = project_back(grad_two_low, output_col).astype(jnp.bfloat16)
    grad_col_mix = grad_mix_flat.reshape(rows_dev, cols_dev, HEADS, HEAD_DIM)
    col_dprobs = jnp.einsum(
        "rchd,schd->chrs", grad_col_mix, values_heads, preferred_element_type=jnp.float32
    )
    col_dscores = col_probs * (col_dprobs - jnp.sum(col_probs * col_dprobs, axis=-1, keepdims=True))
    col_dscores = col_dscores.astype(jnp.bfloat16)
    grad_col_q = (
        jnp.einsum("chrs,schd->rchd", col_dscores, keys_heads, preferred_element_type=jnp.float32)
        * col_scale
    )
    grad_col_q = grad_col_q.reshape(rows_dev, cols_dev, model_width).astype(jnp.bfloat16)
    row_count = lax.axis_size("seq") * rows_dev
    key_part = (
        jnp.einsum("chrs,rchd->schd", col_dscores, col_heads_q, preferred_element_type=jnp.float32)
        * col_scale
    )
    value_part = jnp.einsum(
        "chrs,rchd->schd", col_probs_low, grad_col_mix, preferred_element_type=jnp.float32
    )
    key_value_grads = lax.psum_scatter(
        jnp.concatenate(
            [
                key_part.reshape(row_count, cols_dev, model_width),
                value_part.reshape(row_count, cols_dev, model_width),
            ],
            axis=-1,
        ),
        "seq",
        scatter_dimension=0,
        tiled=True,
    )
    grad_col_k = key_value_grads[..., :model_width].astype(jnp.bfloat16)
    grad_col_v = key_value_grads[..., model_width:].astype(jnp.bfloat16)
    grad_query_col = weight_grad(normed_two, grad_col_q)
    grad_key_col = weight_grad(normed_two, grad_col_k)
    grad_value_col = weight_grad(normed_two, grad_col_v)
    back_input = (
        project_back(grad_col_q, query_col)
        + project_back(grad_col_k, key_col)
        + project_back(grad_col_v, value_col)
    )
    back_stream, grad_gain_two, grad_shift_two = norm_back_two(back_input)
    grad_one = grad_two + back_stream
    grad_one_low = grad_one.astype(jnp.bfloat16)
    grad_output_row = weight_grad(row_mix, grad_one_low)
    grad_row_mix = project_back(grad_one_low, output_row).astype(jnp.bfloat16)
    grad_row_mix = grad_row_mix.reshape(rows_dev, cols_dev, HEADS, HEAD_DIM)
    dprobs_part = jnp.einsum(
        "rchd,rehd->hce", grad_row_mix, values_ext, preferred_element_type=jnp.float32
    )
    row_dprobs = lax.psum(dprobs_part.astype(jnp.bfloat16), "seq").astype(jnp.float32)
    ent_cot = jnp.asarray(entropy_weight, dtype=jnp.float32) / (HEADS * count_early)
    row_dscores = ent_back((row_dprobs, ent_cot))[0].astype(jnp.bfloat16)
    grad_row_q = (
        jnp.einsum("hce,rehd->rchd", row_dscores, keys_ext, preferred_element_type=jnp.float32)
        * row_scale
    )
    grad_row_q = grad_row_q.reshape(rows_dev, cols_dev, model_width).astype(jnp.bfloat16)
    grad_keys_ext = (
        jnp.einsum("hce,rchd->rehd", row_dscores, queries_heads, preferred_element_type=jnp.float32)
        * row_scale
    )
    grad_values_ext = jnp.einsum(
        "hce,rchd->rehd", row_probs_low, grad_row_mix, preferred_element_type=jnp.float32
    )
    grad_ext = jnp.stack([grad_keys_ext, grad_values_ext]).reshape(
        2, rows_dev, ext_cols, model_width
    )
    rims = jnp.concatenate([grad_ext[:, :, :WINDOW], grad_ext[:, :, WINDOW + cols_dev :]], axis=2)
    returned = with_halo(rims.astype(jnp.bfloat16), (("col", 2),), WINDOW).astype(rims.dtype)
    interior = grad_ext[:, :, WINDOW : WINDOW + cols_dev]
    interior = interior.at[:, :, :WINDOW].add(returned[:, :, :WINDOW])
    interior = interior.at[:, :, cols_dev - WINDOW :].add(returned[:, :, 3 * WINDOW :])
    grad_row_k = interior[0].astype(jnp.bfloat16)
    grad_row_v = interior[1].astype(jnp.bfloat16)
    grad_query_row = weight_grad(normed_one, grad_row_q)
    grad_key_row = weight_grad(normed_one, grad_row_k)
    grad_value_row = weight_grad(normed_one, grad_row_v)
    back_input = (
        project_back(grad_row_q, query_row)
        + project_back(grad_row_k, key_row)
        + project_back(grad_row_v, value_row)
    )
    back_stream, grad_gain_one, grad_shift_one = norm_back_one(back_input)
    input_grad = (grad_one + back_stream).astype(jnp.bfloat16)
    shares = (
        lax.psum_scatter(
            grad_gain_one.astype(jnp.bfloat16), "seq", scatter_dimension=0, tiled=True
        ).astype(jnp.float32),
        lax.psum_scatter(
            grad_shift_one.astype(jnp.bfloat16), "seq", scatter_dimension=0, tiled=True
        ).astype(jnp.float32),
        lax.psum_scatter(
            grad_gain_two.astype(jnp.bfloat16), "seq", scatter_dimension=0, tiled=True
        ).astype(jnp.float32),
        lax.psum_scatter(
            grad_shift_two.astype(jnp.bfloat16), "seq", scatter_dimension=0, tiled=True
        ).astype(jnp.float32),
        lax.psum_scatter(
            grad_gain_three.astype(jnp.bfloat16), "seq", scatter_dimension=0, tiled=True
        ).astype(jnp.float32),
        lax.psum_scatter(
            grad_shift_three.astype(jnp.bfloat16), "seq", scatter_dimension=0, tiled=True
        ).astype(jnp.float32),
        lax.psum_scatter(
            grad_query_row.astype(jnp.bfloat16), "seq", scatter_dimension=0, tiled=True
        ).astype(jnp.float32),
        lax.psum_scatter(
            grad_key_row.astype(jnp.bfloat16), "seq", scatter_dimension=0, tiled=True
        ).astype(jnp.float32),
        lax.psum_scatter(
            grad_value_row.astype(jnp.bfloat16), "seq", scatter_dimension=0, tiled=True
        ).astype(jnp.float32),
        lax.psum_scatter(
            grad_output_row.astype(jnp.bfloat16), "seq", scatter_dimension=0, tiled=True
        ).astype(jnp.float32),
        lax.psum_scatter(
            grad_query_col.astype(jnp.bfloat16), "seq", scatter_dimension=0, tiled=True
        ).astype(jnp.float32),
        lax.psum_scatter(
            grad_key_col.astype(jnp.bfloat16), "seq", scatter_dimension=0, tiled=True
        ).astype(jnp.float32),
        lax.psum_scatter(
            grad_value_col.astype(jnp.bfloat16), "seq", scatter_dimension=0, tiled=True
        ).astype(jnp.float32),
        lax.psum_scatter(
            grad_output_col.astype(jnp.bfloat16), "seq", scatter_dimension=0, tiled=True
        ).astype(jnp.float32),
        lax.psum_scatter(
            grad_feed_up.astype(jnp.bfloat16), "seq", scatter_dimension=0, tiled=True
        ).astype(jnp.float32),
        lax.psum_scatter(
            grad_feed_down.astype(jnp.bfloat16), "seq", scatter_dimension=0, tiled=True
        ).astype(jnp.float32),
    )
    totals = (
        lax.psum(shares[0].astype(jnp.bfloat16), "col").astype(jnp.float32),
        lax.psum(shares[1].astype(jnp.bfloat16), "col").astype(jnp.float32),
        lax.psum(shares[2].astype(jnp.bfloat16), "col").astype(jnp.float32),
        lax.psum(shares[3].astype(jnp.bfloat16), "col").astype(jnp.float32),
        lax.psum(shares[4].astype(jnp.bfloat16), "col").astype(jnp.float32),
        lax.psum(shares[5].astype(jnp.bfloat16), "col").astype(jnp.float32),
        lax.psum(shares[6].astype(jnp.bfloat16), "col").astype(jnp.float32),
        lax.psum(shares[7].astype(jnp.bfloat16), "col").astype(jnp.float32),
        lax.psum(shares[8].astype(jnp.bfloat16), "col").astype(jnp.float32),
        lax.psum(shares[9].astype(jnp.bfloat16), "col").astype(jnp.float32),
        lax.psum(shares[10].astype(jnp.bfloat16), "col").astype(jnp.float32),
        lax.psum(shares[11].astype(jnp.bfloat16), "col").astype(jnp.float32),
        lax.psum(shares[12].astype(jnp.bfloat16), "col").astype(jnp.float32),
        lax.psum(shares[13].astype(jnp.bfloat16), "col").astype(jnp.float32),
        lax.psum(shares[14].astype(jnp.bfloat16), "col").astype(jnp.float32),
        lax.psum(shares[15].astype(jnp.bfloat16), "col").astype(jnp.float32),
    )
    return (
        output,
        entropy,
        input_grad,
        totals[0],
        totals[1],
        totals[2],
        totals[3],
        totals[4],
        totals[5],
        totals[6],
        totals[7],
        totals[8],
        totals[9],
        totals[10],
        totals[11],
        totals[12],
        totals[13],
        totals[14],
        totals[15],
    )


def after(values, *needed):
    return lax.optimization_barrier((values, needed))[0]


def kernel_call(
    body, outs, args, smem=(), scratch=(), flops=1, moved=1, stream=False, room=16
):
    out_shapes = [jax.ShapeDtypeStruct(shape, kind) for shape, kind in outs]

    def whole(item):
        if not stream:
            return pl.BlockSpec(memory_space=pltpu.VMEM)
        rank = len(item.shape)
        return pl.BlockSpec(item.shape, lambda step: (0,) * rank, pipeline_mode=pl.Buffered(1))

    return pl.pallas_call(
        body,
        grid=(1,) if stream else (),
        out_shape=out_shapes,
        in_specs=[
            pl.BlockSpec(memory_space=pltpu.SMEM) if place in smem else whole(item)
            for place, item in enumerate(args)
        ],
        out_specs=[whole(item) for item in out_shapes],
        scratch_shapes=list(scratch),
        compiler_params=pltpu.CompilerParams(vmem_limit_bytes=(56 if stream else room) << 20),
        cost_estimate=pl.CostEstimate(
            flops=int(flops), bytes_accessed=int(moved), transcendentals=0
        ),
        name=body.__name__,
    )(*args)


def dot(left, right):
    return jnp.dot(left, right, preferred_element_type=jnp.float32)


def dot_back(left, right):
    return lax.dot_general(
        left, right, (((1,), (1,)), ((), ())), preferred_element_type=jnp.float32
    )


def dot_tokens(left, right):
    return lax.dot_general(
        left, right, (((0,), (0,)), ((), ())), preferred_element_type=jnp.float32
    )


def unit_norm(inputs):
    centred = inputs - jnp.mean(inputs, axis=-1, keepdims=True)
    scale = lax.rsqrt(jnp.mean(centred * centred, axis=-1, keepdims=True) + norm_eps)
    return centred * scale, scale


def unit_norm_back(given, unit, scale, gain):
    scaled = given * gain
    first = jnp.mean(scaled, axis=-1, keepdims=True)
    second = jnp.mean(scaled * unit, axis=-1, keepdims=True)
    return scale * (scaled - first - unit * second)


def norm_sums(given, unit):
    return jnp.concatenate(
        [
            jnp.sum(given * unit, axis=0, keepdims=True),
            jnp.sum(given, axis=0, keepdims=True),
        ],
        axis=0,
    )


def head_mask(width, model_width):
    rows = lax.broadcasted_iota(jnp.int32, (HEADS * width, model_width), 0) // width
    lanes = lax.broadcasted_iota(jnp.int32, (HEADS * width, model_width), 1) // HEAD_DIM
    return rows == lanes


def spread_heads(block, mask):
    tiled = jnp.concatenate([block] * HEADS, axis=0)
    return jnp.where(mask, tiled, jnp.zeros_like(tiled))


def fold_heads(product, mask, width):
    kept = jnp.where(mask, product, 0.0)
    total = kept[:width]
    for head in range(1, HEADS):
        total = total + kept[head * width : (head + 1) * width]
    return total


def head_of_lane(model_width):
    rows = lax.broadcasted_iota(jnp.int32, (model_width, 128), 0) // HEAD_DIM
    lanes = lax.broadcasted_iota(jnp.int32, (model_width, 128), 1)
    return (rows == lanes).astype(jnp.bfloat16)


def per_head_sum(product, lane_heads):
    return dot(product.astype(jnp.bfloat16), lane_heads)


def slot_span(spot_ref, side, slot, width):
    return pl.ds(pl.multiple_of((slot ^ spot_ref[side]) * width, width), width)


def window_rows(spot_ref, near_ref, left_ref, right_ref, which, slot, width):
    return jnp.concatenate(
        [
            left_ref[which, slot_span(spot_ref, 5, slot, width)],
            near_ref[which, slot * width : (slot + 1) * width],
            right_ref[which, slot_span(spot_ref, 6, slot, width)],
        ],
        axis=0,
    )


def half_of(values, core, width):
    return jnp.where(core == 0, values[:, :width], values[:, width:])


def fast_plan(
    tokens,
    offsets,
    band,
    col_counts,
    norms,
    row_weights,
    col_weights,
    feed_in,
    feed_out,
    cotangent,
):
    f32, bf16 = jnp.float32, jnp.bfloat16
    cols_dev, model = tokens.shape[1:]
    cols_axis, seqs = lax.axis_size("col"), lax.axis_size("seq")
    chips = seqs // 2
    width = cols_dev // chips
    toks = chips * width
    shard = model // seqs
    half = model // 2
    hidden = feed_out.shape[0] * seqs // cols_axis
    fold = HEADS * width
    span = 3 * width
    col_at = lax.axis_index("col")
    seq_at = lax.axis_index("seq")
    chip, core = seq_at // 2, seq_at % 2
    flip = col_at % 2

    def chunk_of(chip_index):
        return jnp.where(flip == 0, chip_index, chips - 1 - chip_index)

    chunk = chunk_of(chip)
    piece = col_at * chips + chunk

    def along_chips(values, step):
        return lax.ppermute(values, "seq", [(i, i ^ (2 * step)) for i in range(seqs)])

    def along_core(values):
        return lax.ppermute(values, "seq", [(i, i ^ 1) for i in range(seqs)])

    def along_cols(values, step):
        return lax.ppermute(values, "col", [(i, i ^ step) for i in range(cols_axis)])

    def pair_cols(values):
        pairs = [
            (c * seqs + i, (c ^ (1 + i % 2)) * seqs + i)
            for c in range(cols_axis)
            for i in range(seqs)
        ]
        return lax.ppermute(values, ("col", "seq"), pairs)

    def pair_chips(values):
        pairs = [(i, (i // 2 ^ (1 + i % 2)) * 2 + i % 2) for i in range(seqs)]
        return lax.ppermute(values, "seq", pairs)

    def place_of(piece_index, core_index):
        block, part = divmod(piece_index, chips)
        chip_index = part if block % 2 == 0 else chips - 1 - part
        return block * seqs + chip_index * 2 + core_index

    rightward = [
        (place_of(i, k), place_of(i + 1, k)) for i in range(cols_axis * chips - 1) for k in (0, 1)
    ]
    leftward = [(target, source) for source, target in rightward]

    def to_right(values):
        return lax.ppermute(values, ("col", "seq"), rightward)

    def to_left(values):
        return lax.ppermute(values, ("col", "seq"), leftward)

    steps = range(1, chips)
    col_steps = range(1, cols_axis)

    def turn_to(other):
        block, rest = other // chips, other % chips
        return chip ^ jnp.where(block % 2 == 0, rest, chips - 1 - rest)

    to_left_turn = turn_to(jnp.maximum(piece - 1, 0))
    to_right_turn = turn_to(jnp.minimum(piece + 1, cols_axis * chips - 1))
    spot = jnp.stack(
        [col_at, chip, core, chunk, col_counts[0], to_left_turn, to_right_turn]
    ).astype(jnp.int32)

    half_width = model // 2
    frequency = jnp.exp(-math.log(1000.0) * jnp.arange(half_width, dtype=f32) / half_width)
    col_place = (jnp.arange(width, dtype=jnp.int32) + piece * width + offsets[1]).astype(f32)
    seq_slots = jnp.stack([(chip ^ step) * 2 + core for step in range(chips)])
    row_place = (seq_slots + offsets[0]).astype(f32)
    waves = 0.5 * jnp.sin(
        jnp.concatenate([col_place, row_place])[:, None] * frequency[None, :]
    )
    band_here = lax.dynamic_slice_in_dim(band, chunk * width, width, axis=0)
    query_index = jnp.arange(width, dtype=jnp.int32)[:, None]
    key_index = jnp.arange(span, dtype=jnp.int32)[None, :]
    distance = key_index - query_index
    choose = jnp.arange(2 * WINDOW + 1, dtype=jnp.int32)
    matches = (distance[:, None, :] == choose[None, :, None]) & (band_here[:, :, None] == 1)
    key_global = (piece - 1) * width + key_index
    inside = (key_global >= 0) & (key_global < cols_axis * cols_dev)
    allowed = ((jnp.any(matches, axis=1) | (distance == WINDOW)) & inside).astype(f32)

    quarter = shard // cols_axis
    lines = 8
    hops = chips - 1
    col_rows = cols_axis * quarter
    row_rows = col_rows + lines

    def chunk_at(spot_ref, chip_index):
        at = jnp.where(spot_ref[0] % 2 == 0, chip_index, chips - 1 - chip_index)
        return pl.ds(pl.multiple_of(at * width, width), width)

    def pack(spot_ref, weights, own_ref, send_refs, block):
        at = pl.multiple_of(spot_ref[0] * quarter, quarter)
        size = len(weights) * quarter
        for index, ref in enumerate(weights):
            own_ref[index * shard : (index + 1) * shard] = ref[...]
            for send_ref in send_refs:
                send_ref[index * quarter : (index + 1) * quarter] = ref[pl.ds(at, quarter)]
        if block is not None:
            for ref, row in [(own_ref, len(weights) * shard)] + [
                (ref, size) for ref in send_refs
            ]:
                ref[row : row + lines] = jnp.zeros((lines, model), bf16)
                ref[row : row + lines, :128] = block

    def pack_row(spot_ref, *refs):
        norm_refs, own_ref, send_ref = refs[4:10], refs[10], refs[11]
        block = jnp.zeros((lines, 128), f32)
        rows = lax.broadcasted_iota(jnp.int32, (lines, 128), 0)
        for index, ref in enumerate(norm_refs):
            line = jnp.pad(ref[...].astype(f32), ((0, 0), (0, 128 - shard)))
            block = jnp.where(rows == index, line, block)
        block = jnp.where(rows == 6, spot_ref[4].astype(f32), block).astype(bf16)
        pack(spot_ref, refs[:4], own_ref, [send_ref], block)

    part = feed_out.shape[0] // cols_axis
    block_cols = feed_out.shape[0]

    def pack_rest(spot_ref, *refs):
        token_refs, in_ref, out_ref = refs[4:6], refs[6], refs[7]
        own_ref, chunk_ref, send_refs = refs[8], refs[10], refs[11:]
        pack(spot_ref, refs[:4], refs[9], send_refs, None)
        for index, ref in enumerate(token_refs):
            chunk_ref[index * width : (index + 1) * width] = ref[0, chunk_at(spot_ref, spot_ref[1])]
            for hop, send_ref in enumerate(send_refs):
                at = col_rows + index * width
                send_ref[at : at + width] = ref[0, chunk_at(spot_ref, spot_ref[1] ^ (hop + 1))]
        first = lax.broadcasted_iota(jnp.int32, (block_cols, 128), 0)
        lanes = lax.broadcasted_iota(jnp.int32, (block_cols, 128), 1)
        chosen = ((first == lanes + spot_ref[0] * part) & (lanes < part)).astype(bf16)
        for index in range(seqs):
            block = in_ref[:, index * block_cols : (index + 1) * block_cols]
            own_ref[0, :, index * part : (index + 1) * part] = dot(block, chosen)[
                :, :part
            ].astype(bf16)
        own_ref[1] = out_ref[pl.ds(pl.multiple_of(spot_ref[0] * part, part), part)]

    def stack_row(*refs):
        for hop, ref in enumerate(refs[:-1]):
            refs[-1][hop * row_rows : (hop + 1) * row_rows] = ref[...]

    def stack_col(own_ref, *refs):
        ins, (out_ref, given_ref) = refs[:-2], refs[-2:]
        for slot, ref in enumerate((own_ref, *ins)):
            at = 0 if slot == 0 else col_rows
            given_ref[slot * width : (slot + 1) * width] = ref[at + width : at + 2 * width]
            if slot:
                out_ref[(slot - 1) * col_rows : slot * col_rows] = ref[:col_rows]

    def spread_plane(near, far):
        def join_cores(near_ref, far_ref, out_ref):
            rows = near_ref.shape[0]
            out_ref[:rows] = near_ref[...]
            out_ref[rows:] = far_ref[...]

        both_cores = kernel_call(join_cores, [((2 * near.shape[0], model), bf16)], [near, far])[0]
        return both_cores, pair_cols(both_cores), along_cols(near, cols_axis - 1)

    def place_rows(spot_ref, refs, outs, rows, unit):
        at_col, at_chip, at_core = spot_ref[0], spot_ref[1], spot_ref[2]
        other = 1 - at_core

        def row_of(from_chip, from_core, offset, size):
            return pl.ds(
                pl.multiple_of((from_chip * 2 + from_core) * shard + offset, quarter), size
            )

        pieces = (
            (refs[2], at_col, at_core, 2),
            (refs[3], at_col ^ (1 + at_core), at_core, 2),
            (refs[4], at_col ^ 3, at_core, 1),
            (refs[5], at_col ^ (1 + other), other, 2),
            (refs[6], at_col ^ 3, other, 1),
        )
        for index, (out_ref, lead) in enumerate(outs):
            for ref, core_at in ((refs[0], at_core), (refs[1], other)):
                out_ref[lead + (row_of(at_chip, core_at, 0, shard),)] = ref[
                    index * shard : (index + 1) * shard
                ]
            for ref, col, core_at, sides in pieces:
                for side in range(sides):
                    for hop in steps:
                        at = row_of(at_chip ^ hop, core_at ^ side, col * quarter, quarter)
                        start = side * unit + (hop - 1) * rows + index * quarter
                        out_ref[lead + (at,)] = ref[start : start + quarter]

    row_own, row_send = kernel_call(
        pack_row,
        [((cols_axis * shard + lines, model), bf16), ((row_rows, model), bf16)],
        [spot, *row_weights, *[item[None] for item in norms]],
        smem=(0,),
        stream=True,
    )
    row_got = [along_chips(row_send, step) for step in steps]
    feed_own, col_own, chunks_own, *col_sends = kernel_call(
        pack_rest,
        [
            ((2, shard, hidden), bf16),
            ((cols_axis * shard, model), bf16),
            ((2 * width, model), bf16),
        ]
        + [((col_rows + 2 * width, model), bf16)] * hops,
        [spot, *col_weights, tokens, cotangent, feed_in, feed_out],
        smem=(0,),
        stream=True,
    )
    row_got = after(row_got, waves, allowed, col_sends)
    feed_other = along_core(feed_own)
    row_hops = kernel_call(stack_row, [((hops * row_rows, model), bf16)], row_got)[0]
    row_far_own = along_core(row_own)
    row_plane, row_pair, row_diagonal = spread_plane(row_hops, along_core(row_hops))
    col_sends = after(col_sends, row_plane)
    col_got = [along_chips(col_sends[step - 1], step) for step in steps]

    def pair_feed(own_ref, other_ref, out_ref):
        out_ref[0] = own_ref[...]
        out_ref[1] = other_ref[...]

    feed_both = kernel_call(
        pair_feed, [((2, 2, shard, hidden), bf16)], [feed_own, after(feed_other, row_plane)]
    )[0]
    row_last = after((row_pair, row_diagonal), row_pair, row_diagonal, col_got, feed_both)
    row_pieces = [row_own, row_far_own, row_plane, row_pair, row_diagonal] + [
        along_core(item) for item in row_last
    ]
    def project_row(spot_ref, waves_ref, *refs):
        token_refs, pieces, outs = refs[:chips], refs[chips : chips + 7], refs[chips + 7 :]
        zero_ref, low_ref, q_ref, kv_ref, weight_ref, last_ref, norm_ref = outs
        place_rows(
            spot_ref,
            pieces,
            [(weight_ref, (index,)) for index in range(3)] + [(last_ref, ())],
            row_rows,
            hops * row_rows,
        )
        first = lax.broadcasted_iota(jnp.int32, (128, model), 0)
        lanes = lax.broadcasted_iota(jnp.int32, (128, model), 1)
        total = jnp.zeros((lines, model), f32)
        for side in (0, 1):
            for hop in range(chips):
                if hop == 0:
                    block = pieces[side][cols_axis * shard : cols_axis * shard + lines, :128]
                else:
                    at = (side * hops + hop) * row_rows - lines
                    block = pieces[2][at : at + lines, :128]
                start = ((spot_ref[1] ^ hop) * 2 + (spot_ref[2] ^ side)) * shard
                chosen = ((lanes == first + start) & (first < shard)).astype(bf16)
                total = total + dot(block, chosen)
        count = spot_ref[4].astype(f32)
        for ref in pieces[3:6]:
            count = count + ref[row_rows - lines : row_rows, :128][6:7, 0:1].astype(f32)
        rows = lax.broadcasted_iota(jnp.int32, (lines, model), 0)
        norm_ref[...] = jnp.where(rows == 6, count, total)
        for slot in range(chips):
            rows = slice(slot * width, (slot + 1) * width)
            at = 0 if slot == 0 else col_rows
            stream = token_refs[slot][at : at + width].astype(f32)
            zero_ref[rows, :half] = stream[:, :half] + waves_ref[:width]
            zero_ref[rows, half:] = stream[:, half:] + waves_ref[width + slot : width + slot + 1]
        unit, _ = unit_norm(zero_ref[...])
        low = (unit * norm_ref[0:1] + norm_ref[1:2]).astype(bf16)
        low_ref[...] = low
        q_ref[...] = dot(low, weight_ref[0]).astype(bf16)
        kv_ref[0] = dot(low, weight_ref[1]).astype(bf16)
        kv_ref[1] = dot(low, weight_ref[2]).astype(bf16)

    big = 2.0 * toks * model * model
    stream_zero, normed_one, row_q, row_kv, weights_row, weights_out, norm_rows = kernel_call(
        project_row,
        [
            ((toks, model), f32),
            ((toks, model), bf16),
            ((toks, model), bf16),
            ((2, toks, model), bf16),
            ((3, model, model), bf16),
            ((model, model), bf16),
            ((lines, model), f32),
        ],
        [spot, waves, chunks_own, *col_got, *row_pieces],
        smem=(0,),
    )
    kv_left = to_right(row_kv)
    kv_right = to_left(row_kv)
    col_unit = hops * col_rows
    col_hops, given_out = kernel_call(
        stack_col,
        [((col_unit, model), bf16), ((toks, model), bf16)],
        [after(chunks_own, row_q), *col_got],
    )
    col_far_own = along_core(col_own)
    col_plane, col_pair, col_diagonal = spread_plane(col_hops, along_core(col_hops))

    feed_pair = pair_chips(after(feed_both, row_q))

    def tied_logits(spot_ref, q_ref, near_ref, left_ref, right_ref, out_ref):
        mask = head_mask(width, model)
        total = None
        for slot in range(chips):
            keys = window_rows(spot_ref, near_ref, left_ref, right_ref, 0, slot, width)
            spread = spread_heads(q_ref[slot * width : (slot + 1) * width], mask)
            term = dot_back(spread, keys)
            total = term if total is None else total + term
        out_ref[...] = total

    logits = kernel_call(
        tied_logits,
        [((fold, span), f32)],
        [spot, row_q, row_kv, kv_left, kv_right],
        smem=(0,),
    )[0]
    logits_other = along_core(logits)
    feed_diagonal = along_chips(after(feed_own, logits), chips - 1)
    given_far = after(along_core(given_out), logits)
    row_scale = 1.0 / math.sqrt(HEAD_DIM * seqs)
    col_scale = 1.0 / math.sqrt(HEAD_DIM)

    def attend_row(
        spot_ref,
        logits_ref,
        other_ref,
        allowed_ref,
        near_ref,
        left_ref,
        right_ref,
        zero_ref,
        norm_ref,
        weight_ref,
        scores_ref,
        probs_ref,
        mix_ref,
        stream_ref,
        low_ref,
        entropy_ref,
    ):
        mask = head_mask(width, model)
        scores = (logits_ref[...] + other_ref[...]) * row_scale
        open_here = jnp.concatenate([allowed_ref[...]] * HEADS, axis=0) > 0.5
        masked = jnp.where(open_here, scores, -1000000000.0)
        largest = jnp.max(masked, axis=-1, keepdims=True)
        powers = jnp.exp(masked - largest)
        total = jnp.sum(powers, axis=-1, keepdims=True)
        probs = powers / total
        kept = jnp.where(open_here, scores, 0.0)
        entropies = largest + jnp.log(total) - jnp.sum(probs * kept, axis=-1, keepdims=True)
        rows = lax.broadcasted_iota(jnp.int32, (fold, 1), 0) % width
        entropies = jnp.where(rows + spot_ref[3] * width < spot_ref[4], entropies, 0.0)
        lanes = lax.broadcasted_iota(jnp.int32, (1, model), 1)
        found = jnp.sum(entropies, axis=0, keepdims=True)
        entropy_ref[...] = jnp.where((lanes == 0) & (spot_ref[2] == 0), found, 0.0)
        scores_ref[...] = kept
        probs_ref[...] = probs
        low_probs = probs.astype(bf16)
        for slot in range(chips):
            values = window_rows(spot_ref, near_ref, left_ref, right_ref, 1, slot, width)
            mix_ref[slot * width : (slot + 1) * width] = fold_heads(
                dot(low_probs, values), mask, width
            ).astype(bf16)
        stream = zero_ref[...] + dot(mix_ref[...], weight_ref[...])
        stream_ref[...] = stream
        unit, _ = unit_norm(stream)
        low_ref[...] = (unit * norm_ref[2:3] + norm_ref[3:4]).astype(bf16)

    scores, probs, row_mix, stream_one, normed_two, entropy_row = kernel_call(
        attend_row,
        [
            ((fold, span), f32),
            ((fold, span), f32),
            ((toks, model), bf16),
            ((toks, model), f32),
            ((toks, model), bf16),
            ((1, model), f32),
        ],
        [
            spot,
            logits,
            logits_other,
            allowed,
            row_kv,
            kv_left,
            kv_right,
            stream_zero,
            norm_rows,
            weights_out,
        ],
        smem=(0,),
    )

    col_last = after((col_pair, col_diagonal), normed_two, feed_pair)
    col_pieces = [col_own, col_far_own, col_plane, col_pair, col_diagonal] + [
        along_core(item) for item in col_last
    ]

    def assemble_col(spot_ref, *refs):
        three_ref, last_ref = refs[7:]
        outs = [(three_ref, (index,)) for index in range(3)] + [(last_ref, ())]
        place_rows(spot_ref, refs[:7], outs, col_rows, col_unit)

    weights_three, weights_last = kernel_call(
        assemble_col,
        [((3, model, model), bf16), ((model, model), bf16)],
        [spot, *col_pieces],
        smem=(0,),
    )

    def project_col(low_ref, weight_ref, q_ref, k_ref, v_ref):
        low = low_ref[...]
        q_ref[...] = dot(low, weight_ref[0]).astype(bf16)
        k_ref[...] = dot(low, weight_ref[1]).astype(bf16)
        v_ref[...] = dot(low, weight_ref[2]).astype(bf16)

    col_q, col_k, col_v = kernel_call(
        project_col,
        [((toks, model), bf16)] * 3,
        [normed_two, weights_three],
    )
    k_other, v_other = along_core(col_k), along_core(col_v)

    def join_given(near_ref, far_ref, out_ref):
        out_ref[:toks] = near_ref[...]
        out_ref[toks:] = far_ref[...]

    given_both = kernel_call(join_given, [((2 * toks, model), bf16)], [given_out, given_far])[0]
    given_pair = pair_cols(given_both)

    def slot_rows(slot):
        return slice(slot * width, (slot + 1) * width)

    def attend_col(
        q_ref,
        k_ref,
        v_ref,
        k2_ref,
        v2_ref,
        one_ref,
        norm_ref,
        weight_ref,
        given_ref,
        probs_ref,
        mix_ref,
        stream_ref,
        low_ref,
        message_ref,
    ):
        lane_heads = head_of_lane(model)
        sides = ((k_ref, v_ref), (k2_ref, v2_ref))
        for slot in range(chips):
            query = q_ref[slot_rows(slot)].astype(f32)
            products = jnp.concatenate(
                [
                    query * sides[s // chips][0][slot_rows(s % chips)].astype(f32)
                    for s in range(seqs)
                ],
                axis=0,
            )
            found = per_head_sum(products, lane_heads) * col_scale
            parts = [found[s * width : (s + 1) * width] for s in range(seqs)]
            largest = parts[0]
            for item in parts[1:]:
                largest = jnp.maximum(largest, item)
            powers = [jnp.exp(item - largest) for item in parts]
            total = powers[0]
            for item in powers[1:]:
                total = total + item
            weights = jnp.concatenate([item / total for item in powers], axis=0)
            probs_ref[slot] = weights
            wide = dot_back(weights.astype(bf16), lane_heads)
            mixed = None
            for s in range(seqs):
                term = wide[s * width : (s + 1) * width] * sides[s // chips][1][
                    slot_rows(s % chips)
                ].astype(f32)
                mixed = term if mixed is None else mixed + term
            mix_ref[slot_rows(slot)] = mixed.astype(bf16)
        stream = one_ref[...] + dot(mix_ref[...], weight_ref[...])
        stream_ref[...] = stream
        unit, _ = unit_norm(stream)
        low = (unit * norm_ref[4:5] + norm_ref[5:6]).astype(bf16)
        low_ref[...] = low
        message_ref[:toks] = low
        message_ref[toks:] = given_ref[...]

    col_probs, col_mix, stream_two, normed_three, message = kernel_call(
        attend_col,
        [
            ((chips, seqs * width, 128), f32),
            ((toks, model), bf16),
            ((toks, model), f32),
            ((toks, model), bf16),
            ((2 * toks, model), bf16),
        ],
        [col_q, col_k, col_v, k_other, v_other, stream_one, norm_rows, weights_last, given_out],
    )
    low_near = [
        normed_three,
        along_cols(normed_three, 1),
        along_cols(normed_three, 2),
        along_cols(message, 3),
    ]

    feed_last = after((feed_pair, feed_diagonal, given_pair), low_near)
    feed_far = [along_core(item) for item in feed_last]

    def assemble_feed(
        spot_ref,
        both_ref,
        pair_ref,
        last_ref,
        pair2_ref,
        last2_ref,
        d0_ref,
        d1_ref,
        d2_ref,
        d3_ref,
        out_ref,
        given_ref,
    ):
        at_chip, at_core = spot_ref[1], spot_ref[2]
        other = 1 - at_core

        def move(rows, from_chip, from_core):
            at = pl.multiple_of((from_chip * 2 + from_core) * shard, shard)
            out_ref[:, pl.ds(at, shard)] = rows

        for side in (0, 1):
            move(both_ref[side], at_chip, at_core ^ side)
            move(pair_ref[side], at_chip ^ (1 + at_core), at_core ^ side)
            move(pair2_ref[side], at_chip ^ (1 + other), other ^ side)
        move(last_ref[...], at_chip ^ 3, at_core)
        move(last2_ref[...], at_chip ^ 3, other)
        given_ref[0] = d0_ref[...]
        given_ref[1 + at_core] = d1_ref[:toks]
        given_ref[2 - at_core] = d2_ref[toks:]
        given_ref[3] = d3_ref[toks:]

    weights_feed, given_all = kernel_call(
        assemble_feed,
        [((2, model, hidden), bf16), ((cols_axis, toks, model), bf16)],
        [
            spot,
            feed_both,
            feed_pair,
            feed_diagonal,
            feed_far[0],
            feed_far[1],
            given_out,
            given_pair,
            feed_far[2],
            low_near[3],
        ],
        smem=(0,),
    )

    def feed_main(a0, a1, a2, a3, given_ref, weight_ref, act_ref, grad_ref, *back_refs):
        up, down = weight_ref[0], weight_ref[1]
        for step, low_ref in enumerate((a0, a1, a2, a3)):
            pre = dot(low_ref[:toks], up)
            bell = 0.5 * (1.0 + lax.erf(pre * (0.5**0.5)))
            slope = bell + pre * jnp.exp(-0.5 * pre * pre) * ((0.5 / math.pi) ** 0.5)
            act_ref[step] = (pre * bell).astype(bf16)
            grad = (slope * dot_back(given_ref[step], down)).astype(bf16)
            grad_ref[step] = grad
            back_refs[step][...] = dot_back(grad, up).astype(bf16)

    feed_big = 2.0 * toks * cols_axis * model * hidden
    feed_results = kernel_call(
        feed_main,
        [((cols_axis, toks, hidden), bf16)] * 2 + [((toks, model), bf16)] * cols_axis,
        [*low_near, given_all, weights_feed],
    )
    act, grad_hidden, back_parts = feed_results[0], feed_results[1], feed_results[2:]
    back_near = [back_parts[0]] + [along_cols(back_parts[step], step) for step in col_steps]

    def feed_weights(
        spot_ref, a0, a1, a2, a3, given_ref, act_ref, grad_ref, weight_ref, mine_ref, give_ref, *outs
    ):
        at_core = spot_ref[2]
        low = jnp.concatenate([a0[...], a1[...], a2[...], a3[:toks]], axis=0)
        given = given_ref[...].reshape(cols_axis * toks, model)
        rows = cols_axis * toks
        acts = act_ref[...].reshape(rows, hidden)
        grads = grad_ref[...].reshape(rows, hidden)
        for step in range(cols_axis):
            outs[step][...] = dot(act_ref[step], weight_ref[1]).astype(bf16)
        for ref, at in ((mine_ref, at_core), (give_ref, 1 - at_core)):
            ref[:model] = dot_tokens(low, half_of(grads, at, half)).astype(bf16)
            ref[model:] = dot_tokens(acts, half_of(given, at, half)).astype(bf16)

    feed_grads = kernel_call(
        feed_weights,
        [((2 * model, half), bf16)] * 2 + [((toks, model), bf16)] * cols_axis,
        [spot, *low_near, given_all, act, grad_hidden, weights_feed],
        smem=(0,),
        flops=6.0 * toks * cols_axis * model * hidden,
        moved=16 << 20,
        room=24,
    )
    feed_mine, feed_give, out_parts = feed_grads[0], feed_grads[1], feed_grads[2:]

    block = 2 * shard
    extra = 2 * lines

    def renew(total, at):
        line = total[at : at + 1]
        whole = line[:, 0:1] + line[:, 1:2]
        high = whole.astype(bf16).astype(f32)
        lanes = lax.broadcasted_iota(jnp.int32, total.shape, 1)
        rows = lax.broadcasted_iota(jnp.int32, total.shape, 0)
        total = jnp.where((rows == at) & (lanes == 0), high, total)
        return jnp.where((rows == at) & (lanes == 1), whole - high, total)

    near_rows = model // 2

    def row_layer_grads(low, mix, low_far, mix_far, mine, got, more):
        norms_too = len(more) == 1
        size = near_rows + (0 if norms_too else toks)
        tail = extra if norms_too else 0

        def row_weight_sums(spot_ref, low_ref, mix_ref, low2_ref, mix2_ref, mine_ref, got_ref, *refs):
            more_refs, (x_ref, y_ref, a_ref, b_ref) = refs[: len(more)], refs[len(more) : -2]
            left_ref, right_ref = refs[-2:]
            left_ref[0, :toks] = low_ref[...]
            left_ref[0, toks:] = low2_ref[...]
            left_ref[1, :toks] = mix_ref[...]
            left_ref[1, toks:] = mix2_ref[...]
            right_ref[:, :toks] = mine_ref[...]
            right_ref[:, toks:] = got_ref[...]
            places = (
                ((a_ref, 0), (b_ref, 0)),
                ((x_ref, 0), (b_ref, 1)),
                ((a_ref, 1), (y_ref, 0)),
                ((x_ref, 1), (y_ref, 1)),
            )
            for step in range(cols_axis):
                matrix = spot_ref[0] ^ step
                left = left_ref[matrix // 3]
                found = dot_tokens(left, right_ref[matrix]).astype(bf16)
                for part_index, (ref, at) in enumerate(places[step]):
                    start = at * size
                    ref[start : start + near_rows] = found[
                        part_index * near_rows : (part_index + 1) * near_rows
                    ]
                    if not norms_too:
                        lanes = slice(part_index * half, (part_index + 1) * half)
                        ref[start + near_rows : start + size] = more_refs[step][:, lanes]
            if norms_too:
                sums_ref = more_refs[0]
                line = jnp.concatenate([sums_ref[:, :half], sums_ref[:, half:]], axis=0)
                line = renew(line, 6).astype(bf16)
                for ref in (x_ref, a_ref):
                    ref[2 * size :] = line

        outs = [((2 * size + tail, half), bf16), ((2 * size, half), bf16)] * 2
        return kernel_call(
            row_weight_sums,
            outs,
            [spot, low, mix, low_far, mix_far, mine, got, *more],
            smem=(0,),
            scratch=[
                pltpu.VMEM((2, 2 * toks, model), bf16),
                pltpu.VMEM((4, 2 * toks, half), bf16),
            ],
        )

    def fold_pairs(parts, got_x, got_y, tail):
        a_part, b_part = parts[2:]
        size = b_part.shape[0] // 2

        def pair_sums(a_ref, x_ref, b_ref, y_ref, keep_ref, give_ref, keep2_ref, give2_ref):
            first = a_ref[...].astype(f32) + x_ref[...].astype(f32)
            second = b_ref[...].astype(f32) + y_ref[...].astype(f32)
            keep_ref[:size] = first[:size].astype(bf16)
            give_ref[:size] = first[size : 2 * size].astype(bf16)
            keep2_ref[...] = second[:size].astype(bf16)
            give2_ref[...] = second[size:].astype(bf16)
            if tail:
                line = renew(first[2 * size :], 6).astype(bf16)
                keep_ref[size:] = line
                give_ref[size:] = line

        return kernel_call(
            pair_sums,
            [((size + tail, half), bf16)] * 2 + [((size, half), bf16)] * 2,
            [a_part, got_x, b_part, got_y],
        )

    def row_layer_chips(keep, got, keep2, got2, tail, stream, slots):
        sent_rows = 2 * width * (bool(stream) + bool(slots))

        def layer_parts(spot_ref, a_ref, ga_ref, b_ref, gb_ref, *refs):
            more, outs, total_ref = refs[: -chips - 1], refs[-chips - 1 : -1], refs[-1]
            first = a_ref[...].astype(f32) + ga_ref[...].astype(f32)
            second = b_ref[...].astype(f32) + gb_ref[...].astype(f32)
            total_ref[:near_rows] = first[:near_rows].astype(bf16)
            total_ref[near_rows:] = second[:near_rows].astype(bf16)
            if stream:
                result = more[0][...] + jnp.concatenate(
                    [first[near_rows:], second[near_rows:]], axis=1
                )
            for hop in range(chips):
                at = pl.multiple_of((spot_ref[1] ^ hop) * block, block)
                outs[hop][:block] = total_ref[pl.ds(at, block)]
                row = block
                if tail:
                    outs[hop][row : row + tail] = renew(first[near_rows:], 6).astype(bf16)
                    row = row + tail
                sent = []
                if stream:
                    sent.append(result[slot_rows(hop)].astype(bf16))
                if slots:
                    sent.append(more[hop - chips][...])
                for slot in sent:
                    outs[hop][row : row + width] = slot[:, :half]
                    outs[hop][row + width : row + 2 * width] = slot[:, half:]
                    row = row + 2 * width

        return kernel_call(
            layer_parts,
            [((block + tail + sent_rows, half), bf16)] * chips,
            [spot, keep, got, keep2, got2, *stream, *slots],
            smem=(0,),
            scratch=[pltpu.VMEM((model, half), bf16)],
        )

    def layer_grads(low, mix, low_far, mix_far, mine, got, more):
        rows = model + (extra if len(more) == 1 else 2 * toks)

        def weight_sums(spot_ref, low_ref, mix_ref, low2_ref, mix2_ref, mine_ref, got_ref, *refs):
            more_refs, outs = refs[: len(more)], refs[len(more) : -2]
            left_ref, right_ref = refs[-2:]
            left_ref[0, :toks] = low_ref[...]
            left_ref[0, toks:] = low2_ref[...]
            left_ref[1, :toks] = mix_ref[...]
            left_ref[1, toks:] = mix2_ref[...]
            right_ref[:, :toks] = mine_ref[...]
            right_ref[:, toks:] = got_ref[...]
            for step in range(cols_axis):
                matrix = spot_ref[0] ^ step
                left = left_ref[matrix // 3]
                outs[step][:model] = dot_tokens(left, right_ref[matrix]).astype(bf16)
                if len(more) == 1:
                    sums_ref = more_refs[0]
                    tail = jnp.concatenate([sums_ref[:, :half], sums_ref[:, half:]], axis=0)
                    outs[step][model:] = renew(tail, 6).astype(bf16)
                else:
                    outs[step][model : model + toks] = more_refs[step][:, :half]
                    outs[step][model + toks :] = more_refs[step][:, half:]

        return kernel_call(
            weight_sums,
            [((rows, half), bf16)] * cols_axis,
            [spot, low, mix, low_far, mix_far, mine, got, *more],
            smem=(0,),
            scratch=[
                pltpu.VMEM((2, 2 * toks, model), bf16),
                pltpu.VMEM((4, 2 * toks, half), bf16),
            ],
        )

    def split_chips(items, count, tail, stream=None, slots=()):
        slot_rows_out = 2 * width * ((stream is not None) + bool(slots))

        def chip_parts(spot_ref, *refs):
            ins, outs, total_ref = refs[: len(items)], refs[-chips - 1 : -1], refs[-1]
            more = refs[len(items) : -chips - 1]
            total = ins[0][...].astype(f32)
            for ref in ins[1:]:
                total = total + ref[...].astype(f32)
            total_ref[...] = total.astype(bf16)
            if stream is not None:
                result = more[0][...] + jnp.concatenate(
                    [total[model : model + toks], total[model + toks :]], axis=1
                )
            for hop in range(chips):
                at = pl.multiple_of((spot_ref[1] ^ hop) * block, block)
                for index in range(count):
                    outs[hop][index * block : (index + 1) * block] = total_ref[
                        pl.ds(index * model + at, block)
                    ]
                row = count * block
                if tail:
                    outs[hop][row : row + tail] = renew(total[count * model :], 6).astype(bf16)
                    row = row + tail
                sent = []
                if stream is not None:
                    sent.append(result[slot_rows(hop)].astype(bf16))
                if slots:
                    sent.append(more[hop - chips][...])
                for slot in sent:
                    outs[hop][row : row + width] = slot[:, :half]
                    outs[hop][row + width : row + 2 * width] = slot[:, half:]
                    row = row + 2 * width

        size = count * block + tail + slot_rows_out
        return kernel_call(
            chip_parts,
            [((size, half), bf16)] * chips,
            [spot, *items] + ([] if stream is None else [stream]) + list(slots),
            smem=(0,),
            scratch=[pltpu.VMEM(items[0].shape, bf16)],
        )

    def split_cores(items, count, tail):
        rows_in = count * block + tail

        def core_parts(spot_ref, *refs):
            ins, (keep_ref, give_ref, total_ref) = refs[: len(items)], refs[len(items) :]
            total = ins[0][:rows_in].astype(f32)
            for ref in ins[1:]:
                total = total + ref[:rows_in].astype(f32)
            total_ref[...] = total.astype(bf16)
            for ref, at in ((keep_ref, spot_ref[2]), (give_ref, 1 - spot_ref[2])):
                for index in range(count):
                    row = pl.multiple_of(index * block + at * shard, shard)
                    ref[index * shard : (index + 1) * shard] = total_ref[pl.ds(row, shard)]
                if tail:
                    ref[count * shard :] = renew(total[count * block :], 6).astype(bf16)

        size = count * shard + tail
        return kernel_call(
            core_parts,
            [((size, half), bf16)] * 2,
            [spot, *items],
            smem=(0,),
            scratch=[pltpu.VMEM((rows_in, half), bf16)],
        )

    def over_chips(parts):
        return [parts[0]] + [along_chips(parts[step], step) for step in steps]

    back_near = after(back_near, feed_mine)

    def attend_col_back(
        spot_ref,
        b0,
        b1,
        b2,
        b3,
        given_ref,
        two_ref,
        norm_ref,
        weight_ref,
        q_ref,
        k_ref,
        v_ref,
        k2_ref,
        v2_ref,
        probs_ref,
        dtwo_ref,
        low_ref,
        dq_ref,
        dkv_ref,
        send_ref,
        sums_ref,
        wide_ref,
    ):
        lane_heads = head_of_lane(model)
        back = b0[...].astype(f32) + b1[...].astype(f32) + b2[...].astype(f32) + b3[...].astype(f32)
        unit, scale = unit_norm(two_ref[...])
        sums_ref[...] = norm_sums(back, unit)
        dtwo = given_ref[0].astype(f32) + unit_norm_back(back, unit, scale, norm_ref[4:5])
        dtwo_ref[...] = dtwo
        low = dtwo.astype(bf16)
        low_ref[...] = low
        dmix = dot_back(low, weight_ref[...]).astype(bf16).astype(f32)
        wide_ref[...] = jnp.zeros_like(wide_ref)
        sides = ((k_ref, v_ref), (k2_ref, v2_ref))
        for slot in range(chips):
            dout = dmix[slot_rows(slot)]
            query = q_ref[slot_rows(slot)].astype(f32)
            products = jnp.concatenate(
                [
                    dout * sides[s // chips][1][slot_rows(s % chips)].astype(f32)
                    for s in range(seqs)
                ],
                axis=0,
            )
            found = per_head_sum(products, lane_heads)
            weights = probs_ref[slot]
            mean = None
            for s in range(seqs):
                rows = slice(s * width, (s + 1) * width)
                term = weights[rows] * found[rows]
                mean = term if mean is None else mean + term
            dscores = (weights * (found - jnp.concatenate([mean] * seqs, axis=0))).astype(bf16)
            wide_d = dot_back(dscores, lane_heads)
            wide_p = dot_back(weights.astype(bf16), lane_heads)
            dquery = None
            for s in range(seqs):
                rows = slice(s * width, (s + 1) * width)
                term = wide_d[rows] * sides[s // chips][0][slot_rows(s % chips)].astype(f32)
                dquery = term if dquery is None else dquery + term
                wide_ref[0, rows] += wide_d[rows] * query
                wide_ref[1, rows] += wide_p[rows] * dout
            dq_ref[slot_rows(slot)] = (dquery * col_scale).astype(bf16)
        dkv_ref[0] = wide_ref[0, :toks] * col_scale
        dkv_ref[1] = wide_ref[1, :toks]
        send_ref[0] = (wide_ref[0, toks:] * col_scale).astype(bf16)
        send_ref[1] = wide_ref[1, toks:].astype(bf16)

    grad_two, grad_two_low, col_dq, col_dkv, col_send, sums_three = kernel_call(
        attend_col_back,
        [
            ((toks, model), f32),
            ((toks, model), bf16),
            ((toks, model), bf16),
            ((2, toks, model), f32),
            ((2, toks, model), bf16),
            ((2, model), f32),
        ],
        [
            spot,
            *back_near,
            given_all,
            stream_two,
            norm_rows,
            weights_last,
            col_q,
            col_k,
            col_v,
            k_other,
            v_other,
            col_probs,
        ],
        smem=(0,),
        scratch=[pltpu.VMEM((2, 2 * toks, model), f32)],
    )
    row_low_far, row_mix_far = along_core(normed_one), along_core(row_mix)
    col_low_far, col_mix_far = along_core(normed_two), along_core(col_mix)
    dkv_got = after(along_core(col_send), row_low_far, row_mix_far)

    def row_entry_back(
        spot_ref,
        dq_ref,
        dkv_ref,
        got_ref,
        low_two_ref,
        dtwo_ref,
        one_ref,
        norm_ref,
        col_ref,
        row_ref,
        near_ref,
        left_ref,
        right_ref,
        mine_ref,
        give_ref,
        done_ref,
        low_ref,
        dmix_ref,
        dprobs_ref,
        sums_ref,
    ):
        at_core = spot_ref[2]
        dq = dq_ref[...]
        dk = (dkv_ref[0] + got_ref[0].astype(f32)).astype(bf16)
        dv = (dkv_ref[1] + got_ref[1].astype(f32)).astype(bf16)
        for index, item in enumerate((dq, dk, dv, low_two_ref[...])):
            mine_ref[index] = half_of(item, at_core, half)
            give_ref[index] = half_of(item, 1 - at_core, half)
        back = dot_back(dq, col_ref[0]) + dot_back(dk, col_ref[1]) + dot_back(dv, col_ref[2])
        unit, scale = unit_norm(one_ref[...])
        sums_ref[...] = norm_sums(back, unit)
        done = dtwo_ref[...] + unit_norm_back(back, unit, scale, norm_ref[2:3])
        done_ref[...] = done
        low = done.astype(bf16)
        low_ref[...] = low
        dmix = dot_back(low, row_ref[...]).astype(bf16)
        dmix_ref[...] = dmix
        mask = head_mask(width, model)
        total = None
        for slot in range(chips):
            values = window_rows(spot_ref, near_ref, left_ref, right_ref, 1, slot, width)
            term = dot_back(spread_heads(dmix[slot_rows(slot)], mask), values)
            total = term if total is None else total + term
        dprobs_ref[...] = total

    (
        col_mine,
        col_give,
        grad_one,
        grad_one_low,
        row_dmix,
        dprobs,
        sums_two,
    ) = kernel_call(
        row_entry_back,
        [
            ((4, toks, half), bf16),
            ((4, toks, half), bf16),
            ((toks, model), f32),
            ((toks, model), bf16),
            ((toks, model), bf16),
            ((fold, span), f32),
            ((2, model), f32),
        ],
        [
            spot,
            col_dq,
            col_dkv,
            dkv_got,
            grad_two_low,
            grad_two,
            stream_one,
            norm_rows,
            weights_three,
            weights_out,
            row_kv,
            kv_left,
            kv_right,
        ],
        smem=(0,),
    )
    dprobs_other = along_core(dprobs)

    def attend_row_back(
        spot_ref,
        weight_ref,
        dprobs_ref,
        other_ref,
        scores_ref,
        probs_ref,
        q_ref,
        near_ref,
        left_ref,
        right_ref,
        dmix_ref,
        dq_ref,
        dkv_ref,
        to_left_ref,
        to_right_ref,
    ):
        mask = head_mask(width, model)
        dprob = dprobs_ref[...] + other_ref[...]
        probs_here, scores_here = probs_ref[...], scores_ref[...]
        rows = lax.broadcasted_iota(jnp.int32, (fold, 1), 0) % width
        weight = jnp.where(rows + spot_ref[3] * width < spot_ref[4], entropy_weight / (HEADS * weight_ref[6:7, 0:1]), 0.0)
        first = dprob - jnp.sum(probs_here * dprob, axis=-1, keepdims=True)
        second = scores_here - jnp.sum(probs_here * scores_here, axis=-1, keepdims=True)
        dscores = (probs_here * (first - weight * second)).astype(bf16)
        low_probs = probs_here.astype(bf16)
        for slot in range(chips):
            at = slot_rows(slot)
            keys = window_rows(spot_ref, near_ref, left_ref, right_ref, 0, slot, width)
            dq_ref[at] = (
                fold_heads(dot(dscores, keys), mask, width) * row_scale
            ).astype(bf16)
            dkeys = dot_tokens(dscores, spread_heads(q_ref[at], mask)) * row_scale
            dvalues = dot_tokens(low_probs, spread_heads(dmix_ref[at], mask))
            for index, item in enumerate((dkeys, dvalues)):
                to_left_ref[index, at] = item[:width].astype(bf16)
                dkv_ref[index, at] = item[width : 2 * width]
                to_right_ref[index, at] = item[2 * width :].astype(bf16)

    row_dq, row_dkv, edge_left, edge_right = kernel_call(
        attend_row_back,
        [
            ((toks, model), bf16),
            ((2, toks, model), f32),
            ((2, toks, model), bf16),
            ((2, toks, model), bf16),
        ],
        [
            spot,
            norm_rows,
            dprobs,
            dprobs_other,
            scores,
            probs,
            row_q,
            row_kv,
            kv_left,
            kv_right,
            row_dmix,
        ],
        smem=(0,),
    )
    col_sums = layer_grads(
        normed_two,
        col_mix,
        col_low_far,
        col_mix_far,
        col_mine,
        after(along_core(col_give), edge_left),
        out_parts,
    )
    edge_from_right = to_left(edge_left)
    edge_from_left = to_right(edge_right)
    feed_slices = split_chips([feed_mine, along_core(after(feed_give, edge_left))], 2, 0)
    feed_keep, feed_swap = split_cores(over_chips(feed_slices), 2, 0)

    def input_back(
        spot_ref,
        dq_ref,
        dkv_ref,
        from_right_ref,
        from_left_ref,
        low_one_ref,
        done_ref,
        zero_ref,
        norm_ref,
        row_ref,
        two_ref,
        three_ref,
        entropy_ref,
        mine_ref,
        give_ref,
        sums_ref,
        *slot_refs,
    ):
        at_core = spot_ref[2]
        dq = dq_ref[...]
        dk, dv = (
            jnp.concatenate(
                [
                    (
                        dkv_ref[index, slot_rows(slot)]
                        + from_left_ref[index, slot_span(spot_ref, 5, slot, width)].astype(f32)
                        + from_right_ref[index, slot_span(spot_ref, 6, slot, width)].astype(f32)
                    ).astype(bf16)
                    for slot in range(chips)
                ],
                axis=0,
            )
            for index in (0, 1)
        )
        for index, item in enumerate((dq, dk, dv, low_one_ref[...])):
            mine_ref[index] = half_of(item, at_core, half)
            give_ref[index] = half_of(item, 1 - at_core, half)
        back = dot_back(dq, row_ref[0]) + dot_back(dk, row_ref[1]) + dot_back(dv, row_ref[2])
        unit, scale = unit_norm(zero_ref[...])
        sums_ref[0:2] = norm_sums(back, unit)
        sums_ref[2:4] = two_ref[...]
        sums_ref[4:6] = three_ref[...]
        sums_ref[6:7] = entropy_ref[...]
        sums_ref[7:8] = jnp.zeros((1, model), f32)
        result = (done_ref[...] + unit_norm_back(back, unit, scale, norm_ref[0:1])).astype(bf16)
        for slot in range(chips):
            slot_refs[slot][...] = result[slot_rows(slot)]

    row_mine, row_give, sums, *grad_slots = kernel_call(
        input_back,
        [
            ((4, toks, half), bf16),
            ((4, toks, half), bf16),
            ((lines, model), f32),
        ]
        + [((width, model), bf16)] * chips,
        [
            spot,
            row_dq,
            row_dkv,
            edge_from_right,
            edge_from_left,
            grad_one_low,
            grad_one,
            stream_zero,
            norm_rows,
            weights_row,
            sums_two,
            sums_three,
            entropy_row,
        ],
        smem=(0,),
    )

    def join_halves(spot_ref, keep_rows, got_rows):
        first = spot_ref[2] == 0
        return jnp.concatenate(
            [jnp.where(first, keep_rows, got_rows), jnp.where(first, got_rows, keep_rows)], axis=1
        )

    def over_cols(whole):
        return [whole] + [along_cols(whole, step) for step in col_steps]

    def order_rows(slices, at):
        def order_slots(spot_ref, *refs):
            for hop, ref in enumerate(refs[:-1]):
                refs[-1][0, chunk_at(spot_ref, spot_ref[1] ^ hop)] = jnp.concatenate(
                    [ref[at : at + width], ref[at + width : at + 2 * width]], axis=1
                )

        return kernel_call(order_slots, [(tokens.shape, bf16)], [spot, *slices], smem=(0,))[0]

    feed_back = along_core(feed_swap)
    col_parts = [col_sums[0]] + [along_cols(col_sums[step], step) for step in col_steps]
    col_slices = split_chips(col_parts, 1, 0, stream=stream_two, slots=grad_slots)
    col_reached = over_chips(col_slices)
    col_keep, col_swap = split_cores(col_reached, 1, 0)

    def join_two(spot_ref, keep_ref, got_ref, keep2_ref, got2_ref, out_ref):
        rows = 2 * shard
        out_ref[:rows] = join_halves(spot_ref, keep_ref[...], got_ref[...])
        out_ref[rows:] = join_halves(spot_ref, keep2_ref[...], got2_ref[...])

    (pair,) = kernel_call(
        join_two,
        [((3 * shard, model), bf16)],
        [spot, feed_keep, feed_back, col_keep, along_core(col_swap)],
        smem=(0,),
    )
    pair_ends = over_cols(pair)

    def spread_pair(spot_ref, u0, u1, u2, u3, in_ref, out_ref, g0, g1, g2, g3, all_ref):
        for step, ref in enumerate((u0, u1, u2, u3)):
            all_ref[spot_ref[0] ^ step] = ref[...]
        for source, grad_ref in enumerate((g0, g1, g2, g3)):
            wide = all_ref[source, :shard].astype(f32)
            for index in range(seqs):
                at = index * block_cols + source * part
                in_ref[:, at : at + part] = wide[:, index * part : (index + 1) * part]
            out_ref[source * part : (source + 1) * part] = all_ref[
                source, shard : 2 * shard
            ].astype(f32)
            grad_ref[...] = all_ref[source, 2 * shard :].astype(f32)

    row_parts = row_layer_grads(
        normed_one,
        row_mix,
        row_low_far,
        row_mix_far,
        row_mine,
        along_core(row_give),
        [sums],
    )
    row_sends = after(row_parts, col_parts, feed_keep)
    row_x, row_y = along_cols(row_sends[0], 1), along_cols(row_sends[1], 2)
    keep, give, keep2, give2 = fold_pairs(row_parts, row_x, row_y, extra)
    row_slices = row_layer_chips(
        keep, along_cols(give, 2), keep2, along_cols(give2, 1), extra, [], []
    )
    row_reached = over_chips(row_slices)
    row_keep, row_swap = split_cores(row_reached, 1, extra)

    def join_row(spot_ref, keep_ref, got_ref, out_ref, norm_ref, entropy_ref):
        out_ref[...] = join_halves(spot_ref, keep_ref[:shard], got_ref[:shard])
        total = keep_ref[shard:].astype(f32) + got_ref[shard:].astype(f32)
        line = total[6:7]
        entropy_ref[...] = line[:, 0:1] + line[:, 1:2]
        wide = jnp.concatenate([total[:lines], total[lines:]], axis=1)
        at = spot_ref[1] * 2 + spot_ref[2]
        found = wide[:, :shard]
        for index in range(1, seqs):
            here = wide[:, index * shard : (index + 1) * shard]
            found = jnp.where(at == index, here, found)
        norm_ref[...] = found

    row_join, norm_here, entropy_sum = kernel_call(
        join_row,
        [((shard, model), bf16), ((lines, shard), f32), ((1, 1), f32)],
        [spot, row_keep, along_core(row_swap)],
        smem=(0,),
    )
    row_ends = over_cols(after(row_join, pair_ends))
    result = order_rows(after(col_reached, row_join), block)
    grad_in = order_rows(after(col_reached, row_join), block + 2 * width)
    grad_feed_in, grad_feed_out, *col_grads = kernel_call(
        spread_pair,
        [(feed_in.shape, f32), (feed_out.shape, f32)] + [((shard, model), f32)] * cols_axis,
        [spot, *after(pair_ends, row_join)],
        smem=(0,),
        scratch=[pltpu.VMEM((cols_axis, 3 * shard, model), bf16)],
        room=24,
    )

    def spread_row(spot_ref, *refs):
        ins, outs, all_ref = refs[:cols_axis], refs[cols_axis:-1], refs[-1]
        for step, ref in enumerate(ins):
            all_ref[spot_ref[0] ^ step] = ref[...]
        for matrix in range(cols_axis):
            outs[matrix][...] = all_ref[matrix].astype(f32)

    row_grads = kernel_call(
        spread_row,
        [((shard, model), f32)] * cols_axis,
        [spot, *row_ends],
        smem=(0,),
        scratch=[pltpu.VMEM((cols_axis, shard, model), bf16)],
    )
    entropy = entropy_sum[0, 0] / (HEADS * norm_rows[6, 0])

    return (
        result,
        entropy,
        grad_in,
        *[norm_here[index] for index in range(6)],
        *row_grads,
        *col_grads,
        grad_feed_in,
        grad_feed_out,
    )


def fits_fast(tokens, feed_out):
    chips = lax.axis_size("seq") // 2
    return (
        lax.axis_size("col") == 4
        and lax.axis_size("seq") == 8
        and tokens.shape[0] == 1
        and tokens.shape[1] == chips * WINDOW
        and tokens.shape[2] == HEADS * HEAD_DIM
        and feed_out.shape[0] * 2 == tokens.shape[2]
    )


def on_device(tokens, offsets, band, col_counts, *rest):
    if not fits_fast(tokens, rest[15]):
        return general_plan(tokens, offsets, band, col_counts, *rest)
    return fast_plan(
        tokens,
        offsets,
        band,
        col_counts,
        rest[0:6],
        rest[6:10],
        rest[10:14],
        rest[14],
        rest[15],
        rest[16],
    )


def solution(mesh):
    return jax.shard_map(
        on_device,
        mesh=mesh,
        in_specs=(
            P("seq", "col", None),
            P(),
            P("col", None),
            P("col"),
            P("seq"),
            P("seq"),
            P("seq"),
            P("seq"),
            P("seq"),
            P("seq"),
            P("seq", None),
            P("seq", None),
            P("seq", None),
            P("seq", None),
            P("seq", None),
            P("seq", None),
            P("seq", None),
            P("seq", None),
            P("seq", None),
            P("seq", None),
            P("seq", "col", None),
        ),
        out_specs=(
            P("seq", "col", None),
            P(),
            P("seq", "col", None),
            P("seq"),
            P("seq"),
            P("seq"),
            P("seq"),
            P("seq"),
            P("seq"),
            P("seq", None),
            P("seq", None),
            P("seq", None),
            P("seq", None),
            P("seq", None),
            P("seq", None),
            P("seq", None),
            P("seq", None),
            P("seq", None),
            P("seq", None),
        ),
        check_vma=False,
    )
```

```python
from functools import partial
import math

import jax
import jax.numpy as jnp
from jax import lax
from jax.experimental import pallas as pl
from jax.experimental.pallas import tpu as pltpu
from jax.sharding import PartitionSpec as P

HEADS = 12
HEAD_DIM = 64
WINDOW = 32


entropy_weight = 8192.0
norm_eps = 1e-05


def with_halo(cells, sides, width):
    for axis, dim in sides:
        count = lax.axis_size(axis)
        ends = count - 1
        head = lax.slice_in_dim(cells, 0, width, axis=dim)
        tail = lax.slice_in_dim(cells, cells.shape[dim] - width, cells.shape[dim], axis=dim)
        cells = jnp.concatenate(
            [
                lax.ppermute(tail, axis, [(i, (i + 1) % count) for i in range(ends)]),
                cells,
                lax.ppermute(head, axis, [((i + 1) % count, i) for i in range(ends)]),
            ],
            axis=dim,
        )
    return cells


def layer_norm(inputs, norm_gain, norm_shift):
    average = jnp.mean(inputs, axis=-1, keepdims=True)
    centred = inputs - average
    variance = jnp.mean(centred * centred, axis=-1, keepdims=True)
    return centred * lax.rsqrt(variance + norm_eps) * norm_gain + norm_shift


def position_table(offsets, row_first, col_first, row_count, col_count, model_width):
    half_width = model_width // 2
    frequency = jnp.exp(-math.log(1000.0) * jnp.arange(half_width, dtype=jnp.float32) / half_width)
    col_place = (jnp.arange(col_count, dtype=jnp.int32) + col_first + offsets[1]).astype(
        jnp.float32
    )
    row_place = (jnp.arange(row_count, dtype=jnp.int32) + row_first + offsets[0]).astype(
        jnp.float32
    )
    col_wave = jnp.sin(col_place[:, None] * frequency[None, :])
    row_wave = jnp.sin(row_place[:, None] * frequency[None, :])
    col_full = jnp.broadcast_to(col_wave[None, :, :], (row_count, col_count, half_width))
    row_full = jnp.broadcast_to(row_wave[:, None, :], (row_count, col_count, half_width))
    return 0.5 * jnp.concatenate([col_full, row_full], axis=-1)


def softmax_entropy(scores, allowed, valid):
    masked = jnp.where(allowed[None], scores, -1000000000.0)
    largest = jnp.max(masked, axis=-1, keepdims=True)
    powers = jnp.exp(masked - largest)
    row_total = jnp.sum(powers, axis=-1, keepdims=True)
    probs_out = powers / row_total
    log_total = largest[..., 0] + jnp.log(row_total[..., 0])
    entropies = log_total - jnp.sum(probs_out * jnp.where(allowed[None], scores, 0.0), axis=-1)
    return (probs_out, jnp.sum(entropies * valid[None, :]))


def plain_softmax(scores):
    largest = jnp.max(scores, axis=-1, keepdims=True)
    powers = jnp.exp(scores - largest)
    return powers / jnp.sum(powers, axis=-1, keepdims=True)


def project(activations, weight):
    return jnp.einsum("rci,ij->rcj", activations, weight, preferred_element_type=jnp.float32)


def project_back(gradient, weight):
    return jnp.einsum("rcj,ij->rci", gradient, weight, preferred_element_type=jnp.float32)


def weight_grad(activations, gradient):
    return jnp.einsum("rci,rcj->ij", activations, gradient, preferred_element_type=jnp.float32)


def general_plan(
    tokens,
    offsets,
    band,
    col_counts,
    norm1_gain,
    norm1_shift,
    norm2_gain,
    norm2_shift,
    norm3_gain,
    norm3_shift,
    row_query,
    row_key,
    row_value,
    row_output,
    col_query,
    col_key,
    col_value,
    col_output,
    feed_in,
    feed_out,
    cotangent,
):
    rows_dev, cols_dev, model_width = tokens.shape
    total_rows = rows_dev * lax.axis_size("seq")
    total_cols = cols_dev * lax.axis_size("col")
    row_first = lax.axis_index("seq") * rows_dev
    col_first = lax.axis_index("col") * cols_dev
    count_here = col_counts[0].astype(jnp.float32)
    count_early = lax.psum(count_here, "col")
    params = (
        lax.all_gather(norm1_gain, "seq", axis=0, tiled=True),
        lax.all_gather(norm1_shift, "seq", axis=0, tiled=True),
        lax.all_gather(norm2_gain, "seq", axis=0, tiled=True),
        lax.all_gather(norm2_shift, "seq", axis=0, tiled=True),
        lax.all_gather(norm3_gain, "seq", axis=0, tiled=True),
        lax.all_gather(norm3_shift, "seq", axis=0, tiled=True),
        lax.all_gather(row_query, "seq", axis=0, tiled=True),
        lax.all_gather(row_key, "seq", axis=0, tiled=True),
        lax.all_gather(row_value, "seq", axis=0, tiled=True),
        lax.all_gather(row_output, "seq", axis=0, tiled=True),
        lax.all_gather(col_query, "seq", axis=0, tiled=True),
        lax.all_gather(col_key, "seq", axis=0, tiled=True),
        lax.all_gather(col_value, "seq", axis=0, tiled=True),
        lax.all_gather(col_output, "seq", axis=0, tiled=True),
        lax.all_gather(feed_in, "seq", axis=0, tiled=True),
        lax.all_gather(feed_out, "seq", axis=0, tiled=True),
    )
    gain_one = params[0].astype(jnp.float32)
    shift_one = params[1].astype(jnp.float32)
    gain_two = params[2].astype(jnp.float32)
    shift_two = params[3].astype(jnp.float32)
    gain_three = params[4].astype(jnp.float32)
    shift_three = params[5].astype(jnp.float32)
    query_row, key_row, value_row, output_row = (params[6], params[7], params[8], params[9])
    query_col, key_col, value_col, output_col = (params[10], params[11], params[12], params[13])
    feed_up, feed_down = (params[14], params[15])
    stream_zero = tokens.astype(jnp.float32) + position_table(
        offsets, row_first, col_first, rows_dev, cols_dev, model_width
    )
    normed_one, norm_back_one = jax.vjp(layer_norm, stream_zero, gain_one, shift_one)
    normed_one = normed_one.astype(jnp.bfloat16)
    row_queries = project(normed_one, query_row).astype(jnp.bfloat16)
    row_keys = project(normed_one, key_row).astype(jnp.bfloat16)
    row_values = project(normed_one, value_row).astype(jnp.bfloat16)
    extended = with_halo(jnp.stack([row_keys, row_values]), (("col", 2),), WINDOW)
    ext_cols = cols_dev + 2 * WINDOW
    queries_heads = row_queries.reshape(rows_dev, cols_dev, HEADS, HEAD_DIM)
    keys_ext = extended[0].reshape(rows_dev, ext_cols, HEADS, HEAD_DIM)
    values_ext = extended[1].reshape(rows_dev, ext_cols, HEADS, HEAD_DIM)
    partial_logits = jnp.einsum(
        "rchd,rehd->hce", queries_heads, keys_ext, preferred_element_type=jnp.float32
    )
    row_scale = 1.0 / math.sqrt(HEAD_DIM * total_rows)
    row_scores = lax.psum(partial_logits, "seq") * row_scale
    query_index = jnp.arange(cols_dev, dtype=jnp.int32)[:, None]
    key_index = jnp.arange(ext_cols, dtype=jnp.int32)[None, :]
    distance = key_index - query_index
    choose = jnp.arange(2 * WINDOW + 1, dtype=jnp.int32)
    matches = (distance[:, None, :] == choose[None, :, None]) & (band[:, :, None] == 1)
    key_global = col_first - WINDOW + key_index
    inside = (key_global >= 0) & (key_global < total_cols)
    allowed = (jnp.any(matches, axis=1) | (distance == WINDOW)) & inside
    valid = (jnp.arange(cols_dev, dtype=jnp.int32) < col_counts[0]).astype(jnp.float32)
    (row_probs, ent_part), ent_back = jax.vjp(
        lambda given: softmax_entropy(given, allowed, valid), row_scores
    )
    payload = ent_part[None]
    sums = lax.psum(payload, "col")
    entropy = sums[0] / (HEADS * count_early)
    row_probs_low = row_probs.astype(jnp.bfloat16)
    row_mix = jnp.einsum(
        "hce,rehd->rchd", row_probs_low, values_ext, preferred_element_type=jnp.float32
    )
    row_mix = row_mix.reshape(rows_dev, cols_dev, model_width).astype(jnp.bfloat16)
    stream_one = stream_zero + project(row_mix, output_row)
    normed_two, norm_back_two = jax.vjp(layer_norm, stream_one, gain_two, shift_two)
    normed_two = normed_two.astype(jnp.bfloat16)
    col_queries = project(normed_two, query_col).astype(jnp.bfloat16)
    col_keys = project(normed_two, key_col).astype(jnp.bfloat16)
    col_values = project(normed_two, value_col).astype(jnp.bfloat16)
    col_scale = 1.0 / math.sqrt(HEAD_DIM)
    keys_all, values_all = (
        lax.all_gather(col_keys, "seq", axis=0, tiled=True),
        lax.all_gather(col_values, "seq", axis=0, tiled=True),
    )
    col_heads_q = col_queries.reshape(rows_dev, cols_dev, HEADS, HEAD_DIM)
    keys_heads = keys_all.reshape(total_rows, cols_dev, HEADS, HEAD_DIM)
    values_heads = values_all.reshape(total_rows, cols_dev, HEADS, HEAD_DIM)
    col_raw = jnp.einsum(
        "rchd,schd->chrs", col_heads_q, keys_heads, preferred_element_type=jnp.float32
    )
    col_probs = plain_softmax(col_raw * col_scale)
    col_probs_low = col_probs.astype(jnp.bfloat16)
    col_mix = jnp.einsum(
        "chrs,schd->rchd", col_probs_low, values_heads, preferred_element_type=jnp.float32
    )
    col_mix = col_mix.reshape(rows_dev, cols_dev, model_width).astype(jnp.bfloat16)
    stream_two = stream_one + project(col_mix, output_col)
    normed_three, norm_back_three = jax.vjp(layer_norm, stream_two, gain_three, shift_three)
    normed_three = normed_three.astype(jnp.bfloat16)
    hidden_pre = project(normed_three, feed_up)
    hidden_act, gelu_back = jax.vjp(partial(jax.nn.gelu, approximate=False), hidden_pre)
    hidden_low = hidden_act.astype(jnp.bfloat16)
    output = (stream_two + project(hidden_low, feed_down)).astype(jnp.bfloat16)
    grad_feed_down = weight_grad(hidden_low, cotangent)
    grad_hidden = gelu_back(project_back(cotangent, feed_down))[0].astype(jnp.bfloat16)
    grad_feed_up = weight_grad(normed_three, grad_hidden)
    back_stream, grad_gain_three, grad_shift_three = norm_back_three(
        project_back(grad_hidden, feed_up)
    )
    grad_two = cotangent.astype(jnp.float32) + back_stream
    grad_two_low = grad_two.astype(jnp.bfloat16)
    grad_output_col = weight_grad(col_mix, grad_two_low)
    grad_mix_flat = project_back(grad_two_low, output_col).astype(jnp.bfloat16)
    grad_col_mix = grad_mix_flat.reshape(rows_dev, cols_dev, HEADS, HEAD_DIM)
    col_dprobs = jnp.einsum(
        "rchd,schd->chrs", grad_col_mix, values_heads, preferred_element_type=jnp.float32
    )
    col_dscores = col_probs * (col_dprobs - jnp.sum(col_probs * col_dprobs, axis=-1, keepdims=True))
    col_dscores = col_dscores.astype(jnp.bfloat16)
    grad_col_q = (
        jnp.einsum("chrs,schd->rchd", col_dscores, keys_heads, preferred_element_type=jnp.float32)
        * col_scale
    )
    grad_col_q = grad_col_q.reshape(rows_dev, cols_dev, model_width).astype(jnp.bfloat16)
    row_count = lax.axis_size("seq") * rows_dev
    key_part = (
        jnp.einsum("chrs,rchd->schd", col_dscores, col_heads_q, preferred_element_type=jnp.float32)
        * col_scale
    )
    value_part = jnp.einsum(
        "chrs,rchd->schd", col_probs_low, grad_col_mix, preferred_element_type=jnp.float32
    )
    key_value_grads = lax.psum_scatter(
        jnp.concatenate(
            [
                key_part.reshape(row_count, cols_dev, model_width),
                value_part.reshape(row_count, cols_dev, model_width),
            ],
            axis=-1,
        ),
        "seq",
        scatter_dimension=0,
        tiled=True,
    )
    grad_col_k = key_value_grads[..., :model_width].astype(jnp.bfloat16)
    grad_col_v = key_value_grads[..., model_width:].astype(jnp.bfloat16)
    grad_query_col = weight_grad(normed_two, grad_col_q)
    grad_key_col = weight_grad(normed_two, grad_col_k)
    grad_value_col = weight_grad(normed_two, grad_col_v)
    back_input = (
        project_back(grad_col_q, query_col)
        + project_back(grad_col_k, key_col)
        + project_back(grad_col_v, value_col)
    )
    back_stream, grad_gain_two, grad_shift_two = norm_back_two(back_input)
    grad_one = grad_two + back_stream
    grad_one_low = grad_one.astype(jnp.bfloat16)
    grad_output_row = weight_grad(row_mix, grad_one_low)
    grad_row_mix = project_back(grad_one_low, output_row).astype(jnp.bfloat16)
    grad_row_mix = grad_row_mix.reshape(rows_dev, cols_dev, HEADS, HEAD_DIM)
    dprobs_part = jnp.einsum(
        "rchd,rehd->hce", grad_row_mix, values_ext, preferred_element_type=jnp.float32
    )
    row_dprobs = lax.psum(dprobs_part.astype(jnp.bfloat16), "seq").astype(jnp.float32)
    ent_cot = jnp.asarray(entropy_weight, dtype=jnp.float32) / (HEADS * count_early)
    row_dscores = ent_back((row_dprobs, ent_cot))[0].astype(jnp.bfloat16)
    grad_row_q = (
        jnp.einsum("hce,rehd->rchd", row_dscores, keys_ext, preferred_element_type=jnp.float32)
        * row_scale
    )
    grad_row_q = grad_row_q.reshape(rows_dev, cols_dev, model_width).astype(jnp.bfloat16)
    grad_keys_ext = (
        jnp.einsum("hce,rchd->rehd", row_dscores, queries_heads, preferred_element_type=jnp.float32)
        * row_scale
    )
    grad_values_ext = jnp.einsum(
        "hce,rchd->rehd", row_probs_low, grad_row_mix, preferred_element_type=jnp.float32
    )
    grad_ext = jnp.stack([grad_keys_ext, grad_values_ext]).reshape(
        2, rows_dev, ext_cols, model_width
    )
    rims = jnp.concatenate([grad_ext[:, :, :WINDOW], grad_ext[:, :, WINDOW + cols_dev :]], axis=2)
    returned = with_halo(rims.astype(jnp.bfloat16), (("col", 2),), WINDOW).astype(rims.dtype)
    interior = grad_ext[:, :, WINDOW : WINDOW + cols_dev]
    interior = interior.at[:, :, :WINDOW].add(returned[:, :, :WINDOW])
    interior = interior.at[:, :, cols_dev - WINDOW :].add(returned[:, :, 3 * WINDOW :])
    grad_row_k = interior[0].astype(jnp.bfloat16)
    grad_row_v = interior[1].astype(jnp.bfloat16)
    grad_query_row = weight_grad(normed_one, grad_row_q)
    grad_key_row = weight_grad(normed_one, grad_row_k)
    grad_value_row = weight_grad(normed_one, grad_row_v)
    back_input = (
        project_back(grad_row_q, query_row)
        + project_back(grad_row_k, key_row)
        + project_back(grad_row_v, value_row)
    )
    back_stream, grad_gain_one, grad_shift_one = norm_back_one(back_input)
    input_grad = (grad_one + back_stream).astype(jnp.bfloat16)
    shares = (
        lax.psum_scatter(
            grad_gain_one.astype(jnp.bfloat16), "seq", scatter_dimension=0, tiled=True
        ).astype(jnp.float32),
        lax.psum_scatter(
            grad_shift_one.astype(jnp.bfloat16), "seq", scatter_dimension=0, tiled=True
        ).astype(jnp.float32),
        lax.psum_scatter(
            grad_gain_two.astype(jnp.bfloat16), "seq", scatter_dimension=0, tiled=True
        ).astype(jnp.float32),
        lax.psum_scatter(
            grad_shift_two.astype(jnp.bfloat16), "seq", scatter_dimension=0, tiled=True
        ).astype(jnp.float32),
        lax.psum_scatter(
            grad_gain_three.astype(jnp.bfloat16), "seq", scatter_dimension=0, tiled=True
        ).astype(jnp.float32),
        lax.psum_scatter(
            grad_shift_three.astype(jnp.bfloat16), "seq", scatter_dimension=0, tiled=True
        ).astype(jnp.float32),
        lax.psum_scatter(
            grad_query_row.astype(jnp.bfloat16), "seq", scatter_dimension=0, tiled=True
        ).astype(jnp.float32),
        lax.psum_scatter(
            grad_key_row.astype(jnp.bfloat16), "seq", scatter_dimension=0, tiled=True
        ).astype(jnp.float32),
        lax.psum_scatter(
            grad_value_row.astype(jnp.bfloat16), "seq", scatter_dimension=0, tiled=True
        ).astype(jnp.float32),
        lax.psum_scatter(
            grad_output_row.astype(jnp.bfloat16), "seq", scatter_dimension=0, tiled=True
        ).astype(jnp.float32),
        lax.psum_scatter(
            grad_query_col.astype(jnp.bfloat16), "seq", scatter_dimension=0, tiled=True
        ).astype(jnp.float32),
        lax.psum_scatter(
            grad_key_col.astype(jnp.bfloat16), "seq", scatter_dimension=0, tiled=True
        ).astype(jnp.float32),
        lax.psum_scatter(
            grad_value_col.astype(jnp.bfloat16), "seq", scatter_dimension=0, tiled=True
        ).astype(jnp.float32),
        lax.psum_scatter(
            grad_output_col.astype(jnp.bfloat16), "seq", scatter_dimension=0, tiled=True
        ).astype(jnp.float32),
        lax.psum_scatter(
            grad_feed_up.astype(jnp.bfloat16), "seq", scatter_dimension=0, tiled=True
        ).astype(jnp.float32),
        lax.psum_scatter(
            grad_feed_down.astype(jnp.bfloat16), "seq", scatter_dimension=0, tiled=True
        ).astype(jnp.float32),
    )
    totals = (
        lax.psum(shares[0].astype(jnp.bfloat16), "col").astype(jnp.float32),
        lax.psum(shares[1].astype(jnp.bfloat16), "col").astype(jnp.float32),
        lax.psum(shares[2].astype(jnp.bfloat16), "col").astype(jnp.float32),
        lax.psum(shares[3].astype(jnp.bfloat16), "col").astype(jnp.float32),
        lax.psum(shares[4].astype(jnp.bfloat16), "col").astype(jnp.float32),
        lax.psum(shares[5].astype(jnp.bfloat16), "col").astype(jnp.float32),
        lax.psum(shares[6].astype(jnp.bfloat16), "col").astype(jnp.float32),
        lax.psum(shares[7].astype(jnp.bfloat16), "col").astype(jnp.float32),
        lax.psum(shares[8].astype(jnp.bfloat16), "col").astype(jnp.float32),
        lax.psum(shares[9].astype(jnp.bfloat16), "col").astype(jnp.float32),
        lax.psum(shares[10].astype(jnp.bfloat16), "col").astype(jnp.float32),
        lax.psum(shares[11].astype(jnp.bfloat16), "col").astype(jnp.float32),
        lax.psum(shares[12].astype(jnp.bfloat16), "col").astype(jnp.float32),
        lax.psum(shares[13].astype(jnp.bfloat16), "col").astype(jnp.float32),
        lax.psum(shares[14].astype(jnp.bfloat16), "col").astype(jnp.float32),
        lax.psum(shares[15].astype(jnp.bfloat16), "col").astype(jnp.float32),
    )
    return (
        output,
        entropy,
        input_grad,
        totals[0],
        totals[1],
        totals[2],
        totals[3],
        totals[4],
        totals[5],
        totals[6],
        totals[7],
        totals[8],
        totals[9],
        totals[10],
        totals[11],
        totals[12],
        totals[13],
        totals[14],
        totals[15],
    )


def after(values, *needed):
    return lax.optimization_barrier((values, needed))[0]


def kernel_call(
    body, outs, args, smem=(), scratch=(), flops=1, moved=1, stream=False, room=16
):
    out_shapes = [jax.ShapeDtypeStruct(shape, kind) for shape, kind in outs]

    def whole(item):
        if not stream:
            return pl.BlockSpec(memory_space=pltpu.VMEM)
        rank = len(item.shape)
        return pl.BlockSpec(item.shape, lambda step: (0,) * rank, pipeline_mode=pl.Buffered(1))

    return pl.pallas_call(
        body,
        grid=(1,) if stream else (),
        out_shape=out_shapes,
        in_specs=[
            pl.BlockSpec(memory_space=pltpu.SMEM) if place in smem else whole(item)
            for place, item in enumerate(args)
        ],
        out_specs=[whole(item) for item in out_shapes],
        scratch_shapes=list(scratch),
        compiler_params=pltpu.CompilerParams(vmem_limit_bytes=(56 if stream else room) << 20),
        cost_estimate=pl.CostEstimate(
            flops=int(flops), bytes_accessed=int(moved), transcendentals=0
        ),
        name=body.__name__,
    )(*args)


def dot(left, right):
    return jnp.dot(left, right, preferred_element_type=jnp.float32)


def dot_back(left, right):
    return lax.dot_general(
        left, right, (((1,), (1,)), ((), ())), preferred_element_type=jnp.float32
    )


def dot_tokens(left, right):
    return lax.dot_general(
        left, right, (((0,), (0,)), ((), ())), preferred_element_type=jnp.float32
    )


def unit_norm(inputs):
    centred = inputs - jnp.mean(inputs, axis=-1, keepdims=True)
    scale = lax.rsqrt(jnp.mean(centred * centred, axis=-1, keepdims=True) + norm_eps)
    return centred * scale, scale


def unit_norm_back(given, unit, scale, gain):
    scaled = given * gain
    first = jnp.mean(scaled, axis=-1, keepdims=True)
    second = jnp.mean(scaled * unit, axis=-1, keepdims=True)
    return scale * (scaled - first - unit * second)


def norm_sums(given, unit):
    return jnp.concatenate(
        [
            jnp.sum(given * unit, axis=0, keepdims=True),
            jnp.sum(given, axis=0, keepdims=True),
        ],
        axis=0,
    )


def head_mask(width, model_width):
    rows = lax.broadcasted_iota(jnp.int32, (HEADS * width, model_width), 0) // width
    lanes = lax.broadcasted_iota(jnp.int32, (HEADS * width, model_width), 1) // HEAD_DIM
    return rows == lanes


def spread_heads(block, mask):
    tiled = jnp.concatenate([block] * HEADS, axis=0)
    return jnp.where(mask, tiled, jnp.zeros_like(tiled))


def fold_heads(product, mask, width):
    kept = jnp.where(mask, product, 0.0)
    total = kept[:width]
    for head in range(1, HEADS):
        total = total + kept[head * width : (head + 1) * width]
    return total


def head_of_lane(model_width):
    rows = lax.broadcasted_iota(jnp.int32, (model_width, 128), 0) // HEAD_DIM
    lanes = lax.broadcasted_iota(jnp.int32, (model_width, 128), 1)
    return (rows == lanes).astype(jnp.bfloat16)


def per_head_sum(product, lane_heads):
    return dot(product.astype(jnp.bfloat16), lane_heads)


def slot_span(spot_ref, side, slot, width):
    return pl.ds(pl.multiple_of((slot ^ spot_ref[side]) * width, width), width)


def window_rows(spot_ref, near_ref, left_ref, right_ref, which, slot, width):
    return jnp.concatenate(
        [
            left_ref[which, slot_span(spot_ref, 5, slot, width)],
            near_ref[which, slot * width : (slot + 1) * width],
            right_ref[which, slot_span(spot_ref, 6, slot, width)],
        ],
        axis=0,
    )


def half_of(values, core, width):
    return jnp.where(core == 0, values[:, :width], values[:, width:])


def fast_plan(
    tokens,
    offsets,
    band,
    col_counts,
    norms,
    row_weights,
    col_weights,
    feed_in,
    feed_out,
    cotangent,
):
    f32, bf16 = jnp.float32, jnp.bfloat16
    cols_dev, model = tokens.shape[1:]
    cols_axis, seqs = lax.axis_size("col"), lax.axis_size("seq")
    chips = seqs // 2
    width = cols_dev // chips
    toks = chips * width
    shard = model // seqs
    half = model // 2
    hidden = feed_out.shape[0] * seqs // cols_axis
    fold = HEADS * width
    span = 3 * width
    col_at = lax.axis_index("col")
    seq_at = lax.axis_index("seq")
    chip, core = seq_at // 2, seq_at % 2
    flip = col_at % 2

    def chunk_of(chip_index):
        return jnp.where(flip == 0, chip_index, chips - 1 - chip_index)

    chunk = chunk_of(chip)
    piece = col_at * chips + chunk

    def along_chips(values, step):
        return lax.ppermute(values, "seq", [(i, i ^ (2 * step)) for i in range(seqs)])

    def along_core(values):
        return lax.ppermute(values, "seq", [(i, i ^ 1) for i in range(seqs)])

    def along_cols(values, step):
        return lax.ppermute(values, "col", [(i, i ^ step) for i in range(cols_axis)])

    def pair_cols(values):
        pairs = [
            (c * seqs + i, (c ^ (1 + i % 2)) * seqs + i)
            for c in range(cols_axis)
            for i in range(seqs)
        ]
        return lax.ppermute(values, ("col", "seq"), pairs)

    def pair_chips(values):
        pairs = [(i, (i // 2 ^ (1 + i % 2)) * 2 + i % 2) for i in range(seqs)]
        return lax.ppermute(values, "seq", pairs)

    def place_of(piece_index, core_index):
        block, part = divmod(piece_index, chips)
        chip_index = part if block % 2 == 0 else chips - 1 - part
        return block * seqs + chip_index * 2 + core_index

    rightward = [
        (place_of(i, k), place_of(i + 1, k)) for i in range(cols_axis * chips - 1) for k in (0, 1)
    ]
    leftward = [(target, source) for source, target in rightward]

    def to_right(values):
        return lax.ppermute(values, ("col", "seq"), rightward)

    def to_left(values):
        return lax.ppermute(values, ("col", "seq"), leftward)

    steps = range(1, chips)
    col_steps = range(1, cols_axis)

    def turn_to(other):
        block, rest = other // chips, other % chips
        return chip ^ jnp.where(block % 2 == 0, rest, chips - 1 - rest)

    to_left_turn = turn_to(jnp.maximum(piece - 1, 0))
    to_right_turn = turn_to(jnp.minimum(piece + 1, cols_axis * chips - 1))
    spot = jnp.stack(
        [col_at, chip, core, chunk, col_counts[0], to_left_turn, to_right_turn]
    ).astype(jnp.int32)

    half_width = model // 2
    frequency = jnp.exp(-math.log(1000.0) * jnp.arange(half_width, dtype=f32) / half_width)
    col_place = (jnp.arange(width, dtype=jnp.int32) + piece * width + offsets[1]).astype(f32)
    seq_slots = jnp.stack([(chip ^ step) * 2 + core for step in range(chips)])
    row_place = (seq_slots + offsets[0]).astype(f32)
    waves = 0.5 * jnp.sin(
        jnp.concatenate([col_place, row_place])[:, None] * frequency[None, :]
    )
    band_here = lax.dynamic_slice_in_dim(band, chunk * width, width, axis=0)
    query_index = jnp.arange(width, dtype=jnp.int32)[:, None]
    key_index = jnp.arange(span, dtype=jnp.int32)[None, :]
    distance = key_index - query_index
    choose = jnp.arange(2 * WINDOW + 1, dtype=jnp.int32)
    matches = (distance[:, None, :] == choose[None, :, None]) & (band_here[:, :, None] == 1)
    key_global = (piece - 1) * width + key_index
    inside = (key_global >= 0) & (key_global < cols_axis * cols_dev)
    allowed = ((jnp.any(matches, axis=1) | (distance == WINDOW)) & inside).astype(f32)

    quarter = shard // cols_axis
    lines = 8
    hops = chips - 1
    col_rows = cols_axis * quarter
    row_rows = col_rows + lines

    def chunk_at(spot_ref, chip_index):
        at = jnp.where(spot_ref[0] % 2 == 0, chip_index, chips - 1 - chip_index)
        return pl.ds(pl.multiple_of(at * width, width), width)

    def pack(spot_ref, weights, own_ref, send_refs, block):
        at = pl.multiple_of(spot_ref[0] * quarter, quarter)
        size = len(weights) * quarter
        for index, ref in enumerate(weights):
            own_ref[index * shard : (index + 1) * shard] = ref[...]
            for send_ref in send_refs:
                send_ref[index * quarter : (index + 1) * quarter] = ref[pl.ds(at, quarter)]
        if block is not None:
            for ref, row in [(own_ref, len(weights) * shard)] + [
                (ref, size) for ref in send_refs
            ]:
                ref[row : row + lines] = jnp.zeros((lines, model), bf16)
                ref[row : row + lines, :128] = block

    def pack_row(spot_ref, *refs):
        norm_refs, own_ref, send_ref = refs[4:10], refs[10], refs[11]
        block = jnp.zeros((lines, 128), f32)
        rows = lax.broadcasted_iota(jnp.int32, (lines, 128), 0)
        for index, ref in enumerate(norm_refs):
            line = jnp.pad(ref[...].astype(f32), ((0, 0), (0, 128 - shard)))
            block = jnp.where(rows == index, line, block)
        block = jnp.where(rows == 6, spot_ref[4].astype(f32), block).astype(bf16)
        pack(spot_ref, refs[:4], own_ref, [send_ref], block)

    part = feed_out.shape[0] // cols_axis
    block_cols = feed_out.shape[0]

    def pack_rest(spot_ref, *refs):
        token_refs, in_ref, out_ref = refs[4:6], refs[6], refs[7]
        own_ref, chunk_ref, send_refs = refs[8], refs[10], refs[11:]
        pack(spot_ref, refs[:4], refs[9], send_refs, None)
        for index, ref in enumerate(token_refs):
            chunk_ref[index * width : (index + 1) * width] = ref[0, chunk_at(spot_ref, spot_ref[1])]
            for hop, send_ref in enumerate(send_refs):
                at = col_rows + index * width
                send_ref[at : at + width] = ref[0, chunk_at(spot_ref, spot_ref[1] ^ (hop + 1))]
        first = lax.broadcasted_iota(jnp.int32, (block_cols, 128), 0)
        lanes = lax.broadcasted_iota(jnp.int32, (block_cols, 128), 1)
        chosen = ((first == lanes + spot_ref[0] * part) & (lanes < part)).astype(bf16)
        for index in range(seqs):
            block = in_ref[:, index * block_cols : (index + 1) * block_cols]
            own_ref[0, :, index * part : (index + 1) * part] = dot(block, chosen)[
                :, :part
            ].astype(bf16)
        own_ref[1] = out_ref[pl.ds(pl.multiple_of(spot_ref[0] * part, part), part)]

    def stack_row(*refs):
        for hop, ref in enumerate(refs[:-1]):
            refs[-1][hop * row_rows : (hop + 1) * row_rows] = ref[...]

    def stack_col(own_ref, *refs):
        ins, (out_ref, given_ref) = refs[:-2], refs[-2:]
        for slot, ref in enumerate((own_ref, *ins)):
            at = 0 if slot == 0 else col_rows
            given_ref[slot * width : (slot + 1) * width] = ref[at + width : at + 2 * width]
            if slot:
                out_ref[(slot - 1) * col_rows : slot * col_rows] = ref[:col_rows]

    def spread_plane(near, far):
        def join_cores(near_ref, far_ref, out_ref):
            rows = near_ref.shape[0]
            out_ref[:rows] = near_ref[...]
            out_ref[rows:] = far_ref[...]

        both_cores = kernel_call(join_cores, [((2 * near.shape[0], model), bf16)], [near, far])[0]
        return both_cores, pair_cols(both_cores), along_cols(near, cols_axis - 1)

    def place_rows(spot_ref, refs, outs, rows, unit):
        at_col, at_chip, at_core = spot_ref[0], spot_ref[1], spot_ref[2]
        other = 1 - at_core

        def row_of(from_chip, from_core, offset, size):
            return pl.ds(
                pl.multiple_of((from_chip * 2 + from_core) * shard + offset, quarter), size
            )

        pieces = (
            (refs[2], at_col, at_core, 2),
            (refs[3], at_col ^ (1 + at_core), at_core, 2),
            (refs[4], at_col ^ 3, at_core, 1),
            (refs[5], at_col ^ (1 + other), other, 2),
            (refs[6], at_col ^ 3, other, 1),
        )
        for index, (out_ref, lead) in enumerate(outs):
            for ref, core_at in ((refs[0], at_core), (refs[1], other)):
                out_ref[lead + (row_of(at_chip, core_at, 0, shard),)] = ref[
                    index * shard : (index + 1) * shard
                ]
            for ref, col, core_at, sides in pieces:
                for side in range(sides):
                    for hop in steps:
                        at = row_of(at_chip ^ hop, core_at ^ side, col * quarter, quarter)
                        start = side * unit + (hop - 1) * rows + index * quarter
                        out_ref[lead + (at,)] = ref[start : start + quarter]

    row_own, row_send = kernel_call(
        pack_row,
        [((cols_axis * shard + lines, model), bf16), ((row_rows, model), bf16)],
        [spot, *row_weights, *[item[None] for item in norms]],
        smem=(0,),
        stream=True,
    )
    row_got = [along_chips(row_send, step) for step in steps]
    feed_own, col_own, chunks_own, *col_sends = kernel_call(
        pack_rest,
        [
            ((2, shard, hidden), bf16),
            ((cols_axis * shard, model), bf16),
            ((2 * width, model), bf16),
        ]
        + [((col_rows + 2 * width, model), bf16)] * hops,
        [spot, *col_weights, tokens, cotangent, feed_in, feed_out],
        smem=(0,),
        stream=True,
    )
    row_got = after(row_got, waves, allowed, col_sends)
    feed_other = along_core(feed_own)
    row_hops = kernel_call(stack_row, [((hops * row_rows, model), bf16)], row_got)[0]
    row_far_own = along_core(row_own)
    row_plane, row_pair, row_diagonal = spread_plane(row_hops, along_core(row_hops))
    col_sends = after(col_sends, row_plane)
    col_got = [along_chips(col_sends[step - 1], step) for step in steps]

    def pair_feed(own_ref, other_ref, out_ref):
        out_ref[0] = own_ref[...]
        out_ref[1] = other_ref[...]

    feed_both = kernel_call(
        pair_feed, [((2, 2, shard, hidden), bf16)], [feed_own, after(feed_other, row_plane)]
    )[0]
    row_last = after((row_pair, row_diagonal), row_pair, row_diagonal, col_got, feed_both)
    row_pieces = [row_own, row_far_own, row_plane, row_pair, row_diagonal] + [
        along_core(item) for item in row_last
    ]
    def project_row(spot_ref, waves_ref, *refs):
        token_refs, pieces, outs = refs[:chips], refs[chips : chips + 7], refs[chips + 7 :]
        zero_ref, low_ref, q_ref, kv_ref, weight_ref, last_ref, norm_ref = outs
        place_rows(
            spot_ref,
            pieces,
            [(weight_ref, (index,)) for index in range(3)] + [(last_ref, ())],
            row_rows,
            hops * row_rows,
        )
        first = lax.broadcasted_iota(jnp.int32, (128, model), 0)
        lanes = lax.broadcasted_iota(jnp.int32, (128, model), 1)
        total = jnp.zeros((lines, model), f32)
        for side in (0, 1):
            for hop in range(chips):
                if hop == 0:
                    block = pieces[side][cols_axis * shard : cols_axis * shard + lines, :128]
                else:
                    at = (side * hops + hop) * row_rows - lines
                    block = pieces[2][at : at + lines, :128]
                start = ((spot_ref[1] ^ hop) * 2 + (spot_ref[2] ^ side)) * shard
                chosen = ((lanes == first + start) & (first < shard)).astype(bf16)
                total = total + dot(block, chosen)
        count = spot_ref[4].astype(f32)
        for ref in pieces[3:6]:
            count = count + ref[row_rows - lines : row_rows, :128][6:7, 0:1].astype(f32)
        rows = lax.broadcasted_iota(jnp.int32, (lines, model), 0)
        norm_ref[...] = jnp.where(rows == 6, count, total)
        for slot in range(chips):
            rows = slice(slot * width, (slot + 1) * width)
            at = 0 if slot == 0 else col_rows
            stream = token_refs[slot][at : at + width].astype(f32)
            zero_ref[rows, :half] = stream[:, :half] + waves_ref[:width]
            zero_ref[rows, half:] = stream[:, half:] + waves_ref[width + slot : width + slot + 1]
        unit, _ = unit_norm(zero_ref[...])
        low = (unit * norm_ref[0:1] + norm_ref[1:2]).astype(bf16)
        low_ref[...] = low
        q_ref[...] = dot(low, weight_ref[0]).astype(bf16)
        kv_ref[0] = dot(low, weight_ref[1]).astype(bf16)
        kv_ref[1] = dot(low, weight_ref[2]).astype(bf16)

    big = 2.0 * toks * model * model
    stream_zero, normed_one, row_q, row_kv, weights_row, weights_out, norm_rows = kernel_call(
        project_row,
        [
            ((toks, model), f32),
            ((toks, model), bf16),
            ((toks, model), bf16),
            ((2, toks, model), bf16),
            ((3, model, model), bf16),
            ((model, model), bf16),
            ((lines, model), f32),
        ],
        [spot, waves, chunks_own, *col_got, *row_pieces],
        smem=(0,),
    )
    kv_left = to_right(row_kv)
    kv_right = to_left(row_kv)
    col_unit = hops * col_rows
    col_hops, given_out = kernel_call(
        stack_col,
        [((col_unit, model), bf16), ((toks, model), bf16)],
        [after(chunks_own, row_q), *col_got],
    )
    col_far_own = along_core(col_own)
    col_plane, col_pair, col_diagonal = spread_plane(col_hops, along_core(col_hops))

    feed_pair = pair_chips(after(feed_both, row_q))

    def tied_logits(spot_ref, q_ref, near_ref, left_ref, right_ref, out_ref):
        mask = head_mask(width, model)
        total = None
        for slot in range(chips):
            keys = window_rows(spot_ref, near_ref, left_ref, right_ref, 0, slot, width)
            spread = spread_heads(q_ref[slot * width : (slot + 1) * width], mask)
            term = dot_back(spread, keys)
            total = term if total is None else total + term
        out_ref[...] = total

    logits = kernel_call(
        tied_logits,
        [((fold, span), f32)],
        [spot, row_q, row_kv, kv_left, kv_right],
        smem=(0,),
    )[0]
    logits_other = along_core(logits)
    feed_diagonal = along_chips(after(feed_own, logits), chips - 1)
    given_far = after(along_core(given_out), logits)
    row_scale = 1.0 / math.sqrt(HEAD_DIM * seqs)
    col_scale = 1.0 / math.sqrt(HEAD_DIM)

    def attend_row(
        spot_ref,
        logits_ref,
        other_ref,
        allowed_ref,
        near_ref,
        left_ref,
        right_ref,
        zero_ref,
        norm_ref,
        weight_ref,
        scores_ref,
        probs_ref,
        mix_ref,
        stream_ref,
        low_ref,
        entropy_ref,
    ):
        mask = head_mask(width, model)
        scores = (logits_ref[...] + other_ref[...]) * row_scale
        open_here = jnp.concatenate([allowed_ref[...]] * HEADS, axis=0) > 0.5
        masked = jnp.where(open_here, scores, -1000000000.0)
        largest = jnp.max(masked, axis=-1, keepdims=True)
        powers = jnp.exp(masked - largest)
        total = jnp.sum(powers, axis=-1, keepdims=True)
        probs = powers / total
        kept = jnp.where(open_here, scores, 0.0)
        entropies = largest + jnp.log(total) - jnp.sum(probs * kept, axis=-1, keepdims=True)
        rows = lax.broadcasted_iota(jnp.int32, (fold, 1), 0) % width
        entropies = jnp.where(rows + spot_ref[3] * width < spot_ref[4], entropies, 0.0)
        lanes = lax.broadcasted_iota(jnp.int32, (1, model), 1)
        found = jnp.sum(entropies, axis=0, keepdims=True)
        entropy_ref[...] = jnp.where((lanes == 0) & (spot_ref[2] == 0), found, 0.0)
        scores_ref[...] = kept
        probs_ref[...] = probs
        low_probs = probs.astype(bf16)
        for slot in range(chips):
            values = window_rows(spot_ref, near_ref, left_ref, right_ref, 1, slot, width)
            mix_ref[slot * width : (slot + 1) * width] = fold_heads(
                dot(low_probs, values), mask, width
            ).astype(bf16)
        stream = zero_ref[...] + dot(mix_ref[...], weight_ref[...])
        stream_ref[...] = stream
        unit, _ = unit_norm(stream)
        low_ref[...] = (unit * norm_ref[2:3] + norm_ref[3:4]).astype(bf16)

    scores, probs, row_mix, stream_one, normed_two, entropy_row = kernel_call(
        attend_row,
        [
            ((fold, span), f32),
            ((fold, span), f32),
            ((toks, model), bf16),
            ((toks, model), f32),
            ((toks, model), bf16),
            ((1, model), f32),
        ],
        [
            spot,
            logits,
            logits_other,
            allowed,
            row_kv,
            kv_left,
            kv_right,
            stream_zero,
            norm_rows,
            weights_out,
        ],
        smem=(0,),
    )

    col_last = after((col_pair, col_diagonal), normed_two, feed_pair)
    col_pieces = [col_own, col_far_own, col_plane, col_pair, col_diagonal] + [
        along_core(item) for item in col_last
    ]

    def assemble_col(spot_ref, *refs):
        three_ref, last_ref = refs[7:]
        outs = [(three_ref, (index,)) for index in range(3)] + [(last_ref, ())]
        place_rows(spot_ref, refs[:7], outs, col_rows, col_unit)

    weights_three, weights_last = kernel_call(
        assemble_col,
        [((3, model, model), bf16), ((model, model), bf16)],
        [spot, *col_pieces],
        smem=(0,),
    )

    def project_col(low_ref, weight_ref, q_ref, k_ref, v_ref):
        low = low_ref[...]
        q_ref[...] = dot(low, weight_ref[0]).astype(bf16)
        k_ref[...] = dot(low, weight_ref[1]).astype(bf16)
        v_ref[...] = dot(low, weight_ref[2]).astype(bf16)

    col_q, col_k, col_v = kernel_call(
        project_col,
        [((toks, model), bf16)] * 3,
        [normed_two, weights_three],
    )
    k_other, v_other = along_core(col_k), along_core(col_v)

    def join_given(near_ref, far_ref, out_ref):
        out_ref[:toks] = near_ref[...]
        out_ref[toks:] = far_ref[...]

    given_both = kernel_call(join_given, [((2 * toks, model), bf16)], [given_out, given_far])[0]
    given_pair = pair_cols(given_both)

    def slot_rows(slot):
        return slice(slot * width, (slot + 1) * width)

    def attend_col(
        q_ref,
        k_ref,
        v_ref,
        k2_ref,
        v2_ref,
        one_ref,
        norm_ref,
        weight_ref,
        given_ref,
        probs_ref,
        mix_ref,
        stream_ref,
        low_ref,
        message_ref,
    ):
        lane_heads = head_of_lane(model)
        sides = ((k_ref, v_ref), (k2_ref, v2_ref))
        for slot in range(chips):
            query = q_ref[slot_rows(slot)]
            products = jnp.concatenate(
                [
                    query * sides[s // chips][0][slot_rows(s % chips)]
                    for s in range(seqs)
                ],
                axis=0,
            )
            found = per_head_sum(products, lane_heads) * col_scale
            parts = [found[s * width : (s + 1) * width] for s in range(seqs)]
            largest = parts[0]
            for item in parts[1:]:
                largest = jnp.maximum(largest, item)
            powers = [jnp.exp(item - largest) for item in parts]
            total = powers[0]
            for item in powers[1:]:
                total = total + item
            weights = jnp.concatenate([item / total for item in powers], axis=0)
            probs_ref[slot] = weights
            wide = dot_back(weights.astype(bf16), lane_heads)
            mixed = None
            for s in range(seqs):
                term = wide[s * width : (s + 1) * width] * sides[s // chips][1][
                    slot_rows(s % chips)
                ].astype(f32)
                mixed = term if mixed is None else mixed + term
            mix_ref[slot_rows(slot)] = mixed.astype(bf16)
        stream = one_ref[...] + dot(mix_ref[...], weight_ref[...])
        stream_ref[...] = stream
        unit, _ = unit_norm(stream)
        low = (unit * norm_ref[4:5] + norm_ref[5:6]).astype(bf16)
        low_ref[...] = low
        message_ref[:toks] = low
        message_ref[toks:] = given_ref[...]

    col_probs, col_mix, stream_two, normed_three, message = kernel_call(
        attend_col,
        [
            ((chips, seqs * width, 128), f32),
            ((toks, model), bf16),
            ((toks, model), f32),
            ((toks, model), bf16),
            ((2 * toks, model), bf16),
        ],
        [col_q, col_k, col_v, k_other, v_other, stream_one, norm_rows, weights_last, given_out],
    )
    low_near = [
        normed_three,
        along_cols(normed_three, 1),
        along_cols(normed_three, 2),
        along_cols(message, 3),
    ]

    feed_last = after((feed_pair, feed_diagonal, given_pair), low_near)
    feed_far = [along_core(item) for item in feed_last]

    def assemble_feed(
        spot_ref,
        both_ref,
        pair_ref,
        last_ref,
        pair2_ref,
        last2_ref,
        d0_ref,
        d1_ref,
        d2_ref,
        d3_ref,
        out_ref,
        given_ref,
    ):
        at_chip, at_core = spot_ref[1], spot_ref[2]
        other = 1 - at_core

        def move(rows, from_chip, from_core):
            at = pl.multiple_of((from_chip * 2 + from_core) * shard, shard)
            out_ref[:, pl.ds(at, shard)] = rows

        for side in (0, 1):
            move(both_ref[side], at_chip, at_core ^ side)
            move(pair_ref[side], at_chip ^ (1 + at_core), at_core ^ side)
            move(pair2_ref[side], at_chip ^ (1 + other), other ^ side)
        move(last_ref[...], at_chip ^ 3, at_core)
        move(last2_ref[...], at_chip ^ 3, other)
        given_ref[0] = d0_ref[...]
        given_ref[1 + at_core] = d1_ref[:toks]
        given_ref[2 - at_core] = d2_ref[toks:]
        given_ref[3] = d3_ref[toks:]

    weights_feed, given_all = kernel_call(
        assemble_feed,
        [((2, model, hidden), bf16), ((cols_axis, toks, model), bf16)],
        [
            spot,
            feed_both,
            feed_pair,
            feed_diagonal,
            feed_far[0],
            feed_far[1],
            given_out,
            given_pair,
            feed_far[2],
            low_near[3],
        ],
        smem=(0,),
    )

    def feed_main(a0, a1, a2, a3, given_ref, weight_ref, act_ref, grad_ref, *back_refs):
        up, down = weight_ref[0], weight_ref[1]
        rows = cols_axis * toks
        low = jnp.concatenate([ref[:toks] for ref in (a0, a1, a2, a3)], axis=0)
        pre = dot(low, up)
        bell = 0.5 * (1.0 + lax.erf(pre * (0.5**0.5)))
        slope = bell + pre * jnp.exp(-0.5 * pre * pre) * ((0.5 / math.pi) ** 0.5)
        act_ref[...] = (pre * bell).astype(bf16).reshape(cols_axis, toks, hidden)
        grad = (slope * dot_back(given_ref[...].reshape(rows, model), down)).astype(bf16)
        grad_ref[...] = grad.reshape(cols_axis, toks, hidden)
        back = dot_back(grad, up).astype(bf16)
        for step in range(cols_axis):
            back_refs[step][...] = back[step * toks : (step + 1) * toks]

    feed_results = kernel_call(
        feed_main,
        [((cols_axis, toks, hidden), bf16)] * 2 + [((toks, model), bf16)] * cols_axis,
        [*low_near, given_all, weights_feed],
    )
    act, grad_hidden, back_parts = feed_results[0], feed_results[1], feed_results[2:]
    back_near = [back_parts[0]] + [along_cols(back_parts[step], step) for step in col_steps]

    def feed_weights(
        spot_ref, a0, a1, a2, a3, given_ref, act_ref, grad_ref, weight_ref, mine_ref, give_ref, *outs
    ):
        at_core = spot_ref[2]
        low = jnp.concatenate([a0[...], a1[...], a2[...], a3[:toks]], axis=0)
        given = given_ref[...].reshape(cols_axis * toks, model)
        rows = cols_axis * toks
        acts = act_ref[...].reshape(rows, hidden)
        grads = grad_ref[...].reshape(rows, hidden)
        for step in range(cols_axis):
            outs[step][...] = dot(act_ref[step], weight_ref[1]).astype(bf16)
        for ref, at in ((mine_ref, at_core), (give_ref, 1 - at_core)):
            ref[:model] = dot_tokens(low, half_of(grads, at, half)).astype(bf16)
            ref[model:] = dot_tokens(acts, half_of(given, at, half)).astype(bf16)

    feed_grads = kernel_call(
        feed_weights,
        [((2 * model, half), bf16)] * 2 + [((toks, model), bf16)] * cols_axis,
        [spot, *low_near, given_all, act, grad_hidden, weights_feed],
        smem=(0,),
        flops=6.0 * toks * cols_axis * model * hidden,
        moved=16 << 20,
        room=24,
    )
    feed_mine, feed_give, out_parts = feed_grads[0], feed_grads[1], feed_grads[2:]

    block = 2 * shard
    extra = 2 * lines

    def renew(total, at):
        line = total[at : at + 1]
        whole = line[:, 0:1] + line[:, 1:2]
        high = whole.astype(bf16).astype(f32)
        lanes = lax.broadcasted_iota(jnp.int32, total.shape, 1)
        rows = lax.broadcasted_iota(jnp.int32, total.shape, 0)
        total = jnp.where((rows == at) & (lanes == 0), high, total)
        return jnp.where((rows == at) & (lanes == 1), whole - high, total)

    near_rows = model // 2

    def row_layer_grads(low, mix, low_far, mix_far, mine, got, more):
        norms_too = len(more) == 1
        size = near_rows + (0 if norms_too else toks)
        tail = extra if norms_too else 0

        def row_weight_sums(spot_ref, low_ref, mix_ref, low2_ref, mix2_ref, mine_ref, got_ref, *refs):
            more_refs, (x_ref, y_ref, a_ref, b_ref) = refs[: len(more)], refs[len(more) : -2]
            left_ref, right_ref = refs[-2:]
            left_ref[0, :toks] = low_ref[...]
            left_ref[0, toks:] = low2_ref[...]
            left_ref[1, :toks] = mix_ref[...]
            left_ref[1, toks:] = mix2_ref[...]
            right_ref[:, :toks] = mine_ref[...]
            right_ref[:, toks:] = got_ref[...]
            places = (
                ((a_ref, 0), (b_ref, 0)),
                ((x_ref, 0), (b_ref, 1)),
                ((a_ref, 1), (y_ref, 0)),
                ((x_ref, 1), (y_ref, 1)),
            )
            for step in range(cols_axis):
                matrix = spot_ref[0] ^ step
                left = left_ref[matrix // 3]
                found = dot_tokens(left, right_ref[matrix]).astype(bf16)
                for part_index, (ref, at) in enumerate(places[step]):
                    start = at * size
                    ref[start : start + near_rows] = found[
                        part_index * near_rows : (part_index + 1) * near_rows
                    ]
                    if not norms_too:
                        lanes = slice(part_index * half, (part_index + 1) * half)
                        ref[start + near_rows : start + size] = more_refs[step][:, lanes]
            if norms_too:
                sums_ref = more_refs[0]
                line = jnp.concatenate([sums_ref[:, :half], sums_ref[:, half:]], axis=0)
                line = renew(line, 6).astype(bf16)
                for ref in (x_ref, a_ref):
                    ref[2 * size :] = line

        outs = [((2 * size + tail, half), bf16), ((2 * size, half), bf16)] * 2
        return kernel_call(
            row_weight_sums,
            outs,
            [spot, low, mix, low_far, mix_far, mine, got, *more],
            smem=(0,),
            scratch=[
                pltpu.VMEM((2, 2 * toks, model), bf16),
                pltpu.VMEM((4, 2 * toks, half), bf16),
            ],
        )

    def fold_pairs(parts, got_x, got_y, tail):
        a_part, b_part = parts[2:]
        size = b_part.shape[0] // 2

        def pair_sums(a_ref, x_ref, b_ref, y_ref, keep_ref, give_ref, keep2_ref, give2_ref):
            first = a_ref[...].astype(f32) + x_ref[...].astype(f32)
            second = b_ref[...].astype(f32) + y_ref[...].astype(f32)
            keep_ref[:size] = first[:size].astype(bf16)
            give_ref[:size] = first[size : 2 * size].astype(bf16)
            keep2_ref[...] = second[:size].astype(bf16)
            give2_ref[...] = second[size:].astype(bf16)
            if tail:
                line = renew(first[2 * size :], 6).astype(bf16)
                keep_ref[size:] = line
                give_ref[size:] = line

        return kernel_call(
            pair_sums,
            [((size + tail, half), bf16)] * 2 + [((size, half), bf16)] * 2,
            [a_part, got_x, b_part, got_y],
        )

    def row_layer_chips(keep, got, keep2, got2, tail, stream, slots):
        sent_rows = 2 * width * (bool(stream) + bool(slots))

        def layer_parts(spot_ref, a_ref, ga_ref, b_ref, gb_ref, *refs):
            more, outs, total_ref = refs[: -chips - 1], refs[-chips - 1 : -1], refs[-1]
            first = a_ref[...].astype(f32) + ga_ref[...].astype(f32)
            second = b_ref[...].astype(f32) + gb_ref[...].astype(f32)
            total_ref[:near_rows] = first[:near_rows].astype(bf16)
            total_ref[near_rows:] = second[:near_rows].astype(bf16)
            if stream:
                result = more[0][...] + jnp.concatenate(
                    [first[near_rows:], second[near_rows:]], axis=1
                )
            for hop in range(chips):
                at = pl.multiple_of((spot_ref[1] ^ hop) * block, block)
                outs[hop][:block] = total_ref[pl.ds(at, block)]
                row = block
                if tail:
                    outs[hop][row : row + tail] = renew(first[near_rows:], 6).astype(bf16)
                    row = row + tail
                sent = []
                if stream:
                    sent.append(result[slot_rows(hop)].astype(bf16))
                if slots:
                    sent.append(more[hop - chips][...])
                for slot in sent:
                    outs[hop][row : row + width] = slot[:, :half]
                    outs[hop][row + width : row + 2 * width] = slot[:, half:]
                    row = row + 2 * width

        return kernel_call(
            layer_parts,
            [((block + tail + sent_rows, half), bf16)] * chips,
            [spot, keep, got, keep2, got2, *stream, *slots],
            smem=(0,),
            scratch=[pltpu.VMEM((model, half), bf16)],
        )

    def layer_grads(low, mix, low_far, mix_far, mine, got, more):
        rows = model + (extra if len(more) == 1 else 2 * toks)

        def weight_sums(spot_ref, low_ref, mix_ref, low2_ref, mix2_ref, mine_ref, got_ref, *refs):
            more_refs, outs = refs[: len(more)], refs[len(more) : -2]
            left_ref, right_ref = refs[-2:]
            left_ref[0, :toks] = low_ref[...]
            left_ref[0, toks:] = low2_ref[...]
            left_ref[1, :toks] = mix_ref[...]
            left_ref[1, toks:] = mix2_ref[...]
            right_ref[:, :toks] = mine_ref[...]
            right_ref[:, toks:] = got_ref[...]
            for step in range(cols_axis):
                matrix = spot_ref[0] ^ step
                left = left_ref[matrix // 3]
                outs[step][:model] = dot_tokens(left, right_ref[matrix]).astype(bf16)
                if len(more) == 1:
                    sums_ref = more_refs[0]
                    tail = jnp.concatenate([sums_ref[:, :half], sums_ref[:, half:]], axis=0)
                    outs[step][model:] = renew(tail, 6).astype(bf16)
                else:
                    outs[step][model : model + toks] = more_refs[step][:, :half]
                    outs[step][model + toks :] = more_refs[step][:, half:]

        return kernel_call(
            weight_sums,
            [((rows, half), bf16)] * cols_axis,
            [spot, low, mix, low_far, mix_far, mine, got, *more],
            smem=(0,),
            scratch=[
                pltpu.VMEM((2, 2 * toks, model), bf16),
                pltpu.VMEM((4, 2 * toks, half), bf16),
            ],
        )

    def split_chips(items, count, tail, stream=None, slots=()):
        slot_rows_out = 2 * width * ((stream is not None) + bool(slots))

        def chip_parts(spot_ref, *refs):
            ins, outs, total_ref = refs[: len(items)], refs[-chips - 1 : -1], refs[-1]
            more = refs[len(items) : -chips - 1]
            total = ins[0][...].astype(f32)
            for ref in ins[1:]:
                total = total + ref[...].astype(f32)
            total_ref[...] = total.astype(bf16)
            if stream is not None:
                result = more[0][...] + jnp.concatenate(
                    [total[model : model + toks], total[model + toks :]], axis=1
                )
            for hop in range(chips):
                at = pl.multiple_of((spot_ref[1] ^ hop) * block, block)
                for index in range(count):
                    outs[hop][index * block : (index + 1) * block] = total_ref[
                        pl.ds(index * model + at, block)
                    ]
                row = count * block
                if tail:
                    outs[hop][row : row + tail] = renew(total[count * model :], 6).astype(bf16)
                    row = row + tail
                sent = []
                if stream is not None:
                    sent.append(result[slot_rows(hop)].astype(bf16))
                if slots:
                    sent.append(more[hop - chips][...])
                for slot in sent:
                    outs[hop][row : row + width] = slot[:, :half]
                    outs[hop][row + width : row + 2 * width] = slot[:, half:]
                    row = row + 2 * width

        size = count * block + tail + slot_rows_out
        return kernel_call(
            chip_parts,
            [((size, half), bf16)] * chips,
            [spot, *items] + ([] if stream is None else [stream]) + list(slots),
            smem=(0,),
            scratch=[pltpu.VMEM(items[0].shape, bf16)],
        )

    def split_cores(items, count, tail):
        rows_in = count * block + tail

        def core_parts(spot_ref, *refs):
            ins, (keep_ref, give_ref, total_ref) = refs[: len(items)], refs[len(items) :]
            total = ins[0][:rows_in].astype(f32)
            for ref in ins[1:]:
                total = total + ref[:rows_in].astype(f32)
            total_ref[...] = total.astype(bf16)
            for ref, at in ((keep_ref, spot_ref[2]), (give_ref, 1 - spot_ref[2])):
                for index in range(count):
                    row = pl.multiple_of(index * block + at * shard, shard)
                    ref[index * shard : (index + 1) * shard] = total_ref[pl.ds(row, shard)]
                if tail:
                    ref[count * shard :] = renew(total[count * block :], 6).astype(bf16)

        size = count * shard + tail
        return kernel_call(
            core_parts,
            [((size, half), bf16)] * 2,
            [spot, *items],
            smem=(0,),
            scratch=[pltpu.VMEM((rows_in, half), bf16)],
        )

    def over_chips(parts):
        return [parts[0]] + [along_chips(parts[step], step) for step in steps]

    back_near = after(back_near, feed_mine)

    def attend_col_back(
        spot_ref,
        b0,
        b1,
        b2,
        b3,
        given_ref,
        two_ref,
        norm_ref,
        weight_ref,
        q_ref,
        k_ref,
        v_ref,
        k2_ref,
        v2_ref,
        probs_ref,
        dtwo_ref,
        low_ref,
        dq_ref,
        dkv_ref,
        send_ref,
        sums_ref,
    ):
        lane_heads = head_of_lane(model)
        back = b0[...].astype(f32) + b1[...].astype(f32) + b2[...].astype(f32) + b3[...].astype(f32)
        unit, scale = unit_norm(two_ref[...])
        sums_ref[...] = norm_sums(back, unit)
        dtwo = given_ref[0].astype(f32) + unit_norm_back(back, unit, scale, norm_ref[4:5])
        dtwo_ref[...] = dtwo
        low = dtwo.astype(bf16)
        low_ref[...] = low
        dmix_low = dot_back(low, weight_ref[...]).astype(bf16)
        dmix = dmix_low.astype(f32)
        sides = ((k_ref, v_ref), (k2_ref, v2_ref))
        rows = seqs * width
        products = jnp.concatenate(
            [
                dmix_low[slot_rows(slot)] * sides[s // chips][1][slot_rows(s % chips)]
                for slot in range(chips)
                for s in range(seqs)
            ],
            axis=0,
        )
        found_all = per_head_sum(products, lane_heads)
        dscores = []
        for slot in range(chips):
            found = found_all[slot * rows : (slot + 1) * rows]
            weights = probs_ref[slot]
            mean = None
            for s in range(seqs):
                at = slice(s * width, (s + 1) * width)
                term = weights[at] * found[at]
                mean = term if mean is None else mean + term
            dscores.append(
                (weights * (found - jnp.concatenate([mean] * seqs, axis=0))).astype(bf16)
            )
        wide_d = dot_back(jnp.concatenate(dscores, axis=0), lane_heads)
        wide_p = dot_back(probs_ref[...].astype(bf16).reshape(chips * rows, 128), lane_heads)

        def piece(wide, slot, s):
            start = slot * rows + s * width
            return wide[start : start + width]

        for slot in range(chips):
            dquery = None
            for s in range(seqs):
                term = piece(wide_d, slot, s) * sides[s // chips][0][
                    slot_rows(s % chips)
                ].astype(f32)
                dquery = term if dquery is None else dquery + term
            dq_ref[slot_rows(slot)] = (dquery * col_scale).astype(bf16)
        for s in range(seqs):
            dkey, dvalue = None, None
            for slot in range(chips):
                key_term = piece(wide_d, slot, s) * q_ref[slot_rows(slot)].astype(f32)
                value_term = piece(wide_p, slot, s) * dmix[slot_rows(slot)]
                dkey = key_term if dkey is None else dkey + key_term
                dvalue = value_term if dvalue is None else dvalue + value_term
            at = slot_rows(s % chips)
            if s < chips:
                dkv_ref[0, at] = dkey * col_scale
                dkv_ref[1, at] = dvalue
            else:
                send_ref[0, at] = (dkey * col_scale).astype(bf16)
                send_ref[1, at] = dvalue.astype(bf16)

    grad_two, grad_two_low, col_dq, col_dkv, col_send, sums_three = kernel_call(
        attend_col_back,
        [
            ((toks, model), f32),
            ((toks, model), bf16),
            ((toks, model), bf16),
            ((2, toks, model), f32),
            ((2, toks, model), bf16),
            ((2, model), f32),
        ],
        [
            spot,
            *back_near,
            given_all,
            stream_two,
            norm_rows,
            weights_last,
            col_q,
            col_k,
            col_v,
            k_other,
            v_other,
            col_probs,
        ],
        smem=(0,),
        room=24,
    )
    row_low_far, row_mix_far = along_core(normed_one), along_core(row_mix)
    col_low_far, col_mix_far = along_core(normed_two), along_core(col_mix)
    dkv_got = after(along_core(col_send), row_low_far, row_mix_far)

    def row_entry_back(
        spot_ref,
        dq_ref,
        dkv_ref,
        got_ref,
        low_two_ref,
        dtwo_ref,
        one_ref,
        norm_ref,
        col_ref,
        row_ref,
        near_ref,
        left_ref,
        right_ref,
        mine_ref,
        give_ref,
        done_ref,
        low_ref,
        dmix_ref,
        dprobs_ref,
        sums_ref,
    ):
        at_core = spot_ref[2]
        dq = dq_ref[...]
        dk = (dkv_ref[0] + got_ref[0].astype(f32)).astype(bf16)
        dv = (dkv_ref[1] + got_ref[1].astype(f32)).astype(bf16)
        for index, item in enumerate((dq, dk, dv, low_two_ref[...])):
            mine_ref[index] = half_of(item, at_core, half)
            give_ref[index] = half_of(item, 1 - at_core, half)
        back = dot_back(dq, col_ref[0]) + dot_back(dk, col_ref[1]) + dot_back(dv, col_ref[2])
        unit, scale = unit_norm(one_ref[...])
        sums_ref[...] = norm_sums(back, unit)
        done = dtwo_ref[...] + unit_norm_back(back, unit, scale, norm_ref[2:3])
        done_ref[...] = done
        low = done.astype(bf16)
        low_ref[...] = low
        dmix = dot_back(low, row_ref[...]).astype(bf16)
        dmix_ref[...] = dmix
        mask = head_mask(width, model)
        total = None
        for slot in range(chips):
            values = window_rows(spot_ref, near_ref, left_ref, right_ref, 1, slot, width)
            term = dot_back(spread_heads(dmix[slot_rows(slot)], mask), values)
            total = term if total is None else total + term
        dprobs_ref[...] = total

    (
        col_mine,
        col_give,
        grad_one,
        grad_one_low,
        row_dmix,
        dprobs,
        sums_two,
    ) = kernel_call(
        row_entry_back,
        [
            ((4, toks, half), bf16),
            ((4, toks, half), bf16),
            ((toks, model), f32),
            ((toks, model), bf16),
            ((toks, model), bf16),
            ((fold, span), f32),
            ((2, model), f32),
        ],
        [
            spot,
            col_dq,
            col_dkv,
            dkv_got,
            grad_two_low,
            grad_two,
            stream_one,
            norm_rows,
            weights_three,
            weights_out,
            row_kv,
            kv_left,
            kv_right,
        ],
        smem=(0,),
    )
    dprobs_other = along_core(dprobs)

    def attend_row_back(
        spot_ref,
        weight_ref,
        dprobs_ref,
        other_ref,
        scores_ref,
        probs_ref,
        q_ref,
        near_ref,
        left_ref,
        right_ref,
        dmix_ref,
        dq_ref,
        dkv_ref,
        to_left_ref,
        to_right_ref,
    ):
        mask = head_mask(width, model)
        dprob = dprobs_ref[...] + other_ref[...]
        probs_here, scores_here = probs_ref[...], scores_ref[...]
        rows = lax.broadcasted_iota(jnp.int32, (fold, 1), 0) % width
        weight = jnp.where(rows + spot_ref[3] * width < spot_ref[4], entropy_weight / (HEADS * weight_ref[6:7, 0:1]), 0.0)
        first = dprob - jnp.sum(probs_here * dprob, axis=-1, keepdims=True)
        second = scores_here - jnp.sum(probs_here * scores_here, axis=-1, keepdims=True)
        dscores = (probs_here * (first - weight * second)).astype(bf16)
        low_probs = probs_here.astype(bf16)
        for slot in range(chips):
            at = slot_rows(slot)
            keys = window_rows(spot_ref, near_ref, left_ref, right_ref, 0, slot, width)
            dq_ref[at] = (
                fold_heads(dot(dscores, keys), mask, width) * row_scale
            ).astype(bf16)
            dkeys = dot_tokens(dscores, spread_heads(q_ref[at], mask)) * row_scale
            dvalues = dot_tokens(low_probs, spread_heads(dmix_ref[at], mask))
            for index, item in enumerate((dkeys, dvalues)):
                to_left_ref[index, at] = item[:width].astype(bf16)
                dkv_ref[index, at] = item[width : 2 * width]
                to_right_ref[index, at] = item[2 * width :].astype(bf16)

    row_dq, row_dkv, edge_left, edge_right = kernel_call(
        attend_row_back,
        [
            ((toks, model), bf16),
            ((2, toks, model), f32),
            ((2, toks, model), bf16),
            ((2, toks, model), bf16),
        ],
        [
            spot,
            norm_rows,
            dprobs,
            dprobs_other,
            scores,
            probs,
            row_q,
            row_kv,
            kv_left,
            kv_right,
            row_dmix,
        ],
        smem=(0,),
    )
    col_sums = layer_grads(
        normed_two,
        col_mix,
        col_low_far,
        col_mix_far,
        col_mine,
        after(along_core(col_give), edge_left),
        out_parts,
    )
    edge_from_right = to_left(edge_left)
    edge_from_left = to_right(edge_right)
    feed_slices = split_chips([feed_mine, along_core(after(feed_give, edge_left))], 2, 0)
    feed_keep, feed_swap = split_cores(over_chips(feed_slices), 2, 0)

    def input_back(
        spot_ref,
        dq_ref,
        dkv_ref,
        from_right_ref,
        from_left_ref,
        low_one_ref,
        done_ref,
        zero_ref,
        norm_ref,
        row_ref,
        two_ref,
        three_ref,
        entropy_ref,
        mine_ref,
        give_ref,
        sums_ref,
        *slot_refs,
    ):
        at_core = spot_ref[2]
        dq = dq_ref[...]
        dk, dv = (
            jnp.concatenate(
                [
                    (
                        dkv_ref[index, slot_rows(slot)]
                        + from_left_ref[index, slot_span(spot_ref, 5, slot, width)].astype(f32)
                        + from_right_ref[index, slot_span(spot_ref, 6, slot, width)].astype(f32)
                    ).astype(bf16)
                    for slot in range(chips)
                ],
                axis=0,
            )
            for index in (0, 1)
        )
        for index, item in enumerate((dq, dk, dv, low_one_ref[...])):
            mine_ref[index] = half_of(item, at_core, half)
            give_ref[index] = half_of(item, 1 - at_core, half)
        back = dot_back(dq, row_ref[0]) + dot_back(dk, row_ref[1]) + dot_back(dv, row_ref[2])
        unit, scale = unit_norm(zero_ref[...])
        sums_ref[0:2] = norm_sums(back, unit)
        sums_ref[2:4] = two_ref[...]
        sums_ref[4:6] = three_ref[...]
        sums_ref[6:7] = entropy_ref[...]
        sums_ref[7:8] = jnp.zeros((1, model), f32)
        result = (done_ref[...] + unit_norm_back(back, unit, scale, norm_ref[0:1])).astype(bf16)
        for slot in range(chips):
            slot_refs[slot][...] = result[slot_rows(slot)]

    row_mine, row_give, sums, *grad_slots = kernel_call(
        input_back,
        [
            ((4, toks, half), bf16),
            ((4, toks, half), bf16),
            ((lines, model), f32),
        ]
        + [((width, model), bf16)] * chips,
        [
            spot,
            row_dq,
            row_dkv,
            edge_from_right,
            edge_from_left,
            grad_one_low,
            grad_one,
            stream_zero,
            norm_rows,
            weights_row,
            sums_two,
            sums_three,
            entropy_row,
        ],
        smem=(0,),
    )

    def join_halves(spot_ref, keep_rows, got_rows):
        first = spot_ref[2] == 0
        return jnp.concatenate(
            [jnp.where(first, keep_rows, got_rows), jnp.where(first, got_rows, keep_rows)], axis=1
        )

    def over_cols(whole):
        return [whole] + [along_cols(whole, step) for step in col_steps]

    def order_rows(slices, at):
        def order_slots(spot_ref, *refs):
            for hop, ref in enumerate(refs[:-1]):
                refs[-1][0, chunk_at(spot_ref, spot_ref[1] ^ hop)] = jnp.concatenate(
                    [ref[at : at + width], ref[at + width : at + 2 * width]], axis=1
                )

        return kernel_call(order_slots, [(tokens.shape, bf16)], [spot, *slices], smem=(0,))[0]

    feed_back = along_core(feed_swap)
    col_parts = [col_sums[0]] + [along_cols(col_sums[step], step) for step in col_steps]
    col_slices = split_chips(col_parts, 1, 0, stream=stream_two, slots=grad_slots)
    col_reached = over_chips(col_slices)
    col_keep, col_swap = split_cores(col_reached, 1, 0)

    def join_two(spot_ref, keep_ref, got_ref, keep2_ref, got2_ref, out_ref):
        rows = 2 * shard
        out_ref[:rows] = join_halves(spot_ref, keep_ref[...], got_ref[...])
        out_ref[rows:] = join_halves(spot_ref, keep2_ref[...], got2_ref[...])

    (pair,) = kernel_call(
        join_two,
        [((3 * shard, model), bf16)],
        [spot, feed_keep, feed_back, col_keep, along_core(col_swap)],
        smem=(0,),
    )
    pair_ends = over_cols(pair)

    def spread_pair(spot_ref, u0, u1, u2, u3, in_ref, out_ref, g0, g1, g2, g3, all_ref):
        for step, ref in enumerate((u0, u1, u2, u3)):
            all_ref[spot_ref[0] ^ step] = ref[...]
        for source, grad_ref in enumerate((g0, g1, g2, g3)):
            wide = all_ref[source, :shard].astype(f32)
            for index in range(seqs):
                at = index * block_cols + source * part
                in_ref[:, at : at + part] = wide[:, index * part : (index + 1) * part]
            out_ref[source * part : (source + 1) * part] = all_ref[
                source, shard : 2 * shard
            ].astype(f32)
            grad_ref[...] = all_ref[source, 2 * shard :].astype(f32)

    row_parts = row_layer_grads(
        normed_one,
        row_mix,
        row_low_far,
        row_mix_far,
        row_mine,
        along_core(row_give),
        [sums],
    )
    row_sends = after(row_parts, col_parts, feed_keep)
    row_x, row_y = along_cols(row_sends[0], 1), along_cols(row_sends[1], 2)
    keep, give, keep2, give2 = fold_pairs(row_parts, row_x, row_y, extra)
    row_slices = row_layer_chips(
        keep, along_cols(give, 2), keep2, along_cols(give2, 1), extra, [], []
    )
    row_reached = over_chips(row_slices)
    row_keep, row_swap = split_cores(row_reached, 1, extra)

    def join_row(spot_ref, keep_ref, got_ref, out_ref, norm_ref, entropy_ref):
        out_ref[...] = join_halves(spot_ref, keep_ref[:shard], got_ref[:shard])
        total = keep_ref[shard:].astype(f32) + got_ref[shard:].astype(f32)
        line = total[6:7]
        entropy_ref[...] = line[:, 0:1] + line[:, 1:2]
        wide = jnp.concatenate([total[:lines], total[lines:]], axis=1)
        at = spot_ref[1] * 2 + spot_ref[2]
        found = wide[:, :shard]
        for index in range(1, seqs):
            here = wide[:, index * shard : (index + 1) * shard]
            found = jnp.where(at == index, here, found)
        norm_ref[...] = found

    row_join, norm_here, entropy_sum = kernel_call(
        join_row,
        [((shard, model), bf16), ((lines, shard), f32), ((1, 1), f32)],
        [spot, row_keep, along_core(row_swap)],
        smem=(0,),
    )
    row_ends = over_cols(after(row_join, pair_ends))
    result = order_rows(after(col_reached, row_join), block)
    grad_in = order_rows(after(col_reached, row_join), block + 2 * width)
    grad_feed_in, grad_feed_out, *col_grads = kernel_call(
        spread_pair,
        [(feed_in.shape, f32), (feed_out.shape, f32)] + [((shard, model), f32)] * cols_axis,
        [spot, *after(pair_ends, row_join)],
        smem=(0,),
        scratch=[pltpu.VMEM((cols_axis, 3 * shard, model), bf16)],
        room=24,
    )

    def spread_row(spot_ref, *refs):
        ins, outs, all_ref = refs[:cols_axis], refs[cols_axis:-1], refs[-1]
        for step, ref in enumerate(ins):
            all_ref[spot_ref[0] ^ step] = ref[...]
        for matrix in range(cols_axis):
            outs[matrix][...] = all_ref[matrix].astype(f32)

    row_grads = kernel_call(
        spread_row,
        [((shard, model), f32)] * cols_axis,
        [spot, *row_ends],
        smem=(0,),
        scratch=[pltpu.VMEM((cols_axis, shard, model), bf16)],
    )
    entropy = entropy_sum[0, 0] / (HEADS * norm_rows[6, 0])

    return (
        result,
        entropy,
        grad_in,
        *[norm_here[index] for index in range(6)],
        *row_grads,
        *col_grads,
        grad_feed_in,
        grad_feed_out,
    )


def fits_fast(tokens, feed_out):
    chips = lax.axis_size("seq") // 2
    return (
        lax.axis_size("col") == 4
        and lax.axis_size("seq") == 8
        and tokens.shape[0] == 1
        and tokens.shape[1] == chips * WINDOW
        and tokens.shape[2] == HEADS * HEAD_DIM
        and feed_out.shape[0] * 2 == tokens.shape[2]
    )


def on_device(tokens, offsets, band, col_counts, *rest):
    if not fits_fast(tokens, rest[15]):
        return general_plan(tokens, offsets, band, col_counts, *rest)
    return fast_plan(
        tokens,
        offsets,
        band,
        col_counts,
        rest[0:6],
        rest[6:10],
        rest[10:14],
        rest[14],
        rest[15],
        rest[16],
    )


def solution(mesh):
    return jax.shard_map(
        on_device,
        mesh=mesh,
        in_specs=(
            P("seq", "col", None),
            P(),
            P("col", None),
            P("col"),
            P("seq"),
            P("seq"),
            P("seq"),
            P("seq"),
            P("seq"),
            P("seq"),
            P("seq", None),
            P("seq", None),
            P("seq", None),
            P("seq", None),
            P("seq", None),
            P("seq", None),
            P("seq", None),
            P("seq", None),
            P("seq", None),
            P("seq", None),
            P("seq", "col", None),
        ),
        out_specs=(
            P("seq", "col", None),
            P(),
            P("seq", "col", None),
            P("seq"),
            P("seq"),
            P("seq"),
            P("seq"),
            P("seq"),
            P("seq"),
            P("seq", None),
            P("seq", None),
            P("seq", None),
            P("seq", None),
            P("seq", None),
            P("seq", None),
            P("seq", None),
            P("seq", None),
            P("seq", None),
            P("seq", None),
        ),
        check_vma=False,
    )
```

```python
from functools import partial
import math

import jax
import jax.numpy as jnp
from jax import lax
from jax.experimental import pallas as pl
from jax.experimental.pallas import tpu as pltpu
from jax.sharding import PartitionSpec as P

HEADS = 12
HEAD_DIM = 64
WINDOW = 32


entropy_weight = 8192.0
norm_eps = 1e-05


def with_halo(cells, sides, width):
    for axis, dim in sides:
        count = lax.axis_size(axis)
        ends = count - 1
        head = lax.slice_in_dim(cells, 0, width, axis=dim)
        tail = lax.slice_in_dim(cells, cells.shape[dim] - width, cells.shape[dim], axis=dim)
        cells = jnp.concatenate(
            [
                lax.ppermute(tail, axis, [(i, (i + 1) % count) for i in range(ends)]),
                cells,
                lax.ppermute(head, axis, [((i + 1) % count, i) for i in range(ends)]),
            ],
            axis=dim,
        )
    return cells


def layer_norm(inputs, norm_gain, norm_shift):
    average = jnp.mean(inputs, axis=-1, keepdims=True)
    centred = inputs - average
    variance = jnp.mean(centred * centred, axis=-1, keepdims=True)
    return centred * lax.rsqrt(variance + norm_eps) * norm_gain + norm_shift


def position_table(offsets, row_first, col_first, row_count, col_count, model_width):
    half_width = model_width // 2
    frequency = jnp.exp(-math.log(1000.0) * jnp.arange(half_width, dtype=jnp.float32) / half_width)
    col_place = (jnp.arange(col_count, dtype=jnp.int32) + col_first + offsets[1]).astype(
        jnp.float32
    )
    row_place = (jnp.arange(row_count, dtype=jnp.int32) + row_first + offsets[0]).astype(
        jnp.float32
    )
    col_wave = jnp.sin(col_place[:, None] * frequency[None, :])
    row_wave = jnp.sin(row_place[:, None] * frequency[None, :])
    col_full = jnp.broadcast_to(col_wave[None, :, :], (row_count, col_count, half_width))
    row_full = jnp.broadcast_to(row_wave[:, None, :], (row_count, col_count, half_width))
    return 0.5 * jnp.concatenate([col_full, row_full], axis=-1)


def softmax_entropy(scores, allowed, valid):
    masked = jnp.where(allowed[None], scores, -1000000000.0)
    largest = jnp.max(masked, axis=-1, keepdims=True)
    powers = jnp.exp(masked - largest)
    row_total = jnp.sum(powers, axis=-1, keepdims=True)
    probs_out = powers / row_total
    log_total = largest[..., 0] + jnp.log(row_total[..., 0])
    entropies = log_total - jnp.sum(probs_out * jnp.where(allowed[None], scores, 0.0), axis=-1)
    return (probs_out, jnp.sum(entropies * valid[None, :]))


def plain_softmax(scores):
    largest = jnp.max(scores, axis=-1, keepdims=True)
    powers = jnp.exp(scores - largest)
    return powers / jnp.sum(powers, axis=-1, keepdims=True)


def project(activations, weight):
    return jnp.einsum("rci,ij->rcj", activations, weight, preferred_element_type=jnp.float32)


def project_back(gradient, weight):
    return jnp.einsum("rcj,ij->rci", gradient, weight, preferred_element_type=jnp.float32)


def weight_grad(activations, gradient):
    return jnp.einsum("rci,rcj->ij", activations, gradient, preferred_element_type=jnp.float32)


def general_plan(
    tokens,
    offsets,
    band,
    col_counts,
    norm1_gain,
    norm1_shift,
    norm2_gain,
    norm2_shift,
    norm3_gain,
    norm3_shift,
    row_query,
    row_key,
    row_value,
    row_output,
    col_query,
    col_key,
    col_value,
    col_output,
    feed_in,
    feed_out,
    cotangent,
):
    rows_dev, cols_dev, model_width = tokens.shape
    total_rows = rows_dev * lax.axis_size("seq")
    total_cols = cols_dev * lax.axis_size("col")
    row_first = lax.axis_index("seq") * rows_dev
    col_first = lax.axis_index("col") * cols_dev
    count_here = col_counts[0].astype(jnp.float32)
    count_early = lax.psum(count_here, "col")
    params = (
        lax.all_gather(norm1_gain, "seq", axis=0, tiled=True),
        lax.all_gather(norm1_shift, "seq", axis=0, tiled=True),
        lax.all_gather(norm2_gain, "seq", axis=0, tiled=True),
        lax.all_gather(norm2_shift, "seq", axis=0, tiled=True),
        lax.all_gather(norm3_gain, "seq", axis=0, tiled=True),
        lax.all_gather(norm3_shift, "seq", axis=0, tiled=True),
        lax.all_gather(row_query, "seq", axis=0, tiled=True),
        lax.all_gather(row_key, "seq", axis=0, tiled=True),
        lax.all_gather(row_value, "seq", axis=0, tiled=True),
        lax.all_gather(row_output, "seq", axis=0, tiled=True),
        lax.all_gather(col_query, "seq", axis=0, tiled=True),
        lax.all_gather(col_key, "seq", axis=0, tiled=True),
        lax.all_gather(col_value, "seq", axis=0, tiled=True),
        lax.all_gather(col_output, "seq", axis=0, tiled=True),
        lax.all_gather(feed_in, "seq", axis=0, tiled=True),
        lax.all_gather(feed_out, "seq", axis=0, tiled=True),
    )
    gain_one = params[0].astype(jnp.float32)
    shift_one = params[1].astype(jnp.float32)
    gain_two = params[2].astype(jnp.float32)
    shift_two = params[3].astype(jnp.float32)
    gain_three = params[4].astype(jnp.float32)
    shift_three = params[5].astype(jnp.float32)
    query_row, key_row, value_row, output_row = (params[6], params[7], params[8], params[9])
    query_col, key_col, value_col, output_col = (params[10], params[11], params[12], params[13])
    feed_up, feed_down = (params[14], params[15])
    stream_zero = tokens.astype(jnp.float32) + position_table(
        offsets, row_first, col_first, rows_dev, cols_dev, model_width
    )
    normed_one, norm_back_one = jax.vjp(layer_norm, stream_zero, gain_one, shift_one)
    normed_one = normed_one.astype(jnp.bfloat16)
    row_queries = project(normed_one, query_row).astype(jnp.bfloat16)
    row_keys = project(normed_one, key_row).astype(jnp.bfloat16)
    row_values = project(normed_one, value_row).astype(jnp.bfloat16)
    extended = with_halo(jnp.stack([row_keys, row_values]), (("col", 2),), WINDOW)
    ext_cols = cols_dev + 2 * WINDOW
    queries_heads = row_queries.reshape(rows_dev, cols_dev, HEADS, HEAD_DIM)
    keys_ext = extended[0].reshape(rows_dev, ext_cols, HEADS, HEAD_DIM)
    values_ext = extended[1].reshape(rows_dev, ext_cols, HEADS, HEAD_DIM)
    partial_logits = jnp.einsum(
        "rchd,rehd->hce", queries_heads, keys_ext, preferred_element_type=jnp.float32
    )
    row_scale = 1.0 / math.sqrt(HEAD_DIM * total_rows)
    row_scores = lax.psum(partial_logits, "seq") * row_scale
    query_index = jnp.arange(cols_dev, dtype=jnp.int32)[:, None]
    key_index = jnp.arange(ext_cols, dtype=jnp.int32)[None, :]
    distance = key_index - query_index
    choose = jnp.arange(2 * WINDOW + 1, dtype=jnp.int32)
    matches = (distance[:, None, :] == choose[None, :, None]) & (band[:, :, None] == 1)
    key_global = col_first - WINDOW + key_index
    inside = (key_global >= 0) & (key_global < total_cols)
    allowed = (jnp.any(matches, axis=1) | (distance == WINDOW)) & inside
    valid = (jnp.arange(cols_dev, dtype=jnp.int32) < col_counts[0]).astype(jnp.float32)
    (row_probs, ent_part), ent_back = jax.vjp(
        lambda given: softmax_entropy(given, allowed, valid), row_scores
    )
    payload = ent_part[None]
    sums = lax.psum(payload, "col")
    entropy = sums[0] / (HEADS * count_early)
    row_probs_low = row_probs.astype(jnp.bfloat16)
    row_mix = jnp.einsum(
        "hce,rehd->rchd", row_probs_low, values_ext, preferred_element_type=jnp.float32
    )
    row_mix = row_mix.reshape(rows_dev, cols_dev, model_width).astype(jnp.bfloat16)
    stream_one = stream_zero + project(row_mix, output_row)
    normed_two, norm_back_two = jax.vjp(layer_norm, stream_one, gain_two, shift_two)
    normed_two = normed_two.astype(jnp.bfloat16)
    col_queries = project(normed_two, query_col).astype(jnp.bfloat16)
    col_keys = project(normed_two, key_col).astype(jnp.bfloat16)
    col_values = project(normed_two, value_col).astype(jnp.bfloat16)
    col_scale = 1.0 / math.sqrt(HEAD_DIM)
    keys_all, values_all = (
        lax.all_gather(col_keys, "seq", axis=0, tiled=True),
        lax.all_gather(col_values, "seq", axis=0, tiled=True),
    )
    col_heads_q = col_queries.reshape(rows_dev, cols_dev, HEADS, HEAD_DIM)
    keys_heads = keys_all.reshape(total_rows, cols_dev, HEADS, HEAD_DIM)
    values_heads = values_all.reshape(total_rows, cols_dev, HEADS, HEAD_DIM)
    col_raw = jnp.einsum(
        "rchd,schd->chrs", col_heads_q, keys_heads, preferred_element_type=jnp.float32
    )
    col_probs = plain_softmax(col_raw * col_scale)
    col_probs_low = col_probs.astype(jnp.bfloat16)
    col_mix = jnp.einsum(
        "chrs,schd->rchd", col_probs_low, values_heads, preferred_element_type=jnp.float32
    )
    col_mix = col_mix.reshape(rows_dev, cols_dev, model_width).astype(jnp.bfloat16)
    stream_two = stream_one + project(col_mix, output_col)
    normed_three, norm_back_three = jax.vjp(layer_norm, stream_two, gain_three, shift_three)
    normed_three = normed_three.astype(jnp.bfloat16)
    hidden_pre = project(normed_three, feed_up)
    hidden_act, gelu_back = jax.vjp(partial(jax.nn.gelu, approximate=False), hidden_pre)
    hidden_low = hidden_act.astype(jnp.bfloat16)
    output = (stream_two + project(hidden_low, feed_down)).astype(jnp.bfloat16)
    grad_feed_down = weight_grad(hidden_low, cotangent)
    grad_hidden = gelu_back(project_back(cotangent, feed_down))[0].astype(jnp.bfloat16)
    grad_feed_up = weight_grad(normed_three, grad_hidden)
    back_stream, grad_gain_three, grad_shift_three = norm_back_three(
        project_back(grad_hidden, feed_up)
    )
    grad_two = cotangent.astype(jnp.float32) + back_stream
    grad_two_low = grad_two.astype(jnp.bfloat16)
    grad_output_col = weight_grad(col_mix, grad_two_low)
    grad_mix_flat = project_back(grad_two_low, output_col).astype(jnp.bfloat16)
    grad_col_mix = grad_mix_flat.reshape(rows_dev, cols_dev, HEADS, HEAD_DIM)
    col_dprobs = jnp.einsum(
        "rchd,schd->chrs", grad_col_mix, values_heads, preferred_element_type=jnp.float32
    )
    col_dscores = col_probs * (col_dprobs - jnp.sum(col_probs * col_dprobs, axis=-1, keepdims=True))
    col_dscores = col_dscores.astype(jnp.bfloat16)
    grad_col_q = (
        jnp.einsum("chrs,schd->rchd", col_dscores, keys_heads, preferred_element_type=jnp.float32)
        * col_scale
    )
    grad_col_q = grad_col_q.reshape(rows_dev, cols_dev, model_width).astype(jnp.bfloat16)
    row_count = lax.axis_size("seq") * rows_dev
    key_part = (
        jnp.einsum("chrs,rchd->schd", col_dscores, col_heads_q, preferred_element_type=jnp.float32)
        * col_scale
    )
    value_part = jnp.einsum(
        "chrs,rchd->schd", col_probs_low, grad_col_mix, preferred_element_type=jnp.float32
    )
    key_value_grads = lax.psum_scatter(
        jnp.concatenate(
            [
                key_part.reshape(row_count, cols_dev, model_width),
                value_part.reshape(row_count, cols_dev, model_width),
            ],
            axis=-1,
        ),
        "seq",
        scatter_dimension=0,
        tiled=True,
    )
    grad_col_k = key_value_grads[..., :model_width].astype(jnp.bfloat16)
    grad_col_v = key_value_grads[..., model_width:].astype(jnp.bfloat16)
    grad_query_col = weight_grad(normed_two, grad_col_q)
    grad_key_col = weight_grad(normed_two, grad_col_k)
    grad_value_col = weight_grad(normed_two, grad_col_v)
    back_input = (
        project_back(grad_col_q, query_col)
        + project_back(grad_col_k, key_col)
        + project_back(grad_col_v, value_col)
    )
    back_stream, grad_gain_two, grad_shift_two = norm_back_two(back_input)
    grad_one = grad_two + back_stream
    grad_one_low = grad_one.astype(jnp.bfloat16)
    grad_output_row = weight_grad(row_mix, grad_one_low)
    grad_row_mix = project_back(grad_one_low, output_row).astype(jnp.bfloat16)
    grad_row_mix = grad_row_mix.reshape(rows_dev, cols_dev, HEADS, HEAD_DIM)
    dprobs_part = jnp.einsum(
        "rchd,rehd->hce", grad_row_mix, values_ext, preferred_element_type=jnp.float32
    )
    row_dprobs = lax.psum(dprobs_part.astype(jnp.bfloat16), "seq").astype(jnp.float32)
    ent_cot = jnp.asarray(entropy_weight, dtype=jnp.float32) / (HEADS * count_early)
    row_dscores = ent_back((row_dprobs, ent_cot))[0].astype(jnp.bfloat16)
    grad_row_q = (
        jnp.einsum("hce,rehd->rchd", row_dscores, keys_ext, preferred_element_type=jnp.float32)
        * row_scale
    )
    grad_row_q = grad_row_q.reshape(rows_dev, cols_dev, model_width).astype(jnp.bfloat16)
    grad_keys_ext = (
        jnp.einsum("hce,rchd->rehd", row_dscores, queries_heads, preferred_element_type=jnp.float32)
        * row_scale
    )
    grad_values_ext = jnp.einsum(
        "hce,rchd->rehd", row_probs_low, grad_row_mix, preferred_element_type=jnp.float32
    )
    grad_ext = jnp.stack([grad_keys_ext, grad_values_ext]).reshape(
        2, rows_dev, ext_cols, model_width
    )
    rims = jnp.concatenate([grad_ext[:, :, :WINDOW], grad_ext[:, :, WINDOW + cols_dev :]], axis=2)
    returned = with_halo(rims.astype(jnp.bfloat16), (("col", 2),), WINDOW).astype(rims.dtype)
    interior = grad_ext[:, :, WINDOW : WINDOW + cols_dev]
    interior = interior.at[:, :, :WINDOW].add(returned[:, :, :WINDOW])
    interior = interior.at[:, :, cols_dev - WINDOW :].add(returned[:, :, 3 * WINDOW :])
    grad_row_k = interior[0].astype(jnp.bfloat16)
    grad_row_v = interior[1].astype(jnp.bfloat16)
    grad_query_row = weight_grad(normed_one, grad_row_q)
    grad_key_row = weight_grad(normed_one, grad_row_k)
    grad_value_row = weight_grad(normed_one, grad_row_v)
    back_input = (
        project_back(grad_row_q, query_row)
        + project_back(grad_row_k, key_row)
        + project_back(grad_row_v, value_row)
    )
    back_stream, grad_gain_one, grad_shift_one = norm_back_one(back_input)
    input_grad = (grad_one + back_stream).astype(jnp.bfloat16)
    shares = (
        lax.psum_scatter(
            grad_gain_one.astype(jnp.bfloat16), "seq", scatter_dimension=0, tiled=True
        ).astype(jnp.float32),
        lax.psum_scatter(
            grad_shift_one.astype(jnp.bfloat16), "seq", scatter_dimension=0, tiled=True
        ).astype(jnp.float32),
        lax.psum_scatter(
            grad_gain_two.astype(jnp.bfloat16), "seq", scatter_dimension=0, tiled=True
        ).astype(jnp.float32),
        lax.psum_scatter(
            grad_shift_two.astype(jnp.bfloat16), "seq", scatter_dimension=0, tiled=True
        ).astype(jnp.float32),
        lax.psum_scatter(
            grad_gain_three.astype(jnp.bfloat16), "seq", scatter_dimension=0, tiled=True
        ).astype(jnp.float32),
        lax.psum_scatter(
            grad_shift_three.astype(jnp.bfloat16), "seq", scatter_dimension=0, tiled=True
        ).astype(jnp.float32),
        lax.psum_scatter(
            grad_query_row.astype(jnp.bfloat16), "seq", scatter_dimension=0, tiled=True
        ).astype(jnp.float32),
        lax.psum_scatter(
            grad_key_row.astype(jnp.bfloat16), "seq", scatter_dimension=0, tiled=True
        ).astype(jnp.float32),
        lax.psum_scatter(
            grad_value_row.astype(jnp.bfloat16), "seq", scatter_dimension=0, tiled=True
        ).astype(jnp.float32),
        lax.psum_scatter(
            grad_output_row.astype(jnp.bfloat16), "seq", scatter_dimension=0, tiled=True
        ).astype(jnp.float32),
        lax.psum_scatter(
            grad_query_col.astype(jnp.bfloat16), "seq", scatter_dimension=0, tiled=True
        ).astype(jnp.float32),
        lax.psum_scatter(
            grad_key_col.astype(jnp.bfloat16), "seq", scatter_dimension=0, tiled=True
        ).astype(jnp.float32),
        lax.psum_scatter(
            grad_value_col.astype(jnp.bfloat16), "seq", scatter_dimension=0, tiled=True
        ).astype(jnp.float32),
        lax.psum_scatter(
            grad_output_col.astype(jnp.bfloat16), "seq", scatter_dimension=0, tiled=True
        ).astype(jnp.float32),
        lax.psum_scatter(
            grad_feed_up.astype(jnp.bfloat16), "seq", scatter_dimension=0, tiled=True
        ).astype(jnp.float32),
        lax.psum_scatter(
            grad_feed_down.astype(jnp.bfloat16), "seq", scatter_dimension=0, tiled=True
        ).astype(jnp.float32),
    )
    totals = (
        lax.psum(shares[0].astype(jnp.bfloat16), "col").astype(jnp.float32),
        lax.psum(shares[1].astype(jnp.bfloat16), "col").astype(jnp.float32),
        lax.psum(shares[2].astype(jnp.bfloat16), "col").astype(jnp.float32),
        lax.psum(shares[3].astype(jnp.bfloat16), "col").astype(jnp.float32),
        lax.psum(shares[4].astype(jnp.bfloat16), "col").astype(jnp.float32),
        lax.psum(shares[5].astype(jnp.bfloat16), "col").astype(jnp.float32),
        lax.psum(shares[6].astype(jnp.bfloat16), "col").astype(jnp.float32),
        lax.psum(shares[7].astype(jnp.bfloat16), "col").astype(jnp.float32),
        lax.psum(shares[8].astype(jnp.bfloat16), "col").astype(jnp.float32),
        lax.psum(shares[9].astype(jnp.bfloat16), "col").astype(jnp.float32),
        lax.psum(shares[10].astype(jnp.bfloat16), "col").astype(jnp.float32),
        lax.psum(shares[11].astype(jnp.bfloat16), "col").astype(jnp.float32),
        lax.psum(shares[12].astype(jnp.bfloat16), "col").astype(jnp.float32),
        lax.psum(shares[13].astype(jnp.bfloat16), "col").astype(jnp.float32),
        lax.psum(shares[14].astype(jnp.bfloat16), "col").astype(jnp.float32),
        lax.psum(shares[15].astype(jnp.bfloat16), "col").astype(jnp.float32),
    )
    return (
        output,
        entropy,
        input_grad,
        totals[0],
        totals[1],
        totals[2],
        totals[3],
        totals[4],
        totals[5],
        totals[6],
        totals[7],
        totals[8],
        totals[9],
        totals[10],
        totals[11],
        totals[12],
        totals[13],
        totals[14],
        totals[15],
    )


def after(values, *needed):
    return lax.optimization_barrier((values, needed))[0]


def kernel_call(
    body, outs, args, smem=(), scratch=(), flops=1, moved=1, stream=False, room=16
):
    out_shapes = [jax.ShapeDtypeStruct(shape, kind) for shape, kind in outs]

    def whole(item):
        if not stream:
            return pl.BlockSpec(memory_space=pltpu.VMEM)
        rank = len(item.shape)
        return pl.BlockSpec(item.shape, lambda step: (0,) * rank, pipeline_mode=pl.Buffered(1))

    return pl.pallas_call(
        body,
        grid=(1,) if stream else (),
        out_shape=out_shapes,
        in_specs=[
            pl.BlockSpec(memory_space=pltpu.SMEM) if place in smem else whole(item)
            for place, item in enumerate(args)
        ],
        out_specs=[whole(item) for item in out_shapes],
        scratch_shapes=list(scratch),
        compiler_params=pltpu.CompilerParams(vmem_limit_bytes=(56 if stream else room) << 20),
        cost_estimate=pl.CostEstimate(
            flops=int(flops), bytes_accessed=int(moved), transcendentals=0
        ),
        name=body.__name__,
    )(*args)


def dot(left, right):
    return jnp.dot(left, right, preferred_element_type=jnp.float32)


def dot_back(left, right):
    return lax.dot_general(
        left, right, (((1,), (1,)), ((), ())), preferred_element_type=jnp.float32
    )


def dot_tokens(left, right):
    return lax.dot_general(
        left, right, (((0,), (0,)), ((), ())), preferred_element_type=jnp.float32
    )


def unit_norm(inputs):
    centred = inputs - jnp.mean(inputs, axis=-1, keepdims=True)
    scale = lax.rsqrt(jnp.mean(centred * centred, axis=-1, keepdims=True) + norm_eps)
    return centred * scale, scale


def unit_norm_back(given, unit, scale, gain):
    scaled = given * gain
    first = jnp.mean(scaled, axis=-1, keepdims=True)
    second = jnp.mean(scaled * unit, axis=-1, keepdims=True)
    return scale * (scaled - first - unit * second)


def norm_sums(given, unit):
    return jnp.concatenate(
        [
            jnp.sum(given * unit, axis=0, keepdims=True),
            jnp.sum(given, axis=0, keepdims=True),
        ],
        axis=0,
    )


def head_mask(width, model_width):
    rows = lax.broadcasted_iota(jnp.int32, (HEADS * width, model_width), 0) // width
    lanes = lax.broadcasted_iota(jnp.int32, (HEADS * width, model_width), 1) // HEAD_DIM
    return rows == lanes


def spread_heads(block, mask):
    tiled = jnp.concatenate([block] * HEADS, axis=0)
    return jnp.where(mask, tiled, jnp.zeros_like(tiled))


def fold_heads(product, mask, width):
    kept = jnp.where(mask, product, 0.0)
    total = kept[:width]
    for head in range(1, HEADS):
        total = total + kept[head * width : (head + 1) * width]
    return total


def head_of_lane(model_width):
    rows = lax.broadcasted_iota(jnp.int32, (model_width, 128), 0) // HEAD_DIM
    lanes = lax.broadcasted_iota(jnp.int32, (model_width, 128), 1)
    return (rows == lanes).astype(jnp.bfloat16)


def per_head_sum(product, lane_heads):
    return dot(product.astype(jnp.bfloat16), lane_heads)


def slot_span(spot_ref, side, slot, width):
    return pl.ds(pl.multiple_of((slot ^ spot_ref[side]) * width, width), width)


def window_rows(spot_ref, near_ref, left_ref, right_ref, which, slot, width):
    return jnp.concatenate(
        [
            left_ref[which, slot_span(spot_ref, 5, slot, width)],
            near_ref[which, slot * width : (slot + 1) * width],
            right_ref[which, slot_span(spot_ref, 6, slot, width)],
        ],
        axis=0,
    )


def half_of(values, core, width):
    return jnp.where(core == 0, values[:, :width], values[:, width:])


def fast_plan(
    tokens,
    offsets,
    band,
    col_counts,
    norms,
    row_weights,
    col_weights,
    feed_in,
    feed_out,
    cotangent,
):
    f32, bf16 = jnp.float32, jnp.bfloat16
    cols_dev, model = tokens.shape[1:]
    cols_axis, seqs = lax.axis_size("col"), lax.axis_size("seq")
    chips = seqs // 2
    width = cols_dev // chips
    toks = chips * width
    shard = model // seqs
    half = model // 2
    hidden = feed_out.shape[0] * seqs // cols_axis
    fold = HEADS * width
    span = 3 * width
    col_at = lax.axis_index("col")
    seq_at = lax.axis_index("seq")
    chip, core = seq_at // 2, seq_at % 2
    flip = col_at % 2

    def chunk_of(chip_index):
        return jnp.where(flip == 0, chip_index, chips - 1 - chip_index)

    chunk = chunk_of(chip)
    piece = col_at * chips + chunk

    def along_chips(values, step):
        return lax.ppermute(values, "seq", [(i, i ^ (2 * step)) for i in range(seqs)])

    def along_core(values):
        return lax.ppermute(values, "seq", [(i, i ^ 1) for i in range(seqs)])

    def along_cols(values, step):
        return lax.ppermute(values, "col", [(i, i ^ step) for i in range(cols_axis)])

    def pair_cols(values):
        pairs = [
            (c * seqs + i, (c ^ (1 + i % 2)) * seqs + i)
            for c in range(cols_axis)
            for i in range(seqs)
        ]
        return lax.ppermute(values, ("col", "seq"), pairs)

    def pair_chips(values):
        pairs = [(i, (i // 2 ^ (1 + i % 2)) * 2 + i % 2) for i in range(seqs)]
        return lax.ppermute(values, "seq", pairs)

    def place_of(piece_index, core_index):
        block, part = divmod(piece_index, chips)
        chip_index = part if block % 2 == 0 else chips - 1 - part
        return block * seqs + chip_index * 2 + core_index

    rightward = [
        (place_of(i, k), place_of(i + 1, k)) for i in range(cols_axis * chips - 1) for k in (0, 1)
    ]
    leftward = [(target, source) for source, target in rightward]

    def to_right(values):
        return lax.ppermute(values, ("col", "seq"), rightward)

    def to_left(values):
        return lax.ppermute(values, ("col", "seq"), leftward)

    steps = range(1, chips)
    col_steps = range(1, cols_axis)

    def turn_to(other):
        block, rest = other // chips, other % chips
        return chip ^ jnp.where(block % 2 == 0, rest, chips - 1 - rest)

    to_left_turn = turn_to(jnp.maximum(piece - 1, 0))
    to_right_turn = turn_to(jnp.minimum(piece + 1, cols_axis * chips - 1))
    spot = jnp.stack(
        [col_at, chip, core, chunk, col_counts[0], to_left_turn, to_right_turn]
    ).astype(jnp.int32)

    half_width = model // 2
    frequency = jnp.exp(-math.log(1000.0) * jnp.arange(half_width, dtype=f32) / half_width)
    col_place = (jnp.arange(width, dtype=jnp.int32) + piece * width + offsets[1]).astype(f32)
    seq_slots = jnp.stack([(chip ^ step) * 2 + core for step in range(chips)])
    row_place = (seq_slots + offsets[0]).astype(f32)
    waves = 0.5 * jnp.sin(
        jnp.concatenate([col_place, row_place])[:, None] * frequency[None, :]
    )
    band_here = lax.dynamic_slice_in_dim(band, chunk * width, width, axis=0)
    query_index = jnp.arange(width, dtype=jnp.int32)[:, None]
    key_index = jnp.arange(span, dtype=jnp.int32)[None, :]
    distance = key_index - query_index
    choose = jnp.arange(2 * WINDOW + 1, dtype=jnp.int32)
    matches = (distance[:, None, :] == choose[None, :, None]) & (band_here[:, :, None] == 1)
    key_global = (piece - 1) * width + key_index
    inside = (key_global >= 0) & (key_global < cols_axis * cols_dev)
    allowed = ((jnp.any(matches, axis=1) | (distance == WINDOW)) & inside).astype(f32)

    quarter = shard // cols_axis
    lines = 8
    hops = chips - 1
    col_rows = cols_axis * quarter
    row_rows = col_rows + lines

    def chunk_at(spot_ref, chip_index):
        at = jnp.where(spot_ref[0] % 2 == 0, chip_index, chips - 1 - chip_index)
        return pl.ds(pl.multiple_of(at * width, width), width)

    def pack(spot_ref, weights, own_ref, send_refs, block):
        at = pl.multiple_of(spot_ref[0] * quarter, quarter)
        size = len(weights) * quarter
        for index, ref in enumerate(weights):
            own_ref[index * shard : (index + 1) * shard] = ref[...]
            for send_ref in send_refs:
                send_ref[index * quarter : (index + 1) * quarter] = ref[pl.ds(at, quarter)]
        if block is not None:
            for ref, row in [(own_ref, len(weights) * shard)] + [
                (ref, size) for ref in send_refs
            ]:
                ref[row : row + lines] = jnp.zeros((lines, model), bf16)
                ref[row : row + lines, :128] = block

    def pack_row(spot_ref, *refs):
        norm_refs, own_ref, send_ref = refs[4:10], refs[10], refs[11]
        block = jnp.zeros((lines, 128), f32)
        rows = lax.broadcasted_iota(jnp.int32, (lines, 128), 0)
        for index, ref in enumerate(norm_refs):
            line = jnp.pad(ref[...].astype(f32), ((0, 0), (0, 128 - shard)))
            block = jnp.where(rows == index, line, block)
        block = jnp.where(rows == 6, spot_ref[4].astype(f32), block).astype(bf16)
        pack(spot_ref, refs[:4], own_ref, [send_ref], block)

    part = feed_out.shape[0] // cols_axis
    block_cols = feed_out.shape[0]

    def pack_rest(spot_ref, *refs):
        token_refs, in_ref, out_ref = refs[4:6], refs[6], refs[7]
        own_ref, chunk_ref, send_refs = refs[8], refs[10], refs[11:]
        pack(spot_ref, refs[:4], refs[9], send_refs, None)
        for index, ref in enumerate(token_refs):
            chunk_ref[index * width : (index + 1) * width] = ref[0, chunk_at(spot_ref, spot_ref[1])]
            for hop, send_ref in enumerate(send_refs):
                at = col_rows + index * width
                send_ref[at : at + width] = ref[0, chunk_at(spot_ref, spot_ref[1] ^ (hop + 1))]
        first = lax.broadcasted_iota(jnp.int32, (block_cols, 128), 0)
        lanes = lax.broadcasted_iota(jnp.int32, (block_cols, 128), 1)
        chosen = ((first == lanes + spot_ref[0] * part) & (lanes < part)).astype(bf16)
        for index in range(seqs):
            block = in_ref[:, index * block_cols : (index + 1) * block_cols]
            own_ref[0, :, index * part : (index + 1) * part] = dot(block, chosen)[
                :, :part
            ].astype(bf16)
        own_ref[1] = out_ref[pl.ds(pl.multiple_of(spot_ref[0] * part, part), part)]

    def stack_row(*refs):
        for hop, ref in enumerate(refs[:-1]):
            refs[-1][hop * row_rows : (hop + 1) * row_rows] = ref[...]

    def stack_col(own_ref, *refs):
        ins, (out_ref, given_ref) = refs[:-2], refs[-2:]
        for slot, ref in enumerate((own_ref, *ins)):
            at = 0 if slot == 0 else col_rows
            given_ref[slot * width : (slot + 1) * width] = ref[at + width : at + 2 * width]
            if slot:
                out_ref[(slot - 1) * col_rows : slot * col_rows] = ref[:col_rows]

    def spread_plane(near, far):
        def join_cores(near_ref, far_ref, out_ref):
            rows = near_ref.shape[0]
            out_ref[:rows] = near_ref[...]
            out_ref[rows:] = far_ref[...]

        both_cores = kernel_call(join_cores, [((2 * near.shape[0], model), bf16)], [near, far])[0]
        return both_cores, pair_cols(both_cores), along_cols(near, cols_axis - 1)

    def place_rows(spot_ref, refs, outs, rows, unit):
        at_col, at_chip, at_core = spot_ref[0], spot_ref[1], spot_ref[2]
        other = 1 - at_core

        def row_of(from_chip, from_core, offset, size):
            return pl.ds(
                pl.multiple_of((from_chip * 2 + from_core) * shard + offset, quarter), size
            )

        pieces = (
            (refs[2], at_col, at_core, 2),
            (refs[3], at_col ^ (1 + at_core), at_core, 2),
            (refs[4], at_col ^ 3, at_core, 1),
            (refs[5], at_col ^ (1 + other), other, 2),
            (refs[6], at_col ^ 3, other, 1),
        )
        for index, (out_ref, lead) in enumerate(outs):
            for ref, core_at in ((refs[0], at_core), (refs[1], other)):
                out_ref[lead + (row_of(at_chip, core_at, 0, shard),)] = ref[
                    index * shard : (index + 1) * shard
                ]
            for ref, col, core_at, sides in pieces:
                for side in range(sides):
                    for hop in steps:
                        at = row_of(at_chip ^ hop, core_at ^ side, col * quarter, quarter)
                        start = side * unit + (hop - 1) * rows + index * quarter
                        out_ref[lead + (at,)] = ref[start : start + quarter]

    row_own, row_send = kernel_call(
        pack_row,
        [((cols_axis * shard + lines, model), bf16), ((row_rows, model), bf16)],
        [spot, *row_weights, *[item[None] for item in norms]],
        smem=(0,),
        stream=True,
    )
    row_got = [along_chips(row_send, step) for step in steps]
    feed_own, col_own, chunks_own, *col_sends = kernel_call(
        pack_rest,
        [
            ((2, shard, hidden), bf16),
            ((cols_axis * shard, model), bf16),
            ((2 * width, model), bf16),
        ]
        + [((col_rows + 2 * width, model), bf16)] * hops,
        [spot, *col_weights, tokens, cotangent, feed_in, feed_out],
        smem=(0,),
        stream=True,
    )
    row_got = after(row_got, waves, allowed, col_sends)
    feed_other = along_core(feed_own)
    row_hops = kernel_call(stack_row, [((hops * row_rows, model), bf16)], row_got)[0]
    row_far_own = along_core(row_own)
    row_plane, row_pair, row_diagonal = spread_plane(row_hops, along_core(row_hops))
    col_sends = after(col_sends, row_plane)
    col_got = [along_chips(col_sends[step - 1], step) for step in steps]

    def pair_feed(own_ref, other_ref, out_ref):
        out_ref[0] = own_ref[...]
        out_ref[1] = other_ref[...]

    feed_both = kernel_call(
        pair_feed, [((2, 2, shard, hidden), bf16)], [feed_own, after(feed_other, row_plane)]
    )[0]
    row_last = after((row_pair, row_diagonal), row_pair, row_diagonal, col_got, feed_both)
    row_pieces = [row_own, row_far_own, row_plane, row_pair, row_diagonal] + [
        along_core(item) for item in row_last
    ]
    def project_row(spot_ref, waves_ref, *refs):
        token_refs, pieces, outs = refs[:chips], refs[chips : chips + 7], refs[chips + 7 :]
        zero_ref, low_ref, q_ref, kv_ref, weight_ref, last_ref, norm_ref = outs
        place_rows(
            spot_ref,
            pieces,
            [(weight_ref, (index,)) for index in range(3)] + [(last_ref, ())],
            row_rows,
            hops * row_rows,
        )
        first = lax.broadcasted_iota(jnp.int32, (128, model), 0)
        lanes = lax.broadcasted_iota(jnp.int32, (128, model), 1)
        total = jnp.zeros((lines, model), f32)
        for side in (0, 1):
            for hop in range(chips):
                if hop == 0:
                    block = pieces[side][cols_axis * shard : cols_axis * shard + lines, :128]
                else:
                    at = (side * hops + hop) * row_rows - lines
                    block = pieces[2][at : at + lines, :128]
                start = ((spot_ref[1] ^ hop) * 2 + (spot_ref[2] ^ side)) * shard
                chosen = ((lanes == first + start) & (first < shard)).astype(bf16)
                total = total + dot(block, chosen)
        count = spot_ref[4].astype(f32)
        for ref in pieces[3:6]:
            count = count + ref[row_rows - lines : row_rows, :128][6:7, 0:1].astype(f32)
        rows = lax.broadcasted_iota(jnp.int32, (lines, model), 0)
        norm_ref[...] = jnp.where(rows == 6, count, total)
        for slot in range(chips):
            rows = slice(slot * width, (slot + 1) * width)
            at = 0 if slot == 0 else col_rows
            stream = token_refs[slot][at : at + width].astype(f32)
            zero_ref[rows, :half] = stream[:, :half] + waves_ref[:width]
            zero_ref[rows, half:] = stream[:, half:] + waves_ref[width + slot : width + slot + 1]
        unit, _ = unit_norm(zero_ref[...])
        low = (unit * norm_ref[0:1] + norm_ref[1:2]).astype(bf16)
        low_ref[...] = low
        q_ref[...] = dot(low, weight_ref[0]).astype(bf16)
        kv_ref[0] = dot(low, weight_ref[1]).astype(bf16)
        kv_ref[1] = dot(low, weight_ref[2]).astype(bf16)

    big = 2.0 * toks * model * model
    stream_zero, normed_one, row_q, row_kv, weights_row, weights_out, norm_rows = kernel_call(
        project_row,
        [
            ((toks, model), f32),
            ((toks, model), bf16),
            ((toks, model), bf16),
            ((2, toks, model), bf16),
            ((3, model, model), bf16),
            ((model, model), bf16),
            ((lines, model), f32),
        ],
        [spot, waves, chunks_own, *col_got, *row_pieces],
        smem=(0,),
    )
    kv_left = to_right(row_kv)
    kv_right = to_left(row_kv)
    col_unit = hops * col_rows
    col_hops, given_out = kernel_call(
        stack_col,
        [((col_unit, model), bf16), ((toks, model), bf16)],
        [after(chunks_own, row_q), *col_got],
    )
    col_far_own = along_core(col_own)
    col_plane, col_pair, col_diagonal = spread_plane(col_hops, along_core(col_hops))

    feed_pair = pair_chips(after(feed_both, row_q))

    def tied_logits(spot_ref, q_ref, near_ref, left_ref, right_ref, out_ref):
        mask = head_mask(width, model)
        total = None
        for slot in range(chips):
            keys = window_rows(spot_ref, near_ref, left_ref, right_ref, 0, slot, width)
            spread = spread_heads(q_ref[slot * width : (slot + 1) * width], mask)
            term = dot_back(spread, keys)
            total = term if total is None else total + term
        out_ref[...] = total

    logits = kernel_call(
        tied_logits,
        [((fold, span), f32)],
        [spot, row_q, row_kv, kv_left, kv_right],
        smem=(0,),
    )[0]
    logits_other = along_core(logits)
    feed_diagonal = along_chips(after(feed_own, logits), chips - 1)
    given_far = after(along_core(given_out), logits)
    row_scale = 1.0 / math.sqrt(HEAD_DIM * seqs)
    col_scale = 1.0 / math.sqrt(HEAD_DIM)

    def attend_row(
        spot_ref,
        logits_ref,
        other_ref,
        allowed_ref,
        near_ref,
        left_ref,
        right_ref,
        zero_ref,
        norm_ref,
        weight_ref,
        scores_ref,
        probs_ref,
        mix_ref,
        stream_ref,
        low_ref,
        entropy_ref,
    ):
        mask = head_mask(width, model)
        scores = (logits_ref[...] + other_ref[...]) * row_scale
        open_here = jnp.concatenate([allowed_ref[...]] * HEADS, axis=0) > 0.5
        masked = jnp.where(open_here, scores, -1000000000.0)
        largest = jnp.max(masked, axis=-1, keepdims=True)
        powers = jnp.exp(masked - largest)
        total = jnp.sum(powers, axis=-1, keepdims=True)
        probs = powers / total
        kept = jnp.where(open_here, scores, 0.0)
        entropies = largest + jnp.log(total) - jnp.sum(probs * kept, axis=-1, keepdims=True)
        rows = lax.broadcasted_iota(jnp.int32, (fold, 1), 0) % width
        entropies = jnp.where(rows + spot_ref[3] * width < spot_ref[4], entropies, 0.0)
        lanes = lax.broadcasted_iota(jnp.int32, (1, model), 1)
        found = jnp.sum(entropies, axis=0, keepdims=True)
        entropy_ref[...] = jnp.where((lanes == 0) & (spot_ref[2] == 0), found, 0.0)
        scores_ref[...] = kept
        probs_ref[...] = probs
        low_probs = probs.astype(bf16)
        for slot in range(chips):
            values = window_rows(spot_ref, near_ref, left_ref, right_ref, 1, slot, width)
            mix_ref[slot * width : (slot + 1) * width] = fold_heads(
                dot(low_probs, values), mask, width
            ).astype(bf16)
        stream = zero_ref[...] + dot(mix_ref[...], weight_ref[...])
        stream_ref[...] = stream
        unit, _ = unit_norm(stream)
        low_ref[...] = (unit * norm_ref[2:3] + norm_ref[3:4]).astype(bf16)

    scores, probs, row_mix, stream_one, normed_two, entropy_row = kernel_call(
        attend_row,
        [
            ((fold, span), f32),
            ((fold, span), f32),
            ((toks, model), bf16),
            ((toks, model), f32),
            ((toks, model), bf16),
            ((1, model), f32),
        ],
        [
            spot,
            logits,
            logits_other,
            allowed,
            row_kv,
            kv_left,
            kv_right,
            stream_zero,
            norm_rows,
            weights_out,
        ],
        smem=(0,),
    )

    col_last = after((col_pair, col_diagonal), normed_two, feed_pair)
    col_pieces = [col_own, col_far_own, col_plane, col_pair, col_diagonal] + [
        along_core(item) for item in col_last
    ]

    def assemble_col(spot_ref, *refs):
        three_ref, last_ref = refs[7:]
        outs = [(three_ref, (index,)) for index in range(3)] + [(last_ref, ())]
        place_rows(spot_ref, refs[:7], outs, col_rows, col_unit)

    weights_three, weights_last = kernel_call(
        assemble_col,
        [((3, model, model), bf16), ((model, model), bf16)],
        [spot, *col_pieces],
        smem=(0,),
    )

    def project_col(low_ref, weight_ref, q_ref, k_ref, v_ref):
        low = low_ref[...]
        q_ref[...] = dot(low, weight_ref[0]).astype(bf16)
        k_ref[...] = dot(low, weight_ref[1]).astype(bf16)
        v_ref[...] = dot(low, weight_ref[2]).astype(bf16)

    col_q, col_k, col_v = kernel_call(
        project_col,
        [((toks, model), bf16)] * 3,
        [normed_two, weights_three],
    )
    k_other, v_other = along_core(col_k), along_core(col_v)

    def join_given(near_ref, far_ref, out_ref):
        out_ref[:toks] = near_ref[...]
        out_ref[toks:] = far_ref[...]

    given_both = kernel_call(join_given, [((2 * toks, model), bf16)], [given_out, given_far])[0]
    given_pair = pair_cols(given_both)

    def slot_rows(slot):
        return slice(slot * width, (slot + 1) * width)

    def attend_col(
        q_ref,
        k_ref,
        v_ref,
        k2_ref,
        v2_ref,
        one_ref,
        norm_ref,
        weight_ref,
        given_ref,
        probs_ref,
        mix_ref,
        stream_ref,
        low_ref,
        message_ref,
    ):
        lane_heads = head_of_lane(model)
        sides = ((k_ref, v_ref), (k2_ref, v2_ref))
        rows = seqs * width
        products = jnp.concatenate(
            [
                q_ref[slot_rows(slot)] * sides[s // chips][0][slot_rows(s % chips)]
                for slot in range(chips)
                for s in range(seqs)
            ],
            axis=0,
        )
        found_all = per_head_sum(products, lane_heads) * col_scale
        weights_all = []
        for slot in range(chips):
            start = slot * rows
            parts = [
                found_all[start + s * width : start + (s + 1) * width] for s in range(seqs)
            ]
            largest = parts[0]
            for item in parts[1:]:
                largest = jnp.maximum(largest, item)
            powers = [jnp.exp(item - largest) for item in parts]
            total = powers[0]
            for item in powers[1:]:
                total = total + item
            weights = jnp.concatenate([item / total for item in powers], axis=0)
            probs_ref[slot] = weights
            weights_all.append(weights.astype(bf16))
        wide = dot_back(jnp.concatenate(weights_all, axis=0), lane_heads)
        for slot in range(chips):
            mixed = None
            for s in range(seqs):
                start = slot * rows + s * width
                term = wide[start : start + width] * sides[s // chips][1][
                    slot_rows(s % chips)
                ].astype(f32)
                mixed = term if mixed is None else mixed + term
            mix_ref[slot_rows(slot)] = mixed.astype(bf16)
        stream = one_ref[...] + dot(mix_ref[...], weight_ref[...])
        stream_ref[...] = stream
        unit, _ = unit_norm(stream)
        low = (unit * norm_ref[4:5] + norm_ref[5:6]).astype(bf16)
        low_ref[...] = low
        message_ref[:toks] = low
        message_ref[toks:] = given_ref[...]

    col_probs, col_mix, stream_two, normed_three, message = kernel_call(
        attend_col,
        [
            ((chips, seqs * width, 128), f32),
            ((toks, model), bf16),
            ((toks, model), f32),
            ((toks, model), bf16),
            ((2 * toks, model), bf16),
        ],
        [col_q, col_k, col_v, k_other, v_other, stream_one, norm_rows, weights_last, given_out],
    )
    low_near = [
        normed_three,
        along_cols(normed_three, 1),
        along_cols(normed_three, 2),
        along_cols(message, 3),
    ]

    feed_last = after((feed_pair, feed_diagonal, given_pair), low_near)
    feed_far = [along_core(item) for item in feed_last]

    def assemble_feed(
        spot_ref,
        both_ref,
        pair_ref,
        last_ref,
        pair2_ref,
        last2_ref,
        d0_ref,
        d1_ref,
        d2_ref,
        d3_ref,
        out_ref,
        given_ref,
    ):
        at_chip, at_core = spot_ref[1], spot_ref[2]
        other = 1 - at_core

        def move(rows, from_chip, from_core):
            at = pl.multiple_of((from_chip * 2 + from_core) * shard, shard)
            out_ref[:, pl.ds(at, shard)] = rows

        for side in (0, 1):
            move(both_ref[side], at_chip, at_core ^ side)
            move(pair_ref[side], at_chip ^ (1 + at_core), at_core ^ side)
            move(pair2_ref[side], at_chip ^ (1 + other), other ^ side)
        move(last_ref[...], at_chip ^ 3, at_core)
        move(last2_ref[...], at_chip ^ 3, other)
        given_ref[0] = d0_ref[...]
        given_ref[1 + at_core] = d1_ref[:toks]
        given_ref[2 - at_core] = d2_ref[toks:]
        given_ref[3] = d3_ref[toks:]

    weights_feed, given_all = kernel_call(
        assemble_feed,
        [((2, model, hidden), bf16), ((cols_axis, toks, model), bf16)],
        [
            spot,
            feed_both,
            feed_pair,
            feed_diagonal,
            feed_far[0],
            feed_far[1],
            given_out,
            given_pair,
            feed_far[2],
            low_near[3],
        ],
        smem=(0,),
    )

    def feed_main(a0, a1, a2, a3, given_ref, weight_ref, act_ref, grad_ref, *back_refs):
        up, down = weight_ref[0], weight_ref[1]
        rows = cols_axis * toks
        low = jnp.concatenate([ref[:toks] for ref in (a0, a1, a2, a3)], axis=0)
        pre = dot(low, up)
        bell = 0.5 * (1.0 + lax.erf(pre * (0.5**0.5)))
        slope = bell + pre * jnp.exp(-0.5 * pre * pre) * ((0.5 / math.pi) ** 0.5)
        act_ref[...] = (pre * bell).astype(bf16).reshape(cols_axis, toks, hidden)
        grad = (slope * dot_back(given_ref[...].reshape(rows, model), down)).astype(bf16)
        grad_ref[...] = grad.reshape(cols_axis, toks, hidden)
        back = dot_back(grad, up).astype(bf16)
        for step in range(cols_axis):
            back_refs[step][...] = back[step * toks : (step + 1) * toks]

    feed_results = kernel_call(
        feed_main,
        [((cols_axis, toks, hidden), bf16)] * 2 + [((toks, model), bf16)] * cols_axis,
        [*low_near, given_all, weights_feed],
    )
    act, grad_hidden, back_parts = feed_results[0], feed_results[1], feed_results[2:]
    back_near = [back_parts[0]] + [along_cols(back_parts[step], step) for step in col_steps]

    def feed_weights(
        spot_ref, a0, a1, a2, a3, given_ref, act_ref, grad_ref, weight_ref, mine_ref, give_ref, *outs
    ):
        at_core = spot_ref[2]
        low = jnp.concatenate([a0[...], a1[...], a2[...], a3[:toks]], axis=0)
        given = given_ref[...].reshape(cols_axis * toks, model)
        rows = cols_axis * toks
        acts = act_ref[...].reshape(rows, hidden)
        grads = grad_ref[...].reshape(rows, hidden)
        for step in range(cols_axis):
            outs[step][...] = dot(act_ref[step], weight_ref[1]).astype(bf16)
        for ref, at in ((mine_ref, at_core), (give_ref, 1 - at_core)):
            ref[:model] = dot_tokens(low, half_of(grads, at, half)).astype(bf16)
            ref[model:] = dot_tokens(acts, half_of(given, at, half)).astype(bf16)

    feed_grads = kernel_call(
        feed_weights,
        [((2 * model, half), bf16)] * 2 + [((toks, model), bf16)] * cols_axis,
        [spot, *low_near, given_all, act, grad_hidden, weights_feed],
        smem=(0,),
        flops=6.0 * toks * cols_axis * model * hidden,
        moved=16 << 20,
        room=24,
    )
    feed_mine, feed_give, out_parts = feed_grads[0], feed_grads[1], feed_grads[2:]

    block = 2 * shard
    extra = 2 * lines

    def renew(total, at):
        line = total[at : at + 1]
        whole = line[:, 0:1] + line[:, 1:2]
        high = whole.astype(bf16).astype(f32)
        lanes = lax.broadcasted_iota(jnp.int32, total.shape, 1)
        rows = lax.broadcasted_iota(jnp.int32, total.shape, 0)
        total = jnp.where((rows == at) & (lanes == 0), high, total)
        return jnp.where((rows == at) & (lanes == 1), whole - high, total)

    near_rows = model // 2

    def row_layer_grads(low, mix, low_far, mix_far, mine, got, more):
        norms_too = len(more) == 1
        size = near_rows + (0 if norms_too else toks)
        tail = extra if norms_too else 0

        def row_weight_sums(spot_ref, low_ref, mix_ref, low2_ref, mix2_ref, mine_ref, got_ref, *refs):
            more_refs, (x_ref, y_ref, a_ref, b_ref) = refs[: len(more)], refs[len(more) : -2]
            left_ref, right_ref = refs[-2:]
            left_ref[0, :toks] = low_ref[...]
            left_ref[0, toks:] = low2_ref[...]
            left_ref[1, :toks] = mix_ref[...]
            left_ref[1, toks:] = mix2_ref[...]
            right_ref[:, :toks] = mine_ref[...]
            right_ref[:, toks:] = got_ref[...]
            places = (
                ((a_ref, 0), (b_ref, 0)),
                ((x_ref, 0), (b_ref, 1)),
                ((a_ref, 1), (y_ref, 0)),
                ((x_ref, 1), (y_ref, 1)),
            )
            for step in range(cols_axis):
                matrix = spot_ref[0] ^ step
                left = left_ref[matrix // 3]
                found = dot_tokens(left, right_ref[matrix]).astype(bf16)
                for part_index, (ref, at) in enumerate(places[step]):
                    start = at * size
                    ref[start : start + near_rows] = found[
                        part_index * near_rows : (part_index + 1) * near_rows
                    ]
                    if not norms_too:
                        lanes = slice(part_index * half, (part_index + 1) * half)
                        ref[start + near_rows : start + size] = more_refs[step][:, lanes]
            if norms_too:
                sums_ref = more_refs[0]
                line = jnp.concatenate([sums_ref[:, :half], sums_ref[:, half:]], axis=0)
                line = renew(line, 6).astype(bf16)
                for ref in (x_ref, a_ref):
                    ref[2 * size :] = line

        outs = [((2 * size + tail, half), bf16), ((2 * size, half), bf16)] * 2
        return kernel_call(
            row_weight_sums,
            outs,
            [spot, low, mix, low_far, mix_far, mine, got, *more],
            smem=(0,),
            scratch=[
                pltpu.VMEM((2, 2 * toks, model), bf16),
                pltpu.VMEM((4, 2 * toks, half), bf16),
            ],
        )

    def fold_pairs(parts, got_x, got_y, tail):
        a_part, b_part = parts[2:]
        size = b_part.shape[0] // 2

        def pair_sums(a_ref, x_ref, b_ref, y_ref, keep_ref, give_ref, keep2_ref, give2_ref):
            first = a_ref[...].astype(f32) + x_ref[...].astype(f32)
            second = b_ref[...].astype(f32) + y_ref[...].astype(f32)
            keep_ref[:size] = first[:size].astype(bf16)
            give_ref[:size] = first[size : 2 * size].astype(bf16)
            keep2_ref[...] = second[:size].astype(bf16)
            give2_ref[...] = second[size:].astype(bf16)
            if tail:
                line = renew(first[2 * size :], 6).astype(bf16)
                keep_ref[size:] = line
                give_ref[size:] = line

        return kernel_call(
            pair_sums,
            [((size + tail, half), bf16)] * 2 + [((size, half), bf16)] * 2,
            [a_part, got_x, b_part, got_y],
        )

    def row_layer_chips(keep, got, keep2, got2, tail, stream, slots):
        sent_rows = 2 * width * (bool(stream) + bool(slots))

        def layer_parts(spot_ref, a_ref, ga_ref, b_ref, gb_ref, *refs):
            more, outs, total_ref = refs[: -chips - 1], refs[-chips - 1 : -1], refs[-1]
            first = a_ref[...].astype(f32) + ga_ref[...].astype(f32)
            second = b_ref[...].astype(f32) + gb_ref[...].astype(f32)
            total_ref[:near_rows] = first[:near_rows].astype(bf16)
            total_ref[near_rows:] = second[:near_rows].astype(bf16)
            if stream:
                result = more[0][...] + jnp.concatenate(
                    [first[near_rows:], second[near_rows:]], axis=1
                )
            for hop in range(chips):
                at = pl.multiple_of((spot_ref[1] ^ hop) * block, block)
                outs[hop][:block] = total_ref[pl.ds(at, block)]
                row = block
                if tail:
                    outs[hop][row : row + tail] = renew(first[near_rows:], 6).astype(bf16)
                    row = row + tail
                sent = []
                if stream:
                    sent.append(result[slot_rows(hop)].astype(bf16))
                if slots:
                    sent.append(more[hop - chips][...])
                for slot in sent:
                    outs[hop][row : row + width] = slot[:, :half]
                    outs[hop][row + width : row + 2 * width] = slot[:, half:]
                    row = row + 2 * width

        return kernel_call(
            layer_parts,
            [((block + tail + sent_rows, half), bf16)] * chips,
            [spot, keep, got, keep2, got2, *stream, *slots],
            smem=(0,),
            scratch=[pltpu.VMEM((model, half), bf16)],
        )

    def layer_grads(low, mix, low_far, mix_far, mine, got, more):
        rows = model + (extra if len(more) == 1 else 2 * toks)

        def weight_sums(spot_ref, low_ref, mix_ref, low2_ref, mix2_ref, mine_ref, got_ref, *refs):
            more_refs, outs = refs[: len(more)], refs[len(more) : -2]
            left_ref, right_ref = refs[-2:]
            left_ref[0, :toks] = low_ref[...]
            left_ref[0, toks:] = low2_ref[...]
            left_ref[1, :toks] = mix_ref[...]
            left_ref[1, toks:] = mix2_ref[...]
            right_ref[:, :toks] = mine_ref[...]
            right_ref[:, toks:] = got_ref[...]
            for step in range(cols_axis):
                matrix = spot_ref[0] ^ step
                left = left_ref[matrix // 3]
                outs[step][:model] = dot_tokens(left, right_ref[matrix]).astype(bf16)
                if len(more) == 1:
                    sums_ref = more_refs[0]
                    tail = jnp.concatenate([sums_ref[:, :half], sums_ref[:, half:]], axis=0)
                    outs[step][model:] = renew(tail, 6).astype(bf16)
                else:
                    outs[step][model : model + toks] = more_refs[step][:, :half]
                    outs[step][model + toks :] = more_refs[step][:, half:]

        return kernel_call(
            weight_sums,
            [((rows, half), bf16)] * cols_axis,
            [spot, low, mix, low_far, mix_far, mine, got, *more],
            smem=(0,),
            scratch=[
                pltpu.VMEM((2, 2 * toks, model), bf16),
                pltpu.VMEM((4, 2 * toks, half), bf16),
            ],
        )

    def split_chips(items, count, tail, stream=None, slots=()):
        slot_rows_out = 2 * width * ((stream is not None) + bool(slots))

        def chip_parts(spot_ref, *refs):
            ins, outs, total_ref = refs[: len(items)], refs[-chips - 1 : -1], refs[-1]
            more = refs[len(items) : -chips - 1]
            total = ins[0][...].astype(f32)
            for ref in ins[1:]:
                total = total + ref[...].astype(f32)
            total_ref[...] = total.astype(bf16)
            if stream is not None:
                result = more[0][...] + jnp.concatenate(
                    [total[model : model + toks], total[model + toks :]], axis=1
                )
            for hop in range(chips):
                at = pl.multiple_of((spot_ref[1] ^ hop) * block, block)
                for index in range(count):
                    outs[hop][index * block : (index + 1) * block] = total_ref[
                        pl.ds(index * model + at, block)
                    ]
                row = count * block
                if tail:
                    outs[hop][row : row + tail] = renew(total[count * model :], 6).astype(bf16)
                    row = row + tail
                sent = []
                if stream is not None:
                    sent.append(result[slot_rows(hop)].astype(bf16))
                if slots:
                    sent.append(more[hop - chips][...])
                for slot in sent:
                    outs[hop][row : row + width] = slot[:, :half]
                    outs[hop][row + width : row + 2 * width] = slot[:, half:]
                    row = row + 2 * width

        size = count * block + tail + slot_rows_out
        return kernel_call(
            chip_parts,
            [((size, half), bf16)] * chips,
            [spot, *items] + ([] if stream is None else [stream]) + list(slots),
            smem=(0,),
            scratch=[pltpu.VMEM(items[0].shape, bf16)],
        )

    def split_cores(items, count, tail):
        rows_in = count * block + tail

        def core_parts(spot_ref, *refs):
            ins, (keep_ref, give_ref, total_ref) = refs[: len(items)], refs[len(items) :]
            total = ins[0][:rows_in].astype(f32)
            for ref in ins[1:]:
                total = total + ref[:rows_in].astype(f32)
            total_ref[...] = total.astype(bf16)
            for ref, at in ((keep_ref, spot_ref[2]), (give_ref, 1 - spot_ref[2])):
                for index in range(count):
                    row = pl.multiple_of(index * block + at * shard, shard)
                    ref[index * shard : (index + 1) * shard] = total_ref[pl.ds(row, shard)]
                if tail:
                    ref[count * shard :] = renew(total[count * block :], 6).astype(bf16)

        size = count * shard + tail
        return kernel_call(
            core_parts,
            [((size, half), bf16)] * 2,
            [spot, *items],
            smem=(0,),
            scratch=[pltpu.VMEM((rows_in, half), bf16)],
        )

    def over_chips(parts):
        return [parts[0]] + [along_chips(parts[step], step) for step in steps]

    back_near = after(back_near, feed_mine)

    def attend_col_back(
        spot_ref,
        b0,
        b1,
        b2,
        b3,
        given_ref,
        two_ref,
        norm_ref,
        weight_ref,
        q_ref,
        k_ref,
        v_ref,
        k2_ref,
        v2_ref,
        probs_ref,
        dtwo_ref,
        low_ref,
        dq_ref,
        dkv_ref,
        send_ref,
        sums_ref,
    ):
        lane_heads = head_of_lane(model)
        back = b0[...].astype(f32) + b1[...].astype(f32) + b2[...].astype(f32) + b3[...].astype(f32)
        unit, scale = unit_norm(two_ref[...])
        sums_ref[...] = norm_sums(back, unit)
        dtwo = given_ref[0].astype(f32) + unit_norm_back(back, unit, scale, norm_ref[4:5])
        dtwo_ref[...] = dtwo
        low = dtwo.astype(bf16)
        low_ref[...] = low
        dmix_low = dot_back(low, weight_ref[...]).astype(bf16)
        dmix = dmix_low.astype(f32)
        sides = ((k_ref, v_ref), (k2_ref, v2_ref))
        rows = seqs * width
        products = jnp.concatenate(
            [
                dmix_low[slot_rows(slot)] * sides[s // chips][1][slot_rows(s % chips)]
                for slot in range(chips)
                for s in range(seqs)
            ],
            axis=0,
        )
        found_all = per_head_sum(products, lane_heads)
        dscores = []
        for slot in range(chips):
            found = found_all[slot * rows : (slot + 1) * rows]
            weights = probs_ref[slot]
            mean = None
            for s in range(seqs):
                at = slice(s * width, (s + 1) * width)
                term = weights[at] * found[at]
                mean = term if mean is None else mean + term
            dscores.append(
                (weights * (found - jnp.concatenate([mean] * seqs, axis=0))).astype(bf16)
            )
        wide_d = dot_back(jnp.concatenate(dscores, axis=0), lane_heads)
        wide_p = dot_back(probs_ref[...].astype(bf16).reshape(chips * rows, 128), lane_heads)

        def piece(wide, slot, s):
            start = slot * rows + s * width
            return wide[start : start + width]

        for slot in range(chips):
            dquery = None
            for s in range(seqs):
                term = piece(wide_d, slot, s) * sides[s // chips][0][
                    slot_rows(s % chips)
                ].astype(f32)
                dquery = term if dquery is None else dquery + term
            dq_ref[slot_rows(slot)] = (dquery * col_scale).astype(bf16)
        for s in range(seqs):
            dkey, dvalue = None, None
            for slot in range(chips):
                key_term = piece(wide_d, slot, s) * q_ref[slot_rows(slot)].astype(f32)
                value_term = piece(wide_p, slot, s) * dmix[slot_rows(slot)]
                dkey = key_term if dkey is None else dkey + key_term
                dvalue = value_term if dvalue is None else dvalue + value_term
            at = slot_rows(s % chips)
            if s < chips:
                dkv_ref[0, at] = dkey * col_scale
                dkv_ref[1, at] = dvalue
            else:
                send_ref[0, at] = (dkey * col_scale).astype(bf16)
                send_ref[1, at] = dvalue.astype(bf16)

    grad_two, grad_two_low, col_dq, col_dkv, col_send, sums_three = kernel_call(
        attend_col_back,
        [
            ((toks, model), f32),
            ((toks, model), bf16),
            ((toks, model), bf16),
            ((2, toks, model), f32),
            ((2, toks, model), bf16),
            ((2, model), f32),
        ],
        [
            spot,
            *back_near,
            given_all,
            stream_two,
            norm_rows,
            weights_last,
            col_q,
            col_k,
            col_v,
            k_other,
            v_other,
            col_probs,
        ],
        smem=(0,),
        room=24,
    )
    row_low_far, row_mix_far = along_core(normed_one), along_core(row_mix)
    col_low_far, col_mix_far = along_core(normed_two), along_core(col_mix)
    dkv_got = after(along_core(col_send), row_low_far, row_mix_far)

    def row_entry_back(
        spot_ref,
        dq_ref,
        dkv_ref,
        got_ref,
        low_two_ref,
        dtwo_ref,
        one_ref,
        norm_ref,
        col_ref,
        row_ref,
        near_ref,
        left_ref,
        right_ref,
        mine_ref,
        give_ref,
        done_ref,
        low_ref,
        dmix_ref,
        dprobs_ref,
        sums_ref,
    ):
        at_core = spot_ref[2]
        dq = dq_ref[...]
        dk = (dkv_ref[0] + got_ref[0].astype(f32)).astype(bf16)
        dv = (dkv_ref[1] + got_ref[1].astype(f32)).astype(bf16)
        for index, item in enumerate((dq, dk, dv, low_two_ref[...])):
            mine_ref[index] = half_of(item, at_core, half)
            give_ref[index] = half_of(item, 1 - at_core, half)
        back = dot_back(dq, col_ref[0]) + dot_back(dk, col_ref[1]) + dot_back(dv, col_ref[2])
        unit, scale = unit_norm(one_ref[...])
        sums_ref[...] = norm_sums(back, unit)
        done = dtwo_ref[...] + unit_norm_back(back, unit, scale, norm_ref[2:3])
        done_ref[...] = done
        low = done.astype(bf16)
        low_ref[...] = low
        dmix = dot_back(low, row_ref[...]).astype(bf16)
        dmix_ref[...] = dmix
        mask = head_mask(width, model)
        total = None
        for slot in range(chips):
            values = window_rows(spot_ref, near_ref, left_ref, right_ref, 1, slot, width)
            term = dot_back(spread_heads(dmix[slot_rows(slot)], mask), values)
            total = term if total is None else total + term
        dprobs_ref[...] = total

    (
        col_mine,
        col_give,
        grad_one,
        grad_one_low,
        row_dmix,
        dprobs,
        sums_two,
    ) = kernel_call(
        row_entry_back,
        [
            ((4, toks, half), bf16),
            ((4, toks, half), bf16),
            ((toks, model), f32),
            ((toks, model), bf16),
            ((toks, model), bf16),
            ((fold, span), f32),
            ((2, model), f32),
        ],
        [
            spot,
            col_dq,
            col_dkv,
            dkv_got,
            grad_two_low,
            grad_two,
            stream_one,
            norm_rows,
            weights_three,
            weights_out,
            row_kv,
            kv_left,
            kv_right,
        ],
        smem=(0,),
    )
    dprobs_other = along_core(dprobs)

    def attend_row_back(
        spot_ref,
        weight_ref,
        dprobs_ref,
        other_ref,
        scores_ref,
        probs_ref,
        q_ref,
        near_ref,
        left_ref,
        right_ref,
        dmix_ref,
        dq_ref,
        dkv_ref,
        to_left_ref,
        to_right_ref,
    ):
        mask = head_mask(width, model)
        dprob = dprobs_ref[...] + other_ref[...]
        probs_here, scores_here = probs_ref[...], scores_ref[...]
        rows = lax.broadcasted_iota(jnp.int32, (fold, 1), 0) % width
        weight = jnp.where(rows + spot_ref[3] * width < spot_ref[4], entropy_weight / (HEADS * weight_ref[6:7, 0:1]), 0.0)
        first = dprob - jnp.sum(probs_here * dprob, axis=-1, keepdims=True)
        second = scores_here - jnp.sum(probs_here * scores_here, axis=-1, keepdims=True)
        dscores = (probs_here * (first - weight * second)).astype(bf16)
        low_probs = probs_here.astype(bf16)
        for slot in range(chips):
            at = slot_rows(slot)
            keys = window_rows(spot_ref, near_ref, left_ref, right_ref, 0, slot, width)
            dq_ref[at] = (
                fold_heads(dot(dscores, keys), mask, width) * row_scale
            ).astype(bf16)
            dkeys = dot_tokens(dscores, spread_heads(q_ref[at], mask)) * row_scale
            dvalues = dot_tokens(low_probs, spread_heads(dmix_ref[at], mask))
            for index, item in enumerate((dkeys, dvalues)):
                to_left_ref[index, at] = item[:width].astype(bf16)
                dkv_ref[index, at] = item[width : 2 * width]
                to_right_ref[index, at] = item[2 * width :].astype(bf16)

    row_dq, row_dkv, edge_left, edge_right = kernel_call(
        attend_row_back,
        [
            ((toks, model), bf16),
            ((2, toks, model), f32),
            ((2, toks, model), bf16),
            ((2, toks, model), bf16),
        ],
        [
            spot,
            norm_rows,
            dprobs,
            dprobs_other,
            scores,
            probs,
            row_q,
            row_kv,
            kv_left,
            kv_right,
            row_dmix,
        ],
        smem=(0,),
    )
    col_sums = layer_grads(
        normed_two,
        col_mix,
        col_low_far,
        col_mix_far,
        col_mine,
        after(along_core(col_give), edge_left),
        out_parts,
    )
    edge_from_right = to_left(edge_left)
    edge_from_left = to_right(edge_right)
    feed_slices = split_chips([feed_mine, along_core(after(feed_give, edge_left))], 2, 0)
    feed_keep, feed_swap = split_cores(over_chips(feed_slices), 2, 0)

    def input_back(
        spot_ref,
        dq_ref,
        dkv_ref,
        from_right_ref,
        from_left_ref,
        low_one_ref,
        done_ref,
        zero_ref,
        norm_ref,
        row_ref,
        two_ref,
        three_ref,
        entropy_ref,
        mine_ref,
        give_ref,
        sums_ref,
        *slot_refs,
    ):
        at_core = spot_ref[2]
        dq = dq_ref[...]
        dk, dv = (
            jnp.concatenate(
                [
                    (
                        dkv_ref[index, slot_rows(slot)]
                        + from_left_ref[index, slot_span(spot_ref, 5, slot, width)].astype(f32)
                        + from_right_ref[index, slot_span(spot_ref, 6, slot, width)].astype(f32)
                    ).astype(bf16)
                    for slot in range(chips)
                ],
                axis=0,
            )
            for index in (0, 1)
        )
        for index, item in enumerate((dq, dk, dv, low_one_ref[...])):
            mine_ref[index] = half_of(item, at_core, half)
            give_ref[index] = half_of(item, 1 - at_core, half)
        back = dot_back(dq, row_ref[0]) + dot_back(dk, row_ref[1]) + dot_back(dv, row_ref[2])
        unit, scale = unit_norm(zero_ref[...])
        sums_ref[0:2] = norm_sums(back, unit)
        sums_ref[2:4] = two_ref[...]
        sums_ref[4:6] = three_ref[...]
        sums_ref[6:7] = entropy_ref[...]
        sums_ref[7:8] = jnp.zeros((1, model), f32)
        result = (done_ref[...] + unit_norm_back(back, unit, scale, norm_ref[0:1])).astype(bf16)
        for slot in range(chips):
            slot_refs[slot][...] = result[slot_rows(slot)]

    row_mine, row_give, sums, *grad_slots = kernel_call(
        input_back,
        [
            ((4, toks, half), bf16),
            ((4, toks, half), bf16),
            ((lines, model), f32),
        ]
        + [((width, model), bf16)] * chips,
        [
            spot,
            row_dq,
            row_dkv,
            edge_from_right,
            edge_from_left,
            grad_one_low,
            grad_one,
            stream_zero,
            norm_rows,
            weights_row,
            sums_two,
            sums_three,
            entropy_row,
        ],
        smem=(0,),
    )

    def join_halves(spot_ref, keep_rows, got_rows):
        first = spot_ref[2] == 0
        return jnp.concatenate(
            [jnp.where(first, keep_rows, got_rows), jnp.where(first, got_rows, keep_rows)], axis=1
        )

    def over_cols(whole):
        return [whole] + [along_cols(whole, step) for step in col_steps]

    def order_rows(slices, at):
        def order_slots(spot_ref, *refs):
            for hop, ref in enumerate(refs[:-1]):
                refs[-1][0, chunk_at(spot_ref, spot_ref[1] ^ hop)] = jnp.concatenate(
                    [ref[at : at + width], ref[at + width : at + 2 * width]], axis=1
                )

        return kernel_call(order_slots, [(tokens.shape, bf16)], [spot, *slices], smem=(0,))[0]

    feed_back = along_core(feed_swap)
    col_parts = [col_sums[0]] + [along_cols(col_sums[step], step) for step in col_steps]
    col_slices = split_chips(col_parts, 1, 0, stream=stream_two, slots=grad_slots)
    col_reached = over_chips(col_slices)
    col_keep, col_swap = split_cores(col_reached, 1, 0)

    def join_two(spot_ref, keep_ref, got_ref, keep2_ref, got2_ref, out_ref):
        rows = 2 * shard
        out_ref[:rows] = join_halves(spot_ref, keep_ref[...], got_ref[...])
        out_ref[rows:] = join_halves(spot_ref, keep2_ref[...], got2_ref[...])

    (pair,) = kernel_call(
        join_two,
        [((3 * shard, model), bf16)],
        [spot, feed_keep, feed_back, col_keep, along_core(col_swap)],
        smem=(0,),
    )
    pair_ends = over_cols(pair)

    def spread_pair(spot_ref, u0, u1, u2, u3, in_ref, out_ref, g0, g1, g2, g3, all_ref):
        for step, ref in enumerate((u0, u1, u2, u3)):
            all_ref[spot_ref[0] ^ step] = ref[...]
        for source, grad_ref in enumerate((g0, g1, g2, g3)):
            wide = all_ref[source, :shard].astype(f32)
            for index in range(seqs):
                at = index * block_cols + source * part
                in_ref[:, at : at + part] = wide[:, index * part : (index + 1) * part]
            out_ref[source * part : (source + 1) * part] = all_ref[
                source, shard : 2 * shard
            ].astype(f32)
            grad_ref[...] = all_ref[source, 2 * shard :].astype(f32)

    row_parts = row_layer_grads(
        normed_one,
        row_mix,
        row_low_far,
        row_mix_far,
        row_mine,
        along_core(row_give),
        [sums],
    )
    row_sends = after(row_parts, col_parts, feed_keep)
    row_x, row_y = along_cols(row_sends[0], 1), along_cols(row_sends[1], 2)
    keep, give, keep2, give2 = fold_pairs(row_parts, row_x, row_y, extra)
    row_slices = row_layer_chips(
        keep, along_cols(give, 2), keep2, along_cols(give2, 1), extra, [], []
    )
    row_reached = over_chips(row_slices)
    result = order_rows(col_reached, block)
    grad_in = order_rows(col_reached, block + 2 * width)
    row_keep, row_swap = split_cores(after(row_reached, result, grad_in), 1, extra)

    row_got_back = along_core(row_swap)

    def join_row(spot_ref, keep_ref, got_ref, out_ref):
        out_ref[...] = join_halves(spot_ref, keep_ref[:shard], got_ref[:shard])

    (row_join,) = kernel_call(
        join_row, [((shard, model), bf16)], [spot, row_keep, row_got_back], smem=(0,)
    )

    def pick_norms(spot_ref, keep_ref, got_ref, norm_ref, entropy_ref):
        total = keep_ref[shard:].astype(f32) + got_ref[shard:].astype(f32)
        line = total[6:7]
        entropy_ref[...] = line[:, 0:1] + line[:, 1:2]
        wide = jnp.concatenate([total[:lines], total[lines:]], axis=1)
        at = spot_ref[1] * 2 + spot_ref[2]
        found = wide[:, :shard]
        for index in range(1, seqs):
            here = wide[:, index * shard : (index + 1) * shard]
            found = jnp.where(at == index, here, found)
        norm_ref[...] = found

    norm_here, entropy_sum = kernel_call(
        pick_norms,
        [((lines, shard), f32), ((1, 1), f32)],
        [spot, row_keep, after(row_got_back, row_join)],
        smem=(0,),
    )
    row_ends = over_cols(after(row_join, pair_ends))
    grad_feed_in, grad_feed_out, *col_grads = kernel_call(
        spread_pair,
        [(feed_in.shape, f32), (feed_out.shape, f32)] + [((shard, model), f32)] * cols_axis,
        [spot, *after(pair_ends, row_join)],
        smem=(0,),
        scratch=[pltpu.VMEM((cols_axis, 3 * shard, model), bf16)],
        room=24,
    )

    def spread_row(spot_ref, *refs):
        ins, outs, all_ref = refs[:cols_axis], refs[cols_axis:-1], refs[-1]
        for step, ref in enumerate(ins):
            all_ref[spot_ref[0] ^ step] = ref[...]
        for matrix in range(cols_axis):
            outs[matrix][...] = all_ref[matrix].astype(f32)

    row_grads = kernel_call(
        spread_row,
        [((shard, model), f32)] * cols_axis,
        [spot, *row_ends],
        smem=(0,),
        scratch=[pltpu.VMEM((cols_axis, shard, model), bf16)],
    )
    entropy = entropy_sum[0, 0] / (HEADS * norm_rows[6, 0])

    return (
        result,
        entropy,
        grad_in,
        *[norm_here[index] for index in range(6)],
        *row_grads,
        *col_grads,
        grad_feed_in,
        grad_feed_out,
    )


def fits_fast(tokens, feed_out):
    chips = lax.axis_size("seq") // 2
    return (
        lax.axis_size("col") == 4
        and lax.axis_size("seq") == 8
        and tokens.shape[0] == 1
        and tokens.shape[1] == chips * WINDOW
        and tokens.shape[2] == HEADS * HEAD_DIM
        and feed_out.shape[0] * 2 == tokens.shape[2]
    )


def on_device(tokens, offsets, band, col_counts, *rest):
    if not fits_fast(tokens, rest[15]):
        return general_plan(tokens, offsets, band, col_counts, *rest)
    return fast_plan(
        tokens,
        offsets,
        band,
        col_counts,
        rest[0:6],
        rest[6:10],
        rest[10:14],
        rest[14],
        rest[15],
        rest[16],
    )


def solution(mesh):
    return jax.shard_map(
        on_device,
        mesh=mesh,
        in_specs=(
            P("seq", "col", None),
            P(),
            P("col", None),
            P("col"),
            P("seq"),
            P("seq"),
            P("seq"),
            P("seq"),
            P("seq"),
            P("seq"),
            P("seq", None),
            P("seq", None),
            P("seq", None),
            P("seq", None),
            P("seq", None),
            P("seq", None),
            P("seq", None),
            P("seq", None),
            P("seq", None),
            P("seq", None),
            P("seq", "col", None),
        ),
        out_specs=(
            P("seq", "col", None),
            P(),
            P("seq", "col", None),
            P("seq"),
            P("seq"),
            P("seq"),
            P("seq"),
            P("seq"),
            P("seq"),
            P("seq", None),
            P("seq", None),
            P("seq", None),
            P("seq", None),
            P("seq", None),
            P("seq", None),
            P("seq", None),
            P("seq", None),
            P("seq", None),
            P("seq", None),
        ),
        check_vma=False,
    )
```
